32 devices in a mesh: weights: 4 (over y, x), context: 2 (over core), tensor: 4 (over z).
Axes of the slice: x: 2, y: 2, z: 4, core: 2. Of those that a mesh axis runs over, the one named last changes fastest.
Arguments:
- layer_in: bfloat16 [4, 1024, 2048], P('weights', 'context'), may hold values from -6 to 6
- norm_gains: bfloat16 [2048, 2], P(('weights', 'context')), may hold values from 0.5 to 1.5
- qkv_weight: bfloat16 [2048, 3, 2048], P(('weights', 'context'), None, 'tensor'), may hold values from -0.125 to 0.125
- qk_gains: bfloat16 [128, 2, 16], P(('weights', 'context'), None, 'tensor'), may hold values from 0.5 to 1.5
- out_weight: bfloat16 [2048, 2048], P(('weights', 'context'), 'tensor'), may hold values from -0.5 to 0.5
- router: bfloat16 [2048, 16], P(('weights', 'context')), may hold values from -0.0625 to 0.0625
- expert_in: bfloat16 [16, 2, 2048, 1024], P(('weights', 'context'), None, None, 'tensor'), may hold values from -0.125 to 0.125
- expert_out: bfloat16 [16, 1024, 2048], P(('weights', 'context'), 'tensor'), may hold values from -1.75 to 1.75
- grad_out: bfloat16 [4, 1024, 2048], P('weights', 'context'), may hold values from -6 to 6
- segments: int32 [4, 1024], P('weights'), may hold values from 0 to 15, never falling along the last dimension, each value on 1 to 512 neighbouring positions
- routes: int32 [4, 1024, 8], P('weights', 'context'), may hold values from 0 to 15, all different within a row
- route_order: int32 [4, 2, 4096], P('weights', 'context'), may hold values from 0 to 4095, each once within a row
Outputs:
- layer_out: bfloat16 [4, 1024, 2048], P('weights', 'context')
- grad_in: float32 [4, 1024, 2048], P('weights', 'context')
- grad_norm_gains: float32 [2048, 2], P(('weights', 'context', 'tensor'))
- grad_qkv: float32 [2048, 3, 2048], P(('weights', 'context'), None, 'tensor')
- grad_qk_gains: float32 [128, 2, 16], P(('weights', 'context'), None, 'tensor')
- grad_out_weight: float32 [2048, 2048], P(('weights', 'context'), 'tensor')
- grad_router: float32 [2048, 16], P(('weights', 'context'), 'tensor')
- grad_expert_in: float32 [16, 2, 2048, 1024], P(('weights', 'context'), None, None, 'tensor')
- grad_expert_out: float32 [16, 1024, 2048], P(('weights', 'context'), 'tensor')
The draws below stay inside these ranges and needn't reach their ends.
Inputs may be any that keep to these rules, and one draw needn't show every extreme that they name: `segments`: segment numbers never fall along a sequence; each segment covers 1 to 512 tokens, and one covers exactly 512. The 8 routes of a token name different experts; every expert is named by some token. `route_order`: within each device block the 4096 values, over pairs in token-major order, are each of 0 to 4095 once.
All inputs are finite; a program needn't handle non-finite values.
Results may differ from the reference program's by a relative error of at most 0.015.
Values may be sent and summed in bfloat16 or wider, within the bound.
A program may use at most 384 MiB of HBM per device.

```python
import math
import jax
import jax.numpy as jnp
import numpy as np
from jax import lax

D = 2048
HEADS = 16
HD = 128
FF = 1024
TOP = 8
LEN = 1024
SEQ_DEV = 1
EXPERTS = 16
HALF = 512
TOK_DEV = 512
SEQS = 4
PAIRS = 4096
CAP = 288
N_WEIGHTS = 4
N_CONTEXT = 2


def block_levels(rng, shape, cuts, least, largest):
    def one(position, shards_of):
        steps = jax.random.uniform(jax.random.fold_in(jax.random.fold_in(rng, 6), position), (shards_of,), jnp.float32, least / len(cuts), largest / len(cuts))
        return jnp.repeat(jnp.exp(steps), shape[position] // shards_of).reshape((-1,) + (1,) * (len(shape) - position - 1))

    factor_of = one(*cuts[0])
    for cut in cuts[1:]:
        factor_of = factor_of * one(*cut)
    return factor_of


def different_ones(stream_key, rows, number_of, top, lift):
    ranking = jax.random.permutation(jax.random.fold_in(stream_key, 1), number_of)
    favour = ranking
    for power in range(3):
        favour = favour * favour // number_of
    favour = favour * lift // number_of
    chance = jax.random.randint(jax.random.fold_in(stream_key, 2), (rows, number_of), 0, 4096) + favour
    fixed_rows = jax.random.permutation(jax.random.fold_in(stream_key, 3), rows)[jnp.arange(number_of) % rows]
    chance = jnp.where(jnp.arange(rows)[:, None] == fixed_rows[None, :], 1 << 14, chance)
    merit = chance * number_of + jnp.arange(number_of)
    return lax.top_k(merit.astype(jnp.int32), top)[1].astype(jnp.int32)


def profile(number_of, total, bound, skew):
    loads = [(1 << 20) // math.isqrt(standing ** skew) + 1 for standing in range(2, number_of + 1)]
    spare, holding = total - bound - (number_of - 1), [1] * (number_of - 1)
    while spare > 0:
        movable = [i for i in range(number_of - 1) if holding[i] < bound]
        pool, remaining = sum([loads[i] for i in movable]), spare
        for i in movable:
            addition = min(bound - holding[i], max(1, remaining * loads[i] // pool), spare)
            holding[i] = holding[i] + addition
            spare = spare - addition
    return np.array([bound] + holding)


def uneven_parts(rng, count, total, bound, skew):
    if count == 2:
        one = jax.random.randint(rng, (), max(1, total - bound), min(bound, total - 1) + 1)
        return jnp.stack([one, total - one])
    lengths = jnp.asarray(profile(count, total, bound, skew), jnp.int32)
    twos = (count - 1) // 2
    donor, sink = lengths[1:1 + 2 * twos:2], lengths[2:2 + 2 * twos:2]
    slack = jnp.minimum(donor - 1, bound - sink)
    shifted = jax.random.randint(jax.random.fold_in(rng, 1), (twos,), 0, 1 << 20) % (slack + 1)
    lengths = lengths.at[1:1 + 2 * twos:2].set(donor - shifted).at[2:2 + 2 * twos:2].set(sink + shifted)
    return lengths[jax.random.permutation(jax.random.fold_in(rng, 2), count)]


def scatter_about(own_key, dims, scale, reach, cuts=(), kind=jnp.bfloat16):
    values = jax.random.normal(own_key, dims, jnp.float32) * scale
    if len(cuts) > 0:
        values = block_levels(own_key, dims, cuts, -0.22, 0.18) * values
    return jnp.clip(values, min=-reach, max=reach).astype(kind)


def setup_inputs(seed: int = 0) -> dict:
    arg_keys = jax.random.split(jax.random.key(seed), 13)
    layer_in = scatter_about(arg_keys[0], (SEQS, LEN, D), 1.0, 6.0, ((0, 4), (1, 2)))
    norm_gains = jnp.clip(1.0 + 0.1 * jax.random.normal(arg_keys[1], (D, 2), jnp.float32), 0.5, 1.5).astype(jnp.bfloat16)
    qkv_weight = scatter_about(arg_keys[2], (D, 3, D), D ** -0.5, 0.125, ((0, 8), (2, 4)))
    qk_gains = jnp.clip(1.0 + 0.1 * jax.random.normal(arg_keys[3], (HD, 2, HEADS), jnp.float32), 0.5, 1.5).astype(jnp.bfloat16)
    out_weight = scatter_about(arg_keys[4], (D, D), (D // 16) ** -0.5, 0.5, ((0, 8), (1, 4)))
    router = scatter_about(arg_keys[5], (D, EXPERTS), (4 * D) ** -0.5, 0.0625, ((0, 8),))
    expert_in = scatter_about(arg_keys[6], (EXPERTS, 2, D, FF), D ** -0.5, 0.125, ((0, 8), (3, 4)))
    expert_out = scatter_about(arg_keys[7], (EXPERTS, FF, D), (EXPERTS * 0.6 / FF ** 0.5), 1.75, ((0, 8), (1, 4)))
    grad_out = scatter_about(arg_keys[8], (SEQS, LEN, D), 1.0, 6.0, ((0, 4), (1, 2)))
    segments = jax.vmap(lambda own: jnp.searchsorted(jnp.cumsum(uneven_parts(own, max(LEN // 64, 3), LEN, HALF, 2)), jnp.arange(LEN), side="right"))(jax.random.split(arg_keys[9], SEQS)).reshape((SEQS, LEN)).astype(jnp.int32)
    routes = different_ones(arg_keys[10], SEQS * LEN, EXPERTS, TOP, 4096).reshape((SEQS, LEN, TOP))
    route_order = jax.vmap(lambda own: jax.random.permutation(own, PAIRS))(jax.random.split(arg_keys[11], N_WEIGHTS * N_CONTEXT)).reshape((N_WEIGHTS, N_CONTEXT, PAIRS)).astype(jnp.int32)
    return dict(layer_in=layer_in, norm_gains=norm_gains, qkv_weight=qkv_weight, qk_gains=qk_gains, out_weight=out_weight, router=router, expert_in=expert_in, expert_out=expert_out, grad_out=grad_out, segments=segments, routes=routes, route_order=route_order)


epsilon = 1e-05
rotary_base = 10000.0

@jax.custom_vjp
def low(v):
    return lax.optimization_barrier(v.astype(jnp.bfloat16)).astype(jnp.float32)

@jax.custom_vjp
def low_back(v):
    return v

def low_keep(v):
    return (low(v), None)

def low_pass(kept, grad):
    return (grad,)

def back_keep(v):
    return (v, None)

def back_low(kept, grad):
    return (low(grad),)
low.defvjp(low_keep, low_pass)
low_back.defvjp(back_keep, back_low)

def rotate_half(values_in):
    middle = values_in.shape[-1] // 2
    return jnp.concatenate([-values_in[..., middle:], values_in[..., :middle]], axis=-1)

def rotary_tables(positions, head_size):
    frequency = rotary_base ** (-(2.0 * jnp.arange(head_size // 2, dtype=jnp.float32)) / head_size)
    angle_table = positions.astype(jnp.float32)[:, None] * frequency[None, :]
    angle_table = jnp.concatenate([angle_table, angle_table], axis=1)
    return (jnp.cos(angle_table), jnp.sin(angle_table))

def place_pairs(pair_expert, rank, expert_total, capacity):
    pair_count = pair_expert.shape[0]
    by_rank = jnp.zeros((pair_count,), jnp.int32).at[rank].set(jnp.arange(pair_count, dtype=jnp.int32))
    sorted_expert = pair_expert[by_rank]
    onehot = (sorted_expert[:, None] == jnp.arange(expert_total, dtype=jnp.int32)[None, :]).astype(jnp.int32)
    running = jnp.cumsum(onehot, axis=0)
    sorted_slot = (lax.optimization_barrier(jnp.sum(running * onehot, axis=1)) - 1).astype(jnp.int32)
    slot_index = jnp.zeros((pair_count,), jnp.int32).at[by_rank].set(sorted_slot)
    kept_pair = slot_index < capacity
    dest_row = jnp.where(kept_pair, pair_expert * capacity + slot_index, expert_total * capacity).astype(jnp.int32)
    slot_pair = jnp.full((expert_total * capacity + 1,), pair_count, jnp.int32).at[dest_row].set(jnp.arange(pair_count, dtype=jnp.int32))[:-1]
    return (kept_pair, dest_row, slot_pair)

def attention_sequence(seq_input, seg_ids, gain_table, qkv_matrix, qk_gain, out_matrix):
    highest = lax.Precision.HIGHEST
    scale_one = lax.rsqrt(lax.optimization_barrier(jnp.mean(seq_input * seq_input, axis=1, keepdims=True)) + epsilon)
    normed_one = low(seq_input * scale_one * gain_table[:, 0])
    projected = jnp.einsum('td,dgf->tgf', normed_one, qkv_matrix, precision=highest)
    query_raw = low_back(projected[:, 0])
    key_raw = low_back(projected[:, 1])
    value_low = low(low_back(projected[:, 2])).reshape(LEN, HEADS, HD)
    query_scale = lax.rsqrt(lax.optimization_barrier(jnp.mean(query_raw * query_raw, axis=1, keepdims=True)) + epsilon)
    key_scale = lax.rsqrt(lax.optimization_barrier(jnp.mean(key_raw * key_raw, axis=1, keepdims=True)) + epsilon)
    query_gain = qk_gain[:, 0, :].T.reshape(D)
    key_gain = qk_gain[:, 1, :].T.reshape(D)
    query_hat = (query_raw * query_scale * query_gain).reshape(LEN, HEADS, HD)
    key_hat = (key_raw * key_scale * key_gain).reshape(LEN, HEADS, HD)
    positions = jnp.arange(LEN, dtype=jnp.int32)
    cosine_table, sine_table = rotary_tables(positions, HD)
    cosine_table = cosine_table[:, None, :]
    sine_table = sine_table[:, None, :]
    query_rot = low(query_hat * cosine_table + rotate_half(query_hat) * sine_table)
    key_rot = low(key_hat * cosine_table + rotate_half(key_hat) * sine_table)
    allowed = (positions[None, :] <= positions[:, None]) & (seg_ids[:, None] == seg_ids[None, :])
    scores = low_back(jnp.einsum('qhd,khd->hqk', query_rot, key_rot, precision=highest) / math.sqrt(HD))
    scores = jnp.where(allowed[None], scores, -1e+30)
    attn_probs = low(jax.nn.softmax(scores, axis=-1))
    attended = jnp.einsum('hqk,khd->qhd', attn_probs, value_low, precision=highest).reshape(LEN, D)
    attended_low = low(low_back(attended))
    return seq_input + low_back(jnp.dot(attended_low, out_matrix.T, precision=highest))

def expert_block(hidden, block_routes, block_rank, gain_table, router_matrix, in_experts, out_experts):
    highest = lax.Precision.HIGHEST
    scale_two = lax.rsqrt(lax.optimization_barrier(jnp.mean(hidden * hidden, axis=1, keepdims=True)) + epsilon)
    normed_two = low(hidden * scale_two * gain_table[:, 1])
    logits = low_back(jnp.dot(normed_two, router_matrix, precision=highest))
    router_probs = jax.nn.softmax(logits, axis=1)
    kept_pair, dest_row, slot_pair = place_pairs(block_routes.reshape(PAIRS), block_rank, EXPERTS, CAP)
    padded = jnp.concatenate([normed_two, jnp.zeros((1, D), normed_two.dtype)], axis=0)
    slot_inputs = padded[slot_pair // TOP].reshape(EXPERTS, CAP, D)
    both_pre = jnp.einsum('ecd,egdf->ecgf', slot_inputs, in_experts, precision=highest)
    gate_pre = low_back(both_pre[:, :, 0])
    up_pre = low_back(both_pre[:, :, 1])
    activated = low(jax.nn.silu(gate_pre) * up_pre)
    results = low_back(jnp.einsum('ecf,efd->ecd', activated, out_experts, precision=highest)).reshape(EXPERTS * CAP, D)
    padded_results = jnp.concatenate([results, jnp.zeros((1, D), results.dtype)], axis=0)
    picked = padded_results[dest_row].reshape(TOK_DEV, TOP, D)
    gate_weight = jnp.take_along_axis(router_probs, block_routes, axis=1) * kept_pair.reshape(TOK_DEV, TOP).astype(router_probs.dtype)
    return hidden + lax.optimization_barrier(jnp.sum(gate_weight[:, :, None] * picked, axis=1))

def reference(layer_in, norm_gains, qkv_weight, qk_gains, out_weight, router, expert_in, expert_out, grad_out, segments, routes, route_order):
    promoted = tuple((array.astype(jnp.float32) for array in (layer_in, norm_gains, qkv_weight, qk_gains, out_weight, router, expert_in, expert_out)))
    route_blocks = routes.reshape(N_WEIGHTS, SEQ_DEV, N_CONTEXT, HALF, TOP).transpose(0, 2, 1, 3, 4).reshape(-1, TOK_DEV, TOP)
    rank_blocks = route_order.reshape(-1, PAIRS)

    def forward(layer_float, gain_table, qkv_matrix, qk_gain, out_matrix, router_matrix, in_experts, out_experts):

        def seq_step(carried, seq_item):
            return (carried, attention_sequence(seq_item[0], seq_item[1], gain_table, qkv_matrix, qk_gain, out_matrix))
        unused, hidden = lax.scan(jax.checkpoint(seq_step), jnp.zeros((), jnp.float32), (layer_float, segments))
        blocks = hidden.reshape(N_WEIGHTS, SEQ_DEV, N_CONTEXT, HALF, D).transpose(0, 2, 1, 3, 4).reshape(-1, TOK_DEV, D)

        def block_step(block_item):
            return expert_block(block_item[0], block_item[1], block_item[2], gain_table, router_matrix, in_experts, out_experts)
        mixed = lax.map(jax.checkpoint(block_step), (blocks, route_blocks, rank_blocks))
        return mixed.reshape(N_WEIGHTS, N_CONTEXT, SEQ_DEV, HALF, D).transpose(0, 2, 1, 3, 4).reshape(SEQS, LEN, D)
    result, pullback = jax.vjp(forward, *promoted)
    gradients = pullback(grad_out.astype(jnp.float32))
    return (result.astype(jnp.bfloat16), gradients[0], gradients[1], gradients[2], gradients[3], gradients[4], gradients[5], gradients[6], gradients[7])
```

```python
import functools
import math

import jax
import jax.numpy as jnp
from jax import lax
from jax.experimental import pallas as pl
from jax.experimental.pallas import tpu as pltpu
from jax.sharding import PartitionSpec as P

epsilon = 1e-05
rotary_base = 10000.0
WEIGHTS, CONTEXT, TENSOR = ("weights", "context", "tensor")
GROUP = (WEIGHTS, CONTEXT)
EVERYONE = (WEIGHTS, CONTEXT, TENSOR)
MESH = pl.DeviceIdType.MESH
BY_SCORE = "sqhd,skhd->shqk"
BY_QUERY = "shqk,skhd->sqhd"
BY_KEY = "shqk,sqhd->skhd"


def passed_along(value, axis, steps):
    count = lax.axis_size(axis)
    leading, last = (max(0, -steps), min(count, count - steps))
    return lax.ppermute(value, axis, [(source, source + steps) for source in range(leading, last)])


def rotate_half(values_in):
    middle = values_in.shape[-1] // 2
    return jnp.concatenate([-values_in[..., middle:], values_in[..., :middle]], axis=-1)


def rotate_back(grads_in):
    middle = grads_in.shape[-1] // 2
    return jnp.concatenate([grads_in[..., middle:], -grads_in[..., :middle]], axis=-1)


def rotary_tables(positions, head_size):
    frequency = rotary_base ** (-(2.0 * jnp.arange(head_size // 2, dtype=jnp.float32)) / head_size)
    angle_table = positions.astype(jnp.float32)[:, None] * frequency[None, :]
    angle_table = jnp.concatenate([angle_table, angle_table], axis=1)
    return (jnp.cos(angle_table), jnp.sin(angle_table))


def pair_slots(token_routes, token_ranks, expert_total):
    unused = token_routes.size
    hot = token_routes.T[None] == jnp.arange(expert_total, dtype=jnp.int32)[:, None, None]
    rank_of = jnp.min(jnp.where(hot, token_ranks.T[None], unused), axis=1)
    slot_of = jnp.sum((rank_of[:, :, None] < rank_of[:, None, :]).astype(jnp.int32), axis=1)
    return (rank_of < unused, slot_of)


def place_pairs(pair_expert, rank, expert_total, capacity, top_count):
    pair_count = pair_expert.shape[0]
    token_routes = pair_expert.reshape(-1, top_count)
    slot_of = pair_slots(token_routes, rank.reshape(-1, top_count), expert_total)[1]
    slot_index = jnp.take_along_axis(slot_of.T, token_routes, axis=1).reshape(pair_count)
    kept_pair = slot_index < capacity
    dest_row = jnp.where(kept_pair, pair_expert * capacity + slot_index, expert_total * capacity)
    slot_pair = (
        jnp.full((expert_total * capacity + 1,), pair_count, jnp.int32)
        .at[dest_row]
        .set(jnp.arange(pair_count, dtype=jnp.int32))[:-1]
    )
    return (kept_pair, dest_row, slot_pair)


def row_sums(partial_rows):
    return lax.psum(partial_rows, TENSOR)


def tensor_sum(partial_rows):
    return lax.psum(partial_rows, TENSOR)


def to_owners(slot_rows):
    return lax.all_to_all(
        slot_rows, GROUP, split_axis=0, concat_axis=0, tiled=True
    )


def expert_front(slot_inputs, expert_in):
    both_pre = jnp.einsum(
        "sncd,ngdf->sncgf", slot_inputs, expert_in, preferred_element_type=jnp.float32
    )
    return (both_pre[..., 0, :], both_pre[..., 1, :])


def per_device_slots(
    layer_in,
    norm_gains,
    qkv_weight,
    qk_gains,
    out_weight,
    router,
    expert_in,
    expert_out,
    grad_out,
    segments,
    routes,
    route_order,
):
    group_count = lax.axis_size(GROUP)
    tensor_count = lax.axis_size(TENSOR)
    context_rank = lax.axis_index(CONTEXT)
    tensor_rank = lax.axis_index(TENSOR)
    seq_count, half_len, model_width = layer_in.shape
    token_count = seq_count * half_len
    top_count = routes.shape[2]
    qkv_full, out_full, qk_gain_full, gain_full, router_full = (
        lax.all_gather(qkv_weight, GROUP, axis=0, tiled=True),
        lax.all_gather(out_weight, GROUP, axis=0, tiled=True),
        lax.all_gather(qk_gains, GROUP, axis=0, tiled=True),
        lax.all_gather(norm_gains, GROUP, axis=0, tiled=True),
        lax.all_gather(router, GROUP, axis=0, tiled=True),
    )
    head_size = qk_gain_full.shape[0]
    local_heads = qk_gain_full.shape[2]
    expert_total = router_full.shape[1]
    gain_attn = gain_full[:, 0].astype(jnp.float32)
    gain_ffn = gain_full[:, 1].astype(jnp.float32)
    query_gain = qk_gain_full[:, 0, :].astype(jnp.float32).T.reshape(-1)
    key_gain = qk_gain_full[:, 1, :].astype(jnp.float32).T.reshape(-1)
    inv_root = 1.0 / math.sqrt(head_size)
    residual = layer_in.reshape(token_count, model_width).astype(jnp.float32)
    scale_one = lax.rsqrt(jnp.mean(residual * residual, axis=1, keepdims=True) + epsilon)
    unit_one = residual * scale_one
    normed_one = (unit_one * gain_attn).astype(jnp.bfloat16)
    projected = jnp.einsum("td,dgf->tgf", normed_one, qkv_full, preferred_element_type=jnp.float32)
    query_raw = projected[:, 0]
    key_raw = projected[:, 1]
    value_raw = projected[:, 2]
    square_sums = row_sums(
        jnp.stack(
            [jnp.sum(query_raw * query_raw, axis=1), jnp.sum(key_raw * key_raw, axis=1)], axis=1
        )
    )
    query_scale = lax.rsqrt(square_sums[:, 0:1] / model_width + epsilon)
    key_scale = lax.rsqrt(square_sums[:, 1:2] / model_width + epsilon)
    heads_shape = (seq_count, half_len, local_heads, head_size)
    query_hat = (query_raw * query_scale * query_gain).reshape(heads_shape)
    key_hat = (key_raw * key_scale * key_gain).reshape(heads_shape)
    query_pos = context_rank * half_len + jnp.arange(half_len, dtype=jnp.int32)
    cosine_table, sine_table = rotary_tables(query_pos, head_size)
    cosine_table = cosine_table[None, :, None, :]
    sine_table = sine_table[None, :, None, :]
    query_rot = (query_hat * cosine_table + rotate_half(query_hat) * sine_table).astype(
        jnp.bfloat16
    )
    key_rot = (key_hat * cosine_table + rotate_half(key_hat) * sine_table).astype(jnp.bfloat16)
    value_low = value_raw.astype(jnp.bfloat16).reshape(heads_shape)
    key_prev, value_prev = passed_along((key_rot, value_low), CONTEXT, 1)
    all_keys = jnp.concatenate([key_prev, key_rot], axis=1)
    all_values = jnp.concatenate([value_prev, value_low], axis=1)
    key_pos = jnp.concatenate([query_pos - half_len, query_pos])
    seg_query = lax.dynamic_slice_in_dim(segments, context_rank * half_len, half_len, 1)
    seg_prev = lax.dynamic_slice_in_dim(
        segments, jnp.maximum(context_rank - 1, 0) * half_len, half_len, 1
    )
    seg_keys = jnp.concatenate([seg_prev, seg_query], axis=1)
    causal = (key_pos[None, :] >= 0) & (key_pos[None, :] <= query_pos[:, None])
    allowed = causal[None] & (seg_query[:, :, None] == seg_keys[:, None, :])

    def score_block(queries, key_rows):
        raw_scores = (
            jnp.einsum(BY_SCORE, queries, key_rows, preferred_element_type=jnp.float32)
            * inv_root
        )
        return jnp.where(allowed[:, None], raw_scores, -1e30)

    scores = score_block(query_rot, all_keys)
    row_max = jnp.max(scores, axis=-1, keepdims=True)
    exponent = jnp.exp(scores - row_max)
    row_total = jnp.sum(exponent, axis=-1, keepdims=True)
    log_total = row_max + jnp.log(row_total)
    attn_probs = (exponent / row_total).astype(jnp.bfloat16)
    attended = jnp.einsum(
        BY_QUERY, attn_probs, all_values, preferred_element_type=jnp.float32
    )
    attended_low = attended.reshape(token_count, -1).astype(jnp.bfloat16)
    attn_partial = jnp.einsum(
        "tf,df->td", attended_low, out_full, preferred_element_type=jnp.float32
    )
    hidden = residual + tensor_sum(attn_partial)
    scale_two = lax.rsqrt(jnp.mean(hidden * hidden, axis=1, keepdims=True) + epsilon)
    unit_two = hidden * scale_two
    normed_two = (unit_two * gain_ffn).astype(jnp.bfloat16)
    logits = jnp.dot(normed_two, router_full, preferred_element_type=jnp.float32)
    router_probs = jax.nn.softmax(logits, axis=1)
    capacity = token_count * top_count * 9 // (8 * expert_total)
    local_experts = expert_in.shape[0]
    pair_count = token_count * top_count
    token_routes = routes.reshape(token_count, top_count)
    kept_pair, dest_row, slot_pair = place_pairs(
        token_routes.reshape(pair_count), route_order.reshape(pair_count), expert_total, capacity, top_count
    )
    zero_row = jnp.zeros((1, model_width), jnp.bfloat16)
    zero_wide = jnp.zeros((1, model_width), jnp.float32)
    slot_shape = (group_count, local_experts, capacity, model_width)
    dispatch_rows = jnp.concatenate([normed_two, zero_row], axis=0)[slot_pair // top_count].reshape(
        slot_shape
    )
    received = lax.all_to_all(
        dispatch_rows, GROUP, split_axis=0, concat_axis=0, tiled=True
    )
    gate_pre, up_pre = expert_front(received, expert_in)
    sigmoid_gate = jax.nn.sigmoid(gate_pre)
    silu_gate = gate_pre * sigmoid_gate
    activated = (silu_gate * up_pre).astype(jnp.bfloat16)
    expert_partial = jnp.einsum(
        "sncf,nfd->sncd", activated, expert_out, preferred_element_type=jnp.float32
    )
    kept_float = kept_pair.reshape(token_count, top_count).astype(jnp.float32)
    gate_weight = jnp.take_along_axis(router_probs, token_routes, axis=1) * kept_float
    upstream = grad_out.reshape(token_count, model_width).astype(jnp.float32)
    returned = to_owners(expert_partial).reshape(expert_total * capacity, model_width)
    picked = jnp.concatenate([returned, zero_wide], axis=0)[dest_row].reshape(
        token_count, top_count, model_width
    )
    moe_partial = jnp.sum(gate_weight[:, :, None] * picked, axis=1)
    dot_partial = jnp.sum(upstream[:, None, :] * picked, axis=2)
    moe_total, dot_total = lax.psum((moe_partial, dot_partial), TENSOR)
    layer_out = (hidden + moe_total).astype(jnp.bfloat16).reshape(layer_in.shape)
    d_gate = dot_total * kept_float
    route_hot = (
        token_routes[:, :, None] == jnp.arange(expert_total, dtype=jnp.int32)[None, None, :]
    ).astype(jnp.float32)
    d_probs = jnp.sum(d_gate[:, :, None] * route_hot, axis=1)
    d_logits = (
        router_probs * (d_probs - jnp.sum(router_probs * d_probs, axis=1, keepdims=True))
    ).astype(jnp.bfloat16)
    d_pair = (
        (gate_weight[:, :, None] * upstream[:, None, :])
        .astype(jnp.bfloat16)
        .reshape(pair_count, model_width)
    )
    d_slots = jnp.concatenate([d_pair, zero_row], axis=0)[slot_pair].reshape(slot_shape)
    d_received = lax.all_to_all(
        d_slots, GROUP, split_axis=0, concat_axis=0, tiled=True
    )
    d_activated = jnp.einsum(
        "sncd,nfd->sncf", d_received, expert_out, preferred_element_type=jnp.float32
    )
    grad_expert_out = jnp.einsum(
        "sncf,sncd->nfd", activated, d_received, preferred_element_type=jnp.float32
    )
    d_gate_pre = d_activated * up_pre * sigmoid_gate * (1.0 + gate_pre * (1.0 - sigmoid_gate))
    d_up_pre = d_activated * silu_gate
    d_both = jnp.stack([d_gate_pre, d_up_pre], axis=3).astype(jnp.bfloat16)
    d_inputs = jnp.einsum("sncgf,ngdf->sncd", d_both, expert_in, preferred_element_type=jnp.float32)
    grad_expert_in = jnp.einsum(
        "sncd,sncgf->ngdf", received, d_both, preferred_element_type=jnp.float32
    )
    d_returned = to_owners(d_inputs).reshape(expert_total * capacity, model_width)
    d_normed_part = jnp.sum(
        jnp.concatenate([d_returned, zero_wide], axis=0)[dest_row].reshape(
            token_count, top_count, model_width
        ),
        axis=1,
    )
    d_normed_two = tensor_sum(d_normed_part) + jnp.dot(
        d_logits, router_full.T, preferred_element_type=jnp.float32
    )
    d_router = jnp.dot(normed_two.T, d_logits, preferred_element_type=jnp.float32)
    d_gain_ffn = jnp.sum(d_normed_two * unit_two, axis=0)
    scaled_ffn = gain_ffn * d_normed_two
    d_hidden = upstream + scale_two * (
        scaled_ffn - unit_two * jnp.mean(scaled_ffn * unit_two, axis=1, keepdims=True)
    )
    d_hidden_low = d_hidden.astype(jnp.bfloat16)
    d_out_weight = jnp.einsum(
        "td,tf->df", d_hidden_low, attended_low, preferred_element_type=jnp.float32
    )
    d_attended = (
        jnp.dot(d_hidden_low, out_full, preferred_element_type=jnp.float32)
        .astype(jnp.bfloat16)
        .reshape(heads_shape)
    )
    probs_again = jnp.exp(score_block(query_rot, all_keys) - log_total)
    probs_again_low = probs_again.astype(jnp.bfloat16)
    d_probs_att = jnp.einsum(
        BY_SCORE, d_attended, all_values, preferred_element_type=jnp.float32
    )
    d_values_all = jnp.einsum(
        BY_KEY, probs_again_low, d_attended, preferred_element_type=jnp.float32
    )
    row_dot = jnp.sum(probs_again * d_probs_att, axis=-1, keepdims=True)
    d_scores = (probs_again * (d_probs_att - row_dot)).astype(jnp.bfloat16)
    d_query_rot = (
        jnp.einsum(BY_QUERY, d_scores, all_keys, preferred_element_type=jnp.float32)
        * inv_root
    )
    d_keys_all = (
        jnp.einsum(BY_KEY, d_scores, query_rot, preferred_element_type=jnp.float32)
        * inv_root
    )
    back_key, back_value = (
        passed_along(d_keys_all[:, :half_len].astype(jnp.bfloat16), CONTEXT, -1).astype(
            jnp.float32
        ),
        passed_along(d_values_all[:, :half_len].astype(jnp.bfloat16), CONTEXT, -1).astype(
            jnp.float32
        ),
    )
    d_key_rot = d_keys_all[:, half_len:] + back_key
    d_value = (d_values_all[:, half_len:] + back_value).reshape(token_count, -1)
    d_query_hat = (d_query_rot * cosine_table + rotate_back(d_query_rot * sine_table)).reshape(
        token_count, -1
    )
    d_key_hat = (d_key_rot * cosine_table + rotate_back(d_key_rot * sine_table)).reshape(
        token_count, -1
    )
    centre = row_sums(
        jnp.stack(
            [
                jnp.sum(query_gain * d_query_hat * query_raw, axis=1),
                jnp.sum(key_gain * d_key_hat * key_raw, axis=1),
            ],
            axis=1,
        )
    )
    d_query_raw = (
        query_scale * query_gain * d_query_hat
        - query_raw * (query_scale**3 / model_width) * centre[:, 0:1]
    )
    d_key_raw = (
        key_scale * key_gain * d_key_hat - key_raw * (key_scale**3 / model_width) * centre[:, 1:2]
    )
    d_query_gain = (
        jnp.sum(d_query_hat * query_raw * query_scale, axis=0).reshape(local_heads, head_size).T
    )
    d_key_gain = jnp.sum(d_key_hat * key_raw * key_scale, axis=0).reshape(local_heads, head_size).T
    d_qk_gains = jnp.stack([d_query_gain, d_key_gain], axis=1)
    d_projected = jnp.stack([d_query_raw, d_key_raw, d_value], axis=1).astype(jnp.bfloat16)
    d_normed_one = tensor_sum(
        jnp.einsum("tgf,dgf->td", d_projected, qkv_full, preferred_element_type=jnp.float32)
    )
    d_qkv = jnp.einsum("td,tgf->dgf", normed_one, d_projected, preferred_element_type=jnp.float32)
    d_gain_attn = jnp.sum(d_normed_one * unit_one, axis=0)
    scaled_attn = gain_attn * d_normed_one
    grad_in = d_hidden + scale_one * (
        scaled_attn - unit_one * jnp.mean(scaled_attn * unit_one, axis=1, keepdims=True)
    )
    d_norm_gains = jnp.stack([d_gain_attn, d_gain_ffn], axis=1)
    grad_qkv, grad_out_weight, grad_qk_gains, gain_rows, router_rows = (
        lax.psum_scatter(d_qkv, GROUP, scatter_dimension=0, tiled=True),
        lax.psum_scatter(d_out_weight, GROUP, scatter_dimension=0, tiled=True),
        lax.psum_scatter(d_qk_gains, GROUP, scatter_dimension=0, tiled=True),
        lax.psum_scatter(d_norm_gains, GROUP, scatter_dimension=0, tiled=True),
        lax.psum_scatter(d_router, GROUP, scatter_dimension=0, tiled=True),
    )
    gain_share = gain_rows.shape[0] // tensor_count
    grad_norm_gains = lax.dynamic_slice_in_dim(gain_rows, tensor_rank * gain_share, gain_share, 0)
    router_share = expert_total // tensor_count
    grad_router = lax.dynamic_slice_in_dim(router_rows, tensor_rank * router_share, router_share, 1)
    return (
        layer_out,
        grad_in.reshape(layer_in.shape),
        grad_norm_gains,
        grad_qkv,
        grad_qk_gains,
        grad_out_weight,
        grad_router,
        grad_expert_in,
        grad_expert_out,
    )


def contract_last(left, right):
    return lax.dot_general(
        left, right, (((1,), (1,)), ((), ())), preferred_element_type=jnp.float32
    )


def share_order(z):
    upper, odd = (z // 2, z % 2)
    return (z, z + 1 - 2 * upper, 2 + upper - 2 * odd, 3 - 3 * upper)


def experts_kernel(
    experts,
    x_ref,
    grads_ref,
    kept_ref,
    router_ref,
    in_ref,
    out_w_ref,
    x_out,
    dx_out,
    moe_out,
    gated_out,
    both_out,
    x_all,
    w_in,
    w_out,
    grads,
    dx_buf,
    moe_buf,
    gated,
    both,
    own_sem,
    weight_sem,
    grads_sem,
    store_sem,
    send_z,
    send_x,
    send_y,
    send_c,
    recv,
):
    w, c, z = (lax.axis_index(a) for a in (WEIGHTS, CONTEXT, TENSOR))
    wx, wy = (w + 1 - 2 * (w % 2), (w + 2) % 4)
    wd = wx + wy - w
    share, width = x_ref.shape
    half = width // 2
    lo, hi = (pl.ds(0, half), pl.ds(half, half))
    dev_x, dev_y, dev_c = ((wx, c, z), (wy, c, z), (w, 1 - c, z))
    order = share_order(z)
    hidden = out_w_ref.shape[1]
    group = w * 2 + c

    def loads():
        return [
        pltpu.make_async_copy(
            in_ref.at[n, g], w_in.at[:, pl.ds((2 * n + g) * hidden, hidden)], weight_sem.at[2 * n + g]
        )
        for n in range(2)
        for g in range(2)
    ] + [
        pltpu.make_async_copy(
            out_w_ref.at[n], w_out.at[pl.ds(n * hidden, hidden)], weight_sem.at[4 + n]
        )
        for n in range(2)
    ]

    for load in loads():
        load.start()

    def grads_load(zj, cc, slot):
        return pltpu.make_async_copy(grads_ref.at[:, cc, zj], grads.at[slot], grads_sem.at[slot])

    grads_load(z, c, 0).start()
    keep = lambda: pltpu.make_async_copy(x_ref, x_all.at[z, c, w], own_sem)
    keep().start()

    barrier = pltpu.get_barrier_semaphore()
    around = [(w, c, (z + 1) % 4), (w, c, (z + 3) % 4)]
    for device in [dev_x, dev_y, dev_c] + around:
        pl.semaphore_signal(barrier, inc=1, device_id=device, device_id_type=MESH)
    pl.semaphore_wait(barrier, 5)

    def view(chunk, cols):
        return x_all.at[chunk] if cols is None else x_all.at[chunk[0], chunk[1], chunk[2], :, cols]

    def copy(src, chunk, cols, slot, sem, device):
        return pltpu.make_async_remote_copy(
            src_ref=src,
            dst_ref=view(chunk, cols),
            send_sem=sem[0].at[sem[1:]],
            recv_sem=recv.at[chunk[0], chunk[1], slot],
            device_id=device,
            device_id_type=MESH,
        )

    sent = []
    devices_z = ((w, c, z + 1), (w, c, z - 1))

    def start(chunk, cols, slot, sem, device, src=None):
        copy(view(chunk, cols) if src is None else src, chunk, cols, slot, sem, device).start()
        sent.append((chunk, cols, slot, sem, device))

    def arrived(chunk, cols, slot):
        copy(view(chunk, cols), chunk, cols, slot, (send_c, 0, 0), dev_c).wait_recv()

    def spread(j):
        chunk = (order[j], c, w)
        src = x_ref if j == 0 else None
        start(chunk, None, 1, (send_x, j, 0), dev_x, src)
        start(chunk, None, 2, (send_y, j, 0), dev_y, src)
        start(chunk, None, 0, (send_c, j, 0), dev_c, src)

    def onward(j):
        chunk = (order[j], c, w)

        def moved(side):
            src = x_ref if j == 0 else view(chunk, None)
            return copy(src, chunk, None, 0, (send_z, j, side), devices_z[side])

        return (
            ((order[j] <= z) & (z < 3), functools.partial(moved, 0)),
            ((order[j] >= z) & (z > 0), functools.partial(moved, 1)),
        )

    def along(j):
        for there, moved in onward(j):
            pl.when(there)(lambda: moved().start())

    def share_in(j):
        arrived((order[j], c, w), None, 0)
        along(j)
        spread(j)

    def relay(j):
        from_x, from_y = ((order[j], c, wx), (order[j], c, wy))
        arrived(from_x, None, 1)
        start(from_x, lo, 3, (send_y, j, 1), dev_y)
        start(from_x, None, 1, (send_c, j, 1), dev_c)
        arrived(from_y, None, 2)
        start(from_y, hi, 4, (send_x, j, 1), dev_x)
        start(from_y, None, 2, (send_c, j, 2), dev_c)

    def across(j):
        chunk = (order[j], c, wd)
        for cols, slot in ((lo, 3), (hi, 4)):
            arrived(chunk, cols, slot)
            start(chunk, cols, slot, (send_c, j, slot), dev_c)

    def sibling(j):
        for ww, cols, slot in ((w, None, 0), (wx, None, 1), (wy, None, 2), (wd, lo, 3), (wd, hi, 4)):
            arrived((order[j], 1 - c, ww), cols, slot)

    def before(step):
        j = step // 2
        if step == 0:
            along(0)
            spread(0)
            share_in(1)
            relay(0)
            across(0)
            keep().wait()
            for load in loads():
                load.wait()
        elif step % 2 == 0:
            across(j)
        else:
            if j + 2 < 4:
                share_in(j + 2)
            if j + 1 < 4:
                relay(j + 1)
            sibling(j)

    code = order[0] + 4 * order[1] + 16 * order[2] + 64 * order[3]

    def tile_of(step):
        j = step // 2
        power = 1 + 3 * j + (9 * j * (j - 1)) // 2 + (27 * j * (j - 1) * (j - 2)) // 6
        return ((code // power) % 4, (c + step) % 2)

    lanes = lax.broadcasted_iota(jnp.int32, (4 * share, 128), 1)

    def stores(step):
        zj, cc = tile_of(step)
        return [
            pltpu.make_async_copy(src, dst.at[:, cc, zj], store_sem.at[i])
            for i, (src, dst) in enumerate(
                (
                    (x_all.at[zj, cc], x_out),
                    (dx_buf, dx_out),
                    (moe_buf, moe_out),
                    (gated, gated_out),
                    (both, both_out),
                )
            )
        ]

    def one_tile(step, carry):
        for k in range(8):
            pl.when(step == k)(functools.partial(before, k))
        zj, cc = tile_of(step)
        slot = step % 2
        grads_load(zj, cc, slot).wait()

        @pl.when(step < 7)
        def _():
            zn, cn = tile_of(step + 1)
            grads_load(zn, cn, 1 - slot).start()

        rows = x_all[zj, cc].reshape(4 * share, width)
        upstream = grads[slot].reshape(4 * share, width)
        logits = jnp.dot(rows, router_ref[...], preferred_element_type=jnp.float32)
        logits = jnp.where(lanes < experts, logits, -1e30)
        raised = jnp.exp(logits - jnp.max(logits, axis=1, keepdims=True))
        gates = raised / jnp.sum(raised, axis=1, keepdims=True)
        gates = gates * kept_ref[:, cc, zj].reshape(4 * share, 128).astype(jnp.float32)

        @pl.when(step > 0)
        def _():
            for store in stores(step - 1):
                store.wait()

        d_gate = jnp.zeros((4 * share, 128), jnp.float32)
        for n in range(2):
            here = lanes == group * 2 + n
            gate = jnp.sum(jnp.where(here, gates, 0.0), axis=1, keepdims=True)
            at = 2 * n * hidden
            gate_pre = jnp.dot(
                rows, w_in[:, at : at + hidden], preferred_element_type=jnp.float32
            )
            up_pre = jnp.dot(
                rows, w_in[:, at + hidden : at + 2 * hidden], preferred_element_type=jnp.float32
            )
            back = contract_last(upstream, w_out[n * hidden : (n + 1) * hidden, :])
            sigmoid = 1.0 / (1.0 + jnp.exp(-gate_pre))
            silu = gate_pre * sigmoid
            activated = silu * up_pre
            d_gate = jnp.where(here, jnp.sum(activated * back, axis=1, keepdims=True), d_gate)
            back = gate * back
            d_pre = back * up_pre * sigmoid * (1.0 + gate_pre * (1.0 - sigmoid))
            shape = (4, share, hidden)
            gated[:, :, n * hidden : (n + 1) * hidden] = (
                (gate * activated).astype(jnp.bfloat16).reshape(shape)
            )
            both[:, :, at : at + hidden] = d_pre.astype(jnp.bfloat16).reshape(shape)
            both[:, :, at + hidden : at + 2 * hidden] = (
                (back * silu).astype(jnp.bfloat16).reshape(shape)
            )
        dx_buf[:, :, width:] = d_gate.astype(jnp.bfloat16).reshape(4, share, 128)
        d_rows = both[...].reshape(4 * share, 4 * hidden)
        g_rows = gated[...].reshape(4 * share, 2 * hidden)

        def columns(m, carried):
            cols = pl.ds(pl.multiple_of(m * 256, 256), 256)
            dx_buf[:, :, cols] = (
                contract_last(d_rows, w_in[cols, :]).astype(jnp.bfloat16).reshape(4, share, 256)
            )
            moe_buf[:, :, cols] = (
                jnp.dot(g_rows, w_out[:, cols], preferred_element_type=jnp.float32)
                .astype(jnp.bfloat16)
                .reshape(4, share, 256)
            )
            return carried

        lax.fori_loop(0, width // 256, columns, None)
        for store in stores(step):
            store.start()
        return carry

    lax.fori_loop(0, 8, one_tile, None)
    for store in stores(7):
        store.wait()
    for chunk, cols, slot, sem, device in sent:
        copy(view(chunk, cols), chunk, cols, slot, sem, device).wait_send()
    for j in range(4):
        for there, moved in onward(j):
            pl.when(there)(lambda: moved().wait_send())


def experts_call(rows, grads, kept, router, expert_in, expert_out, experts):
    share, width = rows.shape
    hidden = expert_out.shape[1]
    blocks = (4, 2, 4, share)
    bf16 = jnp.bfloat16
    dma = pltpu.SemaphoreType.DMA
    anywhere, vmem = (pl.BlockSpec(memory_space=pl.ANY), pl.BlockSpec(memory_space=pltpu.VMEM))
    outs = (width, width + 128, width, 2 * hidden, 4 * hidden)
    return pl.pallas_call(
        functools.partial(experts_kernel, experts),
        out_shape=tuple(jax.ShapeDtypeStruct(blocks + (n,), bf16) for n in outs),
        in_specs=[anywhere, anywhere, vmem, vmem, anywhere, anywhere],
        out_specs=(anywhere,) * 5,
        scratch_shapes=[
            pltpu.VMEM((4, 2, 4, share, width), bf16),
            pltpu.VMEM((width, 4 * hidden), bf16),
            pltpu.VMEM((2 * hidden, width), bf16),
            pltpu.VMEM((2, 4, share, width), bf16),
            pltpu.VMEM((4, share, width + 128), bf16),
            pltpu.VMEM((4, share, width), bf16),
            pltpu.VMEM((4, share, 2 * hidden), bf16),
            pltpu.VMEM((4, share, 4 * hidden), bf16),
            dma,
            dma((6,)),
            dma((2,)),
            dma((5,)),
            dma((4, 2)),
            dma((4, 2)),
            dma((4, 2)),
            dma((4, 5)),
            dma((4, 2, 5)),
        ],
        compiler_params=pltpu.CompilerParams(
            collective_id=0, has_side_effects=True, vmem_limit_bytes=62 << 20
        ),
    )(rows, grads, kept, router, expert_in, expert_out)


def gathered(rows, axes):
    return lax.all_gather(rows, axes, axis=0, tiled=True)


def scattered(rows, axes):
    return lax.psum_scatter(rows, axes, scatter_dimension=0, tiled=True)


def fit_rows(values, rows):
    flat = values.reshape(-1)
    columns = -(-flat.shape[0] // rows)
    return jnp.pad(flat, (0, rows * columns - flat.shape[0])).reshape(rows, columns)


def per_device_dense(
    layer_in,
    norm_gains,
    qkv_weight,
    qk_gains,
    out_weight,
    router,
    expert_in,
    expert_out,
    grad_out,
    segments,
    routes,
    route_order,
):
    group = GROUP
    everyone = EVERYONE
    group_count = lax.axis_size(group)
    tensor_count = lax.axis_size(TENSOR)
    context_rank = lax.axis_index(CONTEXT)
    tensor_rank = lax.axis_index(TENSOR)
    seq_count, half_len, model_width = layer_in.shape
    token_count = seq_count * half_len
    top_count = routes.shape[2]
    weight_rows, _, head_width = qkv_weight.shape
    expert_total = router.shape[1]
    local_experts = expert_in.shape[0]
    hidden_width = expert_in.shape[3]
    head_rows, _, local_heads = qk_gains.shape
    head_size = head_rows * group_count
    share = token_count // tensor_count
    bf16, f32 = jnp.bfloat16, jnp.float32

    capacity = token_count * top_count * 9 // (8 * expert_total)
    routed, slot_of = pair_slots(
        routes.reshape(token_count, top_count),
        route_order.reshape(token_count, top_count),
        expert_total,
    )
    kept = routed & (slot_of < capacity)

    front_small = jnp.concatenate(
        [norm_gains, fit_rows(qk_gains, weight_rows)], axis=1
    )
    front = gathered(
        jnp.concatenate([qkv_weight.reshape(weight_rows, -1), front_small], axis=1), group
    )
    back_small = jnp.concatenate(
        [router, fit_rows(kept.astype(bf16), weight_rows)], axis=1
    )
    back = gathered(jnp.concatenate([out_weight, back_small], axis=1), group)
    qkv_full = front[:, : 3 * head_width]
    gain_full = front[:, 3 * head_width : 3 * head_width + 2].astype(f32)
    gain_attn, gain_ffn = (gain_full[:, 0], gain_full[:, 1])
    qk_gain_full = (
        front[:, 3 * head_width + 2 :]
        .reshape(group_count, -1)[:, : head_rows * 2 * local_heads]
        .reshape(head_size, 2, local_heads)
        .astype(f32)
    )
    query_gain = qk_gain_full[:, 0, :].T.reshape(-1)
    key_gain = qk_gain_full[:, 1, :].T.reshape(-1)
    out_full = back[:, :head_width]
    router_full = back[:, head_width : head_width + expert_total]
    kept_all = (
        back[:, head_width + expert_total :]
        .reshape(group_count, -1)[:, : expert_total * token_count]
        .reshape(group_count, expert_total, token_count)
    )
    grads_all = gathered(grad_out.reshape(token_count, model_width), group)

    inv_root = 1.0 / math.sqrt(head_size)
    residual = layer_in.reshape(token_count, model_width).astype(f32)
    scale_one = lax.rsqrt(jnp.mean(residual * residual, axis=1, keepdims=True) + epsilon)
    normed_one = (residual * scale_one * gain_attn).astype(bf16)
    projected = jnp.dot(normed_one, qkv_full, preferred_element_type=f32)
    query_raw = projected[:, :head_width]
    key_raw = projected[:, head_width : 2 * head_width]
    value_raw = projected[:, 2 * head_width :]
    square_sums = row_sums(
        jnp.stack(
            [jnp.sum(query_raw * query_raw, axis=1), jnp.sum(key_raw * key_raw, axis=1)], axis=1
        )
    )
    query_scale = lax.rsqrt(square_sums[:, 0:1] / model_width + epsilon)
    key_scale = lax.rsqrt(square_sums[:, 1:2] / model_width + epsilon)
    heads_shape = (seq_count, half_len, local_heads, head_size)
    query_hat = (query_raw * query_scale * query_gain).reshape(heads_shape)
    key_hat = (key_raw * key_scale * key_gain).reshape(heads_shape)
    query_pos = context_rank * half_len + jnp.arange(half_len, dtype=jnp.int32)
    cosine_table, sine_table = rotary_tables(query_pos, head_size)
    cosine_table = cosine_table[None, :, None, :]
    sine_table = sine_table[None, :, None, :]
    query_rot = (query_hat * cosine_table + rotate_half(query_hat) * sine_table).astype(bf16)
    key_rot = (key_hat * cosine_table + rotate_half(key_hat) * sine_table).astype(bf16)
    value_low = value_raw.astype(bf16).reshape(heads_shape)
    key_prev, value_prev = passed_along((key_rot, value_low), CONTEXT, 1)
    all_keys = jnp.concatenate([key_prev, key_rot], axis=1)
    all_values = jnp.concatenate([value_prev, value_low], axis=1)
    key_pos = jnp.concatenate([query_pos - half_len, query_pos])
    seg_query = lax.dynamic_slice_in_dim(segments, context_rank * half_len, half_len, 1)
    seg_prev = lax.dynamic_slice_in_dim(
        segments, jnp.maximum(context_rank - 1, 0) * half_len, half_len, 1
    )
    seg_keys = jnp.concatenate([seg_prev, seg_query], axis=1)
    causal = (key_pos[None, :] >= 0) & (key_pos[None, :] <= query_pos[:, None])
    allowed = causal[None] & (seg_query[:, :, None] == seg_keys[:, None, :])

    def score_block(queries, key_rows):
        raw_scores = (
            jnp.einsum(BY_SCORE, queries, key_rows, preferred_element_type=f32) * inv_root
        )
        return jnp.where(allowed[:, None], raw_scores, -1e30)

    scores = score_block(query_rot, all_keys)
    row_max = jnp.max(scores, axis=-1, keepdims=True)
    exponent = jnp.exp(scores - row_max)
    row_total = jnp.sum(exponent, axis=-1, keepdims=True)
    log_total = row_max + jnp.log(row_total)
    attn_probs = (exponent / row_total).astype(bf16)
    attended = jnp.einsum(BY_QUERY, attn_probs, all_values, preferred_element_type=f32)
    attended_low = attended.reshape(token_count, -1).astype(bf16)
    attn_partial = jnp.einsum("tf,df->td", attended_low, out_full, preferred_element_type=f32)

    own_rows = lambda rows: lax.dynamic_slice_in_dim(rows, tensor_rank * share, share, 0)
    residual_own = own_rows(residual)
    hidden = residual_own + scattered(attn_partial.astype(bf16), TENSOR).astype(f32)
    scale_two = lax.rsqrt(jnp.mean(hidden * hidden, axis=1, keepdims=True) + epsilon)
    unit_two = hidden * scale_two
    normed_two = (unit_two * gain_ffn).astype(bf16)
    upstream = own_rows(grad_out.reshape(token_count, model_width)).astype(f32)

    blocks = (4, 2, 4, share)
    pad_experts = lambda rows: jnp.pad(rows, ((0, 0), (0, 128 - expert_total)))
    kept_rows = kept_all.transpose(0, 2, 1).reshape(-1, expert_total)
    normed_all, d_sums, moe_partial, gated, d_both = (
        rows.reshape(group_count * token_count, -1)
        for rows in experts_call(
            normed_two,
            grads_all.reshape(blocks + (model_width,)),
            pad_experts(kept_rows).reshape(blocks + (128,)),
            pad_experts(router_full),
            expert_in,
            expert_out,
            expert_total,
        )
    )
    d_sums = scattered(scattered(d_sums, group), TENSOR).astype(f32)
    moe_own = scattered(scattered(moe_partial, group), TENSOR).astype(f32)
    layer_out = gathered((hidden + moe_own).astype(bf16), TENSOR).reshape(layer_in.shape)
    grad_expert_in = jnp.einsum(
        "td,tngf->ngdf",
        normed_all,
        d_both.reshape(-1, local_experts, 2, hidden_width),
        preferred_element_type=f32,
    )
    grad_expert_out = jnp.dot(gated.T, grads_all, preferred_element_type=f32).reshape(
        expert_out.shape
    )

    kept_own = own_rows(kept.T).astype(f32)
    probs_own = jax.nn.softmax(
        jnp.dot(normed_two, router_full, preferred_element_type=f32), axis=1
    )
    d_probs = d_sums[:, model_width : model_width + expert_total] * kept_own
    d_logits = (
        probs_own * (d_probs - jnp.sum(probs_own * d_probs, axis=1, keepdims=True))
    ).astype(bf16)
    d_normed_two = d_sums[:, :model_width] + jnp.dot(
        d_logits, router_full.T, preferred_element_type=f32
    )
    d_router = jnp.dot(normed_two.T, d_logits, preferred_element_type=f32)
    d_gain_ffn = jnp.sum(d_normed_two * unit_two, axis=0)
    scaled_ffn = gain_ffn * d_normed_two
    d_hidden = upstream + scale_two * (
        scaled_ffn - unit_two * jnp.mean(scaled_ffn * unit_two, axis=1, keepdims=True)
    )
    d_hidden_low = gathered(d_hidden.astype(bf16), TENSOR)

    d_attended = (
        jnp.dot(d_hidden_low, out_full, preferred_element_type=f32)
        .astype(bf16)
        .reshape(heads_shape)
    )
    d_out_weight = jnp.einsum("td,tf->df", d_hidden_low, attended_low, preferred_element_type=f32)
    probs_again = jnp.exp(score_block(query_rot, all_keys) - log_total)
    probs_again_low = probs_again.astype(bf16)
    d_probs_att = jnp.einsum(
        BY_SCORE, d_attended, all_values, preferred_element_type=f32
    )
    d_values_all = jnp.einsum(
        BY_KEY, probs_again_low, d_attended, preferred_element_type=f32
    )
    row_dot = jnp.sum(probs_again * d_probs_att, axis=-1, keepdims=True)
    d_scores = (probs_again * (d_probs_att - row_dot)).astype(bf16)
    d_query_rot = (
        jnp.einsum(BY_QUERY, d_scores, all_keys, preferred_element_type=f32) * inv_root
    )
    d_keys_all = (
        jnp.einsum(BY_KEY, d_scores, query_rot, preferred_element_type=f32) * inv_root
    )
    back_key, back_value = (
        passed_along(d_keys_all[:, :half_len].astype(bf16), CONTEXT, -1).astype(f32),
        passed_along(d_values_all[:, :half_len].astype(bf16), CONTEXT, -1).astype(f32),
    )
    d_key_rot = d_keys_all[:, half_len:] + back_key
    d_value = (d_values_all[:, half_len:] + back_value).reshape(token_count, -1)
    d_query_hat = (d_query_rot * cosine_table + rotate_back(d_query_rot * sine_table)).reshape(
        token_count, -1
    )
    d_key_hat = (d_key_rot * cosine_table + rotate_back(d_key_rot * sine_table)).reshape(
        token_count, -1
    )
    centre = row_sums(
        jnp.stack(
            [
                jnp.sum(query_gain * d_query_hat * query_raw, axis=1),
                jnp.sum(key_gain * d_key_hat * key_raw, axis=1),
            ],
            axis=1,
        )
    )
    d_query_raw = (
        query_scale * query_gain * d_query_hat
        - query_raw * (query_scale**3 / model_width) * centre[:, 0:1]
    )
    d_key_raw = (
        key_scale * key_gain * d_key_hat - key_raw * (key_scale**3 / model_width) * centre[:, 1:2]
    )
    d_query_gain = (
        jnp.sum(d_query_hat * query_raw * query_scale, axis=0).reshape(local_heads, head_size).T
    )
    d_key_gain = jnp.sum(d_key_hat * key_raw * key_scale, axis=0).reshape(local_heads, head_size).T
    d_qk_gains = jnp.stack([d_query_gain, d_key_gain], axis=1)
    d_projected = jnp.concatenate([d_query_raw, d_key_raw, d_value], axis=1).astype(bf16)
    d_normed_one = scattered(
        jnp.einsum("tf,df->td", d_projected, qkv_full, preferred_element_type=f32).astype(bf16),
        TENSOR,
    ).astype(f32)
    d_qkv = jnp.einsum("td,tf->df", normed_one, d_projected, preferred_element_type=f32)

    scale_own = own_rows(scale_one)
    unit_one = residual_own * scale_own
    d_gain_attn = jnp.sum(d_normed_one * unit_one, axis=0)
    scaled_attn = gain_attn * d_normed_one
    grad_in = d_hidden + scale_own * (
        scaled_attn - unit_one * jnp.mean(scaled_attn * unit_one, axis=1, keepdims=True)
    )
    grad_in = gathered(grad_in.astype(bf16), TENSOR).astype(f32).reshape(layer_in.shape)

    grad_qkv = (
        scattered(d_qkv.astype(bf16), group)
        .astype(f32)
        .reshape(weight_rows, 3, head_width)
    )
    grad_out_weight = scattered(d_out_weight.astype(bf16), group).astype(f32)
    gain_share = weight_rows // tensor_count
    router_share = expert_total // tensor_count
    own_slot = (jnp.arange(tensor_count) == tensor_rank).astype(f32)[None, :, None]
    small = jnp.concatenate(
        [
            jnp.stack([d_gain_attn, d_gain_ffn], axis=1).reshape(group_count, tensor_count, -1),
            d_router.reshape(group_count, weight_rows, tensor_count, router_share)
            .transpose(0, 2, 1, 3)
            .reshape(group_count, tensor_count, -1),
            d_qk_gains.reshape(group_count, 1, -1) * own_slot,
        ],
        axis=2,
    ).reshape(group_count * tensor_count, -1)
    small = scattered(small, everyone)[0]
    ends = (gain_share * 2, gain_share * 2 + weight_rows * router_share)
    return (
        layer_out,
        grad_in,
        small[: ends[0]].reshape(gain_share, 2),
        grad_qkv,
        small[ends[1] :].reshape(head_rows, 2, local_heads),
        grad_out_weight,
        small[ends[0] : ends[1]].reshape(weight_rows, router_share),
        grad_expert_in,
        grad_expert_out,
    )


def solution(mesh):
    placed = (
        P(WEIGHTS, CONTEXT, None),
        P(GROUP, None),
        P(GROUP, None, TENSOR),
        P(GROUP, None, TENSOR),
        P(GROUP, TENSOR),
        P(GROUP, None),
        P(GROUP, None, None, TENSOR),
        P(GROUP, TENSOR, None),
        P(WEIGHTS, CONTEXT, None),
        P(WEIGHTS, None),
        P(WEIGHTS, CONTEXT, None),
        P(WEIGHTS, CONTEXT, None),
    )
    axes = tuple(mesh.shape[axis] for axis in EVERYONE)

    def per_device(*blocks):
        dense = axes == (4, 2, 4) and blocks[5].shape[1] <= 2 * blocks[10].shape[2]
        return (per_device_dense if dense else per_device_slots)(*blocks)

    return jax.shard_map(
        per_device,
        mesh=mesh,
        in_specs=placed,
        out_specs=(
            P(WEIGHTS, CONTEXT, None),
            P(WEIGHTS, CONTEXT, None),
            P(EVERYONE, None),
            P(GROUP, None, TENSOR),
            P(GROUP, None, TENSOR),
            P(GROUP, TENSOR),
            P(GROUP, TENSOR),
            P(GROUP, None, None, TENSOR),
            P(GROUP, TENSOR, None),
        ),
        check_vma=False,
    )
```

```python
import functools
import math

import jax
import jax.numpy as jnp
from jax import lax
from jax.experimental import pallas as pl
from jax.experimental.pallas import tpu as pltpu
from jax.sharding import PartitionSpec as P

epsilon = 1e-05
rotary_base = 10000.0
WEIGHTS, CONTEXT, TENSOR = ("weights", "context", "tensor")
GROUP = (WEIGHTS, CONTEXT)
EVERYONE = (WEIGHTS, CONTEXT, TENSOR)
MESH = pl.DeviceIdType.MESH
BY_SCORE = "sqhd,skhd->shqk"
BY_QUERY = "shqk,skhd->sqhd"
BY_KEY = "shqk,sqhd->skhd"


def passed_along(value, axis, steps):
    count = lax.axis_size(axis)
    leading, last = (max(0, -steps), min(count, count - steps))
    return lax.ppermute(value, axis, [(source, source + steps) for source in range(leading, last)])


def rotate_half(values_in):
    middle = values_in.shape[-1] // 2
    return jnp.concatenate([-values_in[..., middle:], values_in[..., :middle]], axis=-1)


def rotate_back(grads_in):
    middle = grads_in.shape[-1] // 2
    return jnp.concatenate([grads_in[..., middle:], -grads_in[..., :middle]], axis=-1)


def rotary_tables(positions, head_size):
    frequency = rotary_base ** (-(2.0 * jnp.arange(head_size // 2, dtype=jnp.float32)) / head_size)
    angle_table = positions.astype(jnp.float32)[:, None] * frequency[None, :]
    angle_table = jnp.concatenate([angle_table, angle_table], axis=1)
    return (jnp.cos(angle_table), jnp.sin(angle_table))


def pair_slots(token_routes, token_ranks, expert_total):
    unused = token_routes.size
    hot = token_routes.T[None] == jnp.arange(expert_total, dtype=jnp.int32)[:, None, None]
    rank_of = jnp.min(jnp.where(hot, token_ranks.T[None], unused), axis=1)
    slot_of = jnp.sum((rank_of[:, :, None] < rank_of[:, None, :]).astype(jnp.int32), axis=1)
    return (rank_of < unused, slot_of)


def place_pairs(pair_expert, rank, expert_total, capacity, top_count):
    pair_count = pair_expert.shape[0]
    token_routes = pair_expert.reshape(-1, top_count)
    slot_of = pair_slots(token_routes, rank.reshape(-1, top_count), expert_total)[1]
    slot_index = jnp.take_along_axis(slot_of.T, token_routes, axis=1).reshape(pair_count)
    kept_pair = slot_index < capacity
    dest_row = jnp.where(kept_pair, pair_expert * capacity + slot_index, expert_total * capacity)
    slot_pair = (
        jnp.full((expert_total * capacity + 1,), pair_count, jnp.int32)
        .at[dest_row]
        .set(jnp.arange(pair_count, dtype=jnp.int32))[:-1]
    )
    return (kept_pair, dest_row, slot_pair)


def row_sums(partial_rows):
    return lax.psum(partial_rows, TENSOR)


def tensor_sum(partial_rows):
    return lax.psum(partial_rows, TENSOR)


def to_owners(slot_rows):
    return lax.all_to_all(
        slot_rows, GROUP, split_axis=0, concat_axis=0, tiled=True
    )


def expert_front(slot_inputs, expert_in):
    both_pre = jnp.einsum(
        "sncd,ngdf->sncgf", slot_inputs, expert_in, preferred_element_type=jnp.float32
    )
    return (both_pre[..., 0, :], both_pre[..., 1, :])


def per_device_slots(
    layer_in,
    norm_gains,
    qkv_weight,
    qk_gains,
    out_weight,
    router,
    expert_in,
    expert_out,
    grad_out,
    segments,
    routes,
    route_order,
):
    group_count = lax.axis_size(GROUP)
    tensor_count = lax.axis_size(TENSOR)
    context_rank = lax.axis_index(CONTEXT)
    tensor_rank = lax.axis_index(TENSOR)
    seq_count, half_len, model_width = layer_in.shape
    token_count = seq_count * half_len
    top_count = routes.shape[2]
    qkv_full, out_full, qk_gain_full, gain_full, router_full = (
        lax.all_gather(qkv_weight, GROUP, axis=0, tiled=True),
        lax.all_gather(out_weight, GROUP, axis=0, tiled=True),
        lax.all_gather(qk_gains, GROUP, axis=0, tiled=True),
        lax.all_gather(norm_gains, GROUP, axis=0, tiled=True),
        lax.all_gather(router, GROUP, axis=0, tiled=True),
    )
    head_size = qk_gain_full.shape[0]
    local_heads = qk_gain_full.shape[2]
    expert_total = router_full.shape[1]
    gain_attn = gain_full[:, 0].astype(jnp.float32)
    gain_ffn = gain_full[:, 1].astype(jnp.float32)
    query_gain = qk_gain_full[:, 0, :].astype(jnp.float32).T.reshape(-1)
    key_gain = qk_gain_full[:, 1, :].astype(jnp.float32).T.reshape(-1)
    inv_root = 1.0 / math.sqrt(head_size)
    residual = layer_in.reshape(token_count, model_width).astype(jnp.float32)
    scale_one = lax.rsqrt(jnp.mean(residual * residual, axis=1, keepdims=True) + epsilon)
    unit_one = residual * scale_one
    normed_one = (unit_one * gain_attn).astype(jnp.bfloat16)
    projected = jnp.einsum("td,dgf->tgf", normed_one, qkv_full, preferred_element_type=jnp.float32)
    query_raw = projected[:, 0]
    key_raw = projected[:, 1]
    value_raw = projected[:, 2]
    square_sums = row_sums(
        jnp.stack(
            [jnp.sum(query_raw * query_raw, axis=1), jnp.sum(key_raw * key_raw, axis=1)], axis=1
        )
    )
    query_scale = lax.rsqrt(square_sums[:, 0:1] / model_width + epsilon)
    key_scale = lax.rsqrt(square_sums[:, 1:2] / model_width + epsilon)
    heads_shape = (seq_count, half_len, local_heads, head_size)
    query_hat = (query_raw * query_scale * query_gain).reshape(heads_shape)
    key_hat = (key_raw * key_scale * key_gain).reshape(heads_shape)
    query_pos = context_rank * half_len + jnp.arange(half_len, dtype=jnp.int32)
    cosine_table, sine_table = rotary_tables(query_pos, head_size)
    cosine_table = cosine_table[None, :, None, :]
    sine_table = sine_table[None, :, None, :]
    query_rot = (query_hat * cosine_table + rotate_half(query_hat) * sine_table).astype(
        jnp.bfloat16
    )
    key_rot = (key_hat * cosine_table + rotate_half(key_hat) * sine_table).astype(jnp.bfloat16)
    value_low = value_raw.astype(jnp.bfloat16).reshape(heads_shape)
    key_prev, value_prev = passed_along((key_rot, value_low), CONTEXT, 1)
    all_keys = jnp.concatenate([key_prev, key_rot], axis=1)
    all_values = jnp.concatenate([value_prev, value_low], axis=1)
    key_pos = jnp.concatenate([query_pos - half_len, query_pos])
    seg_query = lax.dynamic_slice_in_dim(segments, context_rank * half_len, half_len, 1)
    seg_prev = lax.dynamic_slice_in_dim(
        segments, jnp.maximum(context_rank - 1, 0) * half_len, half_len, 1
    )
    seg_keys = jnp.concatenate([seg_prev, seg_query], axis=1)
    causal = (key_pos[None, :] >= 0) & (key_pos[None, :] <= query_pos[:, None])
    allowed = causal[None] & (seg_query[:, :, None] == seg_keys[:, None, :])

    def score_block(queries, key_rows):
        raw_scores = (
            jnp.einsum(BY_SCORE, queries, key_rows, preferred_element_type=jnp.float32)
            * inv_root
        )
        return jnp.where(allowed[:, None], raw_scores, -1e30)

    scores = score_block(query_rot, all_keys)
    row_max = jnp.max(scores, axis=-1, keepdims=True)
    exponent = jnp.exp(scores - row_max)
    row_total = jnp.sum(exponent, axis=-1, keepdims=True)
    log_total = row_max + jnp.log(row_total)
    attn_probs = (exponent / row_total).astype(jnp.bfloat16)
    attended = jnp.einsum(
        BY_QUERY, attn_probs, all_values, preferred_element_type=jnp.float32
    )
    attended_low = attended.reshape(token_count, -1).astype(jnp.bfloat16)
    attn_partial = jnp.einsum(
        "tf,df->td", attended_low, out_full, preferred_element_type=jnp.float32
    )
    hidden = residual + tensor_sum(attn_partial)
    scale_two = lax.rsqrt(jnp.mean(hidden * hidden, axis=1, keepdims=True) + epsilon)
    unit_two = hidden * scale_two
    normed_two = (unit_two * gain_ffn).astype(jnp.bfloat16)
    logits = jnp.dot(normed_two, router_full, preferred_element_type=jnp.float32)
    router_probs = jax.nn.softmax(logits, axis=1)
    capacity = token_count * top_count * 9 // (8 * expert_total)
    local_experts = expert_in.shape[0]
    pair_count = token_count * top_count
    token_routes = routes.reshape(token_count, top_count)
    kept_pair, dest_row, slot_pair = place_pairs(
        token_routes.reshape(pair_count), route_order.reshape(pair_count), expert_total, capacity, top_count
    )
    zero_row = jnp.zeros((1, model_width), jnp.bfloat16)
    zero_wide = jnp.zeros((1, model_width), jnp.float32)
    slot_shape = (group_count, local_experts, capacity, model_width)
    dispatch_rows = jnp.concatenate([normed_two, zero_row], axis=0)[slot_pair // top_count].reshape(
        slot_shape
    )
    received = lax.all_to_all(
        dispatch_rows, GROUP, split_axis=0, concat_axis=0, tiled=True
    )
    gate_pre, up_pre = expert_front(received, expert_in)
    sigmoid_gate = jax.nn.sigmoid(gate_pre)
    silu_gate = gate_pre * sigmoid_gate
    activated = (silu_gate * up_pre).astype(jnp.bfloat16)
    expert_partial = jnp.einsum(
        "sncf,nfd->sncd", activated, expert_out, preferred_element_type=jnp.float32
    )
    kept_float = kept_pair.reshape(token_count, top_count).astype(jnp.float32)
    gate_weight = jnp.take_along_axis(router_probs, token_routes, axis=1) * kept_float
    upstream = grad_out.reshape(token_count, model_width).astype(jnp.float32)
    returned = to_owners(expert_partial).reshape(expert_total * capacity, model_width)
    picked = jnp.concatenate([returned, zero_wide], axis=0)[dest_row].reshape(
        token_count, top_count, model_width
    )
    moe_partial = jnp.sum(gate_weight[:, :, None] * picked, axis=1)
    dot_partial = jnp.sum(upstream[:, None, :] * picked, axis=2)
    moe_total, dot_total = lax.psum((moe_partial, dot_partial), TENSOR)
    layer_out = (hidden + moe_total).astype(jnp.bfloat16).reshape(layer_in.shape)
    d_gate = dot_total * kept_float
    route_hot = (
        token_routes[:, :, None] == jnp.arange(expert_total, dtype=jnp.int32)[None, None, :]
    ).astype(jnp.float32)
    d_probs = jnp.sum(d_gate[:, :, None] * route_hot, axis=1)
    d_logits = (
        router_probs * (d_probs - jnp.sum(router_probs * d_probs, axis=1, keepdims=True))
    ).astype(jnp.bfloat16)
    d_pair = (
        (gate_weight[:, :, None] * upstream[:, None, :])
        .astype(jnp.bfloat16)
        .reshape(pair_count, model_width)
    )
    d_slots = jnp.concatenate([d_pair, zero_row], axis=0)[slot_pair].reshape(slot_shape)
    d_received = lax.all_to_all(
        d_slots, GROUP, split_axis=0, concat_axis=0, tiled=True
    )
    d_activated = jnp.einsum(
        "sncd,nfd->sncf", d_received, expert_out, preferred_element_type=jnp.float32
    )
    grad_expert_out = jnp.einsum(
        "sncf,sncd->nfd", activated, d_received, preferred_element_type=jnp.float32
    )
    d_gate_pre = d_activated * up_pre * sigmoid_gate * (1.0 + gate_pre * (1.0 - sigmoid_gate))
    d_up_pre = d_activated * silu_gate
    d_both = jnp.stack([d_gate_pre, d_up_pre], axis=3).astype(jnp.bfloat16)
    d_inputs = jnp.einsum("sncgf,ngdf->sncd", d_both, expert_in, preferred_element_type=jnp.float32)
    grad_expert_in = jnp.einsum(
        "sncd,sncgf->ngdf", received, d_both, preferred_element_type=jnp.float32
    )
    d_returned = to_owners(d_inputs).reshape(expert_total * capacity, model_width)
    d_normed_part = jnp.sum(
        jnp.concatenate([d_returned, zero_wide], axis=0)[dest_row].reshape(
            token_count, top_count, model_width
        ),
        axis=1,
    )
    d_normed_two = tensor_sum(d_normed_part) + jnp.dot(
        d_logits, router_full.T, preferred_element_type=jnp.float32
    )
    d_router = jnp.dot(normed_two.T, d_logits, preferred_element_type=jnp.float32)
    d_gain_ffn = jnp.sum(d_normed_two * unit_two, axis=0)
    scaled_ffn = gain_ffn * d_normed_two
    d_hidden = upstream + scale_two * (
        scaled_ffn - unit_two * jnp.mean(scaled_ffn * unit_two, axis=1, keepdims=True)
    )
    d_hidden_low = d_hidden.astype(jnp.bfloat16)
    d_out_weight = jnp.einsum(
        "td,tf->df", d_hidden_low, attended_low, preferred_element_type=jnp.float32
    )
    d_attended = (
        jnp.dot(d_hidden_low, out_full, preferred_element_type=jnp.float32)
        .astype(jnp.bfloat16)
        .reshape(heads_shape)
    )
    probs_again = jnp.exp(score_block(query_rot, all_keys) - log_total)
    probs_again_low = probs_again.astype(jnp.bfloat16)
    d_probs_att = jnp.einsum(
        BY_SCORE, d_attended, all_values, preferred_element_type=jnp.float32
    )
    d_values_all = jnp.einsum(
        BY_KEY, probs_again_low, d_attended, preferred_element_type=jnp.float32
    )
    row_dot = jnp.sum(probs_again * d_probs_att, axis=-1, keepdims=True)
    d_scores = (probs_again * (d_probs_att - row_dot)).astype(jnp.bfloat16)
    d_query_rot = (
        jnp.einsum(BY_QUERY, d_scores, all_keys, preferred_element_type=jnp.float32)
        * inv_root
    )
    d_keys_all = (
        jnp.einsum(BY_KEY, d_scores, query_rot, preferred_element_type=jnp.float32)
        * inv_root
    )
    back_key, back_value = (
        passed_along(d_keys_all[:, :half_len].astype(jnp.bfloat16), CONTEXT, -1).astype(
            jnp.float32
        ),
        passed_along(d_values_all[:, :half_len].astype(jnp.bfloat16), CONTEXT, -1).astype(
            jnp.float32
        ),
    )
    d_key_rot = d_keys_all[:, half_len:] + back_key
    d_value = (d_values_all[:, half_len:] + back_value).reshape(token_count, -1)
    d_query_hat = (d_query_rot * cosine_table + rotate_back(d_query_rot * sine_table)).reshape(
        token_count, -1
    )
    d_key_hat = (d_key_rot * cosine_table + rotate_back(d_key_rot * sine_table)).reshape(
        token_count, -1
    )
    centre = row_sums(
        jnp.stack(
            [
                jnp.sum(query_gain * d_query_hat * query_raw, axis=1),
                jnp.sum(key_gain * d_key_hat * key_raw, axis=1),
            ],
            axis=1,
        )
    )
    d_query_raw = (
        query_scale * query_gain * d_query_hat
        - query_raw * (query_scale**3 / model_width) * centre[:, 0:1]
    )
    d_key_raw = (
        key_scale * key_gain * d_key_hat - key_raw * (key_scale**3 / model_width) * centre[:, 1:2]
    )
    d_query_gain = (
        jnp.sum(d_query_hat * query_raw * query_scale, axis=0).reshape(local_heads, head_size).T
    )
    d_key_gain = jnp.sum(d_key_hat * key_raw * key_scale, axis=0).reshape(local_heads, head_size).T
    d_qk_gains = jnp.stack([d_query_gain, d_key_gain], axis=1)
    d_projected = jnp.stack([d_query_raw, d_key_raw, d_value], axis=1).astype(jnp.bfloat16)
    d_normed_one = tensor_sum(
        jnp.einsum("tgf,dgf->td", d_projected, qkv_full, preferred_element_type=jnp.float32)
    )
    d_qkv = jnp.einsum("td,tgf->dgf", normed_one, d_projected, preferred_element_type=jnp.float32)
    d_gain_attn = jnp.sum(d_normed_one * unit_one, axis=0)
    scaled_attn = gain_attn * d_normed_one
    grad_in = d_hidden + scale_one * (
        scaled_attn - unit_one * jnp.mean(scaled_attn * unit_one, axis=1, keepdims=True)
    )
    d_norm_gains = jnp.stack([d_gain_attn, d_gain_ffn], axis=1)
    grad_qkv, grad_out_weight, grad_qk_gains, gain_rows, router_rows = (
        lax.psum_scatter(d_qkv, GROUP, scatter_dimension=0, tiled=True),
        lax.psum_scatter(d_out_weight, GROUP, scatter_dimension=0, tiled=True),
        lax.psum_scatter(d_qk_gains, GROUP, scatter_dimension=0, tiled=True),
        lax.psum_scatter(d_norm_gains, GROUP, scatter_dimension=0, tiled=True),
        lax.psum_scatter(d_router, GROUP, scatter_dimension=0, tiled=True),
    )
    gain_share = gain_rows.shape[0] // tensor_count
    grad_norm_gains = lax.dynamic_slice_in_dim(gain_rows, tensor_rank * gain_share, gain_share, 0)
    router_share = expert_total // tensor_count
    grad_router = lax.dynamic_slice_in_dim(router_rows, tensor_rank * router_share, router_share, 1)
    return (
        layer_out,
        grad_in.reshape(layer_in.shape),
        grad_norm_gains,
        grad_qkv,
        grad_qk_gains,
        grad_out_weight,
        grad_router,
        grad_expert_in,
        grad_expert_out,
    )


def contract_last(left, right):
    return lax.dot_general(
        left, right, (((1,), (1,)), ((), ())), preferred_element_type=jnp.float32
    )


def share_order(z):
    upper, odd = (z // 2, z % 2)
    return (z, z + 1 - 2 * upper, 2 + upper - 2 * odd, 3 - 3 * upper)


def neighbours(w):
    wx, wy = (w + 1 - 2 * (w % 2), (w + 2) % 4)
    return (wx, wy, wx + wy - w)


def experts_kernel(
    experts,
    x_ref,
    grad_own,
    grad_x,
    grad_y,
    grad_low,
    grad_high,
    kept_ref,
    router_ref,
    in_ref,
    out_w_ref,
    x_out,
    grads_out,
    gated_out,
    both_out,
    dx_own,
    moe_own,
    x_tile,
    w_in,
    w_out,
    grads,
    gated,
    both,
    *scratch,
):
    others, mine, sibs, from_x1, from_y1, from_y2, from_x2, from_z = (
        (scratch[2 * k], scratch[2 * k + 1]) for k in range(8)
    )
    (
        own_sem,
        tile_sem,
        weight_sem,
        grads_sem,
        store_sem,
        send_z,
        send_x,
        send_y,
        send_c,
        recv,
        over_send,
        over_recv,
        sib_send,
        sib_recv,
        credit,
        one_send,
        one_recv,
        two_send,
        two_recv,
        end_send,
        end_recv,
    ) = scratch[16:]
    w, c, z = (lax.axis_index(a) for a in (WEIGHTS, CONTEXT, TENSOR))
    wx, wy, wd = neighbours(w)
    share, width = x_ref.shape
    half = width // 2
    lo, hi = (pl.ds(0, half), pl.ds(half, half))
    dev_x, dev_y, dev_c = ((wx, c, z), (wy, c, z), (w, 1 - c, z))
    order = share_order(z)
    hidden = out_w_ref.shape[1]
    group = w * 2 + c
    bf16, f32 = (jnp.bfloat16, jnp.float32)
    wides = (width + 128, width)

    def loads():
        return [
            pltpu.make_async_copy(
                in_ref.at[n, g],
                w_in.at[:, pl.ds((2 * n + g) * hidden, hidden)],
                weight_sem.at[2 * n + g],
            )
            for n in range(2)
            for g in range(2)
        ] + [
            pltpu.make_async_copy(
                out_w_ref.at[n], w_out.at[pl.ds(n * hidden, hidden)], weight_sem.at[4 + n]
            )
            for n in range(2)
        ]

    for load in loads():
        load.start()
    keep = lambda: pltpu.make_async_copy(x_ref, x_out.at[w, c, z], own_sem)
    keep().start()

    grad_parts = (
        (grad_own, w, None),
        (grad_x, wx, None),
        (grad_y, wy, None),
        (grad_low, wd, lo),
        (grad_high, wd, hi),
    )

    def grad_place(cc, ww, cols):
        return grads_out.at[ww, cc] if cols is None else grads_out.at[ww, cc, :, :, cols]

    def over(i, cc):
        src, ww, cols = grad_parts[i]
        return pltpu.make_async_remote_copy(
            src_ref=src,
            dst_ref=grad_place(cc, ww, cols),
            send_sem=over_send.at[i],
            recv_sem=over_recv.at[i],
            device_id=dev_c,
            device_id_type=MESH,
        )

    barrier = pltpu.get_barrier_semaphore()
    around = [(w, c, (z + k) % 4) for k in range(1, 4)]
    for device in [dev_x, dev_y, dev_c] + around:
        pl.semaphore_signal(barrier, inc=1, device_id=device, device_id_type=MESH)
    pl.semaphore_wait(barrier, 6)


    def view(chunk, cols):
        zz, cc, ww = chunk
        return x_out.at[ww, cc, zz] if cols is None else x_out.at[ww, cc, zz, :, cols]

    def copy(src, chunk, cols, slot, sem, device):
        return pltpu.make_async_remote_copy(
            src_ref=src,
            dst_ref=view(chunk, cols),
            send_sem=sem[0].at[sem[1:]],
            recv_sem=recv.at[chunk[0], chunk[1], slot],
            device_id=device,
            device_id_type=MESH,
        )

    sent = []
    devices_z = ((w, c, z + 1), (w, c, z - 1))

    def start(chunk, cols, slot, sem, device, src=None):
        copy(view(chunk, cols) if src is None else src, chunk, cols, slot, sem, device).start()
        sent.append((chunk, cols, slot, sem, device))

    def arrived(chunk, cols, slot):
        copy(view(chunk, cols), chunk, cols, slot, (send_c, 0, 0), dev_c).wait_recv()

    def spread(j):
        chunk = (order[j], c, w)
        src = x_ref if j == 0 else None
        start(chunk, None, 1, (send_x, j, 0), dev_x, src)
        start(chunk, None, 2, (send_y, j, 0), dev_y, src)
        start(chunk, None, 0, (send_c, j, 0), dev_c, src)

    def onward(j):
        chunk = (order[j], c, w)

        def moved(side):
            src = x_ref if j == 0 else view(chunk, None)
            return copy(src, chunk, None, 0, (send_z, j, side), devices_z[side])

        return (
            ((order[j] <= z) & (z < 3), functools.partial(moved, 0)),
            ((order[j] >= z) & (z > 0), functools.partial(moved, 1)),
        )

    def along(j):
        for there, moved in onward(j):
            pl.when(there)(lambda: moved().start())

    def share_in(j):
        arrived((order[j], c, w), None, 0)
        along(j)
        spread(j)

    def relay(j):
        from_x, from_y = ((order[j], c, wx), (order[j], c, wy))
        arrived(from_x, None, 1)
        start(from_x, lo, 3, (send_y, j, 1), dev_y)
        start(from_x, None, 1, (send_c, j, 1), dev_c)
        arrived(from_y, None, 2)
        start(from_y, hi, 4, (send_x, j, 1), dev_x)
        start(from_y, None, 2, (send_c, j, 2), dev_c)

    def across(j):
        chunk = (order[j], c, wd)
        for cols, slot in ((lo, 3), (hi, 4)):
            arrived(chunk, cols, slot)
            start(chunk, cols, slot, (send_c, j, slot), dev_c)

    def sibling(j):
        for ww, cols, slot in ((w, None, 0), (wx, None, 1), (wy, None, 2), (wd, lo, 3), (wd, hi, 4)):
            arrived((order[j], 1 - c, ww), cols, slot)


    def parts_of(a):
        return (pl.ds(0, half), pl.ds(half, wides[a] - half))

    def to_sibling(a):
        return pltpu.make_async_remote_copy(
            src_ref=others[a],
            dst_ref=sibs[a],
            send_sem=sib_send.at[a],
            recv_sem=sib_recv.at[a],
            device_id=dev_c,
            device_id_type=MESH,
        )

    def first_hops(a, j):
        low, high = parts_of(a)
        moves = (
            (wx, low, from_x1[a].at[j, 0], dev_x),
            (wd, low, from_x1[a].at[j, 1], dev_x),
            (wy, high, from_y1[a].at[j, 0], dev_y),
            (wd, high, from_y1[a].at[j, 1], dev_y),
        )
        return [
            pltpu.make_async_remote_copy(
                src_ref=mine[a].at[j % 2, ww, :, cols],
                dst_ref=dst,
                send_sem=one_send.at[a, j, i],
                recv_sem=one_recv.at[a, j, i],
                device_id=device,
                device_id_type=MESH,
            )
            for i, (ww, cols, dst, device) in enumerate(moves)
        ]

    def second_hops(a, j):
        low, high = parts_of(a)
        moves = ((wy, low, from_y2[a].at[j], dev_y), (wx, high, from_x2[a].at[j], dev_x))
        return [
            pltpu.make_async_remote_copy(
                src_ref=mine[a].at[j % 2, ww, :, cols],
                dst_ref=dst,
                send_sem=two_send.at[a, j, i],
                recv_sem=two_recv.at[a, j, i],
                device_id=device,
                device_id_type=MESH,
            )
            for i, (ww, cols, dst, device) in enumerate(moves)
        ]

    def last_hop(a, source, j):
        return pltpu.make_async_remote_copy(
            src_ref=mine[a].at[j % 2, w],
            dst_ref=from_z[a].at[source],
            send_sem=end_send.at[a, j],
            recv_sem=end_recv.at[a, source],
            device_id=(w, c, order[j]),
            device_id_type=MESH,
        )

    def total(*terms):
        added = terms[0].astype(f32)
        for term in terms[1:]:
            added = added + term.astype(f32)
        return added

    def after_first(j):
        p = j % 2
        for a in range(2):
            low, high = parts_of(a)
            for moved in first_hops(a, j):
                moved.wait_recv()
            mine[a][p, wy, :, low] = total(mine[a][p, wy, :, low], from_x1[a][j, 1]).astype(bf16)
            mine[a][p, wx, :, high] = total(mine[a][p, wx, :, high], from_y1[a][j, 1]).astype(bf16)
            for moved in second_hops(a, j):
                moved.start()

    def after_second(j):
        p = j % 2
        for a in range(2):
            low, high = parts_of(a)
            for moved in second_hops(a, j):
                moved.wait_recv()
            mine[a][p, w, :, low] = total(
                mine[a][p, w, :, low], from_x1[a][j, 0], from_y2[a][j]
            ).astype(bf16)
            mine[a][p, w, :, high] = total(
                mine[a][p, w, :, high], from_y1[a][j, 0], from_x2[a][j]
            ).astype(bf16)
            if j == 0:
                from_z[a][z] = mine[a][p, w]
            else:
                last_hop(a, z, j).start()

    def all_sent(j):
        for a in range(2):
            for moved in first_hops(a, j) + second_hops(a, j):
                moved.wait_send()
            if j > 0:
                last_hop(a, z, j).wait_send()


    code = order[0] + 4 * order[1] + 16 * order[2] + 64 * order[3]

    def tile_of(step):
        j = step // 2
        power = 1 + 3 * j + (9 * j * (j - 1)) // 2 + (27 * j * (j - 1) * (j - 2)) // 6
        return ((code // power) % 4, (c + 1 + step) % 2)

    def other_grads(step):
        zj, cc = tile_of(step)
        return pltpu.make_async_copy(grads_out.at[:, cc, zj], grads.at[0], grads_sem.at[5])

    def my_grads(step):
        zj, cc = tile_of(step)
        return [
            pltpu.make_async_copy(
                src.at[zj],
                grads.at[1, ww] if cols is None else grads.at[1, ww, :, cols],
                grads_sem.at[i],
            )
            for i, (src, ww, cols) in enumerate(grad_parts)
        ]

    def stores(step, own_tile):
        zj, cc = tile_of(step)
        pairs = [(gated, gated_out), (both, both_out)]
        pairs += [(grads.at[1], grads_out)] if own_tile else []
        return [
            pltpu.make_async_copy(src, dst.at[:, cc, zj], store_sem.at[i])
            for i, (src, dst) in enumerate(pairs)
        ]

    lanes = lax.broadcasted_iota(jnp.int32, (4 * share, 128), 1)

    def tile(step, own_tile, parity):
        zj, cc = tile_of(step)
        load = pltpu.make_async_copy(x_out.at[:, cc, zj], x_tile, tile_sem)
        load.start()
        if own_tile:
            for store in stores(step - 1, False):
                store.wait()
            for part in my_grads(step):
                part.wait()

            @pl.when(step < 7)
            def _():
                other_grads(step + 1).start()
        else:

            @pl.when(step > 0)
            def _():
                for store in stores(step - 1, True):
                    store.wait()

            for part in my_grads(step + 1):
                part.start()
            other_grads(step).wait()
        load.wait()
        rows = x_tile[...].reshape(4 * share, width)
        upstream = grads[1 if own_tile else 0].reshape(4 * share, width)
        logits = jnp.dot(rows, router_ref[...], preferred_element_type=f32)
        logits = jnp.where(lanes < experts, logits, -1e30)
        raised = jnp.exp(logits - jnp.max(logits, axis=1, keepdims=True))
        gates = raised / jnp.sum(raised, axis=1, keepdims=True)
        gates = gates * kept_ref[:, cc, zj].reshape(4 * share, 128).astype(f32)
        d_gate = jnp.zeros((4 * share, 128), f32)
        for n in range(2):
            here = lanes == group * 2 + n
            gate = jnp.sum(jnp.where(here, gates, 0.0), axis=1, keepdims=True)
            at = 2 * n * hidden
            gate_pre = jnp.dot(rows, w_in[:, at : at + hidden], preferred_element_type=f32)
            up_pre = jnp.dot(
                rows, w_in[:, at + hidden : at + 2 * hidden], preferred_element_type=f32
            )
            back = contract_last(upstream, w_out[n * hidden : (n + 1) * hidden, :])
            sigmoid = 1.0 / (1.0 + jnp.exp(-gate_pre))
            silu = gate_pre * sigmoid
            activated = silu * up_pre
            d_gate = jnp.where(here, jnp.sum(activated * back, axis=1, keepdims=True), d_gate)
            back = gate * back
            d_pre = back * up_pre * sigmoid * (1.0 + gate_pre * (1.0 - sigmoid))
            shape = (4, share, hidden)
            gated[:, :, n * hidden : (n + 1) * hidden] = (
                (gate * activated).astype(bf16).reshape(shape)
            )
            both[:, :, at : at + hidden] = d_pre.astype(bf16).reshape(shape)
            both[:, :, at + hidden : at + 2 * hidden] = (back * silu).astype(bf16).reshape(shape)
        for store in stores(step, own_tile):
            store.start()
        if own_tile:
            for a in range(2):
                to_sibling(a).wait_recv()
        else:

            @pl.when(step > 0)
            def _():
                for a in range(2):
                    to_sibling(a).wait_send()

        def put(a, cols, count, value):
            value = value.reshape(4, share, count)
            if own_tile:
                value = value + sibs[a][:, :, cols].astype(f32)
                mine[a][parity, :, :, cols] = value.astype(bf16)
            else:
                others[a][:, :, cols] = value.astype(bf16)

        put(0, pl.ds(width, 128), 128, d_gate)
        d_rows = both[...].reshape(4 * share, 4 * hidden)
        g_rows = gated[...].reshape(4 * share, 2 * hidden)

        def columns(m, carried):
            cols = pl.ds(pl.multiple_of(m * 256, 256), 256)
            put(0, cols, 256, contract_last(d_rows, w_in[cols, :]))
            put(1, cols, 256, jnp.dot(g_rows, w_out[:, cols], preferred_element_type=f32))
            return carried

        lax.fori_loop(0, width // 256, columns, None)

    def before_other(j):
        if j == 0:
            for i in range(5):
                over(i, c).start()
            along(0)
            spread(0)
            share_in(1)
            relay(0)
            keep().wait()
            for load in loads():
                load.wait()
            for i in range(5):
                over(i, 1 - c).wait_recv()
            other_grads(0).start()
        if j >= 2:
            after_second(j - 2)
        across(j)
        sibling(j)

    def before_mine(j):
        if j + 2 < 4:
            share_in(j + 2)
        if j + 1 < 4:
            relay(j + 1)
        if j >= 1:
            after_first(j - 1)
        if j >= 2:
            all_sent(j - 2)

    def round_of(j, carry):
        for k in range(4):
            pl.when(j == k)(functools.partial(before_other, k))
        tile(2 * j, False, None)

        @pl.when(j > 0)
        def _():
            pl.semaphore_wait(credit, 1)

        for a in range(2):
            to_sibling(a).start()
        for k in range(4):
            pl.when(j == k)(functools.partial(before_mine, k))
        tile(2 * j + 1, True, j % 2)

        @pl.when(j < 3)
        def _():
            pl.semaphore_signal(credit, inc=1, device_id=dev_c, device_id_type=MESH)

        for k in range(4):

            @pl.when(j == k)
            def _():
                for a in range(2):
                    for moved in first_hops(a, k):
                        moved.start()

        return carry

    lax.fori_loop(0, 4, round_of, None)
    after_second(2)
    after_first(3)
    after_second(3)
    for store in stores(7, True):
        store.wait()
    for a, result in ((0, dx_own), (1, moe_own)):
        to_sibling(a).wait_send()
        for k in range(1, 4):
            last_hop(a, (z + k) % 4, 1).wait_recv()
        result[...] = total(*(from_z[a][k] for k in range(4)))
    all_sent(2)
    all_sent(3)
    for i in range(5):
        over(i, c).wait_send()
    for chunk, cols, slot, sem, device in sent:
        copy(view(chunk, cols), chunk, cols, slot, sem, device).wait_send()
    for j in range(4):
        for there, moved in onward(j):
            pl.when(there)(lambda: moved().wait_send())


def experts_call(rows, grads, kept, router, expert_in, expert_out, experts):
    share, width = rows.shape
    hidden = expert_out.shape[1]
    blocks = (4, 2, 4, share)
    bf16, f32 = (jnp.bfloat16, jnp.float32)
    dma = pltpu.SemaphoreType.DMA
    anywhere, vmem = (pl.BlockSpec(memory_space=pl.ANY), pl.BlockSpec(memory_space=pltpu.VMEM))
    wides = (width + 128, width)
    half = width // 2
    both = lambda shape: [pltpu.VMEM(shape(wide), bf16) for wide in wides]
    return pl.pallas_call(
        functools.partial(experts_kernel, experts),
        out_shape=tuple(
            jax.ShapeDtypeStruct(blocks + (n,), bf16)
            for n in (width, width, 2 * hidden, 4 * hidden)
        )
        + tuple(jax.ShapeDtypeStruct((share, wide), f32) for wide in wides),
        in_specs=[anywhere] * 6 + [vmem, vmem, anywhere, anywhere],
        out_specs=(anywhere,) * 4 + (vmem, vmem),
        scratch_shapes=[
            pltpu.VMEM((4, share, width), bf16),
            pltpu.VMEM((width, 4 * hidden), bf16),
            pltpu.VMEM((2 * hidden, width), bf16),
            pltpu.VMEM((2, 4, share, width), bf16),
            pltpu.VMEM((4, share, 2 * hidden), bf16),
            pltpu.VMEM((4, share, 4 * hidden), bf16),
            *both(lambda wide: (4, share, wide)),
            *both(lambda wide: (2, 4, share, wide)),
            *both(lambda wide: (4, share, wide)),
            *both(lambda wide: (4, 2, share, half)),
            *both(lambda wide: (4, 2, share, wide - half)),
            *both(lambda wide: (4, share, half)),
            *both(lambda wide: (4, share, wide - half)),
            *both(lambda wide: (4, share, wide)),
            dma,
            dma,
            dma((6,)),
            dma((6,)),
            dma((3,)),
            dma((4, 2)),
            dma((4, 2)),
            dma((4, 2)),
            dma((4, 5)),
            dma((4, 2, 5)),
            dma((5,)),
            dma((5,)),
            dma((2,)),
            dma((2,)),
            pltpu.SemaphoreType.REGULAR,
            dma((2, 4, 4)),
            dma((2, 4, 4)),
            dma((2, 4, 2)),
            dma((2, 4, 2)),
            dma((2, 4)),
            dma((2, 4)),
        ],
        compiler_params=pltpu.CompilerParams(
            collective_id=0, has_side_effects=True, vmem_limit_bytes=62 << 20
        ),
    )(rows, *grads, kept, router, expert_in, expert_out)


def swapped(rows, flip):
    return lax.ppermute(rows, WEIGHTS, [(k, k ^ flip) for k in range(4)])


def grads_around(rows, share):
    half = rows.shape[1] // 2
    from_x, from_y = (swapped(rows, 1), swapped(rows, 2))
    parts = (rows, from_x, from_y, swapped(from_x[:, :half], 2), swapped(from_y[:, half:], 1))
    return [part.reshape(-1, share, part.shape[1]) for part in parts]


def gathered(rows, axes):
    return lax.all_gather(rows, axes, axis=0, tiled=True)


def scattered(rows, axes):
    return lax.psum_scatter(rows, axes, scatter_dimension=0, tiled=True)


def fit_rows(values, rows):
    flat = values.reshape(-1)
    columns = -(-flat.shape[0] // rows)
    return jnp.pad(flat, (0, rows * columns - flat.shape[0])).reshape(rows, columns)


def per_device_dense(
    layer_in,
    norm_gains,
    qkv_weight,
    qk_gains,
    out_weight,
    router,
    expert_in,
    expert_out,
    grad_out,
    segments,
    routes,
    route_order,
):
    group = GROUP
    everyone = EVERYONE
    group_count = lax.axis_size(group)
    tensor_count = lax.axis_size(TENSOR)
    context_rank = lax.axis_index(CONTEXT)
    tensor_rank = lax.axis_index(TENSOR)
    seq_count, half_len, model_width = layer_in.shape
    token_count = seq_count * half_len
    top_count = routes.shape[2]
    weight_rows, _, head_width = qkv_weight.shape
    expert_total = router.shape[1]
    local_experts = expert_in.shape[0]
    hidden_width = expert_in.shape[3]
    head_rows, _, local_heads = qk_gains.shape
    head_size = head_rows * group_count
    share = token_count // tensor_count
    bf16, f32 = jnp.bfloat16, jnp.float32

    capacity = token_count * top_count * 9 // (8 * expert_total)
    routed, slot_of = pair_slots(
        routes.reshape(token_count, top_count),
        route_order.reshape(token_count, top_count),
        expert_total,
    )
    kept = routed & (slot_of < capacity)

    front_small = jnp.concatenate(
        [norm_gains, fit_rows(qk_gains, weight_rows)], axis=1
    )
    front = gathered(
        jnp.concatenate([qkv_weight.reshape(weight_rows, -1), front_small], axis=1), group
    )
    own_grads = grad_out.reshape(token_count, model_width)
    front, own_grads = lax.optimization_barrier((front, own_grads))
    around = grads_around(own_grads, share)
    back_small = jnp.concatenate(
        [router, fit_rows(kept.astype(bf16), weight_rows)], axis=1
    )
    back = gathered(jnp.concatenate([out_weight, back_small], axis=1), group)
    qkv_full = front[:, : 3 * head_width]
    gain_full = front[:, 3 * head_width : 3 * head_width + 2].astype(f32)
    gain_attn, gain_ffn = (gain_full[:, 0], gain_full[:, 1])
    qk_gain_full = (
        front[:, 3 * head_width + 2 :]
        .reshape(group_count, -1)[:, : head_rows * 2 * local_heads]
        .reshape(head_size, 2, local_heads)
        .astype(f32)
    )
    query_gain = qk_gain_full[:, 0, :].T.reshape(-1)
    key_gain = qk_gain_full[:, 1, :].T.reshape(-1)
    out_full = back[:, :head_width]
    router_full = back[:, head_width : head_width + expert_total]
    kept_all = (
        back[:, head_width + expert_total :]
        .reshape(group_count, -1)[:, : expert_total * token_count]
        .reshape(group_count, expert_total, token_count)
    )
    inv_root = 1.0 / math.sqrt(head_size)
    residual = layer_in.reshape(token_count, model_width).astype(f32)
    scale_one = lax.rsqrt(jnp.mean(residual * residual, axis=1, keepdims=True) + epsilon)
    normed_one = (residual * scale_one * gain_attn).astype(bf16)
    projected = jnp.dot(normed_one, qkv_full, preferred_element_type=f32)
    query_raw = projected[:, :head_width]
    key_raw = projected[:, head_width : 2 * head_width]
    value_raw = projected[:, 2 * head_width :]
    square_sums = row_sums(
        jnp.stack(
            [jnp.sum(query_raw * query_raw, axis=1), jnp.sum(key_raw * key_raw, axis=1)], axis=1
        )
    )
    query_scale = lax.rsqrt(square_sums[:, 0:1] / model_width + epsilon)
    key_scale = lax.rsqrt(square_sums[:, 1:2] / model_width + epsilon)
    heads_shape = (seq_count, half_len, local_heads, head_size)
    query_hat = (query_raw * query_scale * query_gain).reshape(heads_shape)
    key_hat = (key_raw * key_scale * key_gain).reshape(heads_shape)
    query_pos = context_rank * half_len + jnp.arange(half_len, dtype=jnp.int32)
    cosine_table, sine_table = rotary_tables(query_pos, head_size)
    cosine_table = cosine_table[None, :, None, :]
    sine_table = sine_table[None, :, None, :]
    query_rot = (query_hat * cosine_table + rotate_half(query_hat) * sine_table).astype(bf16)
    key_rot = (key_hat * cosine_table + rotate_half(key_hat) * sine_table).astype(bf16)
    value_low = value_raw.astype(bf16).reshape(heads_shape)
    key_prev, value_prev = passed_along((key_rot, value_low), CONTEXT, 1)
    all_keys = jnp.concatenate([key_prev, key_rot], axis=1)
    all_values = jnp.concatenate([value_prev, value_low], axis=1)
    key_pos = jnp.concatenate([query_pos - half_len, query_pos])
    seg_query = lax.dynamic_slice_in_dim(segments, context_rank * half_len, half_len, 1)
    seg_prev = lax.dynamic_slice_in_dim(
        segments, jnp.maximum(context_rank - 1, 0) * half_len, half_len, 1
    )
    seg_keys = jnp.concatenate([seg_prev, seg_query], axis=1)
    causal = (key_pos[None, :] >= 0) & (key_pos[None, :] <= query_pos[:, None])
    allowed = causal[None] & (seg_query[:, :, None] == seg_keys[:, None, :])

    def score_block(queries, key_rows):
        raw_scores = (
            jnp.einsum(BY_SCORE, queries, key_rows, preferred_element_type=f32) * inv_root
        )
        return jnp.where(allowed[:, None], raw_scores, -1e30)

    scores = score_block(query_rot, all_keys)
    row_max = jnp.max(scores, axis=-1, keepdims=True)
    exponent = jnp.exp(scores - row_max)
    row_total = jnp.sum(exponent, axis=-1, keepdims=True)
    log_total = row_max + jnp.log(row_total)
    attn_probs = (exponent / row_total).astype(bf16)
    attended = jnp.einsum(BY_QUERY, attn_probs, all_values, preferred_element_type=f32)
    attended_low = attended.reshape(token_count, -1).astype(bf16)
    attn_partial = jnp.einsum("tf,df->td", attended_low, out_full, preferred_element_type=f32)

    own_rows = lambda rows: lax.dynamic_slice_in_dim(rows, tensor_rank * share, share, 0)
    residual_own = own_rows(residual)
    hidden = residual_own + scattered(attn_partial.astype(bf16), TENSOR).astype(f32)
    scale_two = lax.rsqrt(jnp.mean(hidden * hidden, axis=1, keepdims=True) + epsilon)
    unit_two = hidden * scale_two
    normed_two = (unit_two * gain_ffn).astype(bf16)
    upstream = own_rows(grad_out.reshape(token_count, model_width)).astype(f32)

    pad_experts = lambda rows: jnp.pad(rows, ((0, 0), (0, 128 - expert_total)))
    kept_rows = kept_all.transpose(0, 2, 1).reshape(-1, expert_total)
    normed_all, grads_all, gated, d_both, d_sums, moe_own = experts_call(
        normed_two,
        around,
        pad_experts(kept_rows).reshape(4, 2, 4, share, 128),
        pad_experts(router_full),
        expert_in,
        expert_out,
        expert_total,
    )
    normed_all, grads_all, gated, d_both = (
        rows.reshape(group_count * token_count, -1)
        for rows in (normed_all, grads_all, gated, d_both)
    )
    layer_out = gathered((hidden + moe_own).astype(bf16), TENSOR).reshape(layer_in.shape)
    grad_expert_in = (
        jnp.dot(normed_all.T, d_both, preferred_element_type=f32)
        .reshape(model_width, local_experts, 2, hidden_width)
        .transpose(1, 2, 0, 3)
    )
    grad_expert_out = jnp.dot(gated.T, grads_all, preferred_element_type=f32).reshape(
        expert_out.shape
    )

    kept_own = own_rows(kept.T).astype(f32)
    probs_own = jax.nn.softmax(
        jnp.dot(normed_two, router_full, preferred_element_type=f32), axis=1
    )
    d_probs = d_sums[:, model_width : model_width + expert_total] * kept_own
    d_logits = (
        probs_own * (d_probs - jnp.sum(probs_own * d_probs, axis=1, keepdims=True))
    ).astype(bf16)
    d_normed_two = d_sums[:, :model_width] + jnp.dot(
        d_logits, router_full.T, preferred_element_type=f32
    )
    d_router = jnp.dot(normed_two.T, d_logits, preferred_element_type=f32)
    d_gain_ffn = jnp.sum(d_normed_two * unit_two, axis=0)
    scaled_ffn = gain_ffn * d_normed_two
    d_hidden = upstream + scale_two * (
        scaled_ffn - unit_two * jnp.mean(scaled_ffn * unit_two, axis=1, keepdims=True)
    )
    d_hidden_low = gathered(d_hidden.astype(bf16), TENSOR)

    d_attended = (
        jnp.dot(d_hidden_low, out_full, preferred_element_type=f32)
        .astype(bf16)
        .reshape(heads_shape)
    )
    d_out_weight = jnp.einsum("td,tf->df", d_hidden_low, attended_low, preferred_element_type=f32)
    probs_again = jnp.exp(score_block(query_rot, all_keys) - log_total)
    probs_again_low = probs_again.astype(bf16)
    d_probs_att = jnp.einsum(
        BY_SCORE, d_attended, all_values, preferred_element_type=f32
    )
    d_values_all = jnp.einsum(
        BY_KEY, probs_again_low, d_attended, preferred_element_type=f32
    )
    row_dot = jnp.sum(probs_again * d_probs_att, axis=-1, keepdims=True)
    d_scores = (probs_again * (d_probs_att - row_dot)).astype(bf16)
    d_query_rot = (
        jnp.einsum(BY_QUERY, d_scores, all_keys, preferred_element_type=f32) * inv_root
    )
    d_keys_all = (
        jnp.einsum(BY_KEY, d_scores, query_rot, preferred_element_type=f32) * inv_root
    )
    back_key, back_value = (
        passed_along(d_keys_all[:, :half_len].astype(bf16), CONTEXT, -1).astype(f32),
        passed_along(d_values_all[:, :half_len].astype(bf16), CONTEXT, -1).astype(f32),
    )
    d_key_rot = d_keys_all[:, half_len:] + back_key
    d_value = (d_values_all[:, half_len:] + back_value).reshape(token_count, -1)
    d_query_hat = (d_query_rot * cosine_table + rotate_back(d_query_rot * sine_table)).reshape(
        token_count, -1
    )
    d_key_hat = (d_key_rot * cosine_table + rotate_back(d_key_rot * sine_table)).reshape(
        token_count, -1
    )
    centre = row_sums(
        jnp.stack(
            [
                jnp.sum(query_gain * d_query_hat * query_raw, axis=1),
                jnp.sum(key_gain * d_key_hat * key_raw, axis=1),
            ],
            axis=1,
        )
    )
    d_query_raw = (
        query_scale * query_gain * d_query_hat
        - query_raw * (query_scale**3 / model_width) * centre[:, 0:1]
    )
    d_key_raw = (
        key_scale * key_gain * d_key_hat - key_raw * (key_scale**3 / model_width) * centre[:, 1:2]
    )
    d_query_gain = (
        jnp.sum(d_query_hat * query_raw * query_scale, axis=0).reshape(local_heads, head_size).T
    )
    d_key_gain = jnp.sum(d_key_hat * key_raw * key_scale, axis=0).reshape(local_heads, head_size).T
    d_qk_gains = jnp.stack([d_query_gain, d_key_gain], axis=1)
    d_projected = jnp.concatenate([d_query_raw, d_key_raw, d_value], axis=1).astype(bf16)
    d_normed_one = scattered(
        jnp.einsum("tf,df->td", d_projected, qkv_full, preferred_element_type=f32).astype(bf16),
        TENSOR,
    ).astype(f32)
    d_qkv = jnp.einsum("td,tf->df", normed_one, d_projected, preferred_element_type=f32)

    scale_own = own_rows(scale_one)
    unit_one = residual_own * scale_own
    d_gain_attn = jnp.sum(d_normed_one * unit_one, axis=0)
    scaled_attn = gain_attn * d_normed_one
    grad_in = d_hidden + scale_own * (
        scaled_attn - unit_one * jnp.mean(scaled_attn * unit_one, axis=1, keepdims=True)
    )
    grad_in = gathered(grad_in.astype(bf16), TENSOR).astype(f32).reshape(layer_in.shape)

    grad_qkv = (
        scattered(d_qkv.astype(bf16), group)
        .astype(f32)
        .reshape(weight_rows, 3, head_width)
    )
    grad_out_weight = scattered(d_out_weight.astype(bf16), group).astype(f32)
    gain_share = weight_rows // tensor_count
    router_share = expert_total // tensor_count
    own_slot = (jnp.arange(tensor_count) == tensor_rank).astype(f32)[None, :, None]
    small = jnp.concatenate(
        [
            jnp.stack([d_gain_attn, d_gain_ffn], axis=1).reshape(group_count, tensor_count, -1),
            d_router.reshape(group_count, weight_rows, tensor_count, router_share)
            .transpose(0, 2, 1, 3)
            .reshape(group_count, tensor_count, -1),
            d_qk_gains.reshape(group_count, 1, -1) * own_slot,
        ],
        axis=2,
    ).reshape(group_count * tensor_count, -1)
    small = scattered(small, everyone)[0]
    ends = (gain_share * 2, gain_share * 2 + weight_rows * router_share)
    return (
        layer_out,
        grad_in,
        small[: ends[0]].reshape(gain_share, 2),
        grad_qkv,
        small[ends[1] :].reshape(head_rows, 2, local_heads),
        grad_out_weight,
        small[ends[0] : ends[1]].reshape(weight_rows, router_share),
        grad_expert_in,
        grad_expert_out,
    )


def solution(mesh):
    placed = (
        P(WEIGHTS, CONTEXT, None),
        P(GROUP, None),
        P(GROUP, None, TENSOR),
        P(GROUP, None, TENSOR),
        P(GROUP, TENSOR),
        P(GROUP, None),
        P(GROUP, None, None, TENSOR),
        P(GROUP, TENSOR, None),
        P(WEIGHTS, CONTEXT, None),
        P(WEIGHTS, None),
        P(WEIGHTS, CONTEXT, None),
        P(WEIGHTS, CONTEXT, None),
    )
    axes = tuple(mesh.shape[axis] for axis in EVERYONE)

    def per_device(*blocks):
        dense = axes == (4, 2, 4) and blocks[5].shape[1] <= 2 * blocks[10].shape[2]
        return (per_device_dense if dense else per_device_slots)(*blocks)

    return jax.shard_map(
        per_device,
        mesh=mesh,
        in_specs=placed,
        out_specs=(
            P(WEIGHTS, CONTEXT, None),
            P(WEIGHTS, CONTEXT, None),
            P(EVERYONE, None),
            P(GROUP, None, TENSOR),
            P(GROUP, None, TENSOR),
            P(GROUP, TENSOR),
            P(GROUP, TENSOR),
            P(GROUP, None, None, TENSOR),
            P(GROUP, TENSOR, None),
        ),
        check_vma=False,
    )
```

```python
import functools
import math

import jax
import jax.numpy as jnp
from jax import lax
from jax.experimental import pallas as pl
from jax.experimental.pallas import tpu as pltpu
from jax.sharding import PartitionSpec as P

epsilon = 1e-05
rotary_base = 10000.0
WEIGHTS, CONTEXT, TENSOR = ("weights", "context", "tensor")
GROUP = (WEIGHTS, CONTEXT)
EVERYONE = (WEIGHTS, CONTEXT, TENSOR)
MESH = pl.DeviceIdType.MESH
BY_SCORE = "sqhd,skhd->shqk"
BY_QUERY = "shqk,skhd->sqhd"
BY_KEY = "shqk,sqhd->skhd"


def passed_along(value, axis, steps):
    count = lax.axis_size(axis)
    leading, last = (max(0, -steps), min(count, count - steps))
    return lax.ppermute(value, axis, [(source, source + steps) for source in range(leading, last)])


def rotate_half(values_in):
    middle = values_in.shape[-1] // 2
    return jnp.concatenate([-values_in[..., middle:], values_in[..., :middle]], axis=-1)


def rotate_back(grads_in):
    middle = grads_in.shape[-1] // 2
    return jnp.concatenate([grads_in[..., middle:], -grads_in[..., :middle]], axis=-1)


def rotary_tables(positions, head_size):
    frequency = rotary_base ** (-(2.0 * jnp.arange(head_size // 2, dtype=jnp.float32)) / head_size)
    angle_table = positions.astype(jnp.float32)[:, None] * frequency[None, :]
    angle_table = jnp.concatenate([angle_table, angle_table], axis=1)
    return (jnp.cos(angle_table), jnp.sin(angle_table))


def pair_slots(token_routes, token_ranks, expert_total):
    unused = token_routes.size
    hot = token_routes.T[None] == jnp.arange(expert_total, dtype=jnp.int32)[:, None, None]
    rank_of = jnp.min(jnp.where(hot, token_ranks.T[None], unused), axis=1)
    slot_of = jnp.sum((rank_of[:, :, None] < rank_of[:, None, :]).astype(jnp.int32), axis=1)
    return (rank_of < unused, slot_of)


def place_pairs(pair_expert, rank, expert_total, capacity, top_count):
    pair_count = pair_expert.shape[0]
    token_routes = pair_expert.reshape(-1, top_count)
    slot_of = pair_slots(token_routes, rank.reshape(-1, top_count), expert_total)[1]
    slot_index = jnp.take_along_axis(slot_of.T, token_routes, axis=1).reshape(pair_count)
    kept_pair = slot_index < capacity
    dest_row = jnp.where(kept_pair, pair_expert * capacity + slot_index, expert_total * capacity)
    slot_pair = (
        jnp.full((expert_total * capacity + 1,), pair_count, jnp.int32)
        .at[dest_row]
        .set(jnp.arange(pair_count, dtype=jnp.int32))[:-1]
    )
    return (kept_pair, dest_row, slot_pair)


def row_sums(partial_rows):
    return lax.psum(partial_rows, TENSOR)


def tensor_sum(partial_rows):
    return lax.psum(partial_rows, TENSOR)


def to_owners(slot_rows):
    return lax.all_to_all(
        slot_rows, GROUP, split_axis=0, concat_axis=0, tiled=True
    )


def expert_front(slot_inputs, expert_in):
    both_pre = jnp.einsum(
        "sncd,ngdf->sncgf", slot_inputs, expert_in, preferred_element_type=jnp.float32
    )
    return (both_pre[..., 0, :], both_pre[..., 1, :])


def per_device_slots(
    layer_in,
    norm_gains,
    qkv_weight,
    qk_gains,
    out_weight,
    router,
    expert_in,
    expert_out,
    grad_out,
    segments,
    routes,
    route_order,
):
    group_count = lax.axis_size(GROUP)
    tensor_count = lax.axis_size(TENSOR)
    context_rank = lax.axis_index(CONTEXT)
    tensor_rank = lax.axis_index(TENSOR)
    seq_count, half_len, model_width = layer_in.shape
    token_count = seq_count * half_len
    top_count = routes.shape[2]
    qkv_full, out_full, qk_gain_full, gain_full, router_full = (
        lax.all_gather(qkv_weight, GROUP, axis=0, tiled=True),
        lax.all_gather(out_weight, GROUP, axis=0, tiled=True),
        lax.all_gather(qk_gains, GROUP, axis=0, tiled=True),
        lax.all_gather(norm_gains, GROUP, axis=0, tiled=True),
        lax.all_gather(router, GROUP, axis=0, tiled=True),
    )
    head_size = qk_gain_full.shape[0]
    local_heads = qk_gain_full.shape[2]
    expert_total = router_full.shape[1]
    gain_attn = gain_full[:, 0].astype(jnp.float32)
    gain_ffn = gain_full[:, 1].astype(jnp.float32)
    query_gain = qk_gain_full[:, 0, :].astype(jnp.float32).T.reshape(-1)
    key_gain = qk_gain_full[:, 1, :].astype(jnp.float32).T.reshape(-1)
    inv_root = 1.0 / math.sqrt(head_size)
    residual = layer_in.reshape(token_count, model_width).astype(jnp.float32)
    scale_one = lax.rsqrt(jnp.mean(residual * residual, axis=1, keepdims=True) + epsilon)
    unit_one = residual * scale_one
    normed_one = (unit_one * gain_attn).astype(jnp.bfloat16)
    projected = jnp.einsum("td,dgf->tgf", normed_one, qkv_full, preferred_element_type=jnp.float32)
    query_raw = projected[:, 0]
    key_raw = projected[:, 1]
    value_raw = projected[:, 2]
    square_sums = row_sums(
        jnp.stack(
            [jnp.sum(query_raw * query_raw, axis=1), jnp.sum(key_raw * key_raw, axis=1)], axis=1
        )
    )
    query_scale = lax.rsqrt(square_sums[:, 0:1] / model_width + epsilon)
    key_scale = lax.rsqrt(square_sums[:, 1:2] / model_width + epsilon)
    heads_shape = (seq_count, half_len, local_heads, head_size)
    query_hat = (query_raw * query_scale * query_gain).reshape(heads_shape)
    key_hat = (key_raw * key_scale * key_gain).reshape(heads_shape)
    query_pos = context_rank * half_len + jnp.arange(half_len, dtype=jnp.int32)
    cosine_table, sine_table = rotary_tables(query_pos, head_size)
    cosine_table = cosine_table[None, :, None, :]
    sine_table = sine_table[None, :, None, :]
    query_rot = (query_hat * cosine_table + rotate_half(query_hat) * sine_table).astype(
        jnp.bfloat16
    )
    key_rot = (key_hat * cosine_table + rotate_half(key_hat) * sine_table).astype(jnp.bfloat16)
    value_low = value_raw.astype(jnp.bfloat16).reshape(heads_shape)
    key_prev, value_prev = passed_along((key_rot, value_low), CONTEXT, 1)
    all_keys = jnp.concatenate([key_prev, key_rot], axis=1)
    all_values = jnp.concatenate([value_prev, value_low], axis=1)
    key_pos = jnp.concatenate([query_pos - half_len, query_pos])
    seg_query = lax.dynamic_slice_in_dim(segments, context_rank * half_len, half_len, 1)
    seg_prev = lax.dynamic_slice_in_dim(
        segments, jnp.maximum(context_rank - 1, 0) * half_len, half_len, 1
    )
    seg_keys = jnp.concatenate([seg_prev, seg_query], axis=1)
    causal = (key_pos[None, :] >= 0) & (key_pos[None, :] <= query_pos[:, None])
    allowed = causal[None] & (seg_query[:, :, None] == seg_keys[:, None, :])

    def score_block(queries, key_rows):
        raw_scores = (
            jnp.einsum(BY_SCORE, queries, key_rows, preferred_element_type=jnp.float32)
            * inv_root
        )
        return jnp.where(allowed[:, None], raw_scores, -1e30)

    scores = score_block(query_rot, all_keys)
    row_max = jnp.max(scores, axis=-1, keepdims=True)
    exponent = jnp.exp(scores - row_max)
    row_total = jnp.sum(exponent, axis=-1, keepdims=True)
    log_total = row_max + jnp.log(row_total)
    attn_probs = (exponent / row_total).astype(jnp.bfloat16)
    attended = jnp.einsum(
        BY_QUERY, attn_probs, all_values, preferred_element_type=jnp.float32
    )
    attended_low = attended.reshape(token_count, -1).astype(jnp.bfloat16)
    attn_partial = jnp.einsum(
        "tf,df->td", attended_low, out_full, preferred_element_type=jnp.float32
    )
    hidden = residual + tensor_sum(attn_partial)
    scale_two = lax.rsqrt(jnp.mean(hidden * hidden, axis=1, keepdims=True) + epsilon)
    unit_two = hidden * scale_two
    normed_two = (unit_two * gain_ffn).astype(jnp.bfloat16)
    logits = jnp.dot(normed_two, router_full, preferred_element_type=jnp.float32)
    router_probs = jax.nn.softmax(logits, axis=1)
    capacity = token_count * top_count * 9 // (8 * expert_total)
    local_experts = expert_in.shape[0]
    pair_count = token_count * top_count
    token_routes = routes.reshape(token_count, top_count)
    kept_pair, dest_row, slot_pair = place_pairs(
        token_routes.reshape(pair_count), route_order.reshape(pair_count), expert_total, capacity, top_count
    )
    zero_row = jnp.zeros((1, model_width), jnp.bfloat16)
    zero_wide = jnp.zeros((1, model_width), jnp.float32)
    slot_shape = (group_count, local_experts, capacity, model_width)
    dispatch_rows = jnp.concatenate([normed_two, zero_row], axis=0)[slot_pair // top_count].reshape(
        slot_shape
    )
    received = lax.all_to_all(
        dispatch_rows, GROUP, split_axis=0, concat_axis=0, tiled=True
    )
    gate_pre, up_pre = expert_front(received, expert_in)
    sigmoid_gate = jax.nn.sigmoid(gate_pre)
    silu_gate = gate_pre * sigmoid_gate
    activated = (silu_gate * up_pre).astype(jnp.bfloat16)
    expert_partial = jnp.einsum(
        "sncf,nfd->sncd", activated, expert_out, preferred_element_type=jnp.float32
    )
    kept_float = kept_pair.reshape(token_count, top_count).astype(jnp.float32)
    gate_weight = jnp.take_along_axis(router_probs, token_routes, axis=1) * kept_float
    upstream = grad_out.reshape(token_count, model_width).astype(jnp.float32)
    returned = to_owners(expert_partial).reshape(expert_total * capacity, model_width)
    picked = jnp.concatenate([returned, zero_wide], axis=0)[dest_row].reshape(
        token_count, top_count, model_width
    )
    moe_partial = jnp.sum(gate_weight[:, :, None] * picked, axis=1)
    dot_partial = jnp.sum(upstream[:, None, :] * picked, axis=2)
    moe_total, dot_total = lax.psum((moe_partial, dot_partial), TENSOR)
    layer_out = (hidden + moe_total).astype(jnp.bfloat16).reshape(layer_in.shape)
    d_gate = dot_total * kept_float
    route_hot = (
        token_routes[:, :, None] == jnp.arange(expert_total, dtype=jnp.int32)[None, None, :]
    ).astype(jnp.float32)
    d_probs = jnp.sum(d_gate[:, :, None] * route_hot, axis=1)
    d_logits = (
        router_probs * (d_probs - jnp.sum(router_probs * d_probs, axis=1, keepdims=True))
    ).astype(jnp.bfloat16)
    d_pair = (
        (gate_weight[:, :, None] * upstream[:, None, :])
        .astype(jnp.bfloat16)
        .reshape(pair_count, model_width)
    )
    d_slots = jnp.concatenate([d_pair, zero_row], axis=0)[slot_pair].reshape(slot_shape)
    d_received = lax.all_to_all(
        d_slots, GROUP, split_axis=0, concat_axis=0, tiled=True
    )
    d_activated = jnp.einsum(
        "sncd,nfd->sncf", d_received, expert_out, preferred_element_type=jnp.float32
    )
    grad_expert_out = jnp.einsum(
        "sncf,sncd->nfd", activated, d_received, preferred_element_type=jnp.float32
    )
    d_gate_pre = d_activated * up_pre * sigmoid_gate * (1.0 + gate_pre * (1.0 - sigmoid_gate))
    d_up_pre = d_activated * silu_gate
    d_both = jnp.stack([d_gate_pre, d_up_pre], axis=3).astype(jnp.bfloat16)
    d_inputs = jnp.einsum("sncgf,ngdf->sncd", d_both, expert_in, preferred_element_type=jnp.float32)
    grad_expert_in = jnp.einsum(
        "sncd,sncgf->ngdf", received, d_both, preferred_element_type=jnp.float32
    )
    d_returned = to_owners(d_inputs).reshape(expert_total * capacity, model_width)
    d_normed_part = jnp.sum(
        jnp.concatenate([d_returned, zero_wide], axis=0)[dest_row].reshape(
            token_count, top_count, model_width
        ),
        axis=1,
    )
    d_normed_two = tensor_sum(d_normed_part) + jnp.dot(
        d_logits, router_full.T, preferred_element_type=jnp.float32
    )
    d_router = jnp.dot(normed_two.T, d_logits, preferred_element_type=jnp.float32)
    d_gain_ffn = jnp.sum(d_normed_two * unit_two, axis=0)
    scaled_ffn = gain_ffn * d_normed_two
    d_hidden = upstream + scale_two * (
        scaled_ffn - unit_two * jnp.mean(scaled_ffn * unit_two, axis=1, keepdims=True)
    )
    d_hidden_low = d_hidden.astype(jnp.bfloat16)
    d_out_weight = jnp.einsum(
        "td,tf->df", d_hidden_low, attended_low, preferred_element_type=jnp.float32
    )
    d_attended = (
        jnp.dot(d_hidden_low, out_full, preferred_element_type=jnp.float32)
        .astype(jnp.bfloat16)
        .reshape(heads_shape)
    )
    probs_again = jnp.exp(score_block(query_rot, all_keys) - log_total)
    probs_again_low = probs_again.astype(jnp.bfloat16)
    d_probs_att = jnp.einsum(
        BY_SCORE, d_attended, all_values, preferred_element_type=jnp.float32
    )
    d_values_all = jnp.einsum(
        BY_KEY, probs_again_low, d_attended, preferred_element_type=jnp.float32
    )
    row_dot = jnp.sum(probs_again * d_probs_att, axis=-1, keepdims=True)
    d_scores = (probs_again * (d_probs_att - row_dot)).astype(jnp.bfloat16)
    d_query_rot = (
        jnp.einsum(BY_QUERY, d_scores, all_keys, preferred_element_type=jnp.float32)
        * inv_root
    )
    d_keys_all = (
        jnp.einsum(BY_KEY, d_scores, query_rot, preferred_element_type=jnp.float32)
        * inv_root
    )
    back_key, back_value = (
        passed_along(d_keys_all[:, :half_len].astype(jnp.bfloat16), CONTEXT, -1).astype(
            jnp.float32
        ),
        passed_along(d_values_all[:, :half_len].astype(jnp.bfloat16), CONTEXT, -1).astype(
            jnp.float32
        ),
    )
    d_key_rot = d_keys_all[:, half_len:] + back_key
    d_value = (d_values_all[:, half_len:] + back_value).reshape(token_count, -1)
    d_query_hat = (d_query_rot * cosine_table + rotate_back(d_query_rot * sine_table)).reshape(
        token_count, -1
    )
    d_key_hat = (d_key_rot * cosine_table + rotate_back(d_key_rot * sine_table)).reshape(
        token_count, -1
    )
    centre = row_sums(
        jnp.stack(
            [
                jnp.sum(query_gain * d_query_hat * query_raw, axis=1),
                jnp.sum(key_gain * d_key_hat * key_raw, axis=1),
            ],
            axis=1,
        )
    )
    d_query_raw = (
        query_scale * query_gain * d_query_hat
        - query_raw * (query_scale**3 / model_width) * centre[:, 0:1]
    )
    d_key_raw = (
        key_scale * key_gain * d_key_hat - key_raw * (key_scale**3 / model_width) * centre[:, 1:2]
    )
    d_query_gain = (
        jnp.sum(d_query_hat * query_raw * query_scale, axis=0).reshape(local_heads, head_size).T
    )
    d_key_gain = jnp.sum(d_key_hat * key_raw * key_scale, axis=0).reshape(local_heads, head_size).T
    d_qk_gains = jnp.stack([d_query_gain, d_key_gain], axis=1)
    d_projected = jnp.stack([d_query_raw, d_key_raw, d_value], axis=1).astype(jnp.bfloat16)
    d_normed_one = tensor_sum(
        jnp.einsum("tgf,dgf->td", d_projected, qkv_full, preferred_element_type=jnp.float32)
    )
    d_qkv = jnp.einsum("td,tgf->dgf", normed_one, d_projected, preferred_element_type=jnp.float32)
    d_gain_attn = jnp.sum(d_normed_one * unit_one, axis=0)
    scaled_attn = gain_attn * d_normed_one
    grad_in = d_hidden + scale_one * (
        scaled_attn - unit_one * jnp.mean(scaled_attn * unit_one, axis=1, keepdims=True)
    )
    d_norm_gains = jnp.stack([d_gain_attn, d_gain_ffn], axis=1)
    grad_qkv, grad_out_weight, grad_qk_gains, gain_rows, router_rows = (
        lax.psum_scatter(d_qkv, GROUP, scatter_dimension=0, tiled=True),
        lax.psum_scatter(d_out_weight, GROUP, scatter_dimension=0, tiled=True),
        lax.psum_scatter(d_qk_gains, GROUP, scatter_dimension=0, tiled=True),
        lax.psum_scatter(d_norm_gains, GROUP, scatter_dimension=0, tiled=True),
        lax.psum_scatter(d_router, GROUP, scatter_dimension=0, tiled=True),
    )
    gain_share = gain_rows.shape[0] // tensor_count
    grad_norm_gains = lax.dynamic_slice_in_dim(gain_rows, tensor_rank * gain_share, gain_share, 0)
    router_share = expert_total // tensor_count
    grad_router = lax.dynamic_slice_in_dim(router_rows, tensor_rank * router_share, router_share, 1)
    return (
        layer_out,
        grad_in.reshape(layer_in.shape),
        grad_norm_gains,
        grad_qkv,
        grad_qk_gains,
        grad_out_weight,
        grad_router,
        grad_expert_in,
        grad_expert_out,
    )


def contract_last(left, right):
    return lax.dot_general(
        left, right, (((1,), (1,)), ((), ())), preferred_element_type=jnp.float32
    )


def share_order(z):
    upper, odd = (z // 2, z % 2)
    return (z, z + 1 - 2 * upper, 2 + upper - 2 * odd, 3 - 3 * upper)


def neighbours(w):
    wx, wy = (w + 1 - 2 * (w % 2), (w + 2) % 4)
    return (wx, wy, wx + wy - w)


def experts_kernel(
    experts,
    x_ref,
    grad_own,
    grad_x,
    grad_y,
    grad_low,
    grad_high,
    kept_ref,
    router_ref,
    in_ref,
    out_w_ref,
    x_out,
    grads_out,
    gated_out,
    both_out,
    dx_own,
    moe_own,
    x_tile,
    w_in,
    w_out,
    grads,
    gated,
    both,
    *scratch,
):
    others, mine, sibs, from_x1, from_y1, from_y2, from_x2, from_z = (
        (scratch[2 * k], scratch[2 * k + 1]) for k in range(8)
    )
    (
        own_sem,
        tile_sem,
        weight_sem,
        grads_sem,
        store_sem,
        send_z,
        send_x,
        send_y,
        send_c,
        recv,
        over_send,
        over_recv,
        sib_send,
        sib_recv,
        credit,
        one_send,
        one_recv,
        two_send,
        two_recv,
        end_send,
        end_recv,
    ) = scratch[16:]
    w, c, z = (lax.axis_index(a) for a in (WEIGHTS, CONTEXT, TENSOR))
    wx, wy, wd = neighbours(w)
    share, width = x_ref.shape
    half = width // 2
    lo, hi = (pl.ds(0, half), pl.ds(half, half))
    dev_x, dev_y, dev_c = ((wx, c, z), (wy, c, z), (w, 1 - c, z))
    order = share_order(z)
    hidden = out_w_ref.shape[1]
    group = w * 2 + c
    bf16, f32 = (jnp.bfloat16, jnp.float32)
    wides = (width + 128, width)

    def loads():
        return [
            pltpu.make_async_copy(
                in_ref.at[n, g],
                w_in.at[:, pl.ds((2 * n + g) * hidden, hidden)],
                weight_sem.at[2 * n + g],
            )
            for n in range(2)
            for g in range(2)
        ] + [
            pltpu.make_async_copy(
                out_w_ref.at[n], w_out.at[pl.ds(n * hidden, hidden)], weight_sem.at[4 + n]
            )
            for n in range(2)
        ]

    for load in loads():
        load.start()
    keep = lambda: pltpu.make_async_copy(x_ref, x_out.at[w, c, z], own_sem)
    keep().start()

    grad_parts = (
        (grad_own, w, None),
        (grad_x, wx, None),
        (grad_y, wy, None),
        (grad_low, wd, lo),
        (grad_high, wd, hi),
    )

    def grad_place(cc, ww, cols):
        return grads_out.at[ww, cc] if cols is None else grads_out.at[ww, cc, :, :, cols]

    def over(i, cc):
        src, ww, cols = grad_parts[i]
        return pltpu.make_async_remote_copy(
            src_ref=src,
            dst_ref=grad_place(cc, ww, cols),
            send_sem=over_send.at[i],
            recv_sem=over_recv.at[i],
            device_id=dev_c,
            device_id_type=MESH,
        )

    barrier = pltpu.get_barrier_semaphore()
    around = [(w, c, (z + k) % 4) for k in range(1, 4)]
    for device in [dev_x, dev_y, dev_c] + around:
        pl.semaphore_signal(barrier, inc=1, device_id=device, device_id_type=MESH)
    pl.semaphore_wait(barrier, 6)


    def view(chunk, cols):
        zz, cc, ww = chunk
        return x_out.at[ww, cc, zz] if cols is None else x_out.at[ww, cc, zz, :, cols]

    def copy(src, chunk, cols, slot, sem, device):
        return pltpu.make_async_remote_copy(
            src_ref=src,
            dst_ref=view(chunk, cols),
            send_sem=sem[0].at[sem[1:]],
            recv_sem=recv.at[chunk[0], chunk[1], slot],
            device_id=device,
            device_id_type=MESH,
        )

    sent = []
    devices_z = ((w, c, z + 1), (w, c, z - 1))

    def start(chunk, cols, slot, sem, device, src=None):
        copy(view(chunk, cols) if src is None else src, chunk, cols, slot, sem, device).start()
        sent.append((chunk, cols, slot, sem, device))

    def arrived(chunk, cols, slot):
        copy(view(chunk, cols), chunk, cols, slot, (send_c, 0, 0), dev_c).wait_recv()

    def spread(j):
        chunk = (order[j], c, w)
        src = x_ref if j == 0 else None
        start(chunk, None, 1, (send_x, j, 0), dev_x, src)
        start(chunk, None, 2, (send_y, j, 0), dev_y, src)
        start(chunk, None, 0, (send_c, j, 0), dev_c, src)

    def onward(j):
        chunk = (order[j], c, w)

        def moved(side):
            src = x_ref if j == 0 else view(chunk, None)
            return copy(src, chunk, None, 0, (send_z, j, side), devices_z[side])

        return (
            ((order[j] <= z) & (z < 3), functools.partial(moved, 0)),
            ((order[j] >= z) & (z > 0), functools.partial(moved, 1)),
        )

    def along(j):
        for there, moved in onward(j):
            pl.when(there)(lambda: moved().start())

    def share_in(j):
        arrived((order[j], c, w), None, 0)
        along(j)
        spread(j)

    def relay(j):
        from_x, from_y = ((order[j], c, wx), (order[j], c, wy))
        arrived(from_x, None, 1)
        start(from_x, lo, 3, (send_y, j, 1), dev_y)
        start(from_x, None, 1, (send_c, j, 1), dev_c)
        arrived(from_y, None, 2)
        start(from_y, hi, 4, (send_x, j, 1), dev_x)
        start(from_y, None, 2, (send_c, j, 2), dev_c)

    def across(j):
        chunk = (order[j], c, wd)
        for cols, slot in ((lo, 3), (hi, 4)):
            arrived(chunk, cols, slot)
            start(chunk, cols, slot, (send_c, j, slot), dev_c)

    def sibling(j):
        for ww, cols, slot in ((w, None, 0), (wx, None, 1), (wy, None, 2), (wd, lo, 3), (wd, hi, 4)):
            arrived((order[j], 1 - c, ww), cols, slot)


    def parts_of(a):
        return (pl.ds(0, half), pl.ds(half, wides[a] - half))

    def to_sibling(a):
        return pltpu.make_async_remote_copy(
            src_ref=others[a],
            dst_ref=sibs[a],
            send_sem=sib_send.at[a],
            recv_sem=sib_recv.at[a],
            device_id=dev_c,
            device_id_type=MESH,
        )

    def first_hops(a, j):
        low, high = parts_of(a)
        moves = (
            (wx, low, from_x1[a].at[j, 0], dev_x),
            (wd, low, from_x1[a].at[j, 1], dev_x),
            (wy, high, from_y1[a].at[j, 0], dev_y),
            (wd, high, from_y1[a].at[j, 1], dev_y),
        )
        return [
            pltpu.make_async_remote_copy(
                src_ref=mine[a].at[j % 2, ww, :, cols],
                dst_ref=dst,
                send_sem=one_send.at[a, j, i],
                recv_sem=one_recv.at[a, j, i],
                device_id=device,
                device_id_type=MESH,
            )
            for i, (ww, cols, dst, device) in enumerate(moves)
        ]

    def second_hops(a, j):
        low, high = parts_of(a)
        moves = ((wy, low, from_y2[a].at[j], dev_y), (wx, high, from_x2[a].at[j], dev_x))
        return [
            pltpu.make_async_remote_copy(
                src_ref=mine[a].at[j % 2, ww, :, cols],
                dst_ref=dst,
                send_sem=two_send.at[a, j, i],
                recv_sem=two_recv.at[a, j, i],
                device_id=device,
                device_id_type=MESH,
            )
            for i, (ww, cols, dst, device) in enumerate(moves)
        ]

    def last_hop(a, source, j):
        return pltpu.make_async_remote_copy(
            src_ref=mine[a].at[j % 2, w],
            dst_ref=from_z[a].at[source],
            send_sem=end_send.at[a, j],
            recv_sem=end_recv.at[a, source],
            device_id=(w, c, order[j]),
            device_id_type=MESH,
        )

    def total(*terms):
        added = terms[0].astype(f32)
        for term in terms[1:]:
            added = added + term.astype(f32)
        return added

    def after_first(j):
        p = j % 2
        for a in range(2):
            low, high = parts_of(a)
            for moved in first_hops(a, j):
                moved.wait_recv()
            mine[a][p, wy, :, low] = total(mine[a][p, wy, :, low], from_x1[a][j, 1]).astype(bf16)
            mine[a][p, wx, :, high] = total(mine[a][p, wx, :, high], from_y1[a][j, 1]).astype(bf16)
            for moved in second_hops(a, j):
                moved.start()

    def after_second(j):
        p = j % 2
        for a in range(2):
            low, high = parts_of(a)
            for moved in second_hops(a, j):
                moved.wait_recv()
            mine[a][p, w, :, low] = total(
                mine[a][p, w, :, low], from_x1[a][j, 0], from_y2[a][j]
            ).astype(bf16)
            mine[a][p, w, :, high] = total(
                mine[a][p, w, :, high], from_y1[a][j, 0], from_x2[a][j]
            ).astype(bf16)
            if j == 0:
                from_z[a][z] = mine[a][p, w]
            else:
                last_hop(a, z, j).start()

    def all_sent(j):
        for a in range(2):
            for moved in first_hops(a, j) + second_hops(a, j):
                moved.wait_send()
            if j > 0:
                last_hop(a, z, j).wait_send()


    code = order[0] + 4 * order[1] + 16 * order[2] + 64 * order[3]

    def tile_of(step):
        j = step // 2
        power = 1 + 3 * j + (9 * j * (j - 1)) // 2 + (27 * j * (j - 1) * (j - 2)) // 6
        return ((code // power) % 4, (c + 1 + step) % 2)

    def other_grads(step):
        zj, cc = tile_of(step)
        return pltpu.make_async_copy(grads_out.at[:, cc, zj], grads.at[0], grads_sem.at[5])

    def my_grads(step):
        zj, cc = tile_of(step)
        return [
            pltpu.make_async_copy(
                src.at[zj],
                grads.at[1, ww] if cols is None else grads.at[1, ww, :, cols],
                grads_sem.at[i],
            )
            for i, (src, ww, cols) in enumerate(grad_parts)
        ]

    def stores(step, own_tile):
        zj, cc = tile_of(step)
        pairs = [(gated, gated_out), (both, both_out)]
        pairs += [(grads.at[1], grads_out)] if own_tile else []
        return [
            pltpu.make_async_copy(src, dst.at[:, cc, zj], store_sem.at[i])
            for i, (src, dst) in enumerate(pairs)
        ]

    lanes = lax.broadcasted_iota(jnp.int32, (4 * share, 128), 1)

    def tile(step, own_tile, parity):
        zj, cc = tile_of(step)
        load = pltpu.make_async_copy(x_out.at[:, cc, zj], x_tile, tile_sem)
        load.start()
        if own_tile:
            for store in stores(step - 1, False):
                store.wait()
            for part in my_grads(step):
                part.wait()

            @pl.when(step < 7)
            def _():
                other_grads(step + 1).start()
        else:

            @pl.when(step > 0)
            def _():
                for store in stores(step - 1, True):
                    store.wait()

            for part in my_grads(step + 1):
                part.start()
            other_grads(step).wait()
        load.wait()
        rows = x_tile[...].reshape(4 * share, width)
        upstream = grads[1 if own_tile else 0].reshape(4 * share, width)
        logits = jnp.dot(rows, router_ref[...], preferred_element_type=f32)
        logits = jnp.where(lanes < experts, logits, -1e30)
        raised = jnp.exp(logits - jnp.max(logits, axis=1, keepdims=True))
        gates = raised / jnp.sum(raised, axis=1, keepdims=True)
        gates = gates * kept_ref[:, cc, zj].reshape(4 * share, 128).astype(f32)
        d_gate = jnp.zeros((4 * share, 128), f32)
        for n in range(2):
            here = lanes == group * 2 + n
            gate = jnp.sum(jnp.where(here, gates, 0.0), axis=1, keepdims=True)
            at = 2 * n * hidden
            gate_pre = jnp.dot(rows, w_in[:, at : at + hidden], preferred_element_type=f32)
            up_pre = jnp.dot(
                rows, w_in[:, at + hidden : at + 2 * hidden], preferred_element_type=f32
            )
            back = contract_last(upstream, w_out[n * hidden : (n + 1) * hidden, :])
            sigmoid = 1.0 / (1.0 + jnp.exp(-gate_pre))
            silu = gate_pre * sigmoid
            activated = silu * up_pre
            d_gate = jnp.where(here, jnp.sum(activated * back, axis=1, keepdims=True), d_gate)
            back = gate * back
            d_pre = back * up_pre * sigmoid * (1.0 + gate_pre * (1.0 - sigmoid))
            shape = (4, share, hidden)
            gated[:, :, n * hidden : (n + 1) * hidden] = (
                (gate * activated).astype(bf16).reshape(shape)
            )
            both[:, :, at : at + hidden] = d_pre.astype(bf16).reshape(shape)
            both[:, :, at + hidden : at + 2 * hidden] = (back * silu).astype(bf16).reshape(shape)
        for store in stores(step, own_tile):
            store.start()
        if own_tile:
            for a in range(2):
                to_sibling(a).wait_recv()
        else:

            @pl.when(step > 0)
            def _():
                for a in range(2):
                    to_sibling(a).wait_send()

        def put(a, cols, count, value):
            value = value.reshape(4, share, count)
            if own_tile:
                value = value + sibs[a][:, :, cols].astype(f32)
                mine[a][parity, :, :, cols] = value.astype(bf16)
            else:
                others[a][:, :, cols] = value.astype(bf16)

        put(0, pl.ds(width, 128), 128, d_gate)
        d_rows = both[...].reshape(4 * share, 4 * hidden)
        g_rows = gated[...].reshape(4 * share, 2 * hidden)

        def columns(m, carried):
            cols = pl.ds(pl.multiple_of(m * 256, 256), 256)
            put(0, cols, 256, contract_last(d_rows, w_in[cols, :]))
            put(1, cols, 256, jnp.dot(g_rows, w_out[:, cols], preferred_element_type=f32))
            return carried

        lax.fori_loop(0, width // 256, columns, None)

    def before_other(j):
        if j == 0:
            for i in range(5):
                over(i, c).start()
            along(0)
            spread(0)
            share_in(1)
            relay(0)
            keep().wait()
            for load in loads():
                load.wait()
            for i in range(5):
                over(i, 1 - c).wait_recv()
            other_grads(0).start()
        if j >= 2:
            after_second(j - 2)
        across(j)
        sibling(j)

    def before_mine(j):
        if j + 2 < 4:
            share_in(j + 2)
        if j + 1 < 4:
            relay(j + 1)
        if j >= 1:
            after_first(j - 1)
        if j >= 2:
            all_sent(j - 2)

    def round_of(j, carry):
        for k in range(4):
            pl.when(j == k)(functools.partial(before_other, k))
        tile(2 * j, False, None)

        @pl.when(j > 0)
        def _():
            pl.semaphore_wait(credit, 1)

        for a in range(2):
            to_sibling(a).start()
        for k in range(4):
            pl.when(j == k)(functools.partial(before_mine, k))
        tile(2 * j + 1, True, j % 2)

        @pl.when(j < 3)
        def _():
            pl.semaphore_signal(credit, inc=1, device_id=dev_c, device_id_type=MESH)

        for k in range(4):

            @pl.when(j == k)
            def _():
                for a in range(2):
                    for moved in first_hops(a, k):
                        moved.start()

        return carry

    lax.fori_loop(0, 4, round_of, None)
    after_second(2)
    after_first(3)
    after_second(3)
    for store in stores(7, True):
        store.wait()
    for a, result in ((0, dx_own), (1, moe_own)):
        to_sibling(a).wait_send()
        for k in range(1, 4):
            last_hop(a, (z + k) % 4, 1).wait_recv()
        result[...] = total(*(from_z[a][k] for k in range(4)))
    all_sent(2)
    all_sent(3)
    for i in range(5):
        over(i, c).wait_send()
    for chunk, cols, slot, sem, device in sent:
        copy(view(chunk, cols), chunk, cols, slot, sem, device).wait_send()
    for j in range(4):
        for there, moved in onward(j):
            pl.when(there)(lambda: moved().wait_send())


def experts_call(rows, grads, kept, router, expert_in, expert_out, experts):
    share, width = rows.shape
    hidden = expert_out.shape[1]
    blocks = (4, 2, 4, share)
    bf16, f32 = (jnp.bfloat16, jnp.float32)
    dma = pltpu.SemaphoreType.DMA
    anywhere, vmem = (pl.BlockSpec(memory_space=pl.ANY), pl.BlockSpec(memory_space=pltpu.VMEM))
    wides = (width + 128, width)
    half = width // 2
    both = lambda shape: [pltpu.VMEM(shape(wide), bf16) for wide in wides]
    return pl.pallas_call(
        functools.partial(experts_kernel, experts),
        out_shape=tuple(
            jax.ShapeDtypeStruct(blocks + (n,), bf16)
            for n in (width, width, 2 * hidden, 4 * hidden)
        )
        + tuple(jax.ShapeDtypeStruct((share, wide), f32) for wide in wides),
        in_specs=[anywhere] * 6 + [vmem, vmem, anywhere, anywhere],
        out_specs=(anywhere,) * 4 + (vmem, vmem),
        scratch_shapes=[
            pltpu.VMEM((4, share, width), bf16),
            pltpu.VMEM((width, 4 * hidden), bf16),
            pltpu.VMEM((2 * hidden, width), bf16),
            pltpu.VMEM((2, 4, share, width), bf16),
            pltpu.VMEM((4, share, 2 * hidden), bf16),
            pltpu.VMEM((4, share, 4 * hidden), bf16),
            *both(lambda wide: (4, share, wide)),
            *both(lambda wide: (2, 4, share, wide)),
            *both(lambda wide: (4, share, wide)),
            *both(lambda wide: (4, 2, share, half)),
            *both(lambda wide: (4, 2, share, wide - half)),
            *both(lambda wide: (4, share, half)),
            *both(lambda wide: (4, share, wide - half)),
            *both(lambda wide: (4, share, wide)),
            dma,
            dma,
            dma((6,)),
            dma((6,)),
            dma((3,)),
            dma((4, 2)),
            dma((4, 2)),
            dma((4, 2)),
            dma((4, 5)),
            dma((4, 2, 5)),
            dma((5,)),
            dma((5,)),
            dma((2,)),
            dma((2,)),
            pltpu.SemaphoreType.REGULAR,
            dma((2, 4, 4)),
            dma((2, 4, 4)),
            dma((2, 4, 2)),
            dma((2, 4, 2)),
            dma((2, 4)),
            dma((2, 4)),
        ],
        compiler_params=pltpu.CompilerParams(
            collective_id=0, has_side_effects=True, vmem_limit_bytes=62 << 20
        ),
    )(rows, *grads, kept, router, expert_in, expert_out)


def finish_kernel(
    rows_ref,
    small_ref,
    rows_out,
    small_out,
    sums,
    from_c,
    from_x,
    from_y,
    from_z,
    send_z,
    recv_z,
    small_send,
    small_recv,
):
    w, c, z = (lax.axis_index(a) for a in EVERYONE)
    wx, wy, wd = neighbours(w)
    dev_x, dev_y, dev_c = ((wx, c, z), (wy, c, z), (w, 1 - c, z))
    order = share_order(z)
    barrier = pltpu.get_barrier_semaphore()
    around = [(w, c, (z + k) % 4) for k in range(1, 4)]
    for device in [dev_x, dev_y, dev_c] + around:
        pl.semaphore_signal(barrier, inc=1, device_id=device, device_id_type=MESH)
    pl.semaphore_wait(barrier, 6)
    rows_out[z] = rows_ref[...]
    sides = ((w, c, z + 1), (w, c, z - 1))

    def moved(j, side):
        return pltpu.make_async_remote_copy(
            src_ref=rows_ref if j == 0 else rows_out.at[order[j]],
            dst_ref=rows_out.at[order[j]],
            send_sem=send_z.at[j, side],
            recv_sem=recv_z.at[order[j]],
            device_id=sides[side],
            device_id_type=MESH,
        )

    def onward(j):
        return (((order[j] <= z) & (z < 3), 0), ((order[j] >= z) & (z > 0), 1))

    def along(j):
        for there, side in onward(j):
            pl.when(there)(lambda: moved(j, side).start())

    def passed_on(j):
        moved(j, 0).wait_recv()
        along(j)

    def small(i, src, dst, device):
        return pltpu.make_async_remote_copy(
            src_ref=src,
            dst_ref=dst,
            send_sem=small_send.at[i],
            recv_sem=small_recv.at[i],
            device_id=device,
            device_id_type=MESH,
        )

    def sibling(k):
        return small(k, small_ref.at[k, 1 - c], from_c.at[k], dev_c)

    def to_x(k):
        return small(4 + k, sums.at[(wx, wd)[k]], from_x.at[k], dev_x)

    def to_y():
        return small(6, sums.at[wy], from_y, dev_y)

    def to_z(target, source):
        return pltpu.make_async_remote_copy(
            src_ref=sums.at[w, target],
            dst_ref=from_z.at[source],
            send_sem=small_send.at[7 + target],
            recv_sem=small_recv.at[7 + source],
            device_id=(w, c, target),
            device_id_type=MESH,
        )

    along(0)
    for k in range(4):
        sibling(k).start()
    for k in range(4):
        sibling(k).wait_recv()
        sums[k] = small_ref[k, c] + from_c[k]
    for k in range(2):
        to_x(k).start()
    for k in range(2):
        to_x(k).wait_recv()
    sums[w] = sums[w] + from_x[0]
    sums[wy] = sums[wy] + from_x[1]
    to_y().start()
    passed_on(1)
    to_y().wait_recv()
    sums[w] = sums[w] + from_y[...]
    for k in range(1, 4):
        to_z((z + k) % 4, z).start()
    passed_on(2)
    added = sums[w, z]
    for k in range(1, 4):
        to_z(z, (z + k) % 4).wait_recv()
    for k in range(1, 4):
        added = added + from_z[(z + k) % 4]
    small_out[...] = added
    passed_on(3)
    for k in range(4):
        sibling(k).wait_send()
    for k in range(2):
        to_x(k).wait_send()
    to_y().wait_send()
    for k in range(1, 4):
        to_z((z + k) % 4, z).wait_send()
    for j in range(4):
        for there, side in onward(j):
            pl.when(there)(lambda: moved(j, side).wait_send())


def finish_call(rows, small):
    dma = pltpu.SemaphoreType.DMA
    vmem = pl.BlockSpec(memory_space=pltpu.VMEM)
    block = small.shape[3:]
    f32 = jnp.float32
    return pl.pallas_call(
        finish_kernel,
        out_shape=(
            jax.ShapeDtypeStruct((4,) + rows.shape, rows.dtype),
            jax.ShapeDtypeStruct(block, f32),
        ),
        in_specs=[vmem, vmem],
        out_specs=(vmem, vmem),
        scratch_shapes=[
            pltpu.VMEM((4, 4) + block, f32),
            pltpu.VMEM((4, 4) + block, f32),
            pltpu.VMEM((2, 4) + block, f32),
            pltpu.VMEM((4,) + block, f32),
            pltpu.VMEM((4,) + block, f32),
            dma((4, 2)),
            dma((4,)),
            dma((11,)),
            dma((11,)),
        ],
        compiler_params=pltpu.CompilerParams(
            collective_id=1, has_side_effects=True, vmem_limit_bytes=32 << 20
        ),
    )(rows, small)


def swapped(rows, flip):
    return lax.ppermute(rows, WEIGHTS, [(k, k ^ flip) for k in range(4)])


def grads_around(rows, from_x, from_y, share):
    half = rows.shape[1] // 2
    parts = (rows, from_x, from_y, swapped(from_x[:, :half], 2), swapped(from_y[:, half:], 1))
    return [part.reshape(-1, share, part.shape[1]) for part in parts]


def gathered(rows, axes):
    return lax.all_gather(rows, axes, axis=0, tiled=True)


def scattered(rows, axes):
    return lax.psum_scatter(rows, axes, scatter_dimension=0, tiled=True)


def fit_rows(values, rows):
    flat = values.reshape(-1)
    columns = -(-flat.shape[0] // rows)
    return jnp.pad(flat, (0, rows * columns - flat.shape[0])).reshape(rows, columns)


def per_device_dense(
    layer_in,
    norm_gains,
    qkv_weight,
    qk_gains,
    out_weight,
    router,
    expert_in,
    expert_out,
    grad_out,
    segments,
    routes,
    route_order,
):
    group = GROUP
    everyone = EVERYONE
    group_count = lax.axis_size(group)
    tensor_count = lax.axis_size(TENSOR)
    context_rank = lax.axis_index(CONTEXT)
    tensor_rank = lax.axis_index(TENSOR)
    seq_count, half_len, model_width = layer_in.shape
    token_count = seq_count * half_len
    top_count = routes.shape[2]
    weight_rows, _, head_width = qkv_weight.shape
    expert_total = router.shape[1]
    local_experts = expert_in.shape[0]
    hidden_width = expert_in.shape[3]
    head_rows, _, local_heads = qk_gains.shape
    head_size = head_rows * group_count
    share = token_count // tensor_count
    bf16, f32 = jnp.bfloat16, jnp.float32

    capacity = token_count * top_count * 9 // (8 * expert_total)
    routed, slot_of = pair_slots(
        routes.reshape(token_count, top_count),
        route_order.reshape(token_count, top_count),
        expert_total,
    )
    kept = routed & (slot_of < capacity)

    front_small = jnp.concatenate(
        [norm_gains, fit_rows(qk_gains, weight_rows)], axis=1
    )
    front = gathered(
        jnp.concatenate([qkv_weight.reshape(weight_rows, -1), front_small], axis=1), group
    )
    own_grads = grad_out.reshape(token_count, model_width)
    front, own_grads = lax.optimization_barrier((front, own_grads))
    from_x, from_y = (swapped(own_grads, 1), swapped(own_grads, 2))
    back_small = jnp.concatenate(
        [router, fit_rows(kept.astype(bf16), weight_rows)], axis=1
    )
    back = gathered(jnp.concatenate([out_weight, back_small], axis=1), group)
    qkv_full = front[:, : 3 * head_width]
    gain_full = front[:, 3 * head_width : 3 * head_width + 2].astype(f32)
    gain_attn, gain_ffn = (gain_full[:, 0], gain_full[:, 1])
    qk_gain_full = (
        front[:, 3 * head_width + 2 :]
        .reshape(group_count, -1)[:, : head_rows * 2 * local_heads]
        .reshape(head_size, 2, local_heads)
        .astype(f32)
    )
    query_gain = qk_gain_full[:, 0, :].T.reshape(-1)
    key_gain = qk_gain_full[:, 1, :].T.reshape(-1)
    out_full = back[:, :head_width]
    router_full = back[:, head_width : head_width + expert_total]
    kept_all = (
        back[:, head_width + expert_total :]
        .reshape(group_count, -1)[:, : expert_total * token_count]
        .reshape(group_count, expert_total, token_count)
    )
    inv_root = 1.0 / math.sqrt(head_size)
    residual = layer_in.reshape(token_count, model_width).astype(f32)
    scale_one = lax.rsqrt(jnp.mean(residual * residual, axis=1, keepdims=True) + epsilon)
    normed_one = (residual * scale_one * gain_attn).astype(bf16)
    projected = jnp.dot(normed_one, qkv_full, preferred_element_type=f32)
    query_raw = projected[:, :head_width]
    key_raw = projected[:, head_width : 2 * head_width]
    value_raw = projected[:, 2 * head_width :]
    square_sums = row_sums(
        jnp.stack(
            [jnp.sum(query_raw * query_raw, axis=1), jnp.sum(key_raw * key_raw, axis=1)], axis=1
        )
    )
    query_scale = lax.rsqrt(square_sums[:, 0:1] / model_width + epsilon)
    key_scale = lax.rsqrt(square_sums[:, 1:2] / model_width + epsilon)
    heads_shape = (seq_count, half_len, local_heads, head_size)
    query_hat = (query_raw * query_scale * query_gain).reshape(heads_shape)
    key_hat = (key_raw * key_scale * key_gain).reshape(heads_shape)
    query_pos = context_rank * half_len + jnp.arange(half_len, dtype=jnp.int32)
    cosine_table, sine_table = rotary_tables(query_pos, head_size)
    cosine_table = cosine_table[None, :, None, :]
    sine_table = sine_table[None, :, None, :]
    query_rot = (query_hat * cosine_table + rotate_half(query_hat) * sine_table).astype(bf16)
    key_rot = (key_hat * cosine_table + rotate_half(key_hat) * sine_table).astype(bf16)
    value_low = value_raw.astype(bf16).reshape(heads_shape)
    key_prev, value_prev = passed_along((key_rot, value_low), CONTEXT, 1)
    all_keys = jnp.concatenate([key_prev, key_rot], axis=1)
    all_values = jnp.concatenate([value_prev, value_low], axis=1)
    key_pos = jnp.concatenate([query_pos - half_len, query_pos])
    seg_query = lax.dynamic_slice_in_dim(segments, context_rank * half_len, half_len, 1)
    seg_prev = lax.dynamic_slice_in_dim(
        segments, jnp.maximum(context_rank - 1, 0) * half_len, half_len, 1
    )
    seg_keys = jnp.concatenate([seg_prev, seg_query], axis=1)
    causal = (key_pos[None, :] >= 0) & (key_pos[None, :] <= query_pos[:, None])
    allowed = causal[None] & (seg_query[:, :, None] == seg_keys[:, None, :])

    def score_block(queries, key_rows):
        raw_scores = (
            jnp.einsum(BY_SCORE, queries, key_rows, preferred_element_type=f32) * inv_root
        )
        return jnp.where(allowed[:, None], raw_scores, -1e30)

    scores = score_block(query_rot, all_keys)
    row_max = jnp.max(scores, axis=-1, keepdims=True)
    exponent = jnp.exp(scores - row_max)
    row_total = jnp.sum(exponent, axis=-1, keepdims=True)
    log_total = row_max + jnp.log(row_total)
    attn_probs = (exponent / row_total).astype(bf16)
    attended = jnp.einsum(BY_QUERY, attn_probs, all_values, preferred_element_type=f32)
    attended_low = attended.reshape(token_count, -1).astype(bf16)
    from_x, from_y, attended_low = lax.optimization_barrier((from_x, from_y, attended_low))
    around = grads_around(own_grads, from_x, from_y, share)
    attn_partial = jnp.einsum("tf,df->td", attended_low, out_full, preferred_element_type=f32)

    own_rows = lambda rows: lax.dynamic_slice_in_dim(rows, tensor_rank * share, share, 0)
    residual_own = own_rows(residual)
    hidden = residual_own + scattered(attn_partial.astype(bf16), TENSOR).astype(f32)
    scale_two = lax.rsqrt(jnp.mean(hidden * hidden, axis=1, keepdims=True) + epsilon)
    unit_two = hidden * scale_two
    normed_two = (unit_two * gain_ffn).astype(bf16)
    upstream = own_rows(grad_out.reshape(token_count, model_width)).astype(f32)

    pad_experts = lambda rows: jnp.pad(rows, ((0, 0), (0, 128 - expert_total)))
    kept_rows = kept_all.transpose(0, 2, 1).reshape(-1, expert_total)
    normed_all, grads_all, gated, d_both, d_sums, moe_own = experts_call(
        normed_two,
        around,
        pad_experts(kept_rows).reshape(4, 2, 4, share, 128),
        pad_experts(router_full),
        expert_in,
        expert_out,
        expert_total,
    )
    normed_all, grads_all, gated, d_both = (
        rows.reshape(group_count * token_count, -1)
        for rows in (normed_all, grads_all, gated, d_both)
    )
    layer_out = gathered((hidden + moe_own).astype(bf16), TENSOR).reshape(layer_in.shape)
    kept_own = own_rows(kept.T).astype(f32)
    probs_own = jax.nn.softmax(
        jnp.dot(normed_two, router_full, preferred_element_type=f32), axis=1
    )
    d_probs = d_sums[:, model_width : model_width + expert_total] * kept_own
    d_logits = (
        probs_own * (d_probs - jnp.sum(probs_own * d_probs, axis=1, keepdims=True))
    ).astype(bf16)
    d_normed_two = d_sums[:, :model_width] + jnp.dot(
        d_logits, router_full.T, preferred_element_type=f32
    )
    d_router = jnp.dot(normed_two.T, d_logits, preferred_element_type=f32)
    d_gain_ffn = jnp.sum(d_normed_two * unit_two, axis=0)
    scaled_ffn = gain_ffn * d_normed_two
    d_hidden = upstream + scale_two * (
        scaled_ffn - unit_two * jnp.mean(scaled_ffn * unit_two, axis=1, keepdims=True)
    )
    d_hidden_low = gathered(d_hidden.astype(bf16), TENSOR)
    grad_expert_in = (
        jnp.dot(normed_all.T, d_both, preferred_element_type=f32)
        .reshape(model_width, local_experts, 2, hidden_width)
        .transpose(1, 2, 0, 3)
    )
    d_hidden_low, grad_expert_in = lax.optimization_barrier((d_hidden_low, grad_expert_in))

    d_attended = (
        jnp.dot(d_hidden_low, out_full, preferred_element_type=f32)
        .astype(bf16)
        .reshape(heads_shape)
    )
    d_out_weight = jnp.einsum("td,tf->df", d_hidden_low, attended_low, preferred_element_type=f32)
    probs_again = jnp.exp(score_block(query_rot, all_keys) - log_total)
    probs_again_low = probs_again.astype(bf16)
    d_probs_att = jnp.einsum(
        BY_SCORE, d_attended, all_values, preferred_element_type=f32
    )
    d_values_all = jnp.einsum(
        BY_KEY, probs_again_low, d_attended, preferred_element_type=f32
    )
    row_dot = jnp.sum(probs_again * d_probs_att, axis=-1, keepdims=True)
    d_scores = (probs_again * (d_probs_att - row_dot)).astype(bf16)
    d_query_rot = (
        jnp.einsum(BY_QUERY, d_scores, all_keys, preferred_element_type=f32) * inv_root
    )
    d_keys_all = (
        jnp.einsum(BY_KEY, d_scores, query_rot, preferred_element_type=f32) * inv_root
    )
    back_key, back_value = (
        passed_along(d_keys_all[:, :half_len].astype(bf16), CONTEXT, -1).astype(f32),
        passed_along(d_values_all[:, :half_len].astype(bf16), CONTEXT, -1).astype(f32),
    )
    d_key_rot = d_keys_all[:, half_len:] + back_key
    d_value = (d_values_all[:, half_len:] + back_value).reshape(token_count, -1)
    d_query_hat = (d_query_rot * cosine_table + rotate_back(d_query_rot * sine_table)).reshape(
        token_count, -1
    )
    d_key_hat = (d_key_rot * cosine_table + rotate_back(d_key_rot * sine_table)).reshape(
        token_count, -1
    )
    centre = row_sums(
        jnp.stack(
            [
                jnp.sum(query_gain * d_query_hat * query_raw, axis=1),
                jnp.sum(key_gain * d_key_hat * key_raw, axis=1),
            ],
            axis=1,
        )
    )
    d_query_raw = (
        query_scale * query_gain * d_query_hat
        - query_raw * (query_scale**3 / model_width) * centre[:, 0:1]
    )
    d_key_raw = (
        key_scale * key_gain * d_key_hat - key_raw * (key_scale**3 / model_width) * centre[:, 1:2]
    )
    d_query_gain = (
        jnp.sum(d_query_hat * query_raw * query_scale, axis=0).reshape(local_heads, head_size).T
    )
    d_key_gain = jnp.sum(d_key_hat * key_raw * key_scale, axis=0).reshape(local_heads, head_size).T
    d_qk_gains = jnp.stack([d_query_gain, d_key_gain], axis=1)
    d_projected = jnp.concatenate([d_query_raw, d_key_raw, d_value], axis=1).astype(bf16)
    d_projected, layer_out = lax.optimization_barrier((d_projected, layer_out))
    d_normed_one = scattered(
        jnp.einsum("tf,df->td", d_projected, qkv_full, preferred_element_type=f32).astype(bf16),
        TENSOR,
    ).astype(f32)
    d_qkv = jnp.einsum("td,tf->df", normed_one, d_projected, preferred_element_type=f32)

    grad_expert_out = jnp.dot(gated.T, grads_all, preferred_element_type=f32).reshape(
        expert_out.shape
    )
    d_normed_one, grad_expert_out = lax.optimization_barrier((d_normed_one, grad_expert_out))

    scale_own = own_rows(scale_one)
    unit_one = residual_own * scale_own
    d_gain_attn = jnp.sum(d_normed_one * unit_one, axis=0)
    scaled_attn = gain_attn * d_normed_one
    grad_in = d_hidden + scale_own * (
        scaled_attn - unit_one * jnp.mean(scaled_attn * unit_one, axis=1, keepdims=True)
    )

    grad_qkv = (
        scattered(d_qkv.astype(bf16), group)
        .astype(f32)
        .reshape(weight_rows, 3, head_width)
    )
    grad_out_weight = scattered(d_out_weight.astype(bf16), group).astype(f32)
    gain_share = weight_rows // tensor_count
    router_share = expert_total // tensor_count
    own_slot = (jnp.arange(tensor_count) == tensor_rank).astype(f32)[None, :, None]
    small = jnp.concatenate(
        [
            jnp.stack([d_gain_attn, d_gain_ffn], axis=1).reshape(group_count, tensor_count, -1),
            d_router.reshape(group_count, weight_rows, tensor_count, router_share)
            .transpose(0, 2, 1, 3)
            .reshape(group_count, tensor_count, -1),
            d_qk_gains.reshape(group_count, 1, -1) * own_slot,
        ],
        axis=2,
    )
    small = jnp.pad(small, ((0, 0), (0, 0), (0, -small.shape[2] % 128)))
    grad_in, small = finish_call(
        grad_in.astype(bf16), small.reshape(4, 2, tensor_count, -1, 128)
    )
    grad_in = grad_in.astype(f32).reshape(layer_in.shape)
    small = small.reshape(-1)
    ends = (gain_share * 2, gain_share * 2 + weight_rows * router_share)
    return (
        layer_out,
        grad_in,
        small[: ends[0]].reshape(gain_share, 2),
        grad_qkv,
        small[ends[1] : ends[1] + d_qk_gains.size // group_count].reshape(
            head_rows, 2, local_heads
        ),
        grad_out_weight,
        small[ends[0] : ends[1]].reshape(weight_rows, router_share),
        grad_expert_in,
        grad_expert_out,
    )


def solution(mesh):
    placed = (
        P(WEIGHTS, CONTEXT, None),
        P(GROUP, None),
        P(GROUP, None, TENSOR),
        P(GROUP, None, TENSOR),
        P(GROUP, TENSOR),
        P(GROUP, None),
        P(GROUP, None, None, TENSOR),
        P(GROUP, TENSOR, None),
        P(WEIGHTS, CONTEXT, None),
        P(WEIGHTS, None),
        P(WEIGHTS, CONTEXT, None),
        P(WEIGHTS, CONTEXT, None),
    )
    axes = tuple(mesh.shape[axis] for axis in EVERYONE)

    def per_device(*blocks):
        dense = axes == (4, 2, 4) and blocks[5].shape[1] <= 2 * blocks[10].shape[2]
        return (per_device_dense if dense else per_device_slots)(*blocks)

    return jax.shard_map(
        per_device,
        mesh=mesh,
        in_specs=placed,
        out_specs=(
            P(WEIGHTS, CONTEXT, None),
            P(WEIGHTS, CONTEXT, None),
            P(EVERYONE, None),
            P(GROUP, None, TENSOR),
            P(GROUP, None, TENSOR),
            P(GROUP, TENSOR),
            P(GROUP, TENSOR),
            P(GROUP, None, None, TENSOR),
            P(GROUP, TENSOR, None),
        ),
        check_vma=False,
    )
```

```python
import functools
import math

import jax
import jax.numpy as jnp
from jax import lax
from jax.experimental import pallas as pl
from jax.experimental.pallas import tpu as pltpu
from jax.sharding import PartitionSpec as P

epsilon = 1e-05
rotary_base = 10000.0
WEIGHTS, CONTEXT, TENSOR = ("weights", "context", "tensor")
GROUP = (WEIGHTS, CONTEXT)
EVERYONE = (WEIGHTS, CONTEXT, TENSOR)
MESH = pl.DeviceIdType.MESH
BY_SCORE = "sqhd,skhd->shqk"
BY_QUERY = "shqk,skhd->sqhd"
BY_KEY = "shqk,sqhd->skhd"


def passed_along(value, axis, steps):
    count = lax.axis_size(axis)
    leading, last = (max(0, -steps), min(count, count - steps))
    return lax.ppermute(value, axis, [(source, source + steps) for source in range(leading, last)])


def rotate_half(values_in):
    middle = values_in.shape[-1] // 2
    return jnp.concatenate([-values_in[..., middle:], values_in[..., :middle]], axis=-1)


def rotate_back(grads_in):
    middle = grads_in.shape[-1] // 2
    return jnp.concatenate([grads_in[..., middle:], -grads_in[..., :middle]], axis=-1)


def rotary_tables(positions, head_size):
    frequency = rotary_base ** (-(2.0 * jnp.arange(head_size // 2, dtype=jnp.float32)) / head_size)
    angle_table = positions.astype(jnp.float32)[:, None] * frequency[None, :]
    angle_table = jnp.concatenate([angle_table, angle_table], axis=1)
    return (jnp.cos(angle_table), jnp.sin(angle_table))


def pair_slots(token_routes, token_ranks, expert_total):
    unused = token_routes.size
    hot = token_routes.T[None] == jnp.arange(expert_total, dtype=jnp.int32)[:, None, None]
    rank_of = jnp.min(jnp.where(hot, token_ranks.T[None], unused), axis=1)
    slot_of = jnp.sum((rank_of[:, :, None] < rank_of[:, None, :]).astype(jnp.int32), axis=1)
    return (rank_of < unused, slot_of)


def place_pairs(pair_expert, rank, expert_total, capacity, top_count):
    pair_count = pair_expert.shape[0]
    token_routes = pair_expert.reshape(-1, top_count)
    slot_of = pair_slots(token_routes, rank.reshape(-1, top_count), expert_total)[1]
    slot_index = jnp.take_along_axis(slot_of.T, token_routes, axis=1).reshape(pair_count)
    kept_pair = slot_index < capacity
    dest_row = jnp.where(kept_pair, pair_expert * capacity + slot_index, expert_total * capacity)
    slot_pair = (
        jnp.full((expert_total * capacity + 1,), pair_count, jnp.int32)
        .at[dest_row]
        .set(jnp.arange(pair_count, dtype=jnp.int32))[:-1]
    )
    return (kept_pair, dest_row, slot_pair)


def row_sums(partial_rows):
    return lax.psum(partial_rows, TENSOR)


def tensor_sum(partial_rows):
    return lax.psum(partial_rows, TENSOR)


def to_owners(slot_rows):
    return lax.all_to_all(
        slot_rows, GROUP, split_axis=0, concat_axis=0, tiled=True
    )


def expert_front(slot_inputs, expert_in):
    both_pre = jnp.einsum(
        "sncd,ngdf->sncgf", slot_inputs, expert_in, preferred_element_type=jnp.float32
    )
    return (both_pre[..., 0, :], both_pre[..., 1, :])


def per_device_slots(
    layer_in,
    norm_gains,
    qkv_weight,
    qk_gains,
    out_weight,
    router,
    expert_in,
    expert_out,
    grad_out,
    segments,
    routes,
    route_order,
):
    group_count = lax.axis_size(GROUP)
    tensor_count = lax.axis_size(TENSOR)
    context_rank = lax.axis_index(CONTEXT)
    tensor_rank = lax.axis_index(TENSOR)
    seq_count, half_len, model_width = layer_in.shape
    token_count = seq_count * half_len
    top_count = routes.shape[2]
    qkv_full, out_full, qk_gain_full, gain_full, router_full = (
        lax.all_gather(qkv_weight, GROUP, axis=0, tiled=True),
        lax.all_gather(out_weight, GROUP, axis=0, tiled=True),
        lax.all_gather(qk_gains, GROUP, axis=0, tiled=True),
        lax.all_gather(norm_gains, GROUP, axis=0, tiled=True),
        lax.all_gather(router, GROUP, axis=0, tiled=True),
    )
    head_size = qk_gain_full.shape[0]
    local_heads = qk_gain_full.shape[2]
    expert_total = router_full.shape[1]
    gain_attn = gain_full[:, 0].astype(jnp.float32)
    gain_ffn = gain_full[:, 1].astype(jnp.float32)
    query_gain = qk_gain_full[:, 0, :].astype(jnp.float32).T.reshape(-1)
    key_gain = qk_gain_full[:, 1, :].astype(jnp.float32).T.reshape(-1)
    inv_root = 1.0 / math.sqrt(head_size)
    residual = layer_in.reshape(token_count, model_width).astype(jnp.float32)
    scale_one = lax.rsqrt(jnp.mean(residual * residual, axis=1, keepdims=True) + epsilon)
    unit_one = residual * scale_one
    normed_one = (unit_one * gain_attn).astype(jnp.bfloat16)
    projected = jnp.einsum("td,dgf->tgf", normed_one, qkv_full, preferred_element_type=jnp.float32)
    query_raw = projected[:, 0]
    key_raw = projected[:, 1]
    value_raw = projected[:, 2]
    square_sums = row_sums(
        jnp.stack(
            [jnp.sum(query_raw * query_raw, axis=1), jnp.sum(key_raw * key_raw, axis=1)], axis=1
        )
    )
    query_scale = lax.rsqrt(square_sums[:, 0:1] / model_width + epsilon)
    key_scale = lax.rsqrt(square_sums[:, 1:2] / model_width + epsilon)
    heads_shape = (seq_count, half_len, local_heads, head_size)
    query_hat = (query_raw * query_scale * query_gain).reshape(heads_shape)
    key_hat = (key_raw * key_scale * key_gain).reshape(heads_shape)
    query_pos = context_rank * half_len + jnp.arange(half_len, dtype=jnp.int32)
    cosine_table, sine_table = rotary_tables(query_pos, head_size)
    cosine_table = cosine_table[None, :, None, :]
    sine_table = sine_table[None, :, None, :]
    query_rot = (query_hat * cosine_table + rotate_half(query_hat) * sine_table).astype(
        jnp.bfloat16
    )
    key_rot = (key_hat * cosine_table + rotate_half(key_hat) * sine_table).astype(jnp.bfloat16)
    value_low = value_raw.astype(jnp.bfloat16).reshape(heads_shape)
    key_prev, value_prev = passed_along((key_rot, value_low), CONTEXT, 1)
    all_keys = jnp.concatenate([key_prev, key_rot], axis=1)
    all_values = jnp.concatenate([value_prev, value_low], axis=1)
    key_pos = jnp.concatenate([query_pos - half_len, query_pos])
    seg_query = lax.dynamic_slice_in_dim(segments, context_rank * half_len, half_len, 1)
    seg_prev = lax.dynamic_slice_in_dim(
        segments, jnp.maximum(context_rank - 1, 0) * half_len, half_len, 1
    )
    seg_keys = jnp.concatenate([seg_prev, seg_query], axis=1)
    causal = (key_pos[None, :] >= 0) & (key_pos[None, :] <= query_pos[:, None])
    allowed = causal[None] & (seg_query[:, :, None] == seg_keys[:, None, :])

    def score_block(queries, key_rows):
        raw_scores = (
            jnp.einsum(BY_SCORE, queries, key_rows, preferred_element_type=jnp.float32)
            * inv_root
        )
        return jnp.where(allowed[:, None], raw_scores, -1e30)

    scores = score_block(query_rot, all_keys)
    row_max = jnp.max(scores, axis=-1, keepdims=True)
    exponent = jnp.exp(scores - row_max)
    row_total = jnp.sum(exponent, axis=-1, keepdims=True)
    log_total = row_max + jnp.log(row_total)
    attn_probs = (exponent / row_total).astype(jnp.bfloat16)
    attended = jnp.einsum(
        BY_QUERY, attn_probs, all_values, preferred_element_type=jnp.float32
    )
    attended_low = attended.reshape(token_count, -1).astype(jnp.bfloat16)
    attn_partial = jnp.einsum(
        "tf,df->td", attended_low, out_full, preferred_element_type=jnp.float32
    )
    hidden = residual + tensor_sum(attn_partial)
    scale_two = lax.rsqrt(jnp.mean(hidden * hidden, axis=1, keepdims=True) + epsilon)
    unit_two = hidden * scale_two
    normed_two = (unit_two * gain_ffn).astype(jnp.bfloat16)
    logits = jnp.dot(normed_two, router_full, preferred_element_type=jnp.float32)
    router_probs = jax.nn.softmax(logits, axis=1)
    capacity = token_count * top_count * 9 // (8 * expert_total)
    local_experts = expert_in.shape[0]
    pair_count = token_count * top_count
    token_routes = routes.reshape(token_count, top_count)
    kept_pair, dest_row, slot_pair = place_pairs(
        token_routes.reshape(pair_count), route_order.reshape(pair_count), expert_total, capacity, top_count
    )
    zero_row = jnp.zeros((1, model_width), jnp.bfloat16)
    zero_wide = jnp.zeros((1, model_width), jnp.float32)
    slot_shape = (group_count, local_experts, capacity, model_width)
    dispatch_rows = jnp.concatenate([normed_two, zero_row], axis=0)[slot_pair // top_count].reshape(
        slot_shape
    )
    received = lax.all_to_all(
        dispatch_rows, GROUP, split_axis=0, concat_axis=0, tiled=True
    )
    gate_pre, up_pre = expert_front(received, expert_in)
    sigmoid_gate = jax.nn.sigmoid(gate_pre)
    silu_gate = gate_pre * sigmoid_gate
    activated = (silu_gate * up_pre).astype(jnp.bfloat16)
    expert_partial = jnp.einsum(
        "sncf,nfd->sncd", activated, expert_out, preferred_element_type=jnp.float32
    )
    kept_float = kept_pair.reshape(token_count, top_count).astype(jnp.float32)
    gate_weight = jnp.take_along_axis(router_probs, token_routes, axis=1) * kept_float
    upstream = grad_out.reshape(token_count, model_width).astype(jnp.float32)
    returned = to_owners(expert_partial).reshape(expert_total * capacity, model_width)
    picked = jnp.concatenate([returned, zero_wide], axis=0)[dest_row].reshape(
        token_count, top_count, model_width
    )
    moe_partial = jnp.sum(gate_weight[:, :, None] * picked, axis=1)
    dot_partial = jnp.sum(upstream[:, None, :] * picked, axis=2)
    moe_total, dot_total = lax.psum((moe_partial, dot_partial), TENSOR)
    layer_out = (hidden + moe_total).astype(jnp.bfloat16).reshape(layer_in.shape)
    d_gate = dot_total * kept_float
    route_hot = (
        token_routes[:, :, None] == jnp.arange(expert_total, dtype=jnp.int32)[None, None, :]
    ).astype(jnp.float32)
    d_probs = jnp.sum(d_gate[:, :, None] * route_hot, axis=1)
    d_logits = (
        router_probs * (d_probs - jnp.sum(router_probs * d_probs, axis=1, keepdims=True))
    ).astype(jnp.bfloat16)
    d_pair = (
        (gate_weight[:, :, None] * upstream[:, None, :])
        .astype(jnp.bfloat16)
        .reshape(pair_count, model_width)
    )
    d_slots = jnp.concatenate([d_pair, zero_row], axis=0)[slot_pair].reshape(slot_shape)
    d_received = lax.all_to_all(
        d_slots, GROUP, split_axis=0, concat_axis=0, tiled=True
    )
    d_activated = jnp.einsum(
        "sncd,nfd->sncf", d_received, expert_out, preferred_element_type=jnp.float32
    )
    grad_expert_out = jnp.einsum(
        "sncf,sncd->nfd", activated, d_received, preferred_element_type=jnp.float32
    )
    d_gate_pre = d_activated * up_pre * sigmoid_gate * (1.0 + gate_pre * (1.0 - sigmoid_gate))
    d_up_pre = d_activated * silu_gate
    d_both = jnp.stack([d_gate_pre, d_up_pre], axis=3).astype(jnp.bfloat16)
    d_inputs = jnp.einsum("sncgf,ngdf->sncd", d_both, expert_in, preferred_element_type=jnp.float32)
    grad_expert_in = jnp.einsum(
        "sncd,sncgf->ngdf", received, d_both, preferred_element_type=jnp.float32
    )
    d_returned = to_owners(d_inputs).reshape(expert_total * capacity, model_width)
    d_normed_part = jnp.sum(
        jnp.concatenate([d_returned, zero_wide], axis=0)[dest_row].reshape(
            token_count, top_count, model_width
        ),
        axis=1,
    )
    d_normed_two = tensor_sum(d_normed_part) + jnp.dot(
        d_logits, router_full.T, preferred_element_type=jnp.float32
    )
    d_router = jnp.dot(normed_two.T, d_logits, preferred_element_type=jnp.float32)
    d_gain_ffn = jnp.sum(d_normed_two * unit_two, axis=0)
    scaled_ffn = gain_ffn * d_normed_two
    d_hidden = upstream + scale_two * (
        scaled_ffn - unit_two * jnp.mean(scaled_ffn * unit_two, axis=1, keepdims=True)
    )
    d_hidden_low = d_hidden.astype(jnp.bfloat16)
    d_out_weight = jnp.einsum(
        "td,tf->df", d_hidden_low, attended_low, preferred_element_type=jnp.float32
    )
    d_attended = (
        jnp.dot(d_hidden_low, out_full, preferred_element_type=jnp.float32)
        .astype(jnp.bfloat16)
        .reshape(heads_shape)
    )
    probs_again = jnp.exp(score_block(query_rot, all_keys) - log_total)
    probs_again_low = probs_again.astype(jnp.bfloat16)
    d_probs_att = jnp.einsum(
        BY_SCORE, d_attended, all_values, preferred_element_type=jnp.float32
    )
    d_values_all = jnp.einsum(
        BY_KEY, probs_again_low, d_attended, preferred_element_type=jnp.float32
    )
    row_dot = jnp.sum(probs_again * d_probs_att, axis=-1, keepdims=True)
    d_scores = (probs_again * (d_probs_att - row_dot)).astype(jnp.bfloat16)
    d_query_rot = (
        jnp.einsum(BY_QUERY, d_scores, all_keys, preferred_element_type=jnp.float32)
        * inv_root
    )
    d_keys_all = (
        jnp.einsum(BY_KEY, d_scores, query_rot, preferred_element_type=jnp.float32)
        * inv_root
    )
    back_key, back_value = (
        passed_along(d_keys_all[:, :half_len].astype(jnp.bfloat16), CONTEXT, -1).astype(
            jnp.float32
        ),
        passed_along(d_values_all[:, :half_len].astype(jnp.bfloat16), CONTEXT, -1).astype(
            jnp.float32
        ),
    )
    d_key_rot = d_keys_all[:, half_len:] + back_key
    d_value = (d_values_all[:, half_len:] + back_value).reshape(token_count, -1)
    d_query_hat = (d_query_rot * cosine_table + rotate_back(d_query_rot * sine_table)).reshape(
        token_count, -1
    )
    d_key_hat = (d_key_rot * cosine_table + rotate_back(d_key_rot * sine_table)).reshape(
        token_count, -1
    )
    centre = row_sums(
        jnp.stack(
            [
                jnp.sum(query_gain * d_query_hat * query_raw, axis=1),
                jnp.sum(key_gain * d_key_hat * key_raw, axis=1),
            ],
            axis=1,
        )
    )
    d_query_raw = (
        query_scale * query_gain * d_query_hat
        - query_raw * (query_scale**3 / model_width) * centre[:, 0:1]
    )
    d_key_raw = (
        key_scale * key_gain * d_key_hat - key_raw * (key_scale**3 / model_width) * centre[:, 1:2]
    )
    d_query_gain = (
        jnp.sum(d_query_hat * query_raw * query_scale, axis=0).reshape(local_heads, head_size).T
    )
    d_key_gain = jnp.sum(d_key_hat * key_raw * key_scale, axis=0).reshape(local_heads, head_size).T
    d_qk_gains = jnp.stack([d_query_gain, d_key_gain], axis=1)
    d_projected = jnp.stack([d_query_raw, d_key_raw, d_value], axis=1).astype(jnp.bfloat16)
    d_normed_one = tensor_sum(
        jnp.einsum("tgf,dgf->td", d_projected, qkv_full, preferred_element_type=jnp.float32)
    )
    d_qkv = jnp.einsum("td,tgf->dgf", normed_one, d_projected, preferred_element_type=jnp.float32)
    d_gain_attn = jnp.sum(d_normed_one * unit_one, axis=0)
    scaled_attn = gain_attn * d_normed_one
    grad_in = d_hidden + scale_one * (
        scaled_attn - unit_one * jnp.mean(scaled_attn * unit_one, axis=1, keepdims=True)
    )
    d_norm_gains = jnp.stack([d_gain_attn, d_gain_ffn], axis=1)
    grad_qkv, grad_out_weight, grad_qk_gains, gain_rows, router_rows = (
        lax.psum_scatter(d_qkv, GROUP, scatter_dimension=0, tiled=True),
        lax.psum_scatter(d_out_weight, GROUP, scatter_dimension=0, tiled=True),
        lax.psum_scatter(d_qk_gains, GROUP, scatter_dimension=0, tiled=True),
        lax.psum_scatter(d_norm_gains, GROUP, scatter_dimension=0, tiled=True),
        lax.psum_scatter(d_router, GROUP, scatter_dimension=0, tiled=True),
    )
    gain_share = gain_rows.shape[0] // tensor_count
    grad_norm_gains = lax.dynamic_slice_in_dim(gain_rows, tensor_rank * gain_share, gain_share, 0)
    router_share = expert_total // tensor_count
    grad_router = lax.dynamic_slice_in_dim(router_rows, tensor_rank * router_share, router_share, 1)
    return (
        layer_out,
        grad_in.reshape(layer_in.shape),
        grad_norm_gains,
        grad_qkv,
        grad_qk_gains,
        grad_out_weight,
        grad_router,
        grad_expert_in,
        grad_expert_out,
    )


def contract_last(left, right):
    return lax.dot_general(
        left, right, (((1,), (1,)), ((), ())), preferred_element_type=jnp.float32
    )


def share_order(z):
    upper, odd = (z // 2, z % 2)
    return (z, z + 1 - 2 * upper, 2 + upper - 2 * odd, 3 - 3 * upper)


def share_turns(z):
    return (z, (z + 2) % 4, 3 - z, z + 1 - 2 * (z % 2))


def neighbours(w):
    wx, wy = (w + 1 - 2 * (w % 2), (w + 2) % 4)
    return (wx, wy, wx + wy - w)


def experts_kernel(
    experts,
    x_ref,
    grad_own,
    grad_x,
    grad_y,
    grad_low,
    grad_high,
    kept_ref,
    router_ref,
    in_ref,
    out_w_ref,
    x_out,
    grads_out,
    gated_out,
    both_out,
    moe_out,
    dx_own,
    x_tile,
    w_in,
    w_out,
    grads,
    gated,
    both,
    moe_tile,
    others,
    mine,
    sibs,
    from_x1,
    from_y1,
    from_y2,
    from_x2,
    from_z,
        own_sem,
        tile_sem,
        weight_sem,
        grads_sem,
        store_sem,
        send_z,
        send_x,
        send_y,
        send_c,
        recv,
        over_send,
        over_recv,
        sib_send,
        sib_recv,
        credit,
        one_send,
        one_recv,
        two_send,
        two_recv,
        end_send,
        end_recv,
):
    w, c, z = (lax.axis_index(a) for a in (WEIGHTS, CONTEXT, TENSOR))
    wx, wy, wd = neighbours(w)
    share, width = x_ref.shape
    half = width // 2
    lo, hi = (pl.ds(0, half), pl.ds(half, half))
    dev_x, dev_y, dev_c = ((wx, c, z), (wy, c, z), (w, 1 - c, z))
    turns = share_turns(z)
    hidden = out_w_ref.shape[1]
    group = w * 2 + c
    bf16, f32 = (jnp.bfloat16, jnp.float32)
    low, high = (pl.ds(0, half), pl.ds(half, half + 128))

    def loads():
        return [
            pltpu.make_async_copy(
                in_ref.at[n, g],
                w_in.at[:, pl.ds((2 * n + g) * hidden, hidden)],
                weight_sem.at[2 * n + g],
            )
            for n in range(2)
            for g in range(2)
        ] + [
            pltpu.make_async_copy(
                out_w_ref.at[n], w_out.at[pl.ds(n * hidden, hidden)], weight_sem.at[4 + n]
            )
            for n in range(2)
        ]

    for load in loads():
        load.start()
    keep = lambda: pltpu.make_async_copy(x_ref, x_out.at[w, c, z], own_sem)
    keep().start()

    grad_parts = (
        (grad_own, w, None),
        (grad_x, wx, None),
        (grad_y, wy, None),
        (grad_low, wd, lo),
        (grad_high, wd, hi),
    )

    def grad_place(cc, ww, cols):
        return grads_out.at[ww, cc] if cols is None else grads_out.at[ww, cc, :, :, cols]

    def over(i, cc):
        src, ww, cols = grad_parts[i]
        return pltpu.make_async_remote_copy(
            src_ref=src,
            dst_ref=grad_place(cc, ww, cols),
            send_sem=over_send.at[i],
            recv_sem=over_recv.at[i],
            device_id=dev_c,
            device_id_type=MESH,
        )

    barrier = pltpu.get_barrier_semaphore()
    around = [(w, c, (z + k) % 4) for k in range(1, 4)]
    for device in [dev_x, dev_y, dev_c] + around:
        pl.semaphore_signal(barrier, inc=1, device_id=device, device_id_type=MESH)
    pl.semaphore_wait(barrier, 6)


    def view(chunk, cols):
        zz, cc, ww = chunk
        return x_out.at[ww, cc, zz] if cols is None else x_out.at[ww, cc, zz, :, cols]

    def copy(src, chunk, cols, slot, sem, device):
        return pltpu.make_async_remote_copy(
            src_ref=src,
            dst_ref=view(chunk, cols),
            send_sem=sem[0].at[sem[1:]],
            recv_sem=recv.at[chunk[0], chunk[1], slot],
            device_id=device,
            device_id_type=MESH,
        )

    sent = []
    devices_z = ((w, c, z + 1), (w, c, z - 1))

    def start(chunk, cols, slot, sem, device, src=None):
        copy(view(chunk, cols) if src is None else src, chunk, cols, slot, sem, device).start()
        sent.append((chunk, cols, slot, sem, device))

    def arrived(chunk, cols, slot):
        copy(view(chunk, cols), chunk, cols, slot, (send_c, 0, 0), dev_c).wait_recv()

    def spread(j):
        chunk = (turns[j], c, w)
        src = x_ref if j == 0 else None
        start(chunk, None, 1, (send_x, j, 0), dev_x, src)
        start(chunk, None, 2, (send_y, j, 0), dev_y, src)
        start(chunk, None, 0, (send_c, j, 0), dev_c, src)

    def onward(j):
        chunk = (turns[j], c, w)

        def moved(side):
            src = x_ref if j == 0 else view(chunk, None)
            return copy(src, chunk, None, 0, (send_z, j, side), devices_z[side])

        return (
            ((turns[j] <= z) & (z < 3), functools.partial(moved, 0)),
            ((turns[j] >= z) & (z > 0), functools.partial(moved, 1)),
        )

    def along(j):
        for there, moved in onward(j):
            pl.when(there)(lambda: moved().start())

    def pass_on(j):
        arrived((turns[j], c, w), None, 0)
        along(j)

    def relay(j):
        from_x, from_y = ((turns[j], c, wx), (turns[j], c, wy))
        arrived(from_x, None, 1)
        start(from_x, lo, 3, (send_y, j, 1), dev_y)
        start(from_x, None, 1, (send_c, j, 1), dev_c)
        arrived(from_y, None, 2)
        start(from_y, hi, 4, (send_x, j, 1), dev_x)
        start(from_y, None, 2, (send_c, j, 2), dev_c)

    def across(j):
        chunk = (turns[j], c, wd)
        for cols, slot in ((lo, 3), (hi, 4)):
            arrived(chunk, cols, slot)
            start(chunk, cols, slot, (send_c, j, slot), dev_c)

    def sibling(j):
        for ww, cols, slot in ((w, None, 0), (wx, None, 1), (wy, None, 2), (wd, lo, 3), (wd, hi, 4)):
            arrived((turns[j], 1 - c, ww), cols, slot)


    def remote(src, dst, send, got, device):
        return pltpu.make_async_remote_copy(
            src_ref=src,
            dst_ref=dst,
            send_sem=send,
            recv_sem=got,
            device_id=device,
            device_id_type=MESH,
        )

    def to_sibling():
        return remote(others, sibs, sib_send, sib_recv, dev_c)

    def first_hops(j):
        moves = (
            (wx, low, from_x1.at[j, 0], dev_x),
            (wd, low, from_x1.at[j, 1], dev_x),
            (wy, high, from_y1.at[j, 0], dev_y),
            (wd, high, from_y1.at[j, 1], dev_y),
        )
        return [
            remote(
                mine.at[j % 2, ww, :, cols], dst, one_send.at[j, i], one_recv.at[j, i], device
            )
            for i, (ww, cols, dst, device) in enumerate(moves)
        ]

    def second_hops(j):
        moves = ((wy, low, from_y2.at[j], dev_y), (wx, high, from_x2.at[j], dev_x))
        return [
            remote(
                mine.at[j % 2, ww, :, cols], dst, two_send.at[j, i], two_recv.at[j, i], device
            )
            for i, (ww, cols, dst, device) in enumerate(moves)
        ]

    def last_hop(source, j):
        return remote(
            mine.at[j % 2, w],
            from_z.at[source],
            end_send.at[j],
            end_recv.at[source],
            (w, c, turns[j]),
        )

    def total(*terms):
        added = terms[0].astype(f32)
        for term in terms[1:]:
            added = added + term.astype(f32)
        return added

    def after_first(j):
        p = j % 2
        for moved in first_hops(j):
            moved.wait_recv()
        mine[p, wy, :, low] = total(mine[p, wy, :, low], from_x1[j, 1]).astype(bf16)
        mine[p, wx, :, high] = total(mine[p, wx, :, high], from_y1[j, 1]).astype(bf16)
        for moved in second_hops(j):
            moved.start()

    def after_second(j):
        p = j % 2
        for moved in second_hops(j):
            moved.wait_recv()
        mine[p, w, :, low] = total(mine[p, w, :, low], from_x1[j, 0], from_y2[j]).astype(bf16)
        mine[p, w, :, high] = total(mine[p, w, :, high], from_y1[j, 0], from_x2[j]).astype(bf16)
        if j == 0:
            from_z[z] = mine[p, w]
        else:
            last_hop(z, j).start()

    def all_sent(j):
        for moved in first_hops(j) + second_hops(j):
            moved.wait_send()
        if j > 0:
            last_hop(z, j).wait_send()


    code = turns[0] + 4 * turns[1] + 16 * turns[2] + 64 * turns[3]

    def tile_of(step):
        j = step // 2
        power = 1 + 3 * j + (9 * j * (j - 1)) // 2 + (27 * j * (j - 1) * (j - 2)) // 6
        return ((code // power) % 4, (c + 1 + step) % 2)

    def other_grads(step):
        zj, cc = tile_of(step)
        return pltpu.make_async_copy(grads_out.at[:, cc, zj], grads.at[0], grads_sem.at[5])

    def my_grads(step):
        zj, cc = tile_of(step)
        return [
            pltpu.make_async_copy(
                src.at[zj],
                grads.at[1, ww] if cols is None else grads.at[1, ww, :, cols],
                grads_sem.at[i],
            )
            for i, (src, ww, cols) in enumerate(grad_parts)
        ]

    def stores(step, own_tile):
        zj, cc = tile_of(step)
        pairs = [(gated, gated_out), (both, both_out)]
        pairs += [(grads.at[1], grads_out)] if own_tile else []
        return [
            pltpu.make_async_copy(src, dst.at[:, cc, zj], store_sem.at[i])
            for i, (src, dst) in enumerate(pairs)
        ]

    def moe_store(step):
        zj, cc = tile_of(step)
        return pltpu.make_async_copy(moe_tile, moe_out.at[:, cc, zj], store_sem.at[3])

    lanes = lax.broadcasted_iota(jnp.int32, (4 * share, 128), 1)

    def tile(step, own_tile, parity):
        zj, cc = tile_of(step)
        load = pltpu.make_async_copy(x_out.at[:, cc, zj], x_tile, tile_sem)
        load.start()
        if own_tile:
            for store in stores(step - 1, False):
                store.wait()
            for part in my_grads(step):
                part.wait()

            @pl.when(step < 7)
            def _():
                other_grads(step + 1).start()
        else:

            @pl.when(step > 0)
            def _():
                for store in stores(step - 1, True):
                    store.wait()

            for part in my_grads(step + 1):
                part.start()
            other_grads(step).wait()
        load.wait()
        rows = x_tile[...].reshape(4 * share, width)
        upstream = grads[1 if own_tile else 0].reshape(4 * share, width)
        logits = jnp.dot(rows, router_ref[...], preferred_element_type=f32)
        logits = jnp.where(lanes < experts, logits, -1e30)
        raised = jnp.exp(logits - jnp.max(logits, axis=1, keepdims=True))
        gates = raised / jnp.sum(raised, axis=1, keepdims=True)
        gates = gates * kept_ref[:, cc, zj].reshape(4 * share, 128).astype(f32)
        d_gate = jnp.zeros((4 * share, 128), f32)
        for n in range(2):
            here = lanes == group * 2 + n
            gate = jnp.sum(jnp.where(here, gates, 0.0), axis=1, keepdims=True)
            at = 2 * n * hidden
            gate_pre = jnp.dot(rows, w_in[:, at : at + hidden], preferred_element_type=f32)
            up_pre = jnp.dot(
                rows, w_in[:, at + hidden : at + 2 * hidden], preferred_element_type=f32
            )
            back = contract_last(upstream, w_out[n * hidden : (n + 1) * hidden, :])
            sigmoid = 1.0 / (1.0 + jnp.exp(-gate_pre))
            silu = gate_pre * sigmoid
            activated = silu * up_pre
            d_gate = jnp.where(here, jnp.sum(activated * back, axis=1, keepdims=True), d_gate)
            back = gate * back
            d_pre = back * up_pre * sigmoid * (1.0 + gate_pre * (1.0 - sigmoid))
            shape = (4, share, hidden)
            gated[:, :, n * hidden : (n + 1) * hidden] = (
                (gate * activated).astype(bf16).reshape(shape)
            )
            both[:, :, at : at + hidden] = d_pre.astype(bf16).reshape(shape)
            both[:, :, at + hidden : at + 2 * hidden] = (back * silu).astype(bf16).reshape(shape)
        for store in stores(step, own_tile):
            store.start()
        if own_tile:
            to_sibling().wait_recv()
            moe_store(step - 1).wait()
        else:

            @pl.when(step > 0)
            def _():
                to_sibling().wait_send()
                moe_store(step - 1).wait()

        def put(cols, count, value):
            value = value.reshape(4, share, count)
            if own_tile:
                value = value + sibs[:, :, cols].astype(f32)
                mine[parity, :, :, cols] = value.astype(bf16)
            else:
                others[:, :, cols] = value.astype(bf16)

        put(pl.ds(width, 128), 128, d_gate)
        d_rows = both[...].reshape(4 * share, 4 * hidden)
        g_rows = gated[...].reshape(4 * share, 2 * hidden)

        def columns(m, carried):
            cols = pl.ds(pl.multiple_of(m * 256, 256), 256)
            put(cols, 256, contract_last(d_rows, w_in[cols, :]))
            moe_tile[:, :, cols] = (
                jnp.dot(g_rows, w_out[:, cols], preferred_element_type=f32)
                .astype(bf16)
                .reshape(4, share, 256)
            )
            return carried

        lax.fori_loop(0, width // 256, columns, None)
        moe_store(step).start()

    def before_other(j):
        if j == 0:
            for i in range(5):
                over(i, c).start()
            along(0)
            spread(0)
            pass_on(3)
            pl.when((z > 0) & (z < 3))(lambda: pass_on(2))
            relay(0)
            pass_on(1)
            spread(1)
            keep().wait()
            for load in loads():
                load.wait()
            for i in range(5):
                over(i, 1 - c).wait_recv()
            other_grads(0).start()
        if j >= 2:
            after_second(j - 2)
        across(j)
        sibling(j)

    def before_mine(j):
        if j == 0:
            pl.when((z == 0) | (z == 3))(lambda: pass_on(2))
        if j + 2 < 4:
            spread(j + 2)
        if j + 1 < 4:
            relay(j + 1)
        if j >= 1:
            after_first(j - 1)
        if j >= 2:
            all_sent(j - 2)

    def round_of(j, carry):
        for k in range(4):
            pl.when(j == k)(functools.partial(before_other, k))
        tile(2 * j, False, None)

        @pl.when(j > 0)
        def _():
            pl.semaphore_wait(credit, 1)

        to_sibling().start()
        for k in range(4):
            pl.when(j == k)(functools.partial(before_mine, k))
        tile(2 * j + 1, True, j % 2)

        @pl.when(j < 3)
        def _():
            pl.semaphore_signal(credit, inc=1, device_id=dev_c, device_id_type=MESH)

        for k in range(4):

            @pl.when(j == k)
            def _():
                for moved in first_hops(k):
                    moved.start()

        return carry

    lax.fori_loop(0, 4, round_of, None)
    after_second(2)
    after_first(3)
    after_second(3)
    for store in stores(7, True):
        store.wait()
    moe_store(7).wait()
    to_sibling().wait_send()
    for k in range(1, 4):
        last_hop((z + k) % 4, 1).wait_recv()
    dx_own[...] = total(*(from_z[k] for k in range(4)))
    all_sent(2)
    all_sent(3)
    for i in range(5):
        over(i, c).wait_send()
    for chunk, cols, slot, sem, device in sent:
        copy(view(chunk, cols), chunk, cols, slot, sem, device).wait_send()
    for j in range(4):
        for there, moved in onward(j):
            pl.when(there)(lambda: moved().wait_send())


def experts_call(rows, grads, kept, router, expert_in, expert_out, experts):
    share, width = rows.shape
    hidden = expert_out.shape[1]
    blocks = (4, 2, 4, share)
    bf16, f32 = (jnp.bfloat16, jnp.float32)
    dma = pltpu.SemaphoreType.DMA
    anywhere, vmem = (pl.BlockSpec(memory_space=pl.ANY), pl.BlockSpec(memory_space=pltpu.VMEM))
    wide, half = (width + 128, width // 2)
    return pl.pallas_call(
        functools.partial(experts_kernel, experts),
        out_shape=tuple(
            jax.ShapeDtypeStruct(blocks + (n,), bf16)
            for n in (width, width, 2 * hidden, 4 * hidden, width)
        )
        + (jax.ShapeDtypeStruct((share, wide), f32),),
        in_specs=[anywhere] * 6 + [vmem, vmem, anywhere, anywhere],
        out_specs=(anywhere,) * 5 + (vmem,),
        scratch_shapes=[
            pltpu.VMEM((4, share, width), bf16),
            pltpu.VMEM((width, 4 * hidden), bf16),
            pltpu.VMEM((2 * hidden, width), bf16),
            pltpu.VMEM((2, 4, share, width), bf16),
            pltpu.VMEM((4, share, 2 * hidden), bf16),
            pltpu.VMEM((4, share, 4 * hidden), bf16),
            pltpu.VMEM((4, share, width), bf16),
            pltpu.VMEM((4, share, wide), bf16),
            pltpu.VMEM((2, 4, share, wide), bf16),
            pltpu.VMEM((4, share, wide), bf16),
            pltpu.VMEM((4, 2, share, half), bf16),
            pltpu.VMEM((4, 2, share, wide - half), bf16),
            pltpu.VMEM((4, share, half), bf16),
            pltpu.VMEM((4, share, wide - half), bf16),
            pltpu.VMEM((4, share, wide), bf16),
            dma,
            dma,
            dma((6,)),
            dma((6,)),
            dma((4,)),
            dma((4, 2)),
            dma((4, 2)),
            dma((4, 2)),
            dma((4, 5)),
            dma((4, 2, 5)),
            dma((5,)),
            dma((5,)),
            dma,
            dma,
            pltpu.SemaphoreType.REGULAR,
            dma((4, 4)),
            dma((4, 4)),
            dma((4, 2)),
            dma((4, 2)),
            dma((4,)),
            dma((4,)),
        ],
        compiler_params=pltpu.CompilerParams(
            collective_id=0, has_side_effects=True, vmem_limit_bytes=62 << 20
        ),
    )(rows, *grads, kept, router, expert_in, expert_out)


def finish_kernel(
    parts_ref,
    x_ref,
    scale_ref,
    gain_ref,
    d_hidden_ref,
    qkv_ref,
    out_ref,
    small_ref,
    rows_out,
    qkv_out,
    out_out,
    small_out,
    own_rows,
    right_in,
    left_in,
    sums,
    from_c,
    from_x,
    from_y,
    from_z,
    mine,
    sibs,
    from_x1,
    from_y1,
    from_y2,
    from_x2,
    right_send,
    right_recv,
    left_send,
    left_recv,
    send_z,
    recv_z,
    small_send,
    small_recv,
    load_sem,
    sib_send,
    sib_recv,
    one_send,
    one_recv,
    two_send,
    two_recv,
):
    w, c, z = (lax.axis_index(a) for a in EVERYONE)
    wx, wy, wd = neighbours(w)
    dev_x, dev_y, dev_c = ((wx, c, z), (wy, c, z), (w, 1 - c, z))
    sides = ((w, c, z + 1), (w, c, z - 1))
    order = share_order(z)
    bf16, f32 = (jnp.bfloat16, jnp.float32)
    half = x_ref.shape[1] // 2
    lo, hi = (slice(0, half), slice(half, 2 * half))
    heads = out_ref.shape[3]
    both = ((qkv_ref, pl.ds(0, 3 * heads)), (out_ref, pl.ds(3 * heads, heads)))

    def loads():
        return [
            pltpu.make_async_copy(ref.at[:, c], mine.at[:, :, cols], load_sem.at[i])
            for i, (ref, cols) in enumerate(both)
        ]

    for load in loads():
        load.start()
    barrier = pltpu.get_barrier_semaphore()
    around = [(w, c, (z + k) % 4) for k in range(1, 4)]
    for device in [dev_x, dev_y, dev_c] + around:
        pl.semaphore_signal(barrier, inc=1, device_id=device, device_id_type=MESH)
    pl.semaphore_wait(barrier, 6)

    def remote(src, dst, send, got, device):
        return pltpu.make_async_remote_copy(
            src_ref=src,
            dst_ref=dst,
            send_sem=send,
            recv_sem=got,
            device_id=device,
            device_id_type=MESH,
        )


    def to_right(s):
        return remote(
            parts_ref.at[s], right_in.at[s], right_send.at[s], right_recv.at[s], sides[0]
        )

    def to_left(s):
        return remote(parts_ref.at[s], left_in.at[s], left_send.at[s], left_recv.at[s], sides[1])

    def pass_right(s):
        @pl.when(z < s)
        def _():
            @pl.when(z > 0)
            def _():
                to_right(s).wait_recv()
                parts_ref[s] = (parts_ref[s].astype(f32) + right_in[s].astype(f32)).astype(bf16)

            to_right(s).start()

    def pass_left(s):
        @pl.when(z > s)
        def _():
            @pl.when(z < 3)
            def _():
                to_left(s).wait_recv()
                parts_ref[s] = (parts_ref[s].astype(f32) + left_in[s].astype(f32)).astype(bf16)

            to_left(s).start()


    def to_sibling():
        return [
            remote(
                ref.at[:, 1 - c], sibs.at[:, :, cols], sib_send.at[i], sib_recv.at[i], dev_c
            )
            for i, (ref, cols) in enumerate(both)
        ]

    def first_hops():
        moves = (
            (wx, lo, from_x1.at[0], dev_x),
            (wd, lo, from_x1.at[1], dev_x),
            (wy, hi, from_y1.at[0], dev_y),
            (wd, hi, from_y1.at[1], dev_y),
        )
        return [
            remote(mine.at[ww, :, cols], dst, one_send.at[i], one_recv.at[i], device)
            for i, (ww, cols, dst, device) in enumerate(moves)
        ]

    def second_hops():
        moves = ((wy, lo, from_y2, dev_y), (wx, hi, from_x2, dev_x))
        return [
            remote(mine.at[ww, :, cols], dst, two_send.at[i], two_recv.at[i], device)
            for i, (ww, cols, dst, device) in enumerate(moves)
        ]

    def add(*terms):
        added = terms[0].astype(f32)
        for term in terms[1:]:
            added = added + term.astype(f32)
        return added

    def weights_first():
        for load in loads():
            load.wait()
        for part in to_sibling():
            part.wait_recv()
        for k in range(4):
            mine[k] = add(mine[k], sibs[k]).astype(bf16)
        for hop in first_hops():
            hop.start()

    def weights_second():
        for hop in first_hops():
            hop.wait_recv()
        mine[wy, :, lo] = add(mine[wy, :, lo], from_x1[1]).astype(bf16)
        mine[wx, :, hi] = add(mine[wx, :, hi], from_y1[1]).astype(bf16)
        for hop in second_hops():
            hop.start()

    def weights_last():
        for hop in second_hops():
            hop.wait_recv()
        low = add(mine[w, :, lo], from_x1[0], from_y2[...])
        high = add(mine[w, :, hi], from_y1[0], from_x2[...])
        for k in range(4):
            part = (low if (k + 1) * heads <= half else high)[
                :, k * heads % half : k * heads % half + heads
            ]
            if k < 3:
                qkv_out[k] = part
            else:
                out_out[...] = part


    def moved(j, side):
        return remote(
            own_rows if j == 0 else rows_out.at[order[j]],
            rows_out.at[order[j]],
            send_z.at[j, side],
            recv_z.at[order[j]],
            sides[side],
        )

    def onward(j):
        return (((order[j] <= z) & (z < 3), 0), ((order[j] >= z) & (z > 0), 1))

    def along(j):
        for there, side in onward(j):
            pl.when(there)(lambda: moved(j, side).start())

    def passed_on(j):
        moved(j, 0).wait_recv()
        along(j)


    def small(i, src, dst, device):
        return remote(src, dst, small_send.at[i], small_recv.at[i], device)

    def small_sibling(k):
        return small(k, small_ref.at[k, 1 - c], from_c.at[k], dev_c)

    def small_x(k):
        return small(4 + k, sums.at[(wx, wd)[k]], from_x.at[k], dev_x)

    def small_y():
        return small(6, sums.at[wy], from_y, dev_y)

    def small_z(target, source):
        return remote(
            sums.at[w],
            from_z.at[source],
            small_send.at[7 + target],
            small_recv.at[7 + source],
            (w, c, target),
        )

    for part in to_sibling():
        part.start()
    for s in range(3):
        pass_right(3 - s)
        pass_left(s)
        if s == 1:
            weights_first()
    d_normed = parts_ref[z].astype(f32)
    right_in[0] = jnp.zeros(right_in.shape[1:], bf16)
    left_in[3] = jnp.zeros(left_in.shape[1:], bf16)

    @pl.when(z > 0)
    def _():
        to_right(z).wait_recv()

    @pl.when(z < 3)
    def _():
        to_left(z).wait_recv()

    d_normed = d_normed + right_in[z].astype(f32) + left_in[z].astype(f32)
    scale = scale_ref[...]
    unit = x_ref[...].astype(f32) * scale
    scaled = gain_ref[...] * d_normed
    shift = jnp.mean(scaled * unit, axis=1, keepdims=True)
    own_rows[...] = (d_hidden_ref[...] + scale * (scaled - unit * shift)).astype(bf16)
    along(0)
    rows_out[z] = own_rows[...]
    d_gain = jnp.sum(d_normed * unit, axis=0, keepdims=True)
    for k in range(8):
        for i in range(2):
            at = (2 * k + i) * 128
            small_ref[k // 2, k % 2, i : i + 1, :] = d_gain[:, at : at + 128]
    for k in range(4):
        small_sibling(k).start()
    for k in range(4):
        small_sibling(k).wait_recv()
        sums[k] = small_ref[k, c] + from_c[k]
    for k in range(2):
        small_x(k).start()
    weights_second()
    for k in range(2):
        small_x(k).wait_recv()
    sums[w] = sums[w] + from_x[0]
    sums[wy] = sums[wy] + from_x[1]
    small_y().start()
    passed_on(1)
    small_y().wait_recv()
    sums[w] = sums[w] + from_y[...]
    for k in range(1, 4):
        small_z((z + k) % 4, z).start()
    passed_on(2)
    weights_last()
    for k in range(1, 4):
        small_z(z, (z + k) % 4).wait_recv()
    from_z[z] = sums[w]
    small_out[...] = add(*(from_z[k] for k in range(4)))
    passed_on(3)
    for s in range(3):

        @pl.when(z < 3 - s)
        def _():
            to_right(3 - s).wait_send()

        @pl.when(z > s)
        def _():
            to_left(s).wait_send()

    for hop in to_sibling() + first_hops() + second_hops():
        hop.wait_send()
    for k in range(4):
        small_sibling(k).wait_send()
    for k in range(2):
        small_x(k).wait_send()
    small_y().wait_send()
    for k in range(1, 4):
        small_z((z + k) % 4, z).wait_send()
    for j in range(4):
        for there, side in onward(j):
            pl.when(there)(lambda: moved(j, side).wait_send())


def finish_call(parts, rows, scale, gain, d_hidden, d_qkv, d_out, small):
    dma = pltpu.SemaphoreType.DMA
    anywhere, vmem = (pl.BlockSpec(memory_space=pl.ANY), pl.BlockSpec(memory_space=pltpu.VMEM))
    share, width = rows.shape
    count, heads = d_out.shape[2:]
    half = width // 2
    block = small.shape[2:]
    bf16, f32 = (jnp.bfloat16, jnp.float32)

    def body(*refs):
        ins, outs, rest = (refs[:8], refs[8:12], refs[12:])
        parts_in, small_in = (ins[0], ins[7])
        parts_own, small_own = rest[:2]
        parts_own[...] = parts_in[...]
        small_own[...] = small_in[...]
        finish_kernel(parts_own, *ins[1:7], small_own, *outs, *rest[2:])

    return pl.pallas_call(
        body,
        out_shape=(
            jax.ShapeDtypeStruct((4, share, width), bf16),
            jax.ShapeDtypeStruct((3, count, heads), f32),
            jax.ShapeDtypeStruct((count, heads), f32),
            jax.ShapeDtypeStruct(block, f32),
        ),
        in_specs=[vmem, vmem, vmem, vmem, vmem, anywhere, anywhere, vmem],
        out_specs=(vmem, vmem, vmem, vmem),
        scratch_shapes=[
            pltpu.VMEM((4, share, width), bf16),
            pltpu.VMEM((4, 2) + block, f32),
            pltpu.VMEM((share, width), bf16),
            pltpu.VMEM((4, share, width), bf16),
            pltpu.VMEM((4, share, width), bf16),
            pltpu.VMEM((4,) + block, f32),
            pltpu.VMEM((4,) + block, f32),
            pltpu.VMEM((2,) + block, f32),
            pltpu.VMEM(block, f32),
            pltpu.VMEM((4,) + block, f32),
            pltpu.VMEM((4, count, width), bf16),
            pltpu.VMEM((4, count, width), bf16),
            pltpu.VMEM((2, count, half), bf16),
            pltpu.VMEM((2, count, half), bf16),
            pltpu.VMEM((count, half), bf16),
            pltpu.VMEM((count, half), bf16),
            dma((4,)),
            dma((4,)),
            dma((4,)),
            dma((4,)),
            dma((4, 2)),
            dma((4,)),
            dma((11,)),
            dma((11,)),
            dma((2,)),
            dma((2,)),
            dma((2,)),
            dma((4,)),
            dma((4,)),
            dma((2,)),
            dma((2,)),
        ],
        compiler_params=pltpu.CompilerParams(
            collective_id=1, has_side_effects=True, vmem_limit_bytes=48 << 20
        ),
    )(parts, rows, scale, gain, d_hidden, d_qkv, d_out, small)


def swapped(rows, flip):
    return lax.ppermute(rows, WEIGHTS, [(k, k ^ flip) for k in range(4)])


def grads_around(rows, from_x, from_y, share):
    half = rows.shape[1] // 2
    parts = (rows, from_x, from_y, swapped(from_x[:, :half], 2), swapped(from_y[:, half:], 1))
    return [part.reshape(-1, share, part.shape[1]) for part in parts]


def shares_around(rows):
    z = lax.axis_index(TENSOR)
    parts = [rows] + [
        lax.ppermute(rows, TENSOR, [(k, (k + step) % 4) for k in range(4)]) for step in (1, 3, 2)
    ]
    whole = jnp.zeros((4,) + rows.shape, rows.dtype)
    for part, step in zip(parts, (0, 1, 3, 2)):
        whole = lax.dynamic_update_index_in_dim(whole, part, (z + 4 - step) % 4, 0)
    return whole.reshape((-1,) + rows.shape[1:])


def gathered(rows, axes):
    return lax.all_gather(rows, axes, axis=0, tiled=True)


def scattered(rows, axes):
    return lax.psum_scatter(rows, axes, scatter_dimension=0, tiled=True)


def fit_rows(values, rows):
    flat = values.reshape(-1)
    columns = -(-flat.shape[0] // rows)
    return jnp.pad(flat, (0, rows * columns - flat.shape[0])).reshape(rows, columns)


def per_device_dense(
    layer_in,
    norm_gains,
    qkv_weight,
    qk_gains,
    out_weight,
    router,
    expert_in,
    expert_out,
    grad_out,
    segments,
    routes,
    route_order,
):
    group = GROUP
    everyone = EVERYONE
    group_count = lax.axis_size(group)
    tensor_count = lax.axis_size(TENSOR)
    context_rank = lax.axis_index(CONTEXT)
    tensor_rank = lax.axis_index(TENSOR)
    seq_count, half_len, model_width = layer_in.shape
    token_count = seq_count * half_len
    top_count = routes.shape[2]
    weight_rows, _, head_width = qkv_weight.shape
    expert_total = router.shape[1]
    local_experts = expert_in.shape[0]
    hidden_width = expert_in.shape[3]
    head_rows, _, local_heads = qk_gains.shape
    head_size = head_rows * group_count
    share = token_count // tensor_count
    bf16, f32 = jnp.bfloat16, jnp.float32

    capacity = token_count * top_count * 9 // (8 * expert_total)
    routed, slot_of = pair_slots(
        routes.reshape(token_count, top_count),
        route_order.reshape(token_count, top_count),
        expert_total,
    )
    kept = routed & (slot_of < capacity)

    front_small = jnp.concatenate(
        [norm_gains, fit_rows(qk_gains, weight_rows)], axis=1
    )
    front = gathered(
        jnp.concatenate([qkv_weight.reshape(weight_rows, -1), front_small], axis=1), group
    )
    own_grads = grad_out.reshape(token_count, model_width)
    front, own_grads = lax.optimization_barrier((front, own_grads))
    from_x, from_y = (swapped(own_grads, 1), swapped(own_grads, 2))
    back_small = jnp.concatenate(
        [router, fit_rows(kept.astype(bf16), weight_rows)], axis=1
    )
    back = gathered(jnp.concatenate([out_weight, back_small], axis=1), group)
    qkv_full = front[:, : 3 * head_width]
    gain_full = front[:, 3 * head_width : 3 * head_width + 2].astype(f32)
    gain_attn, gain_ffn = (gain_full[:, 0], gain_full[:, 1])
    qk_gain_full = (
        front[:, 3 * head_width + 2 :]
        .reshape(group_count, -1)[:, : head_rows * 2 * local_heads]
        .reshape(head_size, 2, local_heads)
        .astype(f32)
    )
    query_gain = qk_gain_full[:, 0, :].T.reshape(-1)
    key_gain = qk_gain_full[:, 1, :].T.reshape(-1)
    out_full = back[:, :head_width]
    router_full = back[:, head_width : head_width + expert_total]
    kept_all = (
        back[:, head_width + expert_total :]
        .reshape(group_count, -1)[:, : expert_total * token_count]
        .reshape(group_count, expert_total, token_count)
    )
    inv_root = 1.0 / math.sqrt(head_size)
    residual = layer_in.reshape(token_count, model_width).astype(f32)
    scale_one = lax.rsqrt(jnp.mean(residual * residual, axis=1, keepdims=True) + epsilon)
    normed_one = (residual * scale_one * gain_attn).astype(bf16)
    projected = jnp.dot(normed_one, qkv_full, preferred_element_type=f32)
    query_raw = projected[:, :head_width]
    key_raw = projected[:, head_width : 2 * head_width]
    value_raw = projected[:, 2 * head_width :]
    square_sums = row_sums(
        jnp.stack(
            [jnp.sum(query_raw * query_raw, axis=1), jnp.sum(key_raw * key_raw, axis=1)], axis=1
        )
    )
    query_scale = lax.rsqrt(square_sums[:, 0:1] / model_width + epsilon)
    key_scale = lax.rsqrt(square_sums[:, 1:2] / model_width + epsilon)
    heads_shape = (seq_count, half_len, local_heads, head_size)
    query_hat = (query_raw * query_scale * query_gain).reshape(heads_shape)
    key_hat = (key_raw * key_scale * key_gain).reshape(heads_shape)
    query_pos = context_rank * half_len + jnp.arange(half_len, dtype=jnp.int32)
    cosine_table, sine_table = rotary_tables(query_pos, head_size)
    cosine_table = cosine_table[None, :, None, :]
    sine_table = sine_table[None, :, None, :]
    query_rot = (query_hat * cosine_table + rotate_half(query_hat) * sine_table).astype(bf16)
    key_rot = (key_hat * cosine_table + rotate_half(key_hat) * sine_table).astype(bf16)
    value_low = value_raw.astype(bf16).reshape(heads_shape)
    key_prev, value_prev = passed_along((key_rot, value_low), CONTEXT, 1)
    all_keys = jnp.concatenate([key_prev, key_rot], axis=1)
    all_values = jnp.concatenate([value_prev, value_low], axis=1)
    key_pos = jnp.concatenate([query_pos - half_len, query_pos])
    seg_query = lax.dynamic_slice_in_dim(segments, context_rank * half_len, half_len, 1)
    seg_prev = lax.dynamic_slice_in_dim(
        segments, jnp.maximum(context_rank - 1, 0) * half_len, half_len, 1
    )
    seg_keys = jnp.concatenate([seg_prev, seg_query], axis=1)
    causal = (key_pos[None, :] >= 0) & (key_pos[None, :] <= query_pos[:, None])
    allowed = causal[None] & (seg_query[:, :, None] == seg_keys[:, None, :])

    def score_block(queries, key_rows):
        raw_scores = (
            jnp.einsum(BY_SCORE, queries, key_rows, preferred_element_type=f32) * inv_root
        )
        return jnp.where(allowed[:, None], raw_scores, -1e30)

    scores = score_block(query_rot, all_keys)
    row_max = jnp.max(scores, axis=-1, keepdims=True)
    exponent = jnp.exp(scores - row_max)
    row_total = jnp.sum(exponent, axis=-1, keepdims=True)
    log_total = row_max + jnp.log(row_total)
    attn_probs = (exponent / row_total).astype(bf16)
    attended = jnp.einsum(BY_QUERY, attn_probs, all_values, preferred_element_type=f32)
    attended_low = attended.reshape(token_count, -1).astype(bf16)
    from_x, from_y, attended_low = lax.optimization_barrier((from_x, from_y, attended_low))
    around = grads_around(own_grads, from_x, from_y, share)
    attn_partial = jnp.einsum("tf,df->td", attended_low, out_full, preferred_element_type=f32)

    own_rows = lambda rows: lax.dynamic_slice_in_dim(rows, tensor_rank * share, share, 0)
    residual_own = own_rows(residual)
    hidden = residual_own + scattered(attn_partial.astype(bf16), TENSOR).astype(f32)
    scale_two = lax.rsqrt(jnp.mean(hidden * hidden, axis=1, keepdims=True) + epsilon)
    unit_two = hidden * scale_two
    normed_two = (unit_two * gain_ffn).astype(bf16)
    upstream = own_rows(grad_out.reshape(token_count, model_width)).astype(f32)

    pad_experts = lambda rows: jnp.pad(rows, ((0, 0), (0, 128 - expert_total)))
    kept_rows = kept_all.transpose(0, 2, 1).reshape(-1, expert_total)
    normed_all, grads_all, gated, d_both, moe_all, d_sums = experts_call(
        normed_two,
        around,
        pad_experts(kept_rows).reshape(4, 2, 4, share, 128),
        pad_experts(router_full),
        expert_in,
        expert_out,
        expert_total,
    )
    normed_all, grads_all, gated, d_both, moe_all = (
        rows.reshape(group_count * token_count, -1)
        for rows in (normed_all, grads_all, gated, d_both, moe_all)
    )
    moe_plane = scattered(moe_all, group)
    kept_own = own_rows(kept.T).astype(f32)
    probs_own = jax.nn.softmax(
        jnp.dot(normed_two, router_full, preferred_element_type=f32), axis=1
    )
    d_probs = d_sums[:, model_width : model_width + expert_total] * kept_own
    d_logits = (
        probs_own * (d_probs - jnp.sum(probs_own * d_probs, axis=1, keepdims=True))
    ).astype(bf16)
    d_normed_two = d_sums[:, :model_width] + jnp.dot(
        d_logits, router_full.T, preferred_element_type=f32
    )
    d_router = jnp.dot(normed_two.T, d_logits, preferred_element_type=f32)
    d_gain_ffn = jnp.sum(d_normed_two * unit_two, axis=0)
    scaled_ffn = gain_ffn * d_normed_two
    d_hidden = upstream + scale_two * (
        scaled_ffn - unit_two * jnp.mean(scaled_ffn * unit_two, axis=1, keepdims=True)
    )
    d_hidden_own, normed_all, grads_all, gated, d_both = lax.optimization_barrier(
        (d_hidden.astype(bf16), normed_all, grads_all, gated, d_both)
    )
    d_hidden_low = shares_around(d_hidden_own)
    grad_expert_in = (
        jnp.dot(normed_all.T, d_both, preferred_element_type=f32)
        .reshape(model_width, local_experts, 2, hidden_width)
        .transpose(1, 2, 0, 3)
    )
    grad_expert_out = jnp.dot(gated.T, grads_all, preferred_element_type=f32).reshape(
        expert_out.shape
    )
    d_hidden_low, grad_expert_in, grad_expert_out = lax.optimization_barrier(
        (d_hidden_low, grad_expert_in, grad_expert_out)
    )

    d_attended = (
        jnp.dot(d_hidden_low, out_full, preferred_element_type=f32)
        .astype(bf16)
        .reshape(heads_shape)
    )
    d_out_weight = jnp.einsum("td,tf->df", d_hidden_low, attended_low, preferred_element_type=f32)
    probs_again = jnp.exp(score_block(query_rot, all_keys) - log_total)
    probs_again_low = probs_again.astype(bf16)
    d_probs_att = jnp.einsum(
        BY_SCORE, d_attended, all_values, preferred_element_type=f32
    )
    d_values_all = jnp.einsum(
        BY_KEY, probs_again_low, d_attended, preferred_element_type=f32
    )
    row_dot = jnp.sum(probs_again * d_probs_att, axis=-1, keepdims=True)
    d_scores = (probs_again * (d_probs_att - row_dot)).astype(bf16)
    d_query_rot = (
        jnp.einsum(BY_QUERY, d_scores, all_keys, preferred_element_type=f32) * inv_root
    )
    d_keys_all = (
        jnp.einsum(BY_KEY, d_scores, query_rot, preferred_element_type=f32) * inv_root
    )
    back_key, back_value = (
        passed_along(d_keys_all[:, :half_len].astype(bf16), CONTEXT, -1).astype(f32),
        passed_along(d_values_all[:, :half_len].astype(bf16), CONTEXT, -1).astype(f32),
    )
    d_key_rot = d_keys_all[:, half_len:] + back_key
    d_value = (d_values_all[:, half_len:] + back_value).reshape(token_count, -1)
    d_query_hat = (d_query_rot * cosine_table + rotate_back(d_query_rot * sine_table)).reshape(
        token_count, -1
    )
    d_key_hat = (d_key_rot * cosine_table + rotate_back(d_key_rot * sine_table)).reshape(
        token_count, -1
    )
    centre_own = (
        jnp.stack(
            [
                jnp.sum(query_gain * d_query_hat * query_raw, axis=1),
                jnp.sum(key_gain * d_key_hat * key_raw, axis=1),
            ],
            axis=1,
        )
    )
    centre, moe_plane = lax.optimization_barrier((row_sums(centre_own), moe_plane))
    moe_own = scattered(moe_plane, TENSOR).astype(f32)
    d_query_raw = (
        query_scale * query_gain * d_query_hat
        - query_raw * (query_scale**3 / model_width) * centre[:, 0:1]
    )
    d_key_raw = (
        key_scale * key_gain * d_key_hat - key_raw * (key_scale**3 / model_width) * centre[:, 1:2]
    )
    d_query_gain = (
        jnp.sum(d_query_hat * query_raw * query_scale, axis=0).reshape(local_heads, head_size).T
    )
    d_key_gain = jnp.sum(d_key_hat * key_raw * key_scale, axis=0).reshape(local_heads, head_size).T
    d_qk_gains = jnp.stack([d_query_gain, d_key_gain], axis=1)
    d_projected = jnp.concatenate([d_query_raw, d_key_raw, d_value], axis=1).astype(bf16)
    d_normed_parts = jnp.einsum(
        "tf,df->td", d_projected, qkv_full, preferred_element_type=f32
    ).astype(bf16)
    d_qkv = jnp.einsum("td,tf->df", normed_one, d_projected, preferred_element_type=f32)

    own_slot = (jnp.arange(tensor_count) == tensor_rank).astype(f32)[None, :, None]
    lines = lambda values: values.reshape(group_count, -1, 128)
    small = jnp.concatenate(
        [
            jnp.zeros((group_count, weight_rows // 128, 128), f32),
            lines(d_gain_ffn),
            lines(d_router),
            lines(d_qk_gains) * own_slot,
        ],
        axis=1,
    )
    d_normed_parts, moe_own = lax.optimization_barrier((d_normed_parts, moe_own))
    layer_out = gathered((hidden + moe_own).astype(bf16), TENSOR).reshape(layer_in.shape)
    grad_in, grad_qkv, grad_out_weight, small = finish_call(
        d_normed_parts.reshape(tensor_count, share, model_width),
        own_rows(layer_in.reshape(token_count, model_width)),
        own_rows(scale_one),
        gain_attn[None],
        d_hidden,
        d_qkv.astype(bf16).reshape(4, 2, weight_rows, -1),
        d_out_weight.astype(bf16).reshape(4, 2, weight_rows, -1),
        small.reshape((4, 2) + small.shape[1:]),
    )
    grad_in = grad_in.astype(f32).reshape(layer_in.shape)
    grad_qkv = grad_qkv.transpose(1, 0, 2)
    lines_of = weight_rows // 128
    gain_share = weight_rows // tensor_count
    router_share = expert_total // tensor_count
    router_lines = weight_rows * expert_total // 128
    part_of = lambda rows, count, axis: lax.dynamic_slice_in_dim(
        rows, tensor_rank * count, count, axis
    )
    gains = small[: 2 * lines_of].reshape(2, weight_rows)
    routers = small[2 * lines_of : 2 * lines_of + router_lines].reshape(weight_rows, expert_total)
    qk_lines = small[2 * lines_of + router_lines :]
    return (
        layer_out,
        grad_in,
        part_of(gains, gain_share, 1).T,
        grad_qkv,
        part_of(qk_lines, 1, 0).reshape(head_rows, 2, local_heads),
        grad_out_weight,
        part_of(routers, router_share, 1),
        grad_expert_in,
        grad_expert_out,
    )


def solution(mesh):
    placed = (
        P(WEIGHTS, CONTEXT, None),
        P(GROUP, None),
        P(GROUP, None, TENSOR),
        P(GROUP, None, TENSOR),
        P(GROUP, TENSOR),
        P(GROUP, None),
        P(GROUP, None, None, TENSOR),
        P(GROUP, TENSOR, None),
        P(WEIGHTS, CONTEXT, None),
        P(WEIGHTS, None),
        P(WEIGHTS, CONTEXT, None),
        P(WEIGHTS, CONTEXT, None),
    )
    axes = tuple(mesh.shape[axis] for axis in EVERYONE)

    def per_device(*blocks):
        dense = axes == (4, 2, 4) and blocks[5].shape[1] <= 2 * blocks[10].shape[2]
        return (per_device_dense if dense else per_device_slots)(*blocks)

    return jax.shard_map(
        per_device,
        mesh=mesh,
        in_specs=placed,
        out_specs=(
            P(WEIGHTS, CONTEXT, None),
            P(WEIGHTS, CONTEXT, None),
            P(EVERYONE, None),
            P(GROUP, None, TENSOR),
            P(GROUP, None, TENSOR),
            P(GROUP, TENSOR),
            P(GROUP, TENSOR),
            P(GROUP, None, None, TENSOR),
            P(GROUP, TENSOR, None),
        ),
        check_vma=False,
    )
```

```python
import functools
import math

import jax
import jax.numpy as jnp
from jax import lax
from jax.experimental import pallas as pl
from jax.experimental.pallas import tpu as pltpu
from jax.sharding import PartitionSpec as P

epsilon = 1e-05
rotary_base = 10000.0
WEIGHTS, CONTEXT, TENSOR = ("weights", "context", "tensor")
GROUP = (WEIGHTS, CONTEXT)
EVERYONE = (WEIGHTS, CONTEXT, TENSOR)
MESH = pl.DeviceIdType.MESH
BY_SCORE = "sqhd,skhd->shqk"
BY_QUERY = "shqk,skhd->sqhd"
BY_KEY = "shqk,sqhd->skhd"


def passed_along(value, axis, steps):
    count = lax.axis_size(axis)
    leading, last = (max(0, -steps), min(count, count - steps))
    return lax.ppermute(value, axis, [(source, source + steps) for source in range(leading, last)])


def rotate_half(values_in):
    middle = values_in.shape[-1] // 2
    return jnp.concatenate([-values_in[..., middle:], values_in[..., :middle]], axis=-1)


def rotate_back(grads_in):
    middle = grads_in.shape[-1] // 2
    return jnp.concatenate([grads_in[..., middle:], -grads_in[..., :middle]], axis=-1)


def rotary_tables(positions, head_size):
    frequency = rotary_base ** (-(2.0 * jnp.arange(head_size // 2, dtype=jnp.float32)) / head_size)
    angle_table = positions.astype(jnp.float32)[:, None] * frequency[None, :]
    angle_table = jnp.concatenate([angle_table, angle_table], axis=1)
    return (jnp.cos(angle_table), jnp.sin(angle_table))


def pair_slots(token_routes, token_ranks, expert_total):
    unused = token_routes.size
    hot = token_routes.T[None] == jnp.arange(expert_total, dtype=jnp.int32)[:, None, None]
    rank_of = jnp.min(jnp.where(hot, token_ranks.T[None], unused), axis=1)
    slot_of = jnp.sum((rank_of[:, :, None] < rank_of[:, None, :]).astype(jnp.int32), axis=1)
    return (rank_of < unused, slot_of)


def place_pairs(pair_expert, rank, expert_total, capacity, top_count):
    pair_count = pair_expert.shape[0]
    token_routes = pair_expert.reshape(-1, top_count)
    slot_of = pair_slots(token_routes, rank.reshape(-1, top_count), expert_total)[1]
    slot_index = jnp.take_along_axis(slot_of.T, token_routes, axis=1).reshape(pair_count)
    kept_pair = slot_index < capacity
    dest_row = jnp.where(kept_pair, pair_expert * capacity + slot_index, expert_total * capacity)
    slot_pair = (
        jnp.full((expert_total * capacity + 1,), pair_count, jnp.int32)
        .at[dest_row]
        .set(jnp.arange(pair_count, dtype=jnp.int32))[:-1]
    )
    return (kept_pair, dest_row, slot_pair)


def row_sums(partial_rows):
    return lax.psum(partial_rows, TENSOR)


def tensor_sum(partial_rows):
    return lax.psum(partial_rows, TENSOR)


def to_owners(slot_rows):
    return lax.all_to_all(
        slot_rows, GROUP, split_axis=0, concat_axis=0, tiled=True
    )


def expert_front(slot_inputs, expert_in):
    both_pre = jnp.einsum(
        "sncd,ngdf->sncgf", slot_inputs, expert_in, preferred_element_type=jnp.float32
    )
    return (both_pre[..., 0, :], both_pre[..., 1, :])


def per_device_slots(
    layer_in,
    norm_gains,
    qkv_weight,
    qk_gains,
    out_weight,
    router,
    expert_in,
    expert_out,
    grad_out,
    segments,
    routes,
    route_order,
):
    group_count = lax.axis_size(GROUP)
    tensor_count = lax.axis_size(TENSOR)
    context_rank = lax.axis_index(CONTEXT)
    tensor_rank = lax.axis_index(TENSOR)
    seq_count, half_len, model_width = layer_in.shape
    token_count = seq_count * half_len
    top_count = routes.shape[2]
    qkv_full, out_full, qk_gain_full, gain_full, router_full = (
        lax.all_gather(qkv_weight, GROUP, axis=0, tiled=True),
        lax.all_gather(out_weight, GROUP, axis=0, tiled=True),
        lax.all_gather(qk_gains, GROUP, axis=0, tiled=True),
        lax.all_gather(norm_gains, GROUP, axis=0, tiled=True),
        lax.all_gather(router, GROUP, axis=0, tiled=True),
    )
    head_size = qk_gain_full.shape[0]
    local_heads = qk_gain_full.shape[2]
    expert_total = router_full.shape[1]
    gain_attn = gain_full[:, 0].astype(jnp.float32)
    gain_ffn = gain_full[:, 1].astype(jnp.float32)
    query_gain = qk_gain_full[:, 0, :].astype(jnp.float32).T.reshape(-1)
    key_gain = qk_gain_full[:, 1, :].astype(jnp.float32).T.reshape(-1)
    inv_root = 1.0 / math.sqrt(head_size)
    residual = layer_in.reshape(token_count, model_width).astype(jnp.float32)
    scale_one = lax.rsqrt(jnp.mean(residual * residual, axis=1, keepdims=True) + epsilon)
    unit_one = residual * scale_one
    normed_one = (unit_one * gain_attn).astype(jnp.bfloat16)
    projected = jnp.einsum("td,dgf->tgf", normed_one, qkv_full, preferred_element_type=jnp.float32)
    query_raw = projected[:, 0]
    key_raw = projected[:, 1]
    value_raw = projected[:, 2]
    square_sums = row_sums(
        jnp.stack(
            [jnp.sum(query_raw * query_raw, axis=1), jnp.sum(key_raw * key_raw, axis=1)], axis=1
        )
    )
    query_scale = lax.rsqrt(square_sums[:, 0:1] / model_width + epsilon)
    key_scale = lax.rsqrt(square_sums[:, 1:2] / model_width + epsilon)
    heads_shape = (seq_count, half_len, local_heads, head_size)
    query_hat = (query_raw * query_scale * query_gain).reshape(heads_shape)
    key_hat = (key_raw * key_scale * key_gain).reshape(heads_shape)
    query_pos = context_rank * half_len + jnp.arange(half_len, dtype=jnp.int32)
    cosine_table, sine_table = rotary_tables(query_pos, head_size)
    cosine_table = cosine_table[None, :, None, :]
    sine_table = sine_table[None, :, None, :]
    query_rot = (query_hat * cosine_table + rotate_half(query_hat) * sine_table).astype(
        jnp.bfloat16
    )
    key_rot = (key_hat * cosine_table + rotate_half(key_hat) * sine_table).astype(jnp.bfloat16)
    value_low = value_raw.astype(jnp.bfloat16).reshape(heads_shape)
    key_prev, value_prev = passed_along((key_rot, value_low), CONTEXT, 1)
    all_keys = jnp.concatenate([key_prev, key_rot], axis=1)
    all_values = jnp.concatenate([value_prev, value_low], axis=1)
    key_pos = jnp.concatenate([query_pos - half_len, query_pos])
    seg_query = lax.dynamic_slice_in_dim(segments, context_rank * half_len, half_len, 1)
    seg_prev = lax.dynamic_slice_in_dim(
        segments, jnp.maximum(context_rank - 1, 0) * half_len, half_len, 1
    )
    seg_keys = jnp.concatenate([seg_prev, seg_query], axis=1)
    causal = (key_pos[None, :] >= 0) & (key_pos[None, :] <= query_pos[:, None])
    allowed = causal[None] & (seg_query[:, :, None] == seg_keys[:, None, :])

    def score_block(queries, key_rows):
        raw_scores = (
            jnp.einsum(BY_SCORE, queries, key_rows, preferred_element_type=jnp.float32)
            * inv_root
        )
        return jnp.where(allowed[:, None], raw_scores, -1e30)

    scores = score_block(query_rot, all_keys)
    row_max = jnp.max(scores, axis=-1, keepdims=True)
    exponent = jnp.exp(scores - row_max)
    row_total = jnp.sum(exponent, axis=-1, keepdims=True)
    log_total = row_max + jnp.log(row_total)
    attn_probs = (exponent / row_total).astype(jnp.bfloat16)
    attended = jnp.einsum(
        BY_QUERY, attn_probs, all_values, preferred_element_type=jnp.float32
    )
    attended_low = attended.reshape(token_count, -1).astype(jnp.bfloat16)
    attn_partial = jnp.einsum(
        "tf,df->td", attended_low, out_full, preferred_element_type=jnp.float32
    )
    hidden = residual + tensor_sum(attn_partial)
    scale_two = lax.rsqrt(jnp.mean(hidden * hidden, axis=1, keepdims=True) + epsilon)
    unit_two = hidden * scale_two
    normed_two = (unit_two * gain_ffn).astype(jnp.bfloat16)
    logits = jnp.dot(normed_two, router_full, preferred_element_type=jnp.float32)
    router_probs = jax.nn.softmax(logits, axis=1)
    capacity = token_count * top_count * 9 // (8 * expert_total)
    local_experts = expert_in.shape[0]
    pair_count = token_count * top_count
    token_routes = routes.reshape(token_count, top_count)
    kept_pair, dest_row, slot_pair = place_pairs(
        token_routes.reshape(pair_count), route_order.reshape(pair_count), expert_total, capacity, top_count
    )
    zero_row = jnp.zeros((1, model_width), jnp.bfloat16)
    zero_wide = jnp.zeros((1, model_width), jnp.float32)
    slot_shape = (group_count, local_experts, capacity, model_width)
    dispatch_rows = jnp.concatenate([normed_two, zero_row], axis=0)[slot_pair // top_count].reshape(
        slot_shape
    )
    received = lax.all_to_all(
        dispatch_rows, GROUP, split_axis=0, concat_axis=0, tiled=True
    )
    gate_pre, up_pre = expert_front(received, expert_in)
    sigmoid_gate = jax.nn.sigmoid(gate_pre)
    silu_gate = gate_pre * sigmoid_gate
    activated = (silu_gate * up_pre).astype(jnp.bfloat16)
    expert_partial = jnp.einsum(
        "sncf,nfd->sncd", activated, expert_out, preferred_element_type=jnp.float32
    )
    kept_float = kept_pair.reshape(token_count, top_count).astype(jnp.float32)
    gate_weight = jnp.take_along_axis(router_probs, token_routes, axis=1) * kept_float
    upstream = grad_out.reshape(token_count, model_width).astype(jnp.float32)
    returned = to_owners(expert_partial).reshape(expert_total * capacity, model_width)
    picked = jnp.concatenate([returned, zero_wide], axis=0)[dest_row].reshape(
        token_count, top_count, model_width
    )
    moe_partial = jnp.sum(gate_weight[:, :, None] * picked, axis=1)
    dot_partial = jnp.sum(upstream[:, None, :] * picked, axis=2)
    moe_total, dot_total = lax.psum((moe_partial, dot_partial), TENSOR)
    layer_out = (hidden + moe_total).astype(jnp.bfloat16).reshape(layer_in.shape)
    d_gate = dot_total * kept_float
    route_hot = (
        token_routes[:, :, None] == jnp.arange(expert_total, dtype=jnp.int32)[None, None, :]
    ).astype(jnp.float32)
    d_probs = jnp.sum(d_gate[:, :, None] * route_hot, axis=1)
    d_logits = (
        router_probs * (d_probs - jnp.sum(router_probs * d_probs, axis=1, keepdims=True))
    ).astype(jnp.bfloat16)
    d_pair = (
        (gate_weight[:, :, None] * upstream[:, None, :])
        .astype(jnp.bfloat16)
        .reshape(pair_count, model_width)
    )
    d_slots = jnp.concatenate([d_pair, zero_row], axis=0)[slot_pair].reshape(slot_shape)
    d_received = lax.all_to_all(
        d_slots, GROUP, split_axis=0, concat_axis=0, tiled=True
    )
    d_activated = jnp.einsum(
        "sncd,nfd->sncf", d_received, expert_out, preferred_element_type=jnp.float32
    )
    grad_expert_out = jnp.einsum(
        "sncf,sncd->nfd", activated, d_received, preferred_element_type=jnp.float32
    )
    d_gate_pre = d_activated * up_pre * sigmoid_gate * (1.0 + gate_pre * (1.0 - sigmoid_gate))
    d_up_pre = d_activated * silu_gate
    d_both = jnp.stack([d_gate_pre, d_up_pre], axis=3).astype(jnp.bfloat16)
    d_inputs = jnp.einsum("sncgf,ngdf->sncd", d_both, expert_in, preferred_element_type=jnp.float32)
    grad_expert_in = jnp.einsum(
        "sncd,sncgf->ngdf", received, d_both, preferred_element_type=jnp.float32
    )
    d_returned = to_owners(d_inputs).reshape(expert_total * capacity, model_width)
    d_normed_part = jnp.sum(
        jnp.concatenate([d_returned, zero_wide], axis=0)[dest_row].reshape(
            token_count, top_count, model_width
        ),
        axis=1,
    )
    d_normed_two = tensor_sum(d_normed_part) + jnp.dot(
        d_logits, router_full.T, preferred_element_type=jnp.float32
    )
    d_router = jnp.dot(normed_two.T, d_logits, preferred_element_type=jnp.float32)
    d_gain_ffn = jnp.sum(d_normed_two * unit_two, axis=0)
    scaled_ffn = gain_ffn * d_normed_two
    d_hidden = upstream + scale_two * (
        scaled_ffn - unit_two * jnp.mean(scaled_ffn * unit_two, axis=1, keepdims=True)
    )
    d_hidden_low = d_hidden.astype(jnp.bfloat16)
    d_out_weight = jnp.einsum(
        "td,tf->df", d_hidden_low, attended_low, preferred_element_type=jnp.float32
    )
    d_attended = (
        jnp.dot(d_hidden_low, out_full, preferred_element_type=jnp.float32)
        .astype(jnp.bfloat16)
        .reshape(heads_shape)
    )
    probs_again = jnp.exp(score_block(query_rot, all_keys) - log_total)
    probs_again_low = probs_again.astype(jnp.bfloat16)
    d_probs_att = jnp.einsum(
        BY_SCORE, d_attended, all_values, preferred_element_type=jnp.float32
    )
    d_values_all = jnp.einsum(
        BY_KEY, probs_again_low, d_attended, preferred_element_type=jnp.float32
    )
    row_dot = jnp.sum(probs_again * d_probs_att, axis=-1, keepdims=True)
    d_scores = (probs_again * (d_probs_att - row_dot)).astype(jnp.bfloat16)
    d_query_rot = (
        jnp.einsum(BY_QUERY, d_scores, all_keys, preferred_element_type=jnp.float32)
        * inv_root
    )
    d_keys_all = (
        jnp.einsum(BY_KEY, d_scores, query_rot, preferred_element_type=jnp.float32)
        * inv_root
    )
    back_key, back_value = (
        passed_along(d_keys_all[:, :half_len].astype(jnp.bfloat16), CONTEXT, -1).astype(
            jnp.float32
        ),
        passed_along(d_values_all[:, :half_len].astype(jnp.bfloat16), CONTEXT, -1).astype(
            jnp.float32
        ),
    )
    d_key_rot = d_keys_all[:, half_len:] + back_key
    d_value = (d_values_all[:, half_len:] + back_value).reshape(token_count, -1)
    d_query_hat = (d_query_rot * cosine_table + rotate_back(d_query_rot * sine_table)).reshape(
        token_count, -1
    )
    d_key_hat = (d_key_rot * cosine_table + rotate_back(d_key_rot * sine_table)).reshape(
        token_count, -1
    )
    centre = row_sums(
        jnp.stack(
            [
                jnp.sum(query_gain * d_query_hat * query_raw, axis=1),
                jnp.sum(key_gain * d_key_hat * key_raw, axis=1),
            ],
            axis=1,
        )
    )
    d_query_raw = (
        query_scale * query_gain * d_query_hat
        - query_raw * (query_scale**3 / model_width) * centre[:, 0:1]
    )
    d_key_raw = (
        key_scale * key_gain * d_key_hat - key_raw * (key_scale**3 / model_width) * centre[:, 1:2]
    )
    d_query_gain = (
        jnp.sum(d_query_hat * query_raw * query_scale, axis=0).reshape(local_heads, head_size).T
    )
    d_key_gain = jnp.sum(d_key_hat * key_raw * key_scale, axis=0).reshape(local_heads, head_size).T
    d_qk_gains = jnp.stack([d_query_gain, d_key_gain], axis=1)
    d_projected = jnp.stack([d_query_raw, d_key_raw, d_value], axis=1).astype(jnp.bfloat16)
    d_normed_one = tensor_sum(
        jnp.einsum("tgf,dgf->td", d_projected, qkv_full, preferred_element_type=jnp.float32)
    )
    d_qkv = jnp.einsum("td,tgf->dgf", normed_one, d_projected, preferred_element_type=jnp.float32)
    d_gain_attn = jnp.sum(d_normed_one * unit_one, axis=0)
    scaled_attn = gain_attn * d_normed_one
    grad_in = d_hidden + scale_one * (
        scaled_attn - unit_one * jnp.mean(scaled_attn * unit_one, axis=1, keepdims=True)
    )
    d_norm_gains = jnp.stack([d_gain_attn, d_gain_ffn], axis=1)
    grad_qkv, grad_out_weight, grad_qk_gains, gain_rows, router_rows = (
        lax.psum_scatter(d_qkv, GROUP, scatter_dimension=0, tiled=True),
        lax.psum_scatter(d_out_weight, GROUP, scatter_dimension=0, tiled=True),
        lax.psum_scatter(d_qk_gains, GROUP, scatter_dimension=0, tiled=True),
        lax.psum_scatter(d_norm_gains, GROUP, scatter_dimension=0, tiled=True),
        lax.psum_scatter(d_router, GROUP, scatter_dimension=0, tiled=True),
    )
    gain_share = gain_rows.shape[0] // tensor_count
    grad_norm_gains = lax.dynamic_slice_in_dim(gain_rows, tensor_rank * gain_share, gain_share, 0)
    router_share = expert_total // tensor_count
    grad_router = lax.dynamic_slice_in_dim(router_rows, tensor_rank * router_share, router_share, 1)
    return (
        layer_out,
        grad_in.reshape(layer_in.shape),
        grad_norm_gains,
        grad_qkv,
        grad_qk_gains,
        grad_out_weight,
        grad_router,
        grad_expert_in,
        grad_expert_out,
    )


def contract_last(left, right):
    return lax.dot_general(
        left, right, (((1,), (1,)), ((), ())), preferred_element_type=jnp.float32
    )


def share_order(z):
    upper, odd = (z // 2, z % 2)
    return (z, z + 1 - 2 * upper, 2 + upper - 2 * odd, 3 - 3 * upper)


def share_turns(z):
    return (z, (z + 2) % 4, 3 - z, z + 1 - 2 * (z % 2))


def neighbours(w):
    wx, wy = (w + 1 - 2 * (w % 2), (w + 2) % 4)
    return (wx, wy, wx + wy - w)


def experts_kernel(
    experts,
    x_ref,
    grad_own,
    grad_x_low,
    grad_x_high,
    grad_y_low,
    grad_y_high,
    grad_low,
    grad_high,
    kept_ref,
    router_ref,
    in_ref,
    out_w_ref,
    x_out,
    grads_out,
    gated_out,
    both_out,
    moe_out,
    dx_own,
    x_tile,
    w_in,
    w_out,
    grads,
    gated,
    both,
    moe_tile,
    others,
    mine,
    sibs,
    from_x1,
    from_y1,
    from_y2,
    from_x2,
    from_z,
        own_sem,
        tile_sem,
        weight_sem,
        grads_sem,
        store_sem,
        send_z,
        send_x,
        send_y,
        send_c,
        recv,
        over_send,
        over_recv,
        sib_send,
        sib_recv,
        credit,
        one_send,
        one_recv,
        two_send,
        two_recv,
        end_send,
        end_recv,
):
    w, c, z = (lax.axis_index(a) for a in (WEIGHTS, CONTEXT, TENSOR))
    wx, wy, wd = neighbours(w)
    share, width = x_ref.shape
    half = width // 2
    lo, hi = (pl.ds(0, half), pl.ds(half, half))
    dev_x, dev_y, dev_c = ((wx, c, z), (wy, c, z), (w, 1 - c, z))
    turns = share_turns(z)
    hidden = out_w_ref.shape[1]
    group = w * 2 + c
    bf16, f32 = (jnp.bfloat16, jnp.float32)
    low, high = (pl.ds(0, half), pl.ds(half, half + 128))

    def loads():
        return [
            pltpu.make_async_copy(
                in_ref.at[n, g],
                w_in.at[:, pl.ds((2 * n + g) * hidden, hidden)],
                weight_sem.at[2 * n + g],
            )
            for n in range(2)
            for g in range(2)
        ] + [
            pltpu.make_async_copy(
                out_w_ref.at[n], w_out.at[pl.ds(n * hidden, hidden)], weight_sem.at[4 + n]
            )
            for n in range(2)
        ]

    for load in loads():
        load.start()
    keep = lambda: pltpu.make_async_copy(x_ref, x_out.at[w, c, z], own_sem)
    keep().start()

    grad_parts = (
        (grad_own, w, None),
        (grad_x_low, wx, lo),
        (grad_x_high, wx, hi),
        (grad_y_low, wy, lo),
        (grad_y_high, wy, hi),
        (grad_low, wd, lo),
        (grad_high, wd, hi),
    )

    def grad_place(cc, ww, cols):
        return grads_out.at[ww, cc] if cols is None else grads_out.at[ww, cc, :, :, cols]

    def over(i, cc):
        src, ww, cols = grad_parts[i]
        return pltpu.make_async_remote_copy(
            src_ref=src,
            dst_ref=grad_place(cc, ww, cols),
            send_sem=over_send.at[i],
            recv_sem=over_recv.at[i],
            device_id=dev_c,
            device_id_type=MESH,
        )

    barrier = pltpu.get_barrier_semaphore()
    around = [(w, c, (z + k) % 4) for k in range(1, 4)]
    for device in [dev_x, dev_y, dev_c] + around:
        pl.semaphore_signal(barrier, inc=1, device_id=device, device_id_type=MESH)
    pl.semaphore_wait(barrier, 6)


    def view(chunk, cols):
        zz, cc, ww = chunk
        return x_out.at[ww, cc, zz] if cols is None else x_out.at[ww, cc, zz, :, cols]

    def copy(src, chunk, cols, slot, sem, device):
        return pltpu.make_async_remote_copy(
            src_ref=src,
            dst_ref=view(chunk, cols),
            send_sem=sem[0].at[sem[1:]],
            recv_sem=recv.at[chunk[0], chunk[1], slot],
            device_id=device,
            device_id_type=MESH,
        )

    sent = []
    devices_z = ((w, c, z + 1), (w, c, z - 1))

    def start(chunk, cols, slot, sem, device, src=None):
        copy(view(chunk, cols) if src is None else src, chunk, cols, slot, sem, device).start()
        sent.append((chunk, cols, slot, sem, device))

    def arrived(chunk, cols, slot):
        copy(view(chunk, cols), chunk, cols, slot, (send_c, 0, 0), dev_c).wait_recv()

    def spread(j):
        chunk = (turns[j], c, w)
        src = x_ref if j == 0 else None
        start(chunk, None, 1, (send_x, j, 0), dev_x, src)
        start(chunk, None, 2, (send_y, j, 0), dev_y, src)
        start(chunk, None, 0, (send_c, j, 0), dev_c, src)

    def onward(j):
        chunk = (turns[j], c, w)

        def moved(side):
            src = x_ref if j == 0 else view(chunk, None)
            return copy(src, chunk, None, 0, (send_z, j, side), devices_z[side])

        return (
            ((turns[j] <= z) & (z < 3), functools.partial(moved, 0)),
            ((turns[j] >= z) & (z > 0), functools.partial(moved, 1)),
        )

    def along(j):
        for there, moved in onward(j):
            pl.when(there)(lambda: moved().start())

    def pass_on(j):
        arrived((turns[j], c, w), None, 0)
        along(j)

    def relay(j):
        from_x, from_y = ((turns[j], c, wx), (turns[j], c, wy))
        arrived(from_x, None, 1)
        start(from_x, lo, 3, (send_y, j, 1), dev_y)
        start(from_x, None, 1, (send_c, j, 1), dev_c)
        arrived(from_y, None, 2)
        start(from_y, hi, 4, (send_x, j, 1), dev_x)
        start(from_y, None, 2, (send_c, j, 2), dev_c)

    def across(j):
        chunk = (turns[j], c, wd)
        for cols, slot in ((lo, 3), (hi, 4)):
            arrived(chunk, cols, slot)
            start(chunk, cols, slot, (send_c, j, slot), dev_c)

    def sibling(j):
        for ww, cols, slot in ((w, None, 0), (wx, None, 1), (wy, None, 2), (wd, lo, 3), (wd, hi, 4)):
            arrived((turns[j], 1 - c, ww), cols, slot)


    def remote(src, dst, send, got, device):
        return pltpu.make_async_remote_copy(
            src_ref=src,
            dst_ref=dst,
            send_sem=send,
            recv_sem=got,
            device_id=device,
            device_id_type=MESH,
        )

    def to_sibling():
        return remote(others, sibs, sib_send, sib_recv, dev_c)

    def first_hops(j):
        moves = (
            (wx, low, from_x1.at[j, 0], dev_x),
            (wd, low, from_x1.at[j, 1], dev_x),
            (wy, high, from_y1.at[j, 0], dev_y),
            (wd, high, from_y1.at[j, 1], dev_y),
        )
        return [
            remote(
                mine.at[j % 2, ww, :, cols], dst, one_send.at[j, i], one_recv.at[j, i], device
            )
            for i, (ww, cols, dst, device) in enumerate(moves)
        ]

    def second_hops(j):
        moves = ((wy, low, from_y2.at[j], dev_y), (wx, high, from_x2.at[j], dev_x))
        return [
            remote(
                mine.at[j % 2, ww, :, cols], dst, two_send.at[j, i], two_recv.at[j, i], device
            )
            for i, (ww, cols, dst, device) in enumerate(moves)
        ]

    def last_hop(source, j):
        return remote(
            mine.at[j % 2, w],
            from_z.at[source],
            end_send.at[j],
            end_recv.at[source],
            (w, c, turns[j]),
        )

    def total(*terms):
        added = terms[0].astype(f32)
        for term in terms[1:]:
            added = added + term.astype(f32)
        return added

    def after_first(j):
        p = j % 2
        for moved in first_hops(j):
            moved.wait_recv()
        mine[p, wy, :, low] = total(mine[p, wy, :, low], from_x1[j, 1]).astype(bf16)
        mine[p, wx, :, high] = total(mine[p, wx, :, high], from_y1[j, 1]).astype(bf16)
        for moved in second_hops(j):
            moved.start()

    def after_second(j):
        p = j % 2
        for moved in second_hops(j):
            moved.wait_recv()
        mine[p, w, :, low] = total(mine[p, w, :, low], from_x1[j, 0], from_y2[j]).astype(bf16)
        mine[p, w, :, high] = total(mine[p, w, :, high], from_y1[j, 0], from_x2[j]).astype(bf16)
        if j == 0:
            from_z[z] = mine[p, w]
        else:
            last_hop(z, j).start()

    def all_sent(j):
        for moved in first_hops(j) + second_hops(j):
            moved.wait_send()
        if j > 0:
            last_hop(z, j).wait_send()


    code = turns[0] + 4 * turns[1] + 16 * turns[2] + 64 * turns[3]

    def tile_of(step):
        j = step // 2
        power = 1 + 3 * j + (9 * j * (j - 1)) // 2 + (27 * j * (j - 1) * (j - 2)) // 6
        return ((code // power) % 4, (c + 1 + step) % 2)

    def other_grads(step):
        zj, cc = tile_of(step)
        return pltpu.make_async_copy(grads_out.at[:, cc, zj], grads.at[0], grads_sem.at[7])

    def my_grads(step):
        zj, cc = tile_of(step)
        return [
            pltpu.make_async_copy(
                src.at[zj],
                grads.at[1, ww] if cols is None else grads.at[1, ww, :, cols],
                grads_sem.at[i],
            )
            for i, (src, ww, cols) in enumerate(grad_parts)
        ]

    def stores(step, own_tile):
        zj, cc = tile_of(step)
        pairs = [(gated, gated_out), (both, both_out)]
        pairs += [(grads.at[1], grads_out)] if own_tile else []
        return [
            pltpu.make_async_copy(src, dst.at[:, cc, zj], store_sem.at[i])
            for i, (src, dst) in enumerate(pairs)
        ]

    def moe_store(step):
        zj, cc = tile_of(step)
        return pltpu.make_async_copy(moe_tile, moe_out.at[:, cc, zj], store_sem.at[3])

    lanes = lax.broadcasted_iota(jnp.int32, (4 * share, 128), 1)

    def tile(step, own_tile, parity):
        zj, cc = tile_of(step)
        load = pltpu.make_async_copy(x_out.at[:, cc, zj], x_tile, tile_sem)
        load.start()
        if own_tile:
            for store in stores(step - 1, False):
                store.wait()
            for part in my_grads(step):
                part.wait()

            @pl.when(step < 7)
            def _():
                other_grads(step + 1).start()
        else:

            @pl.when(step > 0)
            def _():
                for store in stores(step - 1, True):
                    store.wait()

            for part in my_grads(step + 1):
                part.start()
            other_grads(step).wait()
        load.wait()
        rows = x_tile[...].reshape(4 * share, width)
        upstream = grads[1 if own_tile else 0].reshape(4 * share, width)
        logits = jnp.dot(rows, router_ref[...], preferred_element_type=f32)
        logits = jnp.where(lanes < experts, logits, -1e30)
        raised = jnp.exp(logits - jnp.max(logits, axis=1, keepdims=True))
        gates = raised / jnp.sum(raised, axis=1, keepdims=True)
        gates = gates * kept_ref[:, cc, zj].reshape(4 * share, 128).astype(f32)
        d_gate = jnp.zeros((4 * share, 128), f32)
        for n in range(2):
            here = lanes == group * 2 + n
            gate = jnp.sum(jnp.where(here, gates, 0.0), axis=1, keepdims=True)
            at = 2 * n * hidden
            gate_pre = jnp.dot(rows, w_in[:, at : at + hidden], preferred_element_type=f32)
            up_pre = jnp.dot(
                rows, w_in[:, at + hidden : at + 2 * hidden], preferred_element_type=f32
            )
            back = contract_last(upstream, w_out[n * hidden : (n + 1) * hidden, :])
            sigmoid = 1.0 / (1.0 + jnp.exp(-gate_pre))
            silu = gate_pre * sigmoid
            activated = silu * up_pre
            d_gate = jnp.where(here, jnp.sum(activated * back, axis=1, keepdims=True), d_gate)
            back = gate * back
            d_pre = back * up_pre * sigmoid * (1.0 + gate_pre * (1.0 - sigmoid))
            shape = (4, share, hidden)
            gated[:, :, n * hidden : (n + 1) * hidden] = (
                (gate * activated).astype(bf16).reshape(shape)
            )
            both[:, :, at : at + hidden] = d_pre.astype(bf16).reshape(shape)
            both[:, :, at + hidden : at + 2 * hidden] = (back * silu).astype(bf16).reshape(shape)
        for store in stores(step, own_tile):
            store.start()
        if own_tile:
            to_sibling().wait_recv()
            moe_store(step - 1).wait()
        else:

            @pl.when(step > 0)
            def _():
                to_sibling().wait_send()
                moe_store(step - 1).wait()

        def put(cols, count, value):
            value = value.reshape(4, share, count)
            if own_tile:
                value = value + sibs[:, :, cols].astype(f32)
                mine[parity, :, :, cols] = value.astype(bf16)
            else:
                others[:, :, cols] = value.astype(bf16)

        put(pl.ds(width, 128), 128, d_gate)
        d_rows = both[...].reshape(4 * share, 4 * hidden)
        g_rows = gated[...].reshape(4 * share, 2 * hidden)

        def columns(m, carried):
            cols = pl.ds(pl.multiple_of(m * 256, 256), 256)
            put(cols, 256, contract_last(d_rows, w_in[cols, :]))
            moe_tile[:, :, cols] = (
                jnp.dot(g_rows, w_out[:, cols], preferred_element_type=f32)
                .astype(bf16)
                .reshape(4, share, 256)
            )
            return carried

        lax.fori_loop(0, width // 256, columns, None)
        moe_store(step).start()

    def before_other(j):
        if j == 0:
            for i in range(7):
                over(i, c).start()
            along(0)
            spread(0)
            pass_on(3)
            pl.when((z > 0) & (z < 3))(lambda: pass_on(2))
            relay(0)
            pass_on(1)
            spread(1)
            keep().wait()
            for load in loads():
                load.wait()
            for i in range(7):
                over(i, 1 - c).wait_recv()
            other_grads(0).start()
        if j >= 2:
            after_second(j - 2)
        across(j)
        sibling(j)

    def before_mine(j):
        if j == 0:
            pl.when((z == 0) | (z == 3))(lambda: pass_on(2))
        if j + 2 < 4:
            spread(j + 2)
        if j + 1 < 4:
            relay(j + 1)
        if j >= 1:
            after_first(j - 1)
        if j >= 2:
            all_sent(j - 2)

    def round_of(j, carry):
        for k in range(4):
            pl.when(j == k)(functools.partial(before_other, k))
        tile(2 * j, False, None)

        @pl.when(j > 0)
        def _():
            pl.semaphore_wait(credit, 1)

        to_sibling().start()
        for k in range(4):
            pl.when(j == k)(functools.partial(before_mine, k))
        tile(2 * j + 1, True, j % 2)

        @pl.when(j < 3)
        def _():
            pl.semaphore_signal(credit, inc=1, device_id=dev_c, device_id_type=MESH)

        for k in range(4):

            @pl.when(j == k)
            def _():
                for moved in first_hops(k):
                    moved.start()

        return carry

    lax.fori_loop(0, 4, round_of, None)
    after_second(2)
    after_first(3)
    after_second(3)
    for store in stores(7, True):
        store.wait()
    moe_store(7).wait()
    to_sibling().wait_send()
    for k in range(1, 4):
        last_hop((z + k) % 4, 1).wait_recv()
    dx_own[...] = total(*(from_z[k] for k in range(4)))
    all_sent(2)
    all_sent(3)
    for i in range(7):
        over(i, c).wait_send()
    for chunk, cols, slot, sem, device in sent:
        copy(view(chunk, cols), chunk, cols, slot, sem, device).wait_send()
    for j in range(4):
        for there, moved in onward(j):
            pl.when(there)(lambda: moved().wait_send())


def experts_call(rows, grads, kept, router, expert_in, expert_out, experts):
    share, width = rows.shape
    hidden = expert_out.shape[1]
    blocks = (4, 2, 4, share)
    bf16, f32 = (jnp.bfloat16, jnp.float32)
    dma = pltpu.SemaphoreType.DMA
    anywhere, vmem = (pl.BlockSpec(memory_space=pl.ANY), pl.BlockSpec(memory_space=pltpu.VMEM))
    wide, half = (width + 128, width // 2)
    return pl.pallas_call(
        functools.partial(experts_kernel, experts),
        out_shape=tuple(
            jax.ShapeDtypeStruct(blocks + (n,), bf16)
            for n in (width, width, 2 * hidden, 4 * hidden, width)
        )
        + (jax.ShapeDtypeStruct((share, wide), f32),),
        in_specs=[anywhere] * 8 + [vmem, vmem, anywhere, anywhere],
        out_specs=(anywhere,) * 5 + (vmem,),
        scratch_shapes=[
            pltpu.VMEM((4, share, width), bf16),
            pltpu.VMEM((width, 4 * hidden), bf16),
            pltpu.VMEM((2 * hidden, width), bf16),
            pltpu.VMEM((2, 4, share, width), bf16),
            pltpu.VMEM((4, share, 2 * hidden), bf16),
            pltpu.VMEM((4, share, 4 * hidden), bf16),
            pltpu.VMEM((4, share, width), bf16),
            pltpu.VMEM((4, share, wide), bf16),
            pltpu.VMEM((2, 4, share, wide), bf16),
            pltpu.VMEM((4, share, wide), bf16),
            pltpu.VMEM((4, 2, share, half), bf16),
            pltpu.VMEM((4, 2, share, wide - half), bf16),
            pltpu.VMEM((4, share, half), bf16),
            pltpu.VMEM((4, share, wide - half), bf16),
            pltpu.VMEM((4, share, wide), bf16),
            dma,
            dma,
            dma((6,)),
            dma((8,)),
            dma((4,)),
            dma((4, 2)),
            dma((4, 2)),
            dma((4, 2)),
            dma((4, 5)),
            dma((4, 2, 5)),
            dma((7,)),
            dma((7,)),
            dma,
            dma,
            pltpu.SemaphoreType.REGULAR,
            dma((4, 4)),
            dma((4, 4)),
            dma((4, 2)),
            dma((4, 2)),
            dma((4,)),
            dma((4,)),
        ],
        compiler_params=pltpu.CompilerParams(
            collective_id=0, has_side_effects=True, vmem_limit_bytes=62 << 20
        ),
    )(rows, *grads, kept, router, expert_in, expert_out)


def finish_kernel(
    parts_ref,
    x_ref,
    scale_ref,
    gain_ref,
    d_hidden_ref,
    qkv_ref,
    out_ref,
    small_ref,
    rows_out,
    qkv_out,
    out_out,
    small_out,
    own_rows,
    right_in,
    left_in,
    sums,
    from_c,
    from_x,
    from_y,
    from_z,
    mine,
    sibs,
    from_x1,
    from_y1,
    from_y2,
    from_x2,
    right_send,
    right_recv,
    left_send,
    left_recv,
    send_z,
    recv_z,
    small_send,
    small_recv,
    load_sem,
    sib_send,
    sib_recv,
    one_send,
    one_recv,
    two_send,
    two_recv,
):
    w, c, z = (lax.axis_index(a) for a in EVERYONE)
    wx, wy, wd = neighbours(w)
    dev_x, dev_y, dev_c = ((wx, c, z), (wy, c, z), (w, 1 - c, z))
    sides = ((w, c, z + 1), (w, c, z - 1))
    order = share_order(z)
    bf16, f32 = (jnp.bfloat16, jnp.float32)
    half = x_ref.shape[1] // 2
    lo, hi = (slice(0, half), slice(half, 2 * half))
    heads = out_ref.shape[3]
    both = ((qkv_ref, pl.ds(0, 3 * heads)), (out_ref, pl.ds(3 * heads, heads)))

    def loads():
        return [
            pltpu.make_async_copy(ref.at[:, c], mine.at[:, :, cols], load_sem.at[i])
            for i, (ref, cols) in enumerate(both)
        ]

    for load in loads():
        load.start()
    barrier = pltpu.get_barrier_semaphore()
    around = [(w, c, (z + k) % 4) for k in range(1, 4)]
    for device in [dev_x, dev_y, dev_c] + around:
        pl.semaphore_signal(barrier, inc=1, device_id=device, device_id_type=MESH)
    pl.semaphore_wait(barrier, 6)

    def remote(src, dst, send, got, device):
        return pltpu.make_async_remote_copy(
            src_ref=src,
            dst_ref=dst,
            send_sem=send,
            recv_sem=got,
            device_id=device,
            device_id_type=MESH,
        )


    def to_right(s):
        return remote(
            parts_ref.at[s], right_in.at[s], right_send.at[s], right_recv.at[s], sides[0]
        )

    def to_left(s):
        return remote(parts_ref.at[s], left_in.at[s], left_send.at[s], left_recv.at[s], sides[1])

    def pass_right(s):
        @pl.when(z < s)
        def _():
            @pl.when(z > 0)
            def _():
                to_right(s).wait_recv()
                parts_ref[s] = (parts_ref[s].astype(f32) + right_in[s].astype(f32)).astype(bf16)

            to_right(s).start()

    def pass_left(s):
        @pl.when(z > s)
        def _():
            @pl.when(z < 3)
            def _():
                to_left(s).wait_recv()
                parts_ref[s] = (parts_ref[s].astype(f32) + left_in[s].astype(f32)).astype(bf16)

            to_left(s).start()


    def to_sibling():
        return [
            remote(
                ref.at[:, 1 - c], sibs.at[:, :, cols], sib_send.at[i], sib_recv.at[i], dev_c
            )
            for i, (ref, cols) in enumerate(both)
        ]

    def first_hops():
        moves = (
            (wx, lo, from_x1.at[0], dev_x),
            (wd, lo, from_x1.at[1], dev_x),
            (wy, hi, from_y1.at[0], dev_y),
            (wd, hi, from_y1.at[1], dev_y),
        )
        return [
            remote(mine.at[ww, :, cols], dst, one_send.at[i], one_recv.at[i], device)
            for i, (ww, cols, dst, device) in enumerate(moves)
        ]

    def second_hops():
        moves = ((wy, lo, from_y2, dev_y), (wx, hi, from_x2, dev_x))
        return [
            remote(mine.at[ww, :, cols], dst, two_send.at[i], two_recv.at[i], device)
            for i, (ww, cols, dst, device) in enumerate(moves)
        ]

    def add(*terms):
        added = terms[0].astype(f32)
        for term in terms[1:]:
            added = added + term.astype(f32)
        return added

    def weights_first():
        for load in loads():
            load.wait()
        for part in to_sibling():
            part.wait_recv()
        for k in range(4):
            mine[k] = add(mine[k], sibs[k]).astype(bf16)
        for hop in first_hops():
            hop.start()

    def weights_second():
        for hop in first_hops():
            hop.wait_recv()
        mine[wy, :, lo] = add(mine[wy, :, lo], from_x1[1]).astype(bf16)
        mine[wx, :, hi] = add(mine[wx, :, hi], from_y1[1]).astype(bf16)
        for hop in second_hops():
            hop.start()

    def weights_last():
        for hop in second_hops():
            hop.wait_recv()
        low = add(mine[w, :, lo], from_x1[0], from_y2[...])
        high = add(mine[w, :, hi], from_y1[0], from_x2[...])
        for k in range(4):
            part = (low if (k + 1) * heads <= half else high)[
                :, k * heads % half : k * heads % half + heads
            ]
            if k < 3:
                qkv_out[k] = part
            else:
                out_out[...] = part


    def moved(j, side):
        return remote(
            own_rows if j == 0 else rows_out.at[order[j]],
            rows_out.at[order[j]],
            send_z.at[j, side],
            recv_z.at[order[j]],
            sides[side],
        )

    def onward(j):
        return (((order[j] <= z) & (z < 3), 0), ((order[j] >= z) & (z > 0), 1))

    def along(j):
        for there, side in onward(j):
            pl.when(there)(lambda: moved(j, side).start())

    def passed_on(j):
        moved(j, 0).wait_recv()
        along(j)


    def small(i, src, dst, device):
        return remote(src, dst, small_send.at[i], small_recv.at[i], device)

    def small_sibling(k):
        return small(k, small_ref.at[k, 1 - c], from_c.at[k], dev_c)

    def small_x(k):
        return small(4 + k, sums.at[(wx, wd)[k]], from_x.at[k], dev_x)

    def small_y():
        return small(6, sums.at[wy], from_y, dev_y)

    def small_z(target, source):
        return remote(
            sums.at[w],
            from_z.at[source],
            small_send.at[7 + target],
            small_recv.at[7 + source],
            (w, c, target),
        )

    for part in to_sibling():
        part.start()
    for s in range(3):
        pass_right(3 - s)
        pass_left(s)
        if s == 1:
            weights_first()
    d_normed = parts_ref[z].astype(f32)
    right_in[0] = jnp.zeros(right_in.shape[1:], bf16)
    left_in[3] = jnp.zeros(left_in.shape[1:], bf16)

    @pl.when(z > 0)
    def _():
        to_right(z).wait_recv()

    @pl.when(z < 3)
    def _():
        to_left(z).wait_recv()

    d_normed = d_normed + right_in[z].astype(f32) + left_in[z].astype(f32)
    scale = scale_ref[...]
    unit = x_ref[...].astype(f32) * scale
    scaled = gain_ref[...] * d_normed
    shift = jnp.mean(scaled * unit, axis=1, keepdims=True)
    own_rows[...] = (d_hidden_ref[...] + scale * (scaled - unit * shift)).astype(bf16)
    along(0)
    rows_out[z] = own_rows[...]
    d_gain = jnp.sum(d_normed * unit, axis=0, keepdims=True)
    for k in range(8):
        for i in range(2):
            at = (2 * k + i) * 128
            small_ref[k // 2, k % 2, i : i + 1, :] = d_gain[:, at : at + 128]
    for k in range(4):
        small_sibling(k).start()
    for k in range(4):
        small_sibling(k).wait_recv()
        sums[k] = small_ref[k, c] + from_c[k]
    for k in range(2):
        small_x(k).start()
    weights_second()
    for k in range(2):
        small_x(k).wait_recv()
    sums[w] = sums[w] + from_x[0]
    sums[wy] = sums[wy] + from_x[1]
    small_y().start()
    passed_on(1)
    small_y().wait_recv()
    sums[w] = sums[w] + from_y[...]
    for k in range(1, 4):
        small_z((z + k) % 4, z).start()
    passed_on(2)
    weights_last()
    for k in range(1, 4):
        small_z(z, (z + k) % 4).wait_recv()
    from_z[z] = sums[w]
    small_out[...] = add(*(from_z[k] for k in range(4)))
    passed_on(3)
    for s in range(3):

        @pl.when(z < 3 - s)
        def _():
            to_right(3 - s).wait_send()

        @pl.when(z > s)
        def _():
            to_left(s).wait_send()

    for hop in to_sibling() + first_hops() + second_hops():
        hop.wait_send()
    for k in range(4):
        small_sibling(k).wait_send()
    for k in range(2):
        small_x(k).wait_send()
    small_y().wait_send()
    for k in range(1, 4):
        small_z((z + k) % 4, z).wait_send()
    for j in range(4):
        for there, side in onward(j):
            pl.when(there)(lambda: moved(j, side).wait_send())


def finish_call(parts, rows, scale, gain, d_hidden, d_qkv, d_out, small):
    dma = pltpu.SemaphoreType.DMA
    anywhere, vmem = (pl.BlockSpec(memory_space=pl.ANY), pl.BlockSpec(memory_space=pltpu.VMEM))
    share, width = rows.shape
    count, heads = d_out.shape[2:]
    half = width // 2
    block = small.shape[2:]
    bf16, f32 = (jnp.bfloat16, jnp.float32)

    def body(*refs):
        ins, outs, rest = (refs[:8], refs[8:12], refs[12:])
        parts_in, small_in = (ins[0], ins[7])
        parts_own, small_own = rest[:2]
        parts_own[...] = parts_in[...]
        small_own[...] = small_in[...]
        finish_kernel(parts_own, *ins[1:7], small_own, *outs, *rest[2:])

    return pl.pallas_call(
        body,
        out_shape=(
            jax.ShapeDtypeStruct((4, share, width), bf16),
            jax.ShapeDtypeStruct((3, count, heads), f32),
            jax.ShapeDtypeStruct((count, heads), f32),
            jax.ShapeDtypeStruct(block, f32),
        ),
        in_specs=[vmem, vmem, vmem, vmem, vmem, anywhere, anywhere, vmem],
        out_specs=(vmem, vmem, vmem, vmem),
        scratch_shapes=[
            pltpu.VMEM((4, share, width), bf16),
            pltpu.VMEM((4, 2) + block, f32),
            pltpu.VMEM((share, width), bf16),
            pltpu.VMEM((4, share, width), bf16),
            pltpu.VMEM((4, share, width), bf16),
            pltpu.VMEM((4,) + block, f32),
            pltpu.VMEM((4,) + block, f32),
            pltpu.VMEM((2,) + block, f32),
            pltpu.VMEM(block, f32),
            pltpu.VMEM((4,) + block, f32),
            pltpu.VMEM((4, count, width), bf16),
            pltpu.VMEM((4, count, width), bf16),
            pltpu.VMEM((2, count, half), bf16),
            pltpu.VMEM((2, count, half), bf16),
            pltpu.VMEM((count, half), bf16),
            pltpu.VMEM((count, half), bf16),
            dma((4,)),
            dma((4,)),
            dma((4,)),
            dma((4,)),
            dma((4, 2)),
            dma((4,)),
            dma((11,)),
            dma((11,)),
            dma((2,)),
            dma((2,)),
            dma((2,)),
            dma((4,)),
            dma((4,)),
            dma((2,)),
            dma((2,)),
        ],
        compiler_params=pltpu.CompilerParams(
            collective_id=1, has_side_effects=True, vmem_limit_bytes=48 << 20
        ),
    )(parts, rows, scale, gain, d_hidden, d_qkv, d_out, small)


def swapped(rows, flip):
    return lax.ppermute(rows, WEIGHTS, [(k, k ^ flip) for k in range(4)])


def grads_around(rows, x_low, y_high, share):
    half = rows.shape[1] // 2
    parts = (
        rows,
        x_low,
        swapped(rows[:, half:], 1),
        swapped(rows[:, :half], 2),
        y_high,
        swapped(x_low, 2),
        swapped(y_high, 1),
    )
    return [part.reshape(-1, share, part.shape[1]) for part in parts]


def shares_around(rows):
    z = lax.axis_index(TENSOR)
    parts = [rows] + [
        lax.ppermute(rows, TENSOR, [(k, (k + step) % 4) for k in range(4)]) for step in (1, 3, 2)
    ]
    whole = jnp.zeros((4,) + rows.shape, rows.dtype)
    for part, step in zip(parts, (0, 1, 3, 2)):
        whole = lax.dynamic_update_index_in_dim(whole, part, (z + 4 - step) % 4, 0)
    return whole.reshape((-1,) + rows.shape[1:])


def gathered(rows, axes):
    return lax.all_gather(rows, axes, axis=0, tiled=True)


def scattered(rows, axes):
    return lax.psum_scatter(rows, axes, scatter_dimension=0, tiled=True)


def fit_rows(values, rows):
    flat = values.reshape(-1)
    columns = -(-flat.shape[0] // rows)
    return jnp.pad(flat, (0, rows * columns - flat.shape[0])).reshape(rows, columns)


def per_device_dense(
    layer_in,
    norm_gains,
    qkv_weight,
    qk_gains,
    out_weight,
    router,
    expert_in,
    expert_out,
    grad_out,
    segments,
    routes,
    route_order,
):
    group = GROUP
    everyone = EVERYONE
    group_count = lax.axis_size(group)
    tensor_count = lax.axis_size(TENSOR)
    context_rank = lax.axis_index(CONTEXT)
    tensor_rank = lax.axis_index(TENSOR)
    seq_count, half_len, model_width = layer_in.shape
    token_count = seq_count * half_len
    top_count = routes.shape[2]
    weight_rows, _, head_width = qkv_weight.shape
    expert_total = router.shape[1]
    local_experts = expert_in.shape[0]
    hidden_width = expert_in.shape[3]
    head_rows, _, local_heads = qk_gains.shape
    head_size = head_rows * group_count
    share = token_count // tensor_count
    bf16, f32 = jnp.bfloat16, jnp.float32

    capacity = token_count * top_count * 9 // (8 * expert_total)
    routed, slot_of = pair_slots(
        routes.reshape(token_count, top_count),
        route_order.reshape(token_count, top_count),
        expert_total,
    )
    kept = routed & (slot_of < capacity)

    front_small = jnp.concatenate(
        [norm_gains, fit_rows(qk_gains, weight_rows)], axis=1
    )
    front = gathered(
        jnp.concatenate([qkv_weight.reshape(weight_rows, -1), front_small], axis=1), group
    )
    own_grads = grad_out.reshape(token_count, model_width)
    front, own_grads = lax.optimization_barrier((front, own_grads))
    half = model_width // 2
    x_low, y_high = (swapped(own_grads[:, :half], 1), swapped(own_grads[:, half:], 2))
    back_small = jnp.concatenate(
        [router, fit_rows(kept.astype(bf16), weight_rows)], axis=1
    )
    back = gathered(jnp.concatenate([out_weight, back_small], axis=1), group)
    qkv_full = front[:, : 3 * head_width]
    gain_full = front[:, 3 * head_width : 3 * head_width + 2].astype(f32)
    gain_attn, gain_ffn = (gain_full[:, 0], gain_full[:, 1])
    qk_gain_full = (
        front[:, 3 * head_width + 2 :]
        .reshape(group_count, -1)[:, : head_rows * 2 * local_heads]
        .reshape(head_size, 2, local_heads)
        .astype(f32)
    )
    query_gain = qk_gain_full[:, 0, :].T.reshape(-1)
    key_gain = qk_gain_full[:, 1, :].T.reshape(-1)
    out_full = back[:, :head_width]
    router_full = back[:, head_width : head_width + expert_total]
    kept_all = (
        back[:, head_width + expert_total :]
        .reshape(group_count, -1)[:, : expert_total * token_count]
        .reshape(group_count, expert_total, token_count)
    )
    inv_root = 1.0 / math.sqrt(head_size)
    residual = layer_in.reshape(token_count, model_width).astype(f32)
    scale_one = lax.rsqrt(jnp.mean(residual * residual, axis=1, keepdims=True) + epsilon)
    normed_one = (residual * scale_one * gain_attn).astype(bf16)
    projected = jnp.dot(normed_one, qkv_full, preferred_element_type=f32)
    query_raw = projected[:, :head_width]
    key_raw = projected[:, head_width : 2 * head_width]
    value_raw = projected[:, 2 * head_width :]
    square_sums = row_sums(
        jnp.stack(
            [jnp.sum(query_raw * query_raw, axis=1), jnp.sum(key_raw * key_raw, axis=1)], axis=1
        )
    )
    query_scale = lax.rsqrt(square_sums[:, 0:1] / model_width + epsilon)
    key_scale = lax.rsqrt(square_sums[:, 1:2] / model_width + epsilon)
    heads_shape = (seq_count, half_len, local_heads, head_size)
    query_hat = (query_raw * query_scale * query_gain).reshape(heads_shape)
    key_hat = (key_raw * key_scale * key_gain).reshape(heads_shape)
    query_pos = context_rank * half_len + jnp.arange(half_len, dtype=jnp.int32)
    cosine_table, sine_table = rotary_tables(query_pos, head_size)
    cosine_table = cosine_table[None, :, None, :]
    sine_table = sine_table[None, :, None, :]
    query_rot = (query_hat * cosine_table + rotate_half(query_hat) * sine_table).astype(bf16)
    key_rot = (key_hat * cosine_table + rotate_half(key_hat) * sine_table).astype(bf16)
    value_low = value_raw.astype(bf16).reshape(heads_shape)
    key_prev, value_prev = passed_along((key_rot, value_low), CONTEXT, 1)
    all_keys = jnp.concatenate([key_prev, key_rot], axis=1)
    all_values = jnp.concatenate([value_prev, value_low], axis=1)
    key_pos = jnp.concatenate([query_pos - half_len, query_pos])
    seg_query = lax.dynamic_slice_in_dim(segments, context_rank * half_len, half_len, 1)
    seg_prev = lax.dynamic_slice_in_dim(
        segments, jnp.maximum(context_rank - 1, 0) * half_len, half_len, 1
    )
    seg_keys = jnp.concatenate([seg_prev, seg_query], axis=1)
    causal = (key_pos[None, :] >= 0) & (key_pos[None, :] <= query_pos[:, None])
    allowed = causal[None] & (seg_query[:, :, None] == seg_keys[:, None, :])

    def score_block(queries, key_rows):
        raw_scores = (
            jnp.einsum(BY_SCORE, queries, key_rows, preferred_element_type=f32) * inv_root
        )
        return jnp.where(allowed[:, None], raw_scores, -1e30)

    scores = score_block(query_rot, all_keys)
    row_max = jnp.max(scores, axis=-1, keepdims=True)
    exponent = jnp.exp(scores - row_max)
    row_total = jnp.sum(exponent, axis=-1, keepdims=True)
    log_total = row_max + jnp.log(row_total)
    attn_probs = (exponent / row_total).astype(bf16)
    attended = jnp.einsum(BY_QUERY, attn_probs, all_values, preferred_element_type=f32)
    attended_low = attended.reshape(token_count, -1).astype(bf16)
    x_low, y_high, attended_low = lax.optimization_barrier((x_low, y_high, attended_low))
    around = grads_around(own_grads, x_low, y_high, share)
    attn_partial = jnp.einsum("tf,df->td", attended_low, out_full, preferred_element_type=f32)

    own_rows = lambda rows: lax.dynamic_slice_in_dim(rows, tensor_rank * share, share, 0)
    residual_own = own_rows(residual)
    hidden = residual_own + scattered(attn_partial.astype(bf16), TENSOR).astype(f32)
    scale_two = lax.rsqrt(jnp.mean(hidden * hidden, axis=1, keepdims=True) + epsilon)
    unit_two = hidden * scale_two
    normed_two = (unit_two * gain_ffn).astype(bf16)
    upstream = own_rows(grad_out.reshape(token_count, model_width)).astype(f32)

    pad_experts = lambda rows: jnp.pad(rows, ((0, 0), (0, 128 - expert_total)))
    kept_rows = kept_all.transpose(0, 2, 1).reshape(-1, expert_total)
    normed_all, grads_all, gated, d_both, moe_all, d_sums = experts_call(
        normed_two,
        around,
        pad_experts(kept_rows).reshape(4, 2, 4, share, 128),
        pad_experts(router_full),
        expert_in,
        expert_out,
        expert_total,
    )
    normed_all, grads_all, gated, d_both, moe_all = (
        rows.reshape(group_count * token_count, -1)
        for rows in (normed_all, grads_all, gated, d_both, moe_all)
    )
    moe_plane = scattered(moe_all, group)
    kept_own = own_rows(kept.T).astype(f32)
    probs_own = jax.nn.softmax(
        jnp.dot(normed_two, router_full, preferred_element_type=f32), axis=1
    )
    d_probs = d_sums[:, model_width : model_width + expert_total] * kept_own
    d_logits = (
        probs_own * (d_probs - jnp.sum(probs_own * d_probs, axis=1, keepdims=True))
    ).astype(bf16)
    d_normed_two = d_sums[:, :model_width] + jnp.dot(
        d_logits, router_full.T, preferred_element_type=f32
    )
    d_router = jnp.dot(normed_two.T, d_logits, preferred_element_type=f32)
    d_gain_ffn = jnp.sum(d_normed_two * unit_two, axis=0)
    scaled_ffn = gain_ffn * d_normed_two
    d_hidden = upstream + scale_two * (
        scaled_ffn - unit_two * jnp.mean(scaled_ffn * unit_two, axis=1, keepdims=True)
    )
    d_hidden_own, normed_all, grads_all, gated, d_both = lax.optimization_barrier(
        (d_hidden.astype(bf16), normed_all, grads_all, gated, d_both)
    )
    d_hidden_low = shares_around(d_hidden_own)
    grad_expert_in = (
        jnp.dot(normed_all.T, d_both, preferred_element_type=f32)
        .reshape(model_width, local_experts, 2, hidden_width)
        .transpose(1, 2, 0, 3)
    )
    grad_expert_out = jnp.dot(gated.T, grads_all, preferred_element_type=f32).reshape(
        expert_out.shape
    )
    d_hidden_low, grad_expert_in, grad_expert_out = lax.optimization_barrier(
        (d_hidden_low, grad_expert_in, grad_expert_out)
    )

    d_attended = (
        jnp.dot(d_hidden_low, out_full, preferred_element_type=f32)
        .astype(bf16)
        .reshape(heads_shape)
    )
    d_out_weight = jnp.einsum("td,tf->df", d_hidden_low, attended_low, preferred_element_type=f32)
    probs_again = jnp.exp(score_block(query_rot, all_keys) - log_total)
    probs_again_low = probs_again.astype(bf16)
    d_probs_att = jnp.einsum(
        BY_SCORE, d_attended, all_values, preferred_element_type=f32
    )
    d_values_all = jnp.einsum(
        BY_KEY, probs_again_low, d_attended, preferred_element_type=f32
    )
    row_dot = jnp.sum(probs_again * d_probs_att, axis=-1, keepdims=True)
    d_scores = (probs_again * (d_probs_att - row_dot)).astype(bf16)
    d_query_rot = (
        jnp.einsum(BY_QUERY, d_scores, all_keys, preferred_element_type=f32) * inv_root
    )
    d_keys_all = (
        jnp.einsum(BY_KEY, d_scores, query_rot, preferred_element_type=f32) * inv_root
    )
    back_key, back_value = (
        passed_along(d_keys_all[:, :half_len].astype(bf16), CONTEXT, -1).astype(f32),
        passed_along(d_values_all[:, :half_len].astype(bf16), CONTEXT, -1).astype(f32),
    )
    d_key_rot = d_keys_all[:, half_len:] + back_key
    d_value = (d_values_all[:, half_len:] + back_value).reshape(token_count, -1)
    d_query_hat = (d_query_rot * cosine_table + rotate_back(d_query_rot * sine_table)).reshape(
        token_count, -1
    )
    d_key_hat = (d_key_rot * cosine_table + rotate_back(d_key_rot * sine_table)).reshape(
        token_count, -1
    )
    centre_own = (
        jnp.stack(
            [
                jnp.sum(query_gain * d_query_hat * query_raw, axis=1),
                jnp.sum(key_gain * d_key_hat * key_raw, axis=1),
            ],
            axis=1,
        )
    )
    centre, moe_plane = lax.optimization_barrier((row_sums(centre_own), moe_plane))
    moe_own = scattered(moe_plane, TENSOR).astype(f32)
    d_query_raw = (
        query_scale * query_gain * d_query_hat
        - query_raw * (query_scale**3 / model_width) * centre[:, 0:1]
    )
    d_key_raw = (
        key_scale * key_gain * d_key_hat - key_raw * (key_scale**3 / model_width) * centre[:, 1:2]
    )
    d_query_gain = (
        jnp.sum(d_query_hat * query_raw * query_scale, axis=0).reshape(local_heads, head_size).T
    )
    d_key_gain = jnp.sum(d_key_hat * key_raw * key_scale, axis=0).reshape(local_heads, head_size).T
    d_qk_gains = jnp.stack([d_query_gain, d_key_gain], axis=1)
    d_projected = jnp.concatenate([d_query_raw, d_key_raw, d_value], axis=1).astype(bf16)
    d_normed_parts = jnp.einsum(
        "tf,df->td", d_projected, qkv_full, preferred_element_type=f32
    ).astype(bf16)
    d_qkv = jnp.einsum("td,tf->df", normed_one, d_projected, preferred_element_type=f32)

    own_slot = (jnp.arange(tensor_count) == tensor_rank).astype(f32)[None, :, None]
    lines = lambda values: values.reshape(group_count, -1, 128)
    small = jnp.concatenate(
        [
            jnp.zeros((group_count, weight_rows // 128, 128), f32),
            lines(d_gain_ffn),
            lines(d_router),
            lines(d_qk_gains) * own_slot,
        ],
        axis=1,
    )
    d_normed_parts, d_qkv, d_out_weight, moe_own = lax.optimization_barrier(
        (d_normed_parts, d_qkv.astype(bf16), d_out_weight.astype(bf16), moe_own)
    )
    layer_out = gathered((hidden + moe_own).astype(bf16), TENSOR).reshape(layer_in.shape)
    grad_in, grad_qkv, grad_out_weight, small = finish_call(
        d_normed_parts.reshape(tensor_count, share, model_width),
        own_rows(layer_in.reshape(token_count, model_width)),
        own_rows(scale_one),
        gain_attn[None],
        d_hidden,
        d_qkv.reshape(4, 2, weight_rows, -1),
        d_out_weight.reshape(4, 2, weight_rows, -1),
        small.reshape((4, 2) + small.shape[1:]),
    )
    grad_in = grad_in.astype(f32).reshape(layer_in.shape)
    grad_qkv = grad_qkv.transpose(1, 0, 2)
    lines_of = weight_rows // 128
    gain_share = weight_rows // tensor_count
    router_share = expert_total // tensor_count
    router_lines = weight_rows * expert_total // 128
    part_of = lambda rows, count, axis: lax.dynamic_slice_in_dim(
        rows, tensor_rank * count, count, axis
    )
    gains = small[: 2 * lines_of].reshape(2, weight_rows)
    routers = small[2 * lines_of : 2 * lines_of + router_lines].reshape(weight_rows, expert_total)
    qk_lines = small[2 * lines_of + router_lines :]
    return (
        layer_out,
        grad_in,
        part_of(gains, gain_share, 1).T,
        grad_qkv,
        part_of(qk_lines, 1, 0).reshape(head_rows, 2, local_heads),
        grad_out_weight,
        part_of(routers, router_share, 1),
        grad_expert_in,
        grad_expert_out,
    )


def solution(mesh):
    placed = (
        P(WEIGHTS, CONTEXT, None),
        P(GROUP, None),
        P(GROUP, None, TENSOR),
        P(GROUP, None, TENSOR),
        P(GROUP, TENSOR),
        P(GROUP, None),
        P(GROUP, None, None, TENSOR),
        P(GROUP, TENSOR, None),
        P(WEIGHTS, CONTEXT, None),
        P(WEIGHTS, None),
        P(WEIGHTS, CONTEXT, None),
        P(WEIGHTS, CONTEXT, None),
    )
    axes = tuple(mesh.shape[axis] for axis in EVERYONE)

    def per_device(*blocks):
        dense = axes == (4, 2, 4) and blocks[5].shape[1] <= 2 * blocks[10].shape[2]
        return (per_device_dense if dense else per_device_slots)(*blocks)

    return jax.shard_map(
        per_device,
        mesh=mesh,
        in_specs=placed,
        out_specs=(
            P(WEIGHTS, CONTEXT, None),
            P(WEIGHTS, CONTEXT, None),
            P(EVERYONE, None),
            P(GROUP, None, TENSOR),
            P(GROUP, None, TENSOR),
            P(GROUP, TENSOR),
            P(GROUP, TENSOR),
            P(GROUP, None, None, TENSOR),
            P(GROUP, TENSOR, None),
        ),
        check_vma=False,
    )
```

```python
import functools
import math

import jax
import jax.numpy as jnp
from jax import lax
from jax.experimental import pallas as pl
from jax.experimental.pallas import tpu as pltpu
from jax.sharding import PartitionSpec as P

epsilon = 1e-05
rotary_base = 10000.0
WEIGHTS, CONTEXT, TENSOR = ("weights", "context", "tensor")
GROUP = (WEIGHTS, CONTEXT)
EVERYONE = (WEIGHTS, CONTEXT, TENSOR)
MESH = pl.DeviceIdType.MESH
BY_SCORE = "sqhd,skhd->shqk"
BY_QUERY = "shqk,skhd->sqhd"
BY_KEY = "shqk,sqhd->skhd"


def passed_along(value, axis, steps):
    count = lax.axis_size(axis)
    leading, last = (max(0, -steps), min(count, count - steps))
    return lax.ppermute(value, axis, [(source, source + steps) for source in range(leading, last)])


def rotate_half(values_in):
    middle = values_in.shape[-1] // 2
    return jnp.concatenate([-values_in[..., middle:], values_in[..., :middle]], axis=-1)


def rotate_back(grads_in):
    middle = grads_in.shape[-1] // 2
    return jnp.concatenate([grads_in[..., middle:], -grads_in[..., :middle]], axis=-1)


def rotary_tables(positions, head_size):
    frequency = rotary_base ** (-(2.0 * jnp.arange(head_size // 2, dtype=jnp.float32)) / head_size)
    angle_table = positions.astype(jnp.float32)[:, None] * frequency[None, :]
    angle_table = jnp.concatenate([angle_table, angle_table], axis=1)
    return (jnp.cos(angle_table), jnp.sin(angle_table))


def pair_slots(token_routes, token_ranks, expert_total):
    unused = token_routes.size
    hot = token_routes.T[None] == jnp.arange(expert_total, dtype=jnp.int32)[:, None, None]
    rank_of = jnp.min(jnp.where(hot, token_ranks.T[None], unused), axis=1)
    slot_of = jnp.sum((rank_of[:, :, None] < rank_of[:, None, :]).astype(jnp.int32), axis=1)
    return (rank_of < unused, slot_of)


def place_pairs(pair_expert, rank, expert_total, capacity, top_count):
    pair_count = pair_expert.shape[0]
    token_routes = pair_expert.reshape(-1, top_count)
    slot_of = pair_slots(token_routes, rank.reshape(-1, top_count), expert_total)[1]
    slot_index = jnp.take_along_axis(slot_of.T, token_routes, axis=1).reshape(pair_count)
    kept_pair = slot_index < capacity
    dest_row = jnp.where(kept_pair, pair_expert * capacity + slot_index, expert_total * capacity)
    slot_pair = (
        jnp.full((expert_total * capacity + 1,), pair_count, jnp.int32)
        .at[dest_row]
        .set(jnp.arange(pair_count, dtype=jnp.int32))[:-1]
    )
    return (kept_pair, dest_row, slot_pair)


def row_sums(partial_rows):
    return lax.psum(partial_rows, TENSOR)


def tensor_sum(partial_rows):
    return lax.psum(partial_rows, TENSOR)


def to_owners(slot_rows):
    return lax.all_to_all(
        slot_rows, GROUP, split_axis=0, concat_axis=0, tiled=True
    )


def expert_front(slot_inputs, expert_in):
    both_pre = jnp.einsum(
        "sncd,ngdf->sncgf", slot_inputs, expert_in, preferred_element_type=jnp.float32
    )
    return (both_pre[..., 0, :], both_pre[..., 1, :])


def per_device_slots(
    layer_in,
    norm_gains,
    qkv_weight,
    qk_gains,
    out_weight,
    router,
    expert_in,
    expert_out,
    grad_out,
    segments,
    routes,
    route_order,
):
    group_count = lax.axis_size(GROUP)
    tensor_count = lax.axis_size(TENSOR)
    context_rank = lax.axis_index(CONTEXT)
    tensor_rank = lax.axis_index(TENSOR)
    seq_count, half_len, model_width = layer_in.shape
    token_count = seq_count * half_len
    top_count = routes.shape[2]
    qkv_full, out_full, qk_gain_full, gain_full, router_full = (
        lax.all_gather(qkv_weight, GROUP, axis=0, tiled=True),
        lax.all_gather(out_weight, GROUP, axis=0, tiled=True),
        lax.all_gather(qk_gains, GROUP, axis=0, tiled=True),
        lax.all_gather(norm_gains, GROUP, axis=0, tiled=True),
        lax.all_gather(router, GROUP, axis=0, tiled=True),
    )
    head_size = qk_gain_full.shape[0]
    local_heads = qk_gain_full.shape[2]
    expert_total = router_full.shape[1]
    gain_attn = gain_full[:, 0].astype(jnp.float32)
    gain_ffn = gain_full[:, 1].astype(jnp.float32)
    query_gain = qk_gain_full[:, 0, :].astype(jnp.float32).T.reshape(-1)
    key_gain = qk_gain_full[:, 1, :].astype(jnp.float32).T.reshape(-1)
    inv_root = 1.0 / math.sqrt(head_size)
    residual = layer_in.reshape(token_count, model_width).astype(jnp.float32)
    scale_one = lax.rsqrt(jnp.mean(residual * residual, axis=1, keepdims=True) + epsilon)
    unit_one = residual * scale_one
    normed_one = (unit_one * gain_attn).astype(jnp.bfloat16)
    projected = jnp.einsum("td,dgf->tgf", normed_one, qkv_full, preferred_element_type=jnp.float32)
    query_raw = projected[:, 0]
    key_raw = projected[:, 1]
    value_raw = projected[:, 2]
    square_sums = row_sums(
        jnp.stack(
            [jnp.sum(query_raw * query_raw, axis=1), jnp.sum(key_raw * key_raw, axis=1)], axis=1
        )
    )
    query_scale = lax.rsqrt(square_sums[:, 0:1] / model_width + epsilon)
    key_scale = lax.rsqrt(square_sums[:, 1:2] / model_width + epsilon)
    heads_shape = (seq_count, half_len, local_heads, head_size)
    query_hat = (query_raw * query_scale * query_gain).reshape(heads_shape)
    key_hat = (key_raw * key_scale * key_gain).reshape(heads_shape)
    query_pos = context_rank * half_len + jnp.arange(half_len, dtype=jnp.int32)
    cosine_table, sine_table = rotary_tables(query_pos, head_size)
    cosine_table = cosine_table[None, :, None, :]
    sine_table = sine_table[None, :, None, :]
    query_rot = (query_hat * cosine_table + rotate_half(query_hat) * sine_table).astype(
        jnp.bfloat16
    )
    key_rot = (key_hat * cosine_table + rotate_half(key_hat) * sine_table).astype(jnp.bfloat16)
    value_low = value_raw.astype(jnp.bfloat16).reshape(heads_shape)
    key_prev, value_prev = passed_along((key_rot, value_low), CONTEXT, 1)
    all_keys = jnp.concatenate([key_prev, key_rot], axis=1)
    all_values = jnp.concatenate([value_prev, value_low], axis=1)
    key_pos = jnp.concatenate([query_pos - half_len, query_pos])
    seg_query = lax.dynamic_slice_in_dim(segments, context_rank * half_len, half_len, 1)
    seg_prev = lax.dynamic_slice_in_dim(
        segments, jnp.maximum(context_rank - 1, 0) * half_len, half_len, 1
    )
    seg_keys = jnp.concatenate([seg_prev, seg_query], axis=1)
    causal = (key_pos[None, :] >= 0) & (key_pos[None, :] <= query_pos[:, None])
    allowed = causal[None] & (seg_query[:, :, None] == seg_keys[:, None, :])

    def score_block(queries, key_rows):
        raw_scores = (
            jnp.einsum(BY_SCORE, queries, key_rows, preferred_element_type=jnp.float32)
            * inv_root
        )
        return jnp.where(allowed[:, None], raw_scores, -1e30)

    scores = score_block(query_rot, all_keys)
    row_max = jnp.max(scores, axis=-1, keepdims=True)
    exponent = jnp.exp(scores - row_max)
    row_total = jnp.sum(exponent, axis=-1, keepdims=True)
    log_total = row_max + jnp.log(row_total)
    attn_probs = (exponent / row_total).astype(jnp.bfloat16)
    attended = jnp.einsum(
        BY_QUERY, attn_probs, all_values, preferred_element_type=jnp.float32
    )
    attended_low = attended.reshape(token_count, -1).astype(jnp.bfloat16)
    attn_partial = jnp.einsum(
        "tf,df->td", attended_low, out_full, preferred_element_type=jnp.float32
    )
    hidden = residual + tensor_sum(attn_partial)
    scale_two = lax.rsqrt(jnp.mean(hidden * hidden, axis=1, keepdims=True) + epsilon)
    unit_two = hidden * scale_two
    normed_two = (unit_two * gain_ffn).astype(jnp.bfloat16)
    logits = jnp.dot(normed_two, router_full, preferred_element_type=jnp.float32)
    router_probs = jax.nn.softmax(logits, axis=1)
    capacity = token_count * top_count * 9 // (8 * expert_total)
    local_experts = expert_in.shape[0]
    pair_count = token_count * top_count
    token_routes = routes.reshape(token_count, top_count)
    kept_pair, dest_row, slot_pair = place_pairs(
        token_routes.reshape(pair_count), route_order.reshape(pair_count), expert_total, capacity, top_count
    )
    zero_row = jnp.zeros((1, model_width), jnp.bfloat16)
    zero_wide = jnp.zeros((1, model_width), jnp.float32)
    slot_shape = (group_count, local_experts, capacity, model_width)
    dispatch_rows = jnp.concatenate([normed_two, zero_row], axis=0)[slot_pair // top_count].reshape(
        slot_shape
    )
    received = lax.all_to_all(
        dispatch_rows, GROUP, split_axis=0, concat_axis=0, tiled=True
    )
    gate_pre, up_pre = expert_front(received, expert_in)
    sigmoid_gate = jax.nn.sigmoid(gate_pre)
    silu_gate = gate_pre * sigmoid_gate
    activated = (silu_gate * up_pre).astype(jnp.bfloat16)
    expert_partial = jnp.einsum(
        "sncf,nfd->sncd", activated, expert_out, preferred_element_type=jnp.float32
    )
    kept_float = kept_pair.reshape(token_count, top_count).astype(jnp.float32)
    gate_weight = jnp.take_along_axis(router_probs, token_routes, axis=1) * kept_float
    upstream = grad_out.reshape(token_count, model_width).astype(jnp.float32)
    returned = to_owners(expert_partial).reshape(expert_total * capacity, model_width)
    picked = jnp.concatenate([returned, zero_wide], axis=0)[dest_row].reshape(
        token_count, top_count, model_width
    )
    moe_partial = jnp.sum(gate_weight[:, :, None] * picked, axis=1)
    dot_partial = jnp.sum(upstream[:, None, :] * picked, axis=2)
    moe_total, dot_total = lax.psum((moe_partial, dot_partial), TENSOR)
    layer_out = (hidden + moe_total).astype(jnp.bfloat16).reshape(layer_in.shape)
    d_gate = dot_total * kept_float
    route_hot = (
        token_routes[:, :, None] == jnp.arange(expert_total, dtype=jnp.int32)[None, None, :]
    ).astype(jnp.float32)
    d_probs = jnp.sum(d_gate[:, :, None] * route_hot, axis=1)
    d_logits = (
        router_probs * (d_probs - jnp.sum(router_probs * d_probs, axis=1, keepdims=True))
    ).astype(jnp.bfloat16)
    d_pair = (
        (gate_weight[:, :, None] * upstream[:, None, :])
        .astype(jnp.bfloat16)
        .reshape(pair_count, model_width)
    )
    d_slots = jnp.concatenate([d_pair, zero_row], axis=0)[slot_pair].reshape(slot_shape)
    d_received = lax.all_to_all(
        d_slots, GROUP, split_axis=0, concat_axis=0, tiled=True
    )
    d_activated = jnp.einsum(
        "sncd,nfd->sncf", d_received, expert_out, preferred_element_type=jnp.float32
    )
    grad_expert_out = jnp.einsum(
        "sncf,sncd->nfd", activated, d_received, preferred_element_type=jnp.float32
    )
    d_gate_pre = d_activated * up_pre * sigmoid_gate * (1.0 + gate_pre * (1.0 - sigmoid_gate))
    d_up_pre = d_activated * silu_gate
    d_both = jnp.stack([d_gate_pre, d_up_pre], axis=3).astype(jnp.bfloat16)
    d_inputs = jnp.einsum("sncgf,ngdf->sncd", d_both, expert_in, preferred_element_type=jnp.float32)
    grad_expert_in = jnp.einsum(
        "sncd,sncgf->ngdf", received, d_both, preferred_element_type=jnp.float32
    )
    d_returned = to_owners(d_inputs).reshape(expert_total * capacity, model_width)
    d_normed_part = jnp.sum(
        jnp.concatenate([d_returned, zero_wide], axis=0)[dest_row].reshape(
            token_count, top_count, model_width
        ),
        axis=1,
    )
    d_normed_two = tensor_sum(d_normed_part) + jnp.dot(
        d_logits, router_full.T, preferred_element_type=jnp.float32
    )
    d_router = jnp.dot(normed_two.T, d_logits, preferred_element_type=jnp.float32)
    d_gain_ffn = jnp.sum(d_normed_two * unit_two, axis=0)
    scaled_ffn = gain_ffn * d_normed_two
    d_hidden = upstream + scale_two * (
        scaled_ffn - unit_two * jnp.mean(scaled_ffn * unit_two, axis=1, keepdims=True)
    )
    d_hidden_low = d_hidden.astype(jnp.bfloat16)
    d_out_weight = jnp.einsum(
        "td,tf->df", d_hidden_low, attended_low, preferred_element_type=jnp.float32
    )
    d_attended = (
        jnp.dot(d_hidden_low, out_full, preferred_element_type=jnp.float32)
        .astype(jnp.bfloat16)
        .reshape(heads_shape)
    )
    probs_again = jnp.exp(score_block(query_rot, all_keys) - log_total)
    probs_again_low = probs_again.astype(jnp.bfloat16)
    d_probs_att = jnp.einsum(
        BY_SCORE, d_attended, all_values, preferred_element_type=jnp.float32
    )
    d_values_all = jnp.einsum(
        BY_KEY, probs_again_low, d_attended, preferred_element_type=jnp.float32
    )
    row_dot = jnp.sum(probs_again * d_probs_att, axis=-1, keepdims=True)
    d_scores = (probs_again * (d_probs_att - row_dot)).astype(jnp.bfloat16)
    d_query_rot = (
        jnp.einsum(BY_QUERY, d_scores, all_keys, preferred_element_type=jnp.float32)
        * inv_root
    )
    d_keys_all = (
        jnp.einsum(BY_KEY, d_scores, query_rot, preferred_element_type=jnp.float32)
        * inv_root
    )
    back_key, back_value = (
        passed_along(d_keys_all[:, :half_len].astype(jnp.bfloat16), CONTEXT, -1).astype(
            jnp.float32
        ),
        passed_along(d_values_all[:, :half_len].astype(jnp.bfloat16), CONTEXT, -1).astype(
            jnp.float32
        ),
    )
    d_key_rot = d_keys_all[:, half_len:] + back_key
    d_value = (d_values_all[:, half_len:] + back_value).reshape(token_count, -1)
    d_query_hat = (d_query_rot * cosine_table + rotate_back(d_query_rot * sine_table)).reshape(
        token_count, -1
    )
    d_key_hat = (d_key_rot * cosine_table + rotate_back(d_key_rot * sine_table)).reshape(
        token_count, -1
    )
    centre = row_sums(
        jnp.stack(
            [
                jnp.sum(query_gain * d_query_hat * query_raw, axis=1),
                jnp.sum(key_gain * d_key_hat * key_raw, axis=1),
            ],
            axis=1,
        )
    )
    d_query_raw = (
        query_scale * query_gain * d_query_hat
        - query_raw * (query_scale**3 / model_width) * centre[:, 0:1]
    )
    d_key_raw = (
        key_scale * key_gain * d_key_hat - key_raw * (key_scale**3 / model_width) * centre[:, 1:2]
    )
    d_query_gain = (
        jnp.sum(d_query_hat * query_raw * query_scale, axis=0).reshape(local_heads, head_size).T
    )
    d_key_gain = jnp.sum(d_key_hat * key_raw * key_scale, axis=0).reshape(local_heads, head_size).T
    d_qk_gains = jnp.stack([d_query_gain, d_key_gain], axis=1)
    d_projected = jnp.stack([d_query_raw, d_key_raw, d_value], axis=1).astype(jnp.bfloat16)
    d_normed_one = tensor_sum(
        jnp.einsum("tgf,dgf->td", d_projected, qkv_full, preferred_element_type=jnp.float32)
    )
    d_qkv = jnp.einsum("td,tgf->dgf", normed_one, d_projected, preferred_element_type=jnp.float32)
    d_gain_attn = jnp.sum(d_normed_one * unit_one, axis=0)
    scaled_attn = gain_attn * d_normed_one
    grad_in = d_hidden + scale_one * (
        scaled_attn - unit_one * jnp.mean(scaled_attn * unit_one, axis=1, keepdims=True)
    )
    d_norm_gains = jnp.stack([d_gain_attn, d_gain_ffn], axis=1)
    grad_qkv, grad_out_weight, grad_qk_gains, gain_rows, router_rows = (
        lax.psum_scatter(d_qkv, GROUP, scatter_dimension=0, tiled=True),
        lax.psum_scatter(d_out_weight, GROUP, scatter_dimension=0, tiled=True),
        lax.psum_scatter(d_qk_gains, GROUP, scatter_dimension=0, tiled=True),
        lax.psum_scatter(d_norm_gains, GROUP, scatter_dimension=0, tiled=True),
        lax.psum_scatter(d_router, GROUP, scatter_dimension=0, tiled=True),
    )
    gain_share = gain_rows.shape[0] // tensor_count
    grad_norm_gains = lax.dynamic_slice_in_dim(gain_rows, tensor_rank * gain_share, gain_share, 0)
    router_share = expert_total // tensor_count
    grad_router = lax.dynamic_slice_in_dim(router_rows, tensor_rank * router_share, router_share, 1)
    return (
        layer_out,
        grad_in.reshape(layer_in.shape),
        grad_norm_gains,
        grad_qkv,
        grad_qk_gains,
        grad_out_weight,
        grad_router,
        grad_expert_in,
        grad_expert_out,
    )


def contract_last(left, right):
    return lax.dot_general(
        left, right, (((1,), (1,)), ((), ())), preferred_element_type=jnp.float32
    )


def share_order(z):
    upper, odd = (z // 2, z % 2)
    return (z, z + 1 - 2 * upper, 2 + upper - 2 * odd, 3 - 3 * upper)


def share_turns(z):
    return (z, (z + 2) % 4, 3 - z, z + 1 - 2 * (z % 2))


def neighbours(w):
    wx, wy = (w + 1 - 2 * (w % 2), (w + 2) % 4)
    return (wx, wy, wx + wy - w)


def experts_kernel(
    experts,
    x_ref,
    grad_own,
    grad_x_low,
    grad_x_high,
    grad_y_low,
    grad_y_high,
    grad_low,
    grad_high,
    kept_ref,
    router_ref,
    in_ref,
    out_w_ref,
    x_out,
    grads_out,
    gated_out,
    both_out,
    moe_out,
    dx_own,
    x_tile,
    w_in,
    w_out,
    grads,
    gated,
    both,
    moe_tile,
    others,
    mine,
    sibs,
    from_x1,
    from_y1,
    from_y2,
    from_x2,
    from_z,
        own_sem,
        tile_sem,
        weight_sem,
        grads_sem,
        store_sem,
        send_z,
        send_x,
        send_y,
        send_c,
        recv,
        over_send,
        over_recv,
        sib_send,
        sib_recv,
        credit,
        one_send,
        one_recv,
        two_send,
        two_recv,
        end_send,
        end_recv,
):
    w, c, z = (lax.axis_index(a) for a in (WEIGHTS, CONTEXT, TENSOR))
    wx, wy, wd = neighbours(w)
    share, width = x_ref.shape
    half = width // 2
    lo, hi = (pl.ds(0, half), pl.ds(half, half))
    dev_x, dev_y, dev_c = ((wx, c, z), (wy, c, z), (w, 1 - c, z))
    turns = share_turns(z)
    hidden = out_w_ref.shape[1]
    group = w * 2 + c
    bf16, f32 = (jnp.bfloat16, jnp.float32)
    low, high = (pl.ds(0, half), pl.ds(half, half + 128))

    def loads():
        return [
            pltpu.make_async_copy(
                in_ref.at[n, g],
                w_in.at[:, pl.ds((2 * n + g) * hidden, hidden)],
                weight_sem.at[2 * n + g],
            )
            for n in range(2)
            for g in range(2)
        ] + [
            pltpu.make_async_copy(
                out_w_ref.at[n], w_out.at[pl.ds(n * hidden, hidden)], weight_sem.at[4 + n]
            )
            for n in range(2)
        ]

    for load in loads():
        load.start()
    keep = lambda: pltpu.make_async_copy(x_ref, x_out.at[w, c, z], own_sem)
    keep().start()

    grad_parts = (
        (grad_own, w, None),
        (grad_x_low, wx, lo),
        (grad_x_high, wx, hi),
        (grad_y_low, wy, lo),
        (grad_y_high, wy, hi),
        (grad_low, wd, lo),
        (grad_high, wd, hi),
    )

    def grad_place(cc, ww, cols):
        return grads_out.at[ww, cc] if cols is None else grads_out.at[ww, cc, :, :, cols]

    def over(i, cc):
        src, ww, cols = grad_parts[i]
        return pltpu.make_async_remote_copy(
            src_ref=src,
            dst_ref=grad_place(cc, ww, cols),
            send_sem=over_send.at[i],
            recv_sem=over_recv.at[i],
            device_id=dev_c,
            device_id_type=MESH,
        )

    barrier = pltpu.get_barrier_semaphore()
    around = [(w, c, (z + k) % 4) for k in range(1, 4)]
    for device in [dev_x, dev_y, dev_c] + around:
        pl.semaphore_signal(barrier, inc=1, device_id=device, device_id_type=MESH)
    pl.semaphore_wait(barrier, 6)


    def view(chunk, cols):
        zz, cc, ww = chunk
        return x_out.at[ww, cc, zz] if cols is None else x_out.at[ww, cc, zz, :, cols]

    def copy(src, chunk, cols, slot, sem, device):
        return pltpu.make_async_remote_copy(
            src_ref=src,
            dst_ref=view(chunk, cols),
            send_sem=sem[0].at[sem[1:]],
            recv_sem=recv.at[chunk[0], chunk[1], slot],
            device_id=device,
            device_id_type=MESH,
        )

    sent = []
    devices_z = ((w, c, z + 1), (w, c, z - 1))

    def start(chunk, cols, slot, sem, device, src=None):
        copy(view(chunk, cols) if src is None else src, chunk, cols, slot, sem, device).start()
        sent.append((chunk, cols, slot, sem, device))

    def arrived(chunk, cols, slot):
        copy(view(chunk, cols), chunk, cols, slot, (send_c, 0, 0), dev_c).wait_recv()

    def spread(j):
        chunk = (turns[j], c, w)
        src = x_ref if j == 0 else None
        start(chunk, None, 1, (send_x, j, 0), dev_x, src)
        start(chunk, None, 2, (send_y, j, 0), dev_y, src)
        start(chunk, None, 0, (send_c, j, 0), dev_c, src)

    def onward(j):
        chunk = (turns[j], c, w)

        def moved(side):
            src = x_ref if j == 0 else view(chunk, None)
            return copy(src, chunk, None, 0, (send_z, j, side), devices_z[side])

        return (
            ((turns[j] <= z) & (z < 3), functools.partial(moved, 0)),
            ((turns[j] >= z) & (z > 0), functools.partial(moved, 1)),
        )

    def along(j):
        for there, moved in onward(j):
            pl.when(there)(lambda: moved().start())

    def pass_on(j):
        arrived((turns[j], c, w), None, 0)
        along(j)

    def relay(j):
        from_x, from_y = ((turns[j], c, wx), (turns[j], c, wy))
        arrived(from_x, None, 1)
        start(from_x, lo, 3, (send_y, j, 1), dev_y)
        start(from_x, None, 1, (send_c, j, 1), dev_c)
        arrived(from_y, None, 2)
        start(from_y, hi, 4, (send_x, j, 1), dev_x)
        start(from_y, None, 2, (send_c, j, 2), dev_c)

    def across(j):
        chunk = (turns[j], c, wd)
        for cols, slot in ((lo, 3), (hi, 4)):
            arrived(chunk, cols, slot)
            start(chunk, cols, slot, (send_c, j, slot), dev_c)

    def sibling(j):
        for ww, cols, slot in ((w, None, 0), (wx, None, 1), (wy, None, 2), (wd, lo, 3), (wd, hi, 4)):
            arrived((turns[j], 1 - c, ww), cols, slot)


    def remote(src, dst, send, got, device):
        return pltpu.make_async_remote_copy(
            src_ref=src,
            dst_ref=dst,
            send_sem=send,
            recv_sem=got,
            device_id=device,
            device_id_type=MESH,
        )

    def to_sibling():
        return remote(others, sibs, sib_send, sib_recv, dev_c)

    def first_hops(j):
        moves = (
            (wx, low, from_x1.at[j, 0], dev_x),
            (wd, low, from_x1.at[j, 1], dev_x),
            (wy, high, from_y1.at[j, 0], dev_y),
            (wd, high, from_y1.at[j, 1], dev_y),
        )
        return [
            remote(
                mine.at[j % 2, ww, :, cols], dst, one_send.at[j, i], one_recv.at[j, i], device
            )
            for i, (ww, cols, dst, device) in enumerate(moves)
        ]

    def second_hops(j):
        moves = ((wy, low, from_y2.at[j], dev_y), (wx, high, from_x2.at[j], dev_x))
        return [
            remote(
                mine.at[j % 2, ww, :, cols], dst, two_send.at[j, i], two_recv.at[j, i], device
            )
            for i, (ww, cols, dst, device) in enumerate(moves)
        ]

    def last_hop(source, j):
        return remote(
            mine.at[j % 2, w],
            from_z.at[source],
            end_send.at[j],
            end_recv.at[source],
            (w, c, turns[j]),
        )

    def total(*terms):
        added = terms[0].astype(f32)
        for term in terms[1:]:
            added = added + term.astype(f32)
        return added

    def after_first(j):
        p = j % 2
        for moved in first_hops(j):
            moved.wait_recv()
        mine[p, wy, :, low] = total(mine[p, wy, :, low], from_x1[j, 1]).astype(bf16)
        mine[p, wx, :, high] = total(mine[p, wx, :, high], from_y1[j, 1]).astype(bf16)
        for moved in second_hops(j):
            moved.start()

    def after_second(j):
        p = j % 2
        for moved in second_hops(j):
            moved.wait_recv()
        mine[p, w, :, low] = total(mine[p, w, :, low], from_x1[j, 0], from_y2[j]).astype(bf16)
        mine[p, w, :, high] = total(mine[p, w, :, high], from_y1[j, 0], from_x2[j]).astype(bf16)
        if j == 0:
            from_z[z] = mine[p, w]
        else:
            last_hop(z, j).start()

    def all_sent(j):
        for moved in first_hops(j) + second_hops(j):
            moved.wait_send()
        if j > 0:
            last_hop(z, j).wait_send()


    code = turns[0] + 4 * turns[1] + 16 * turns[2] + 64 * turns[3]

    def tile_of(step):
        j = step // 2
        power = 1 + 3 * j + (9 * j * (j - 1)) // 2 + (27 * j * (j - 1) * (j - 2)) // 6
        return ((code // power) % 4, (c + 1 + step) % 2)

    def other_grads(step):
        zj, cc = tile_of(step)
        return pltpu.make_async_copy(grads_out.at[:, cc, zj], grads.at[0], grads_sem.at[7])

    def my_grads(step):
        zj, cc = tile_of(step)
        return [
            pltpu.make_async_copy(
                src.at[zj],
                grads.at[1, ww] if cols is None else grads.at[1, ww, :, cols],
                grads_sem.at[i],
            )
            for i, (src, ww, cols) in enumerate(grad_parts)
        ]

    def stores(step, own_tile):
        zj, cc = tile_of(step)
        pairs = [(gated, gated_out), (both, both_out)]
        pairs += [(grads.at[1], grads_out)] if own_tile else []
        return [
            pltpu.make_async_copy(src, dst.at[:, cc, zj], store_sem.at[i])
            for i, (src, dst) in enumerate(pairs)
        ]

    def moe_store(step):
        zj, cc = tile_of(step)
        return pltpu.make_async_copy(moe_tile, moe_out.at[:, cc, zj], store_sem.at[3])

    lanes = lax.broadcasted_iota(jnp.int32, (4 * share, 128), 1)

    def tile(step, own_tile, parity):
        zj, cc = tile_of(step)
        load = pltpu.make_async_copy(x_out.at[:, cc, zj], x_tile, tile_sem)
        load.start()
        if own_tile:
            for store in stores(step - 1, False):
                store.wait()
            for part in my_grads(step):
                part.wait()

            @pl.when(step < 7)
            def _():
                other_grads(step + 1).start()
        else:

            @pl.when(step > 0)
            def _():
                for store in stores(step - 1, True):
                    store.wait()

            for part in my_grads(step + 1):
                part.start()
            other_grads(step).wait()
        load.wait()
        rows = x_tile[...].reshape(4 * share, width)
        upstream = grads[1 if own_tile else 0].reshape(4 * share, width)
        logits = jnp.dot(rows, router_ref[...], preferred_element_type=f32)
        logits = jnp.where(lanes < experts, logits, -1e30)
        raised = jnp.exp(logits - jnp.max(logits, axis=1, keepdims=True))
        gates = raised / jnp.sum(raised, axis=1, keepdims=True)
        gates = gates * kept_ref[:, cc, zj].reshape(4 * share, 128).astype(f32)
        d_gate = jnp.zeros((4 * share, 128), f32)
        for n in range(2):
            here = lanes == group * 2 + n
            gate = jnp.sum(jnp.where(here, gates, 0.0), axis=1, keepdims=True)
            at = 2 * n * hidden
            gate_pre = jnp.dot(rows, w_in[:, at : at + hidden], preferred_element_type=f32)
            up_pre = jnp.dot(
                rows, w_in[:, at + hidden : at + 2 * hidden], preferred_element_type=f32
            )
            back = contract_last(upstream, w_out[n * hidden : (n + 1) * hidden, :])
            sigmoid = 1.0 / (1.0 + jnp.exp(-gate_pre))
            silu = gate_pre * sigmoid
            activated = silu * up_pre
            d_gate = jnp.where(here, jnp.sum(activated * back, axis=1, keepdims=True), d_gate)
            back = gate * back
            d_pre = back * up_pre * sigmoid * (1.0 + gate_pre * (1.0 - sigmoid))
            shape = (4, share, hidden)
            gated[:, :, n * hidden : (n + 1) * hidden] = (
                (gate * activated).astype(bf16).reshape(shape)
            )
            both[:, :, at : at + hidden] = d_pre.astype(bf16).reshape(shape)
            both[:, :, at + hidden : at + 2 * hidden] = (back * silu).astype(bf16).reshape(shape)
        for store in stores(step, own_tile):
            store.start()
        if own_tile:
            to_sibling().wait_recv()
            moe_store(step - 1).wait()
        else:

            @pl.when(step > 0)
            def _():
                to_sibling().wait_send()
                moe_store(step - 1).wait()

        def put(cols, count, value):
            value = value.reshape(4, share, count)
            if own_tile:
                value = value + sibs[:, :, cols].astype(f32)
                mine[parity, :, :, cols] = value.astype(bf16)
            else:
                others[:, :, cols] = value.astype(bf16)

        put(pl.ds(width, 128), 128, d_gate)
        d_rows = both[...].reshape(4 * share, 4 * hidden)
        g_rows = gated[...].reshape(4 * share, 2 * hidden)

        def columns(m, carried):
            cols = pl.ds(pl.multiple_of(m * 256, 256), 256)
            put(cols, 256, contract_last(d_rows, w_in[cols, :]))
            moe_tile[:, :, cols] = (
                jnp.dot(g_rows, w_out[:, cols], preferred_element_type=f32)
                .astype(bf16)
                .reshape(4, share, 256)
            )
            return carried

        lax.fori_loop(0, width // 256, columns, None)
        moe_store(step).start()

    def before_other(j):
        if j == 0:
            for i in range(7):
                over(i, c).start()
            along(0)
            spread(0)
            pass_on(3)
            pl.when((z > 0) & (z < 3))(lambda: pass_on(2))
            relay(0)
            pass_on(1)
            spread(1)
            keep().wait()
            for load in loads():
                load.wait()
            for i in range(7):
                over(i, 1 - c).wait_recv()
            other_grads(0).start()
        if j >= 2:
            after_second(j - 2)
        across(j)
        sibling(j)

    def before_mine(j):
        if j == 0:
            pl.when((z == 0) | (z == 3))(lambda: pass_on(2))
        if j + 2 < 4:
            spread(j + 2)
        if j + 1 < 4:
            relay(j + 1)
        if j >= 1:
            after_first(j - 1)
        if j >= 2:
            all_sent(j - 2)

    def round_of(j, carry):
        for k in range(4):
            pl.when(j == k)(functools.partial(before_other, k))
        tile(2 * j, False, None)

        @pl.when(j > 0)
        def _():
            pl.semaphore_wait(credit, 1)

        to_sibling().start()
        for k in range(4):
            pl.when(j == k)(functools.partial(before_mine, k))
        tile(2 * j + 1, True, j % 2)

        @pl.when(j < 3)
        def _():
            pl.semaphore_signal(credit, inc=1, device_id=dev_c, device_id_type=MESH)

        for k in range(4):

            @pl.when(j == k)
            def _():
                for moved in first_hops(k):
                    moved.start()

        return carry

    lax.fori_loop(0, 4, round_of, None)
    after_second(2)
    after_first(3)
    after_second(3)
    for store in stores(7, True):
        store.wait()
    moe_store(7).wait()
    to_sibling().wait_send()
    for k in range(1, 4):
        last_hop((z + k) % 4, 1).wait_recv()
    dx_own[...] = total(*(from_z[k] for k in range(4)))
    all_sent(2)
    all_sent(3)
    for i in range(7):
        over(i, c).wait_send()
    for chunk, cols, slot, sem, device in sent:
        copy(view(chunk, cols), chunk, cols, slot, sem, device).wait_send()
    for j in range(4):
        for there, moved in onward(j):
            pl.when(there)(lambda: moved().wait_send())


def experts_call(rows, grads, kept, router, expert_in, expert_out, experts):
    share, width = rows.shape
    hidden = expert_out.shape[1]
    blocks = (4, 2, 4, share)
    bf16, f32 = (jnp.bfloat16, jnp.float32)
    dma = pltpu.SemaphoreType.DMA
    anywhere, vmem = (pl.BlockSpec(memory_space=pl.ANY), pl.BlockSpec(memory_space=pltpu.VMEM))
    wide, half = (width + 128, width // 2)
    return pl.pallas_call(
        functools.partial(experts_kernel, experts),
        out_shape=tuple(
            jax.ShapeDtypeStruct(blocks + (n,), bf16)
            for n in (width, width, 2 * hidden, 4 * hidden, width)
        )
        + (jax.ShapeDtypeStruct((share, wide), f32),),
        in_specs=[anywhere] * 8 + [vmem, vmem, anywhere, anywhere],
        out_specs=(anywhere,) * 5 + (vmem,),
        scratch_shapes=[
            pltpu.VMEM((4, share, width), bf16),
            pltpu.VMEM((width, 4 * hidden), bf16),
            pltpu.VMEM((2 * hidden, width), bf16),
            pltpu.VMEM((2, 4, share, width), bf16),
            pltpu.VMEM((4, share, 2 * hidden), bf16),
            pltpu.VMEM((4, share, 4 * hidden), bf16),
            pltpu.VMEM((4, share, width), bf16),
            pltpu.VMEM((4, share, wide), bf16),
            pltpu.VMEM((2, 4, share, wide), bf16),
            pltpu.VMEM((4, share, wide), bf16),
            pltpu.VMEM((4, 2, share, half), bf16),
            pltpu.VMEM((4, 2, share, wide - half), bf16),
            pltpu.VMEM((4, share, half), bf16),
            pltpu.VMEM((4, share, wide - half), bf16),
            pltpu.VMEM((4, share, wide), bf16),
            dma,
            dma,
            dma((6,)),
            dma((8,)),
            dma((4,)),
            dma((4, 2)),
            dma((4, 2)),
            dma((4, 2)),
            dma((4, 5)),
            dma((4, 2, 5)),
            dma((7,)),
            dma((7,)),
            dma,
            dma,
            pltpu.SemaphoreType.REGULAR,
            dma((4, 4)),
            dma((4, 4)),
            dma((4, 2)),
            dma((4, 2)),
            dma((4,)),
            dma((4,)),
        ],
        compiler_params=pltpu.CompilerParams(
            collective_id=0, has_side_effects=True, vmem_limit_bytes=62 << 20
        ),
    )(rows, *grads, kept, router, expert_in, expert_out)


def finish_kernel(
    parts_ref,
    x_ref,
    scale_ref,
    gain_ref,
    d_hidden_ref,
    qkv_ref,
    out_ref,
    layer_ref,
    small_ref,
    rows_out,
    layer_out,
    qkv_out,
    out_out,
    small_out,
    own_rows,
    right_in,
    left_in,
    sums,
    from_c,
    from_x,
    from_y,
    from_z,
    mine,
    sibs,
    from_x1,
    from_y1,
    from_y2,
    from_x2,
    right_send,
    right_recv,
    left_send,
    left_recv,
    send_z,
    recv_z,
    small_send,
    small_recv,
    load_sem,
    sib_send,
    sib_recv,
    one_send,
    one_recv,
    two_send,
    two_recv,
):
    w, c, z = (lax.axis_index(a) for a in EVERYONE)
    wx, wy, wd = neighbours(w)
    dev_x, dev_y, dev_c = ((wx, c, z), (wy, c, z), (w, 1 - c, z))
    sides = ((w, c, z + 1), (w, c, z - 1))
    order = share_order(z)
    bf16, f32 = (jnp.bfloat16, jnp.float32)
    half = x_ref.shape[1] // 2
    lo, hi = (slice(0, half), slice(half, 2 * half))
    heads = out_ref.shape[3]
    both = ((qkv_ref, pl.ds(0, 3 * heads)), (out_ref, pl.ds(3 * heads, heads)))

    def loads():
        return [
            pltpu.make_async_copy(ref.at[:, c], mine.at[:, :, cols], load_sem.at[i])
            for i, (ref, cols) in enumerate(both)
        ]

    for load in loads():
        load.start()
    barrier = pltpu.get_barrier_semaphore()
    around = [(w, c, (z + k) % 4) for k in range(1, 4)]
    for device in [dev_x, dev_y, dev_c] + around:
        pl.semaphore_signal(barrier, inc=1, device_id=device, device_id_type=MESH)
    pl.semaphore_wait(barrier, 6)

    def remote(src, dst, send, got, device):
        return pltpu.make_async_remote_copy(
            src_ref=src,
            dst_ref=dst,
            send_sem=send,
            recv_sem=got,
            device_id=device,
            device_id_type=MESH,
        )


    def to_right(s):
        return remote(
            parts_ref.at[s], right_in.at[s], right_send.at[s], right_recv.at[s], sides[0]
        )

    def to_left(s):
        return remote(parts_ref.at[s], left_in.at[s], left_send.at[s], left_recv.at[s], sides[1])

    def pass_right(s):
        @pl.when(z < s)
        def _():
            @pl.when(z > 0)
            def _():
                to_right(s).wait_recv()
                parts_ref[s] = (parts_ref[s].astype(f32) + right_in[s].astype(f32)).astype(bf16)

            to_right(s).start()

    def pass_left(s):
        @pl.when(z > s)
        def _():
            @pl.when(z < 3)
            def _():
                to_left(s).wait_recv()
                parts_ref[s] = (parts_ref[s].astype(f32) + left_in[s].astype(f32)).astype(bf16)

            to_left(s).start()


    def to_sibling():
        return [
            remote(
                ref.at[:, 1 - c], sibs.at[:, :, cols], sib_send.at[i], sib_recv.at[i], dev_c
            )
            for i, (ref, cols) in enumerate(both)
        ]

    def first_hops():
        moves = (
            (wx, lo, from_x1.at[0], dev_x),
            (wd, lo, from_x1.at[1], dev_x),
            (wy, hi, from_y1.at[0], dev_y),
            (wd, hi, from_y1.at[1], dev_y),
        )
        return [
            remote(mine.at[ww, :, cols], dst, one_send.at[i], one_recv.at[i], device)
            for i, (ww, cols, dst, device) in enumerate(moves)
        ]

    def second_hops():
        moves = ((wy, lo, from_y2, dev_y), (wx, hi, from_x2, dev_x))
        return [
            remote(mine.at[ww, :, cols], dst, two_send.at[i], two_recv.at[i], device)
            for i, (ww, cols, dst, device) in enumerate(moves)
        ]

    def add(*terms):
        added = terms[0].astype(f32)
        for term in terms[1:]:
            added = added + term.astype(f32)
        return added

    def weights_first():
        for load in loads():
            load.wait()
        for part in to_sibling():
            part.wait_recv()
        for k in range(4):
            mine[k] = add(mine[k], sibs[k]).astype(bf16)
        for hop in first_hops():
            hop.start()

    def weights_second():
        for hop in first_hops():
            hop.wait_recv()
        mine[wy, :, lo] = add(mine[wy, :, lo], from_x1[1]).astype(bf16)
        mine[wx, :, hi] = add(mine[wx, :, hi], from_y1[1]).astype(bf16)
        for hop in second_hops():
            hop.start()

    def weights_last():
        for hop in second_hops():
            hop.wait_recv()
        low = add(mine[w, :, lo], from_x1[0], from_y2[...])
        high = add(mine[w, :, hi], from_y1[0], from_x2[...])
        for k in range(4):
            part = (low if (k + 1) * heads <= half else high)[
                :, k * heads % half : k * heads % half + heads
            ]
            if k < 3:
                qkv_out[k] = part
            else:
                out_out[...] = part


    spread = ((own_rows, rows_out), (layer_ref, layer_out))

    def moved(i, j, side):
        own, whole = spread[i]
        return remote(
            own if j == 0 else whole.at[order[j]],
            whole.at[order[j]],
            send_z.at[i, j, side],
            recv_z.at[i, order[j]],
            sides[side],
        )

    def onward(j):
        return (((order[j] <= z) & (z < 3), 0), ((order[j] >= z) & (z > 0), 1))

    def along(i, j):
        for there, side in onward(j):
            pl.when(there)(lambda: moved(i, j, side).start())

    def passed_on(i, j):
        moved(i, j, 0).wait_recv()
        along(i, j)


    def small(i, src, dst, device):
        return remote(src, dst, small_send.at[i], small_recv.at[i], device)

    def small_sibling(k):
        return small(k, small_ref.at[k, 1 - c], from_c.at[k], dev_c)

    def small_x(k):
        return small(4 + k, sums.at[(wx, wd)[k]], from_x.at[k], dev_x)

    def small_y():
        return small(6, sums.at[wy], from_y, dev_y)

    def small_z(target, source):
        return remote(
            sums.at[w],
            from_z.at[source],
            small_send.at[7 + target],
            small_recv.at[7 + source],
            (w, c, target),
        )

    for part in to_sibling():
        part.start()
    inner = (z > 0) & (z < 3)
    pl.when(inner)(lambda: along(1, 0))
    for s in range(3):
        pass_right(3 - s)
        pass_left(s)
        if s == 0:
            passed_on(1, 1)
        if s == 1:
            weights_first()
    pl.when((z == 0) | (z == 3))(lambda: along(1, 0))
    d_normed = parts_ref[z].astype(f32)
    right_in[0] = jnp.zeros(right_in.shape[1:], bf16)
    left_in[3] = jnp.zeros(left_in.shape[1:], bf16)

    @pl.when(z > 0)
    def _():
        to_right(z).wait_recv()

    @pl.when(z < 3)
    def _():
        to_left(z).wait_recv()

    d_normed = d_normed + right_in[z].astype(f32) + left_in[z].astype(f32)
    scale = scale_ref[...]
    unit = x_ref[...].astype(f32) * scale
    scaled = gain_ref[...] * d_normed
    shift = jnp.mean(scaled * unit, axis=1, keepdims=True)
    own_rows[...] = (d_hidden_ref[...] + scale * (scaled - unit * shift)).astype(bf16)
    along(0, 0)
    rows_out[z] = own_rows[...]
    layer_out[z] = layer_ref[...]
    d_gain = jnp.sum(d_normed * unit, axis=0, keepdims=True)
    for k in range(8):
        for i in range(2):
            at = (2 * k + i) * 128
            small_ref[k // 2, k % 2, i : i + 1, :] = d_gain[:, at : at + 128]
    for k in range(4):
        small_sibling(k).start()
    for k in range(4):
        small_sibling(k).wait_recv()
        sums[k] = small_ref[k, c] + from_c[k]
    for k in range(2):
        small_x(k).start()
    weights_second()
    for k in range(2):
        small_x(k).wait_recv()
    sums[w] = sums[w] + from_x[0]
    sums[wy] = sums[wy] + from_x[1]
    small_y().start()
    passed_on(1, 2)
    passed_on(0, 1)
    small_y().wait_recv()
    sums[w] = sums[w] + from_y[...]
    for k in range(1, 4):
        small_z((z + k) % 4, z).start()
    passed_on(1, 3)
    passed_on(0, 2)
    weights_last()
    for k in range(1, 4):
        small_z(z, (z + k) % 4).wait_recv()
    from_z[z] = sums[w]
    small_out[...] = add(*(from_z[k] for k in range(4)))
    passed_on(0, 3)
    for s in range(3):

        @pl.when(z < 3 - s)
        def _():
            to_right(3 - s).wait_send()

        @pl.when(z > s)
        def _():
            to_left(s).wait_send()

    for hop in to_sibling() + first_hops() + second_hops():
        hop.wait_send()
    for k in range(4):
        small_sibling(k).wait_send()
    for k in range(2):
        small_x(k).wait_send()
    small_y().wait_send()
    for k in range(1, 4):
        small_z((z + k) % 4, z).wait_send()
    for i in range(2):
        for j in range(4):
            for there, side in onward(j):
                pl.when(there)(lambda: moved(i, j, side).wait_send())


def finish_call(parts, rows, scale, gain, d_hidden, d_qkv, d_out, layer, small):
    dma = pltpu.SemaphoreType.DMA
    anywhere, vmem = (pl.BlockSpec(memory_space=pl.ANY), pl.BlockSpec(memory_space=pltpu.VMEM))
    share, width = rows.shape
    count, heads = d_out.shape[2:]
    half = width // 2
    block = small.shape[2:]
    bf16, f32 = (jnp.bfloat16, jnp.float32)

    def body(*refs):
        ins, outs, rest = (refs[:9], refs[9:14], refs[14:])
        parts_in, small_in = (ins[0], ins[8])
        parts_own, small_own = rest[:2]
        parts_own[...] = parts_in[...]
        small_own[...] = small_in[...]
        finish_kernel(parts_own, *ins[1:8], small_own, *outs, *rest[2:])

    return pl.pallas_call(
        body,
        out_shape=(
            jax.ShapeDtypeStruct((4, share, width), bf16),
            jax.ShapeDtypeStruct((4, share, width), bf16),
            jax.ShapeDtypeStruct((3, count, heads), f32),
            jax.ShapeDtypeStruct((count, heads), f32),
            jax.ShapeDtypeStruct(block, f32),
        ),
        in_specs=[vmem] * 5 + [anywhere, anywhere, vmem, vmem],
        out_specs=(vmem,) * 5,
        scratch_shapes=[
            pltpu.VMEM((4, share, width), bf16),
            pltpu.VMEM((4, 2) + block, f32),
            pltpu.VMEM((share, width), bf16),
            pltpu.VMEM((4, share, width), bf16),
            pltpu.VMEM((4, share, width), bf16),
            pltpu.VMEM((4,) + block, f32),
            pltpu.VMEM((4,) + block, f32),
            pltpu.VMEM((2,) + block, f32),
            pltpu.VMEM(block, f32),
            pltpu.VMEM((4,) + block, f32),
            pltpu.VMEM((4, count, width), bf16),
            pltpu.VMEM((4, count, width), bf16),
            pltpu.VMEM((2, count, half), bf16),
            pltpu.VMEM((2, count, half), bf16),
            pltpu.VMEM((count, half), bf16),
            pltpu.VMEM((count, half), bf16),
            dma((4,)),
            dma((4,)),
            dma((4,)),
            dma((4,)),
            dma((2, 4, 2)),
            dma((2, 4)),
            dma((11,)),
            dma((11,)),
            dma((2,)),
            dma((2,)),
            dma((2,)),
            dma((4,)),
            dma((4,)),
            dma((2,)),
            dma((2,)),
        ],
        compiler_params=pltpu.CompilerParams(
            collective_id=1, has_side_effects=True, vmem_limit_bytes=48 << 20
        ),
    )(parts, rows, scale, gain, d_hidden, d_qkv, d_out, layer, small)


def swapped(rows, flip):
    return lax.ppermute(rows, WEIGHTS, [(k, k ^ flip) for k in range(4)])


def grads_around(rows, x_low, y_high, share):
    half = rows.shape[1] // 2
    parts = (
        rows,
        x_low,
        swapped(rows[:, half:], 1),
        swapped(rows[:, :half], 2),
        y_high,
        swapped(x_low, 2),
        swapped(y_high, 1),
    )
    return [part.reshape(-1, share, part.shape[1]) for part in parts]


def shares_around(rows):
    z = lax.axis_index(TENSOR)
    parts = [rows] + [
        lax.ppermute(rows, TENSOR, [(k, (k + step) % 4) for k in range(4)]) for step in (1, 3, 2)
    ]
    whole = jnp.zeros((4,) + rows.shape, rows.dtype)
    for part, step in zip(parts, (0, 1, 3, 2)):
        whole = lax.dynamic_update_index_in_dim(whole, part, (z + 4 - step) % 4, 0)
    return whole.reshape((-1,) + rows.shape[1:])


def gathered(rows, axes):
    return lax.all_gather(rows, axes, axis=0, tiled=True)


def scattered(rows, axes):
    return lax.psum_scatter(rows, axes, scatter_dimension=0, tiled=True)


def fit_rows(values, rows):
    flat = values.reshape(-1)
    columns = -(-flat.shape[0] // rows)
    return jnp.pad(flat, (0, rows * columns - flat.shape[0])).reshape(rows, columns)


def per_device_dense(
    layer_in,
    norm_gains,
    qkv_weight,
    qk_gains,
    out_weight,
    router,
    expert_in,
    expert_out,
    grad_out,
    segments,
    routes,
    route_order,
):
    group = GROUP
    everyone = EVERYONE
    group_count = lax.axis_size(group)
    tensor_count = lax.axis_size(TENSOR)
    context_rank = lax.axis_index(CONTEXT)
    tensor_rank = lax.axis_index(TENSOR)
    seq_count, half_len, model_width = layer_in.shape
    token_count = seq_count * half_len
    top_count = routes.shape[2]
    weight_rows, _, head_width = qkv_weight.shape
    expert_total = router.shape[1]
    local_experts = expert_in.shape[0]
    hidden_width = expert_in.shape[3]
    head_rows, _, local_heads = qk_gains.shape
    head_size = head_rows * group_count
    share = token_count // tensor_count
    bf16, f32 = jnp.bfloat16, jnp.float32

    capacity = token_count * top_count * 9 // (8 * expert_total)
    routed, slot_of = pair_slots(
        routes.reshape(token_count, top_count),
        route_order.reshape(token_count, top_count),
        expert_total,
    )
    kept = routed & (slot_of < capacity)

    front_small = jnp.concatenate(
        [norm_gains, fit_rows(qk_gains, weight_rows)], axis=1
    )
    front = gathered(
        jnp.concatenate([qkv_weight.reshape(weight_rows, -1), front_small], axis=1), group
    )
    own_grads = grad_out.reshape(token_count, model_width)
    front, own_grads = lax.optimization_barrier((front, own_grads))
    half = model_width // 2
    x_low, y_high = (swapped(own_grads[:, :half], 1), swapped(own_grads[:, half:], 2))
    back_small = jnp.concatenate(
        [router, fit_rows(kept.astype(bf16), weight_rows)], axis=1
    )
    back = gathered(jnp.concatenate([out_weight, back_small], axis=1), group)
    qkv_full = front[:, : 3 * head_width]
    gain_full = front[:, 3 * head_width : 3 * head_width + 2].astype(f32)
    gain_attn, gain_ffn = (gain_full[:, 0], gain_full[:, 1])
    qk_gain_full = (
        front[:, 3 * head_width + 2 :]
        .reshape(group_count, -1)[:, : head_rows * 2 * local_heads]
        .reshape(head_size, 2, local_heads)
        .astype(f32)
    )
    query_gain = qk_gain_full[:, 0, :].T.reshape(-1)
    key_gain = qk_gain_full[:, 1, :].T.reshape(-1)
    out_full = back[:, :head_width]
    router_full = back[:, head_width : head_width + expert_total]
    kept_all = (
        back[:, head_width + expert_total :]
        .reshape(group_count, -1)[:, : expert_total * token_count]
        .reshape(group_count, expert_total, token_count)
    )
    inv_root = 1.0 / math.sqrt(head_size)
    residual = layer_in.reshape(token_count, model_width).astype(f32)
    scale_one = lax.rsqrt(jnp.mean(residual * residual, axis=1, keepdims=True) + epsilon)
    normed_one = (residual * scale_one * gain_attn).astype(bf16)
    projected = jnp.dot(normed_one, qkv_full, preferred_element_type=f32)
    query_raw = projected[:, :head_width]
    key_raw = projected[:, head_width : 2 * head_width]
    value_raw = projected[:, 2 * head_width :]
    square_sums = row_sums(
        jnp.stack(
            [jnp.sum(query_raw * query_raw, axis=1), jnp.sum(key_raw * key_raw, axis=1)], axis=1
        )
    )
    query_scale = lax.rsqrt(square_sums[:, 0:1] / model_width + epsilon)
    key_scale = lax.rsqrt(square_sums[:, 1:2] / model_width + epsilon)
    heads_shape = (seq_count, half_len, local_heads, head_size)
    query_hat = (query_raw * query_scale * query_gain).reshape(heads_shape)
    key_hat = (key_raw * key_scale * key_gain).reshape(heads_shape)
    query_pos = context_rank * half_len + jnp.arange(half_len, dtype=jnp.int32)
    cosine_table, sine_table = rotary_tables(query_pos, head_size)
    cosine_table = cosine_table[None, :, None, :]
    sine_table = sine_table[None, :, None, :]
    query_rot = (query_hat * cosine_table + rotate_half(query_hat) * sine_table).astype(bf16)
    key_rot = (key_hat * cosine_table + rotate_half(key_hat) * sine_table).astype(bf16)
    value_low = value_raw.astype(bf16).reshape(heads_shape)
    key_prev, value_prev = passed_along((key_rot, value_low), CONTEXT, 1)
    all_keys = jnp.concatenate([key_prev, key_rot], axis=1)
    all_values = jnp.concatenate([value_prev, value_low], axis=1)
    key_pos = jnp.concatenate([query_pos - half_len, query_pos])
    seg_query = lax.dynamic_slice_in_dim(segments, context_rank * half_len, half_len, 1)
    seg_prev = lax.dynamic_slice_in_dim(
        segments, jnp.maximum(context_rank - 1, 0) * half_len, half_len, 1
    )
    seg_keys = jnp.concatenate([seg_prev, seg_query], axis=1)
    causal = (key_pos[None, :] >= 0) & (key_pos[None, :] <= query_pos[:, None])
    allowed = causal[None] & (seg_query[:, :, None] == seg_keys[:, None, :])

    def score_block(queries, key_rows):
        raw_scores = (
            jnp.einsum(BY_SCORE, queries, key_rows, preferred_element_type=f32) * inv_root
        )
        return jnp.where(allowed[:, None], raw_scores, -1e30)

    scores = score_block(query_rot, all_keys)
    row_max = jnp.max(scores, axis=-1, keepdims=True)
    exponent = jnp.exp(scores - row_max)
    row_total = jnp.sum(exponent, axis=-1, keepdims=True)
    log_total = row_max + jnp.log(row_total)
    attn_probs = (exponent / row_total).astype(bf16)
    attended = jnp.einsum(BY_QUERY, attn_probs, all_values, preferred_element_type=f32)
    attended_low = attended.reshape(token_count, -1).astype(bf16)
    x_low, y_high, attended_low = lax.optimization_barrier((x_low, y_high, attended_low))
    around = grads_around(own_grads, x_low, y_high, share)
    attn_partial = jnp.einsum("tf,df->td", attended_low, out_full, preferred_element_type=f32)

    own_rows = lambda rows: lax.dynamic_slice_in_dim(rows, tensor_rank * share, share, 0)
    residual_own = own_rows(residual)
    hidden = residual_own + scattered(attn_partial.astype(bf16), TENSOR).astype(f32)
    scale_two = lax.rsqrt(jnp.mean(hidden * hidden, axis=1, keepdims=True) + epsilon)
    unit_two = hidden * scale_two
    normed_two = (unit_two * gain_ffn).astype(bf16)
    upstream = own_rows(grad_out.reshape(token_count, model_width)).astype(f32)

    pad_experts = lambda rows: jnp.pad(rows, ((0, 0), (0, 128 - expert_total)))
    kept_rows = kept_all.transpose(0, 2, 1).reshape(-1, expert_total)
    normed_all, grads_all, gated, d_both, moe_all, d_sums = experts_call(
        normed_two,
        around,
        pad_experts(kept_rows).reshape(4, 2, 4, share, 128),
        pad_experts(router_full),
        expert_in,
        expert_out,
        expert_total,
    )
    normed_all, grads_all, gated, d_both, moe_all = (
        rows.reshape(group_count * token_count, -1)
        for rows in (normed_all, grads_all, gated, d_both, moe_all)
    )
    moe_plane = scattered(moe_all, group)
    kept_own = own_rows(kept.T).astype(f32)
    probs_own = jax.nn.softmax(
        jnp.dot(normed_two, router_full, preferred_element_type=f32), axis=1
    )
    d_probs = d_sums[:, model_width : model_width + expert_total] * kept_own
    d_logits = (
        probs_own * (d_probs - jnp.sum(probs_own * d_probs, axis=1, keepdims=True))
    ).astype(bf16)
    d_normed_two = d_sums[:, :model_width] + jnp.dot(
        d_logits, router_full.T, preferred_element_type=f32
    )
    d_router = jnp.dot(normed_two.T, d_logits, preferred_element_type=f32)
    d_gain_ffn = jnp.sum(d_normed_two * unit_two, axis=0)
    scaled_ffn = gain_ffn * d_normed_two
    d_hidden = upstream + scale_two * (
        scaled_ffn - unit_two * jnp.mean(scaled_ffn * unit_two, axis=1, keepdims=True)
    )
    d_hidden_own, normed_all, grads_all, gated, d_both = lax.optimization_barrier(
        (d_hidden.astype(bf16), normed_all, grads_all, gated, d_both)
    )
    d_hidden_low = shares_around(d_hidden_own)
    grad_expert_in = (
        jnp.dot(normed_all.T, d_both, preferred_element_type=f32)
        .reshape(model_width, local_experts, 2, hidden_width)
        .transpose(1, 2, 0, 3)
    )
    grad_expert_out = jnp.dot(gated.T, grads_all, preferred_element_type=f32).reshape(
        expert_out.shape
    )
    d_hidden_low, grad_expert_in, grad_expert_out = lax.optimization_barrier(
        (d_hidden_low, grad_expert_in, grad_expert_out)
    )

    d_attended = (
        jnp.dot(d_hidden_low, out_full, preferred_element_type=f32)
        .astype(bf16)
        .reshape(heads_shape)
    )
    d_out_weight = jnp.einsum("td,tf->df", d_hidden_low, attended_low, preferred_element_type=f32)
    probs_again = jnp.exp(score_block(query_rot, all_keys) - log_total)
    probs_again_low = probs_again.astype(bf16)
    d_probs_att = jnp.einsum(
        BY_SCORE, d_attended, all_values, preferred_element_type=f32
    )
    d_values_all = jnp.einsum(
        BY_KEY, probs_again_low, d_attended, preferred_element_type=f32
    )
    row_dot = jnp.sum(probs_again * d_probs_att, axis=-1, keepdims=True)
    d_scores = (probs_again * (d_probs_att - row_dot)).astype(bf16)
    d_query_rot = (
        jnp.einsum(BY_QUERY, d_scores, all_keys, preferred_element_type=f32) * inv_root
    )
    d_keys_all = (
        jnp.einsum(BY_KEY, d_scores, query_rot, preferred_element_type=f32) * inv_root
    )
    back_key, back_value = (
        passed_along(d_keys_all[:, :half_len].astype(bf16), CONTEXT, -1).astype(f32),
        passed_along(d_values_all[:, :half_len].astype(bf16), CONTEXT, -1).astype(f32),
    )
    d_key_rot = d_keys_all[:, half_len:] + back_key
    d_value = (d_values_all[:, half_len:] + back_value).reshape(token_count, -1)
    d_query_hat = (d_query_rot * cosine_table + rotate_back(d_query_rot * sine_table)).reshape(
        token_count, -1
    )
    d_key_hat = (d_key_rot * cosine_table + rotate_back(d_key_rot * sine_table)).reshape(
        token_count, -1
    )
    centre_own = (
        jnp.stack(
            [
                jnp.sum(query_gain * d_query_hat * query_raw, axis=1),
                jnp.sum(key_gain * d_key_hat * key_raw, axis=1),
            ],
            axis=1,
        )
    )
    centre, moe_plane = lax.optimization_barrier((row_sums(centre_own), moe_plane))
    moe_own = scattered(moe_plane, TENSOR).astype(f32)
    d_query_raw = (
        query_scale * query_gain * d_query_hat
        - query_raw * (query_scale**3 / model_width) * centre[:, 0:1]
    )
    d_key_raw = (
        key_scale * key_gain * d_key_hat - key_raw * (key_scale**3 / model_width) * centre[:, 1:2]
    )
    d_query_gain = (
        jnp.sum(d_query_hat * query_raw * query_scale, axis=0).reshape(local_heads, head_size).T
    )
    d_key_gain = jnp.sum(d_key_hat * key_raw * key_scale, axis=0).reshape(local_heads, head_size).T
    d_qk_gains = jnp.stack([d_query_gain, d_key_gain], axis=1)
    d_projected = jnp.concatenate([d_query_raw, d_key_raw, d_value], axis=1).astype(bf16)
    d_normed_parts = jnp.einsum(
        "tf,df->td", d_projected, qkv_full, preferred_element_type=f32
    ).astype(bf16)
    d_qkv = jnp.einsum("td,tf->df", normed_one, d_projected, preferred_element_type=f32)

    own_slot = (jnp.arange(tensor_count) == tensor_rank).astype(f32)[None, :, None]
    lines = lambda values: values.reshape(group_count, -1, 128)
    small = jnp.concatenate(
        [
            jnp.zeros((group_count, weight_rows // 128, 128), f32),
            lines(d_gain_ffn),
            lines(d_router),
            lines(d_qk_gains) * own_slot,
        ],
        axis=1,
    )
    d_normed_parts, d_qkv, d_out_weight, moe_own = lax.optimization_barrier(
        (d_normed_parts, d_qkv.astype(bf16), d_out_weight.astype(bf16), moe_own)
    )
    grad_in, layer_out, grad_qkv, grad_out_weight, small = finish_call(
        d_normed_parts.reshape(tensor_count, share, model_width),
        own_rows(layer_in.reshape(token_count, model_width)),
        own_rows(scale_one),
        gain_attn[None],
        d_hidden,
        d_qkv.reshape(4, 2, weight_rows, -1),
        d_out_weight.reshape(4, 2, weight_rows, -1),
        (hidden + moe_own).astype(bf16),
        small.reshape((4, 2) + small.shape[1:]),
    )
    grad_in = grad_in.astype(f32).reshape(layer_in.shape)
    layer_out = layer_out.reshape(layer_in.shape)
    grad_qkv = grad_qkv.transpose(1, 0, 2)
    lines_of = weight_rows // 128
    gain_share = weight_rows // tensor_count
    router_share = expert_total // tensor_count
    router_lines = weight_rows * expert_total // 128
    part_of = lambda rows, count, axis: lax.dynamic_slice_in_dim(
        rows, tensor_rank * count, count, axis
    )
    gains = small[: 2 * lines_of].reshape(2, weight_rows)
    routers = small[2 * lines_of : 2 * lines_of + router_lines].reshape(weight_rows, expert_total)
    qk_lines = small[2 * lines_of + router_lines :]
    return (
        layer_out,
        grad_in,
        part_of(gains, gain_share, 1).T,
        grad_qkv,
        part_of(qk_lines, 1, 0).reshape(head_rows, 2, local_heads),
        grad_out_weight,
        part_of(routers, router_share, 1),
        grad_expert_in,
        grad_expert_out,
    )


def solution(mesh):
    placed = (
        P(WEIGHTS, CONTEXT, None),
        P(GROUP, None),
        P(GROUP, None, TENSOR),
        P(GROUP, None, TENSOR),
        P(GROUP, TENSOR),
        P(GROUP, None),
        P(GROUP, None, None, TENSOR),
        P(GROUP, TENSOR, None),
        P(WEIGHTS, CONTEXT, None),
        P(WEIGHTS, None),
        P(WEIGHTS, CONTEXT, None),
        P(WEIGHTS, CONTEXT, None),
    )
    axes = tuple(mesh.shape[axis] for axis in EVERYONE)

    def per_device(*blocks):
        dense = axes == (4, 2, 4) and blocks[5].shape[1] <= 2 * blocks[10].shape[2]
        return (per_device_dense if dense else per_device_slots)(*blocks)

    return jax.shard_map(
        per_device,
        mesh=mesh,
        in_specs=placed,
        out_specs=(
            P(WEIGHTS, CONTEXT, None),
            P(WEIGHTS, CONTEXT, None),
            P(EVERYONE, None),
            P(GROUP, None, TENSOR),
            P(GROUP, None, TENSOR),
            P(GROUP, TENSOR),
            P(GROUP, TENSOR),
            P(GROUP, None, None, TENSOR),
            P(GROUP, TENSOR, None),
        ),
        check_vma=False,
    )
```

```python
import functools
import math

import jax
import jax.numpy as jnp
from jax import lax
from jax.experimental import pallas as pl
from jax.experimental.pallas import tpu as pltpu
from jax.sharding import PartitionSpec as P

epsilon = 1e-05
rotary_base = 10000.0
WEIGHTS, CONTEXT, TENSOR = ("weights", "context", "tensor")
GROUP = (WEIGHTS, CONTEXT)
EVERYONE = (WEIGHTS, CONTEXT, TENSOR)
MESH = pl.DeviceIdType.MESH
BY_SCORE = "sqhd,skhd->shqk"
BY_QUERY = "shqk,skhd->sqhd"
BY_KEY = "shqk,sqhd->skhd"


def passed_along(value, axis, steps):
    count = lax.axis_size(axis)
    leading, last = (max(0, -steps), min(count, count - steps))
    return lax.ppermute(value, axis, [(source, source + steps) for source in range(leading, last)])


def rotate_half(values_in):
    middle = values_in.shape[-1] // 2
    return jnp.concatenate([-values_in[..., middle:], values_in[..., :middle]], axis=-1)


def rotate_back(grads_in):
    middle = grads_in.shape[-1] // 2
    return jnp.concatenate([grads_in[..., middle:], -grads_in[..., :middle]], axis=-1)


def rotary_tables(positions, head_size):
    frequency = rotary_base ** (-(2.0 * jnp.arange(head_size // 2, dtype=jnp.float32)) / head_size)
    angle_table = positions.astype(jnp.float32)[:, None] * frequency[None, :]
    angle_table = jnp.concatenate([angle_table, angle_table], axis=1)
    return (jnp.cos(angle_table), jnp.sin(angle_table))


def pair_slots(token_routes, token_ranks, expert_total):
    unused = token_routes.size
    hot = token_routes.T[None] == jnp.arange(expert_total, dtype=jnp.int32)[:, None, None]
    rank_of = jnp.min(jnp.where(hot, token_ranks.T[None], unused), axis=1)
    slot_of = jnp.sum((rank_of[:, :, None] < rank_of[:, None, :]).astype(jnp.int32), axis=1)
    return (rank_of < unused, slot_of)


def place_pairs(pair_expert, rank, expert_total, capacity, top_count):
    pair_count = pair_expert.shape[0]
    token_routes = pair_expert.reshape(-1, top_count)
    slot_of = pair_slots(token_routes, rank.reshape(-1, top_count), expert_total)[1]
    slot_index = jnp.take_along_axis(slot_of.T, token_routes, axis=1).reshape(pair_count)
    kept_pair = slot_index < capacity
    dest_row = jnp.where(kept_pair, pair_expert * capacity + slot_index, expert_total * capacity)
    slot_pair = (
        jnp.full((expert_total * capacity + 1,), pair_count, jnp.int32)
        .at[dest_row]
        .set(jnp.arange(pair_count, dtype=jnp.int32))[:-1]
    )
    return (kept_pair, dest_row, slot_pair)


def row_sums(partial_rows):
    return lax.psum(partial_rows, TENSOR)


def tensor_sum(partial_rows):
    return lax.psum(partial_rows, TENSOR)


def to_owners(slot_rows):
    return lax.all_to_all(
        slot_rows, GROUP, split_axis=0, concat_axis=0, tiled=True
    )


def expert_front(slot_inputs, expert_in):
    both_pre = jnp.einsum(
        "sncd,ngdf->sncgf", slot_inputs, expert_in, preferred_element_type=jnp.float32
    )
    return (both_pre[..., 0, :], both_pre[..., 1, :])


def per_device_slots(
    layer_in,
    norm_gains,
    qkv_weight,
    qk_gains,
    out_weight,
    router,
    expert_in,
    expert_out,
    grad_out,
    segments,
    routes,
    route_order,
):
    group_count = lax.axis_size(GROUP)
    tensor_count = lax.axis_size(TENSOR)
    context_rank = lax.axis_index(CONTEXT)
    tensor_rank = lax.axis_index(TENSOR)
    seq_count, half_len, model_width = layer_in.shape
    token_count = seq_count * half_len
    top_count = routes.shape[2]
    qkv_full, out_full, qk_gain_full, gain_full, router_full = (
        lax.all_gather(qkv_weight, GROUP, axis=0, tiled=True),
        lax.all_gather(out_weight, GROUP, axis=0, tiled=True),
        lax.all_gather(qk_gains, GROUP, axis=0, tiled=True),
        lax.all_gather(norm_gains, GROUP, axis=0, tiled=True),
        lax.all_gather(router, GROUP, axis=0, tiled=True),
    )
    head_size = qk_gain_full.shape[0]
    local_heads = qk_gain_full.shape[2]
    expert_total = router_full.shape[1]
    gain_attn = gain_full[:, 0].astype(jnp.float32)
    gain_ffn = gain_full[:, 1].astype(jnp.float32)
    query_gain = qk_gain_full[:, 0, :].astype(jnp.float32).T.reshape(-1)
    key_gain = qk_gain_full[:, 1, :].astype(jnp.float32).T.reshape(-1)
    inv_root = 1.0 / math.sqrt(head_size)
    residual = layer_in.reshape(token_count, model_width).astype(jnp.float32)
    scale_one = lax.rsqrt(jnp.mean(residual * residual, axis=1, keepdims=True) + epsilon)
    unit_one = residual * scale_one
    normed_one = (unit_one * gain_attn).astype(jnp.bfloat16)
    projected = jnp.einsum("td,dgf->tgf", normed_one, qkv_full, preferred_element_type=jnp.float32)
    query_raw = projected[:, 0]
    key_raw = projected[:, 1]
    value_raw = projected[:, 2]
    square_sums = row_sums(
        jnp.stack(
            [jnp.sum(query_raw * query_raw, axis=1), jnp.sum(key_raw * key_raw, axis=1)], axis=1
        )
    )
    query_scale = lax.rsqrt(square_sums[:, 0:1] / model_width + epsilon)
    key_scale = lax.rsqrt(square_sums[:, 1:2] / model_width + epsilon)
    heads_shape = (seq_count, half_len, local_heads, head_size)
    query_hat = (query_raw * query_scale * query_gain).reshape(heads_shape)
    key_hat = (key_raw * key_scale * key_gain).reshape(heads_shape)
    query_pos = context_rank * half_len + jnp.arange(half_len, dtype=jnp.int32)
    cosine_table, sine_table = rotary_tables(query_pos, head_size)
    cosine_table = cosine_table[None, :, None, :]
    sine_table = sine_table[None, :, None, :]
    query_rot = (query_hat * cosine_table + rotate_half(query_hat) * sine_table).astype(
        jnp.bfloat16
    )
    key_rot = (key_hat * cosine_table + rotate_half(key_hat) * sine_table).astype(jnp.bfloat16)
    value_low = value_raw.astype(jnp.bfloat16).reshape(heads_shape)
    key_prev, value_prev = passed_along((key_rot, value_low), CONTEXT, 1)
    all_keys = jnp.concatenate([key_prev, key_rot], axis=1)
    all_values = jnp.concatenate([value_prev, value_low], axis=1)
    key_pos = jnp.concatenate([query_pos - half_len, query_pos])
    seg_query = lax.dynamic_slice_in_dim(segments, context_rank * half_len, half_len, 1)
    seg_prev = lax.dynamic_slice_in_dim(
        segments, jnp.maximum(context_rank - 1, 0) * half_len, half_len, 1
    )
    seg_keys = jnp.concatenate([seg_prev, seg_query], axis=1)
    causal = (key_pos[None, :] >= 0) & (key_pos[None, :] <= query_pos[:, None])
    allowed = causal[None] & (seg_query[:, :, None] == seg_keys[:, None, :])

    def score_block(queries, key_rows):
        raw_scores = (
            jnp.einsum(BY_SCORE, queries, key_rows, preferred_element_type=jnp.float32)
            * inv_root
        )
        return jnp.where(allowed[:, None], raw_scores, -1e30)

    scores = score_block(query_rot, all_keys)
    row_max = jnp.max(scores, axis=-1, keepdims=True)
    exponent = jnp.exp(scores - row_max)
    row_total = jnp.sum(exponent, axis=-1, keepdims=True)
    log_total = row_max + jnp.log(row_total)
    attn_probs = (exponent / row_total).astype(jnp.bfloat16)
    attended = jnp.einsum(
        BY_QUERY, attn_probs, all_values, preferred_element_type=jnp.float32
    )
    attended_low = attended.reshape(token_count, -1).astype(jnp.bfloat16)
    attn_partial = jnp.einsum(
        "tf,df->td", attended_low, out_full, preferred_element_type=jnp.float32
    )
    hidden = residual + tensor_sum(attn_partial)
    scale_two = lax.rsqrt(jnp.mean(hidden * hidden, axis=1, keepdims=True) + epsilon)
    unit_two = hidden * scale_two
    normed_two = (unit_two * gain_ffn).astype(jnp.bfloat16)
    logits = jnp.dot(normed_two, router_full, preferred_element_type=jnp.float32)
    router_probs = jax.nn.softmax(logits, axis=1)
    capacity = token_count * top_count * 9 // (8 * expert_total)
    local_experts = expert_in.shape[0]
    pair_count = token_count * top_count
    token_routes = routes.reshape(token_count, top_count)
    kept_pair, dest_row, slot_pair = place_pairs(
        token_routes.reshape(pair_count), route_order.reshape(pair_count), expert_total, capacity, top_count
    )
    zero_row = jnp.zeros((1, model_width), jnp.bfloat16)
    zero_wide = jnp.zeros((1, model_width), jnp.float32)
    slot_shape = (group_count, local_experts, capacity, model_width)
    dispatch_rows = jnp.concatenate([normed_two, zero_row], axis=0)[slot_pair // top_count].reshape(
        slot_shape
    )
    received = lax.all_to_all(
        dispatch_rows, GROUP, split_axis=0, concat_axis=0, tiled=True
    )
    gate_pre, up_pre = expert_front(received, expert_in)
    sigmoid_gate = jax.nn.sigmoid(gate_pre)
    silu_gate = gate_pre * sigmoid_gate
    activated = (silu_gate * up_pre).astype(jnp.bfloat16)
    expert_partial = jnp.einsum(
        "sncf,nfd->sncd", activated, expert_out, preferred_element_type=jnp.float32
    )
    kept_float = kept_pair.reshape(token_count, top_count).astype(jnp.float32)
    gate_weight = jnp.take_along_axis(router_probs, token_routes, axis=1) * kept_float
    upstream = grad_out.reshape(token_count, model_width).astype(jnp.float32)
    returned = to_owners(expert_partial).reshape(expert_total * capacity, model_width)
    picked = jnp.concatenate([returned, zero_wide], axis=0)[dest_row].reshape(
        token_count, top_count, model_width
    )
    moe_partial = jnp.sum(gate_weight[:, :, None] * picked, axis=1)
    dot_partial = jnp.sum(upstream[:, None, :] * picked, axis=2)
    moe_total, dot_total = lax.psum((moe_partial, dot_partial), TENSOR)
    layer_out = (hidden + moe_total).astype(jnp.bfloat16).reshape(layer_in.shape)
    d_gate = dot_total * kept_float
    route_hot = (
        token_routes[:, :, None] == jnp.arange(expert_total, dtype=jnp.int32)[None, None, :]
    ).astype(jnp.float32)
    d_probs = jnp.sum(d_gate[:, :, None] * route_hot, axis=1)
    d_logits = (
        router_probs * (d_probs - jnp.sum(router_probs * d_probs, axis=1, keepdims=True))
    ).astype(jnp.bfloat16)
    d_pair = (
        (gate_weight[:, :, None] * upstream[:, None, :])
        .astype(jnp.bfloat16)
        .reshape(pair_count, model_width)
    )
    d_slots = jnp.concatenate([d_pair, zero_row], axis=0)[slot_pair].reshape(slot_shape)
    d_received = lax.all_to_all(
        d_slots, GROUP, split_axis=0, concat_axis=0, tiled=True
    )
    d_activated = jnp.einsum(
        "sncd,nfd->sncf", d_received, expert_out, preferred_element_type=jnp.float32
    )
    grad_expert_out = jnp.einsum(
        "sncf,sncd->nfd", activated, d_received, preferred_element_type=jnp.float32
    )
    d_gate_pre = d_activated * up_pre * sigmoid_gate * (1.0 + gate_pre * (1.0 - sigmoid_gate))
    d_up_pre = d_activated * silu_gate
    d_both = jnp.stack([d_gate_pre, d_up_pre], axis=3).astype(jnp.bfloat16)
    d_inputs = jnp.einsum("sncgf,ngdf->sncd", d_both, expert_in, preferred_element_type=jnp.float32)
    grad_expert_in = jnp.einsum(
        "sncd,sncgf->ngdf", received, d_both, preferred_element_type=jnp.float32
    )
    d_returned = to_owners(d_inputs).reshape(expert_total * capacity, model_width)
    d_normed_part = jnp.sum(
        jnp.concatenate([d_returned, zero_wide], axis=0)[dest_row].reshape(
            token_count, top_count, model_width
        ),
        axis=1,
    )
    d_normed_two = tensor_sum(d_normed_part) + jnp.dot(
        d_logits, router_full.T, preferred_element_type=jnp.float32
    )
    d_router = jnp.dot(normed_two.T, d_logits, preferred_element_type=jnp.float32)
    d_gain_ffn = jnp.sum(d_normed_two * unit_two, axis=0)
    scaled_ffn = gain_ffn * d_normed_two
    d_hidden = upstream + scale_two * (
        scaled_ffn - unit_two * jnp.mean(scaled_ffn * unit_two, axis=1, keepdims=True)
    )
    d_hidden_low = d_hidden.astype(jnp.bfloat16)
    d_out_weight = jnp.einsum(
        "td,tf->df", d_hidden_low, attended_low, preferred_element_type=jnp.float32
    )
    d_attended = (
        jnp.dot(d_hidden_low, out_full, preferred_element_type=jnp.float32)
        .astype(jnp.bfloat16)
        .reshape(heads_shape)
    )
    probs_again = jnp.exp(score_block(query_rot, all_keys) - log_total)
    probs_again_low = probs_again.astype(jnp.bfloat16)
    d_probs_att = jnp.einsum(
        BY_SCORE, d_attended, all_values, preferred_element_type=jnp.float32
    )
    d_values_all = jnp.einsum(
        BY_KEY, probs_again_low, d_attended, preferred_element_type=jnp.float32
    )
    row_dot = jnp.sum(probs_again * d_probs_att, axis=-1, keepdims=True)
    d_scores = (probs_again * (d_probs_att - row_dot)).astype(jnp.bfloat16)
    d_query_rot = (
        jnp.einsum(BY_QUERY, d_scores, all_keys, preferred_element_type=jnp.float32)
        * inv_root
    )
    d_keys_all = (
        jnp.einsum(BY_KEY, d_scores, query_rot, preferred_element_type=jnp.float32)
        * inv_root
    )
    back_key, back_value = (
        passed_along(d_keys_all[:, :half_len].astype(jnp.bfloat16), CONTEXT, -1).astype(
            jnp.float32
        ),
        passed_along(d_values_all[:, :half_len].astype(jnp.bfloat16), CONTEXT, -1).astype(
            jnp.float32
        ),
    )
    d_key_rot = d_keys_all[:, half_len:] + back_key
    d_value = (d_values_all[:, half_len:] + back_value).reshape(token_count, -1)
    d_query_hat = (d_query_rot * cosine_table + rotate_back(d_query_rot * sine_table)).reshape(
        token_count, -1
    )
    d_key_hat = (d_key_rot * cosine_table + rotate_back(d_key_rot * sine_table)).reshape(
        token_count, -1
    )
    centre = row_sums(
        jnp.stack(
            [
                jnp.sum(query_gain * d_query_hat * query_raw, axis=1),
                jnp.sum(key_gain * d_key_hat * key_raw, axis=1),
            ],
            axis=1,
        )
    )
    d_query_raw = (
        query_scale * query_gain * d_query_hat
        - query_raw * (query_scale**3 / model_width) * centre[:, 0:1]
    )
    d_key_raw = (
        key_scale * key_gain * d_key_hat - key_raw * (key_scale**3 / model_width) * centre[:, 1:2]
    )
    d_query_gain = (
        jnp.sum(d_query_hat * query_raw * query_scale, axis=0).reshape(local_heads, head_size).T
    )
    d_key_gain = jnp.sum(d_key_hat * key_raw * key_scale, axis=0).reshape(local_heads, head_size).T
    d_qk_gains = jnp.stack([d_query_gain, d_key_gain], axis=1)
    d_projected = jnp.stack([d_query_raw, d_key_raw, d_value], axis=1).astype(jnp.bfloat16)
    d_normed_one = tensor_sum(
        jnp.einsum("tgf,dgf->td", d_projected, qkv_full, preferred_element_type=jnp.float32)
    )
    d_qkv = jnp.einsum("td,tgf->dgf", normed_one, d_projected, preferred_element_type=jnp.float32)
    d_gain_attn = jnp.sum(d_normed_one * unit_one, axis=0)
    scaled_attn = gain_attn * d_normed_one
    grad_in = d_hidden + scale_one * (
        scaled_attn - unit_one * jnp.mean(scaled_attn * unit_one, axis=1, keepdims=True)
    )
    d_norm_gains = jnp.stack([d_gain_attn, d_gain_ffn], axis=1)
    grad_qkv, grad_out_weight, grad_qk_gains, gain_rows, router_rows = (
        lax.psum_scatter(d_qkv, GROUP, scatter_dimension=0, tiled=True),
        lax.psum_scatter(d_out_weight, GROUP, scatter_dimension=0, tiled=True),
        lax.psum_scatter(d_qk_gains, GROUP, scatter_dimension=0, tiled=True),
        lax.psum_scatter(d_norm_gains, GROUP, scatter_dimension=0, tiled=True),
        lax.psum_scatter(d_router, GROUP, scatter_dimension=0, tiled=True),
    )
    gain_share = gain_rows.shape[0] // tensor_count
    grad_norm_gains = lax.dynamic_slice_in_dim(gain_rows, tensor_rank * gain_share, gain_share, 0)
    router_share = expert_total // tensor_count
    grad_router = lax.dynamic_slice_in_dim(router_rows, tensor_rank * router_share, router_share, 1)
    return (
        layer_out,
        grad_in.reshape(layer_in.shape),
        grad_norm_gains,
        grad_qkv,
        grad_qk_gains,
        grad_out_weight,
        grad_router,
        grad_expert_in,
        grad_expert_out,
    )


def contract_last(left, right):
    return lax.dot_general(
        left, right, (((1,), (1,)), ((), ())), preferred_element_type=jnp.float32
    )


def share_order(z):
    upper, odd = (z // 2, z % 2)
    return (z, z + 1 - 2 * upper, 2 + upper - 2 * odd, 3 - 3 * upper)


def share_turns(z):
    return (z, (z + 2) % 4, 3 - z, z + 1 - 2 * (z % 2))


def neighbours(w):
    wx, wy = (w + 1 - 2 * (w % 2), (w + 2) % 4)
    return (wx, wy, wx + wy - w)


def experts_kernel(
    experts,
    x_ref,
    grad_own,
    grad_x_low,
    grad_x_high,
    grad_y_low,
    grad_y_high,
    grad_low,
    grad_high,
    kept_ref,
    router_ref,
    in_ref,
    out_w_ref,
    x_out,
    grads_out,
    gated_out,
    both_out,
    moe_out,
    dx_own,
    x_tile,
    w_in,
    w_out,
    grads,
    gated,
    both,
    moe_tile,
    others,
    mine,
    sibs,
    from_x1,
    from_y1,
    from_y2,
    from_x2,
    from_z,
        own_sem,
        tile_sem,
        weight_sem,
        grads_sem,
        store_sem,
        send_z,
        send_x,
        send_y,
        send_c,
        recv,
        over_send,
        over_recv,
        sib_send,
        sib_recv,
        credit,
        one_send,
        one_recv,
        two_send,
        two_recv,
        end_send,
        end_recv,
):
    w, c, z = (lax.axis_index(a) for a in (WEIGHTS, CONTEXT, TENSOR))
    wx, wy, wd = neighbours(w)
    share, width = x_ref.shape
    half = width // 2
    lo, hi = (pl.ds(0, half), pl.ds(half, half))
    dev_x, dev_y, dev_c = ((wx, c, z), (wy, c, z), (w, 1 - c, z))
    turns = share_turns(z)
    hidden = out_w_ref.shape[1]
    group = w * 2 + c
    bf16, f32 = (jnp.bfloat16, jnp.float32)
    low, high = (pl.ds(0, half), pl.ds(half, half + 128))

    def loads():
        return [
            pltpu.make_async_copy(
                in_ref.at[n, g],
                w_in.at[:, pl.ds((2 * n + g) * hidden, hidden)],
                weight_sem.at[2 * n + g],
            )
            for n in range(2)
            for g in range(2)
        ] + [
            pltpu.make_async_copy(
                out_w_ref.at[n], w_out.at[pl.ds(n * hidden, hidden)], weight_sem.at[4 + n]
            )
            for n in range(2)
        ]

    for load in loads():
        load.start()
    keep = lambda: pltpu.make_async_copy(x_ref, x_out.at[w, c, z], own_sem)
    keep().start()

    grad_parts = (
        (grad_own, w, None),
        (grad_x_low, wx, lo),
        (grad_x_high, wx, hi),
        (grad_y_low, wy, lo),
        (grad_y_high, wy, hi),
        (grad_low, wd, lo),
        (grad_high, wd, hi),
    )

    def grad_place(cc, ww, cols):
        return grads_out.at[ww, cc] if cols is None else grads_out.at[ww, cc, :, :, cols]

    def over(i, cc):
        src, ww, cols = grad_parts[i]
        return pltpu.make_async_remote_copy(
            src_ref=src,
            dst_ref=grad_place(cc, ww, cols),
            send_sem=over_send.at[i],
            recv_sem=over_recv.at[i],
            device_id=dev_c,
            device_id_type=MESH,
        )

    barrier = pltpu.get_barrier_semaphore()
    around = [(w, c, (z + k) % 4) for k in range(1, 4)]
    for device in [dev_x, dev_y, dev_c] + around:
        pl.semaphore_signal(barrier, inc=1, device_id=device, device_id_type=MESH)
    pl.semaphore_wait(barrier, 6)


    def view(chunk, cols):
        zz, cc, ww = chunk
        return x_out.at[ww, cc, zz] if cols is None else x_out.at[ww, cc, zz, :, cols]

    def copy(src, chunk, cols, slot, sem, device):
        return pltpu.make_async_remote_copy(
            src_ref=src,
            dst_ref=view(chunk, cols),
            send_sem=sem[0].at[sem[1:]],
            recv_sem=recv.at[chunk[0], chunk[1], slot],
            device_id=device,
            device_id_type=MESH,
        )

    sent = []
    devices_z = ((w, c, z + 1), (w, c, z - 1))

    def start(chunk, cols, slot, sem, device, src=None):
        copy(view(chunk, cols) if src is None else src, chunk, cols, slot, sem, device).start()
        sent.append((chunk, cols, slot, sem, device))

    def arrived(chunk, cols, slot):
        copy(view(chunk, cols), chunk, cols, slot, (send_c, 0, 0), dev_c).wait_recv()

    def spread(j):
        chunk = (turns[j], c, w)
        src = x_ref if j == 0 else None
        start(chunk, None, 1, (send_x, j, 0), dev_x, src)
        start(chunk, None, 2, (send_y, j, 0), dev_y, src)
        start(chunk, None, 0, (send_c, j, 0), dev_c, src)

    def onward(j):
        chunk = (turns[j], c, w)

        def moved(side):
            src = x_ref if j == 0 else view(chunk, None)
            return copy(src, chunk, None, 0, (send_z, j, side), devices_z[side])

        return (
            ((turns[j] <= z) & (z < 3), functools.partial(moved, 0)),
            ((turns[j] >= z) & (z > 0), functools.partial(moved, 1)),
        )

    def along(j):
        for there, moved in onward(j):
            pl.when(there)(lambda: moved().start())

    def pass_on(j):
        arrived((turns[j], c, w), None, 0)
        along(j)

    def relay(j):
        from_x, from_y = ((turns[j], c, wx), (turns[j], c, wy))
        arrived(from_x, None, 1)
        start(from_x, lo, 3, (send_y, j, 1), dev_y)
        start(from_x, None, 1, (send_c, j, 1), dev_c)
        arrived(from_y, None, 2)
        start(from_y, hi, 4, (send_x, j, 1), dev_x)
        start(from_y, None, 2, (send_c, j, 2), dev_c)

    def across(j):
        chunk = (turns[j], c, wd)
        for cols, slot in ((lo, 3), (hi, 4)):
            arrived(chunk, cols, slot)
            start(chunk, cols, slot, (send_c, j, slot), dev_c)

    def sibling(j):
        for ww, cols, slot in ((w, None, 0), (wx, None, 1), (wy, None, 2), (wd, lo, 3), (wd, hi, 4)):
            arrived((turns[j], 1 - c, ww), cols, slot)


    def remote(src, dst, send, got, device):
        return pltpu.make_async_remote_copy(
            src_ref=src,
            dst_ref=dst,
            send_sem=send,
            recv_sem=got,
            device_id=device,
            device_id_type=MESH,
        )

    def to_sibling():
        return remote(others, sibs, sib_send, sib_recv, dev_c)

    def first_hops(j):
        moves = (
            (wx, low, from_x1.at[j, 0], dev_x),
            (wd, low, from_x1.at[j, 1], dev_x),
            (wy, high, from_y1.at[j, 0], dev_y),
            (wd, high, from_y1.at[j, 1], dev_y),
        )
        return [
            remote(
                mine.at[j % 2, ww, :, cols], dst, one_send.at[j, i], one_recv.at[j, i], device
            )
            for i, (ww, cols, dst, device) in enumerate(moves)
        ]

    def second_hops(j):
        moves = ((wy, low, from_y2.at[j], dev_y), (wx, high, from_x2.at[j], dev_x))
        return [
            remote(
                mine.at[j % 2, ww, :, cols], dst, two_send.at[j, i], two_recv.at[j, i], device
            )
            for i, (ww, cols, dst, device) in enumerate(moves)
        ]

    def last_hop(source, j):
        return remote(
            mine.at[j % 2, w],
            from_z.at[source],
            end_send.at[j],
            end_recv.at[source],
            (w, c, turns[j]),
        )

    def total(*terms):
        added = terms[0].astype(f32)
        for term in terms[1:]:
            added = added + term.astype(f32)
        return added

    def after_first(j):
        p = j % 2
        for moved in first_hops(j):
            moved.wait_recv()
        mine[p, wy, :, low] = total(mine[p, wy, :, low], from_x1[j, 1]).astype(bf16)
        mine[p, wx, :, high] = total(mine[p, wx, :, high], from_y1[j, 1]).astype(bf16)
        for moved in second_hops(j):
            moved.start()

    def after_second(j):
        p = j % 2
        for moved in second_hops(j):
            moved.wait_recv()
        mine[p, w, :, low] = total(mine[p, w, :, low], from_x1[j, 0], from_y2[j]).astype(bf16)
        mine[p, w, :, high] = total(mine[p, w, :, high], from_y1[j, 0], from_x2[j]).astype(bf16)
        if j == 0:
            from_z[z] = mine[p, w]
        else:
            last_hop(z, j).start()

    def all_sent(j):
        for moved in first_hops(j) + second_hops(j):
            moved.wait_send()
        if j > 0:
            last_hop(z, j).wait_send()


    code = turns[0] + 4 * turns[1] + 16 * turns[2] + 64 * turns[3]

    def tile_of(step):
        j = step // 2
        power = 1 + 3 * j + (9 * j * (j - 1)) // 2 + (27 * j * (j - 1) * (j - 2)) // 6
        return ((code // power) % 4, (c + 1 + step) % 2)

    def other_grads(step):
        zj, cc = tile_of(step)
        return pltpu.make_async_copy(grads_out.at[:, cc, zj], grads.at[0], grads_sem.at[7])

    def my_grads(step):
        zj, cc = tile_of(step)
        return [
            pltpu.make_async_copy(
                src.at[zj],
                grads.at[1, ww] if cols is None else grads.at[1, ww, :, cols],
                grads_sem.at[i],
            )
            for i, (src, ww, cols) in enumerate(grad_parts)
        ]

    def stores(step, own_tile):
        zj, cc = tile_of(step)
        pairs = [(gated, gated_out), (both, both_out)]
        pairs += [(grads.at[1], grads_out)] if own_tile else []
        return [
            pltpu.make_async_copy(src, dst.at[:, cc, zj], store_sem.at[i])
            for i, (src, dst) in enumerate(pairs)
        ]

    def moe_store(step):
        zj, cc = tile_of(step)
        return pltpu.make_async_copy(moe_tile, moe_out.at[:, cc, zj], store_sem.at[3])

    lanes = lax.broadcasted_iota(jnp.int32, (4 * share, 128), 1)

    def tile(step, own_tile, parity):
        zj, cc = tile_of(step)
        load = pltpu.make_async_copy(x_out.at[:, cc, zj], x_tile, tile_sem)
        load.start()
        if own_tile:
            for store in stores(step - 1, False):
                store.wait()
            for part in my_grads(step):
                part.wait()

            @pl.when(step < 7)
            def _():
                other_grads(step + 1).start()
        else:

            @pl.when(step > 0)
            def _():
                for store in stores(step - 1, True):
                    store.wait()

            for part in my_grads(step + 1):
                part.start()
            other_grads(step).wait()
        load.wait()
        rows = x_tile[...].reshape(4 * share, width)
        upstream = grads[1 if own_tile else 0].reshape(4 * share, width)
        logits = jnp.dot(rows, router_ref[...], preferred_element_type=f32)
        logits = jnp.where(lanes < experts, logits, -1e30)
        raised = jnp.exp(logits - jnp.max(logits, axis=1, keepdims=True))
        gates = raised / jnp.sum(raised, axis=1, keepdims=True)
        gates = gates * kept_ref[:, cc, zj].reshape(4 * share, 128).astype(f32)
        d_gate = jnp.zeros((4 * share, 128), f32)
        for n in range(2):
            here = lanes == group * 2 + n
            gate = jnp.sum(jnp.where(here, gates, 0.0), axis=1, keepdims=True)
            at = 2 * n * hidden
            gate_pre = jnp.dot(rows, w_in[:, at : at + hidden], preferred_element_type=f32)
            up_pre = jnp.dot(
                rows, w_in[:, at + hidden : at + 2 * hidden], preferred_element_type=f32
            )
            back = contract_last(upstream, w_out[n * hidden : (n + 1) * hidden, :])
            sigmoid = 1.0 / (1.0 + jnp.exp(-gate_pre))
            silu = gate_pre * sigmoid
            activated = silu * up_pre
            d_gate = jnp.where(here, jnp.sum(activated * back, axis=1, keepdims=True), d_gate)
            back = gate * back
            d_pre = back * up_pre * sigmoid * (1.0 + gate_pre * (1.0 - sigmoid))
            shape = (4, share, hidden)
            gated[:, :, n * hidden : (n + 1) * hidden] = (
                (gate * activated).astype(bf16).reshape(shape)
            )
            both[:, :, at : at + hidden] = d_pre.astype(bf16).reshape(shape)
            both[:, :, at + hidden : at + 2 * hidden] = (back * silu).astype(bf16).reshape(shape)
        for store in stores(step, own_tile):
            store.start()
        if own_tile:
            to_sibling().wait_recv()
            moe_store(step - 1).wait()
        else:

            @pl.when(step > 0)
            def _():
                to_sibling().wait_send()
                moe_store(step - 1).wait()

        def put(cols, count, value):
            value = value.reshape(4, share, count)
            if own_tile:
                value = value + sibs[:, :, cols].astype(f32)
                mine[parity, :, :, cols] = value.astype(bf16)
            else:
                others[:, :, cols] = value.astype(bf16)

        put(pl.ds(width, 128), 128, d_gate)
        d_rows = both[...].reshape(4 * share, 4 * hidden)
        g_rows = gated[...].reshape(4 * share, 2 * hidden)

        def columns(m, carried):
            cols = pl.ds(pl.multiple_of(m * 256, 256), 256)
            put(cols, 256, contract_last(d_rows, w_in[cols, :]))
            moe_tile[:, :, cols] = (
                jnp.dot(g_rows, w_out[:, cols], preferred_element_type=f32)
                .astype(bf16)
                .reshape(4, share, 256)
            )
            return carried

        lax.fori_loop(0, width // 256, columns, None)
        moe_store(step).start()

    def before_other(j):
        if j == 0:
            for i in range(7):
                over(i, c).start()
            along(0)
            spread(0)
            pass_on(3)
            pl.when((z > 0) & (z < 3))(lambda: pass_on(2))
            relay(0)
            pass_on(1)
            spread(1)
            keep().wait()
            for load in loads():
                load.wait()
            for i in range(7):
                over(i, 1 - c).wait_recv()
            other_grads(0).start()
        if j >= 2:
            after_second(j - 2)
        across(j)
        sibling(j)

    def before_mine(j):
        if j == 0:
            pl.when((z == 0) | (z == 3))(lambda: pass_on(2))
        if j + 2 < 4:
            spread(j + 2)
        if j + 1 < 4:
            relay(j + 1)
        if j >= 1:
            after_first(j - 1)
        if j >= 2:
            all_sent(j - 2)

    def round_of(j, carry):
        for k in range(4):
            pl.when(j == k)(functools.partial(before_other, k))
        tile(2 * j, False, None)

        @pl.when(j > 0)
        def _():
            pl.semaphore_wait(credit, 1)

        to_sibling().start()
        for k in range(4):
            pl.when(j == k)(functools.partial(before_mine, k))
        tile(2 * j + 1, True, j % 2)

        @pl.when(j < 3)
        def _():
            pl.semaphore_signal(credit, inc=1, device_id=dev_c, device_id_type=MESH)

        for k in range(4):

            @pl.when(j == k)
            def _():
                for moved in first_hops(k):
                    moved.start()

        return carry

    lax.fori_loop(0, 4, round_of, None)
    after_second(2)
    after_first(3)
    after_second(3)
    for store in stores(7, True):
        store.wait()
    moe_store(7).wait()
    to_sibling().wait_send()
    for k in range(1, 4):
        last_hop((z + k) % 4, 1).wait_recv()
    dx_own[...] = total(*(from_z[k] for k in range(4)))
    all_sent(2)
    all_sent(3)
    for i in range(7):
        over(i, c).wait_send()
    for chunk, cols, slot, sem, device in sent:
        copy(view(chunk, cols), chunk, cols, slot, sem, device).wait_send()
    for j in range(4):
        for there, moved in onward(j):
            pl.when(there)(lambda: moved().wait_send())


def experts_call(rows, grads, kept, router, expert_in, expert_out, experts):
    share, width = rows.shape
    hidden = expert_out.shape[1]
    blocks = (4, 2, 4, share)
    bf16, f32 = (jnp.bfloat16, jnp.float32)
    dma = pltpu.SemaphoreType.DMA
    anywhere, vmem = (pl.BlockSpec(memory_space=pl.ANY), pl.BlockSpec(memory_space=pltpu.VMEM))
    wide, half = (width + 128, width // 2)
    return pl.pallas_call(
        functools.partial(experts_kernel, experts),
        out_shape=tuple(
            jax.ShapeDtypeStruct(blocks + (n,), bf16)
            for n in (width, width, 2 * hidden, 4 * hidden, width)
        )
        + (jax.ShapeDtypeStruct((share, wide), f32),),
        in_specs=[anywhere] * 8 + [vmem, vmem, anywhere, anywhere],
        out_specs=(anywhere,) * 5 + (vmem,),
        scratch_shapes=[
            pltpu.VMEM((4, share, width), bf16),
            pltpu.VMEM((width, 4 * hidden), bf16),
            pltpu.VMEM((2 * hidden, width), bf16),
            pltpu.VMEM((2, 4, share, width), bf16),
            pltpu.VMEM((4, share, 2 * hidden), bf16),
            pltpu.VMEM((4, share, 4 * hidden), bf16),
            pltpu.VMEM((4, share, width), bf16),
            pltpu.VMEM((4, share, wide), bf16),
            pltpu.VMEM((2, 4, share, wide), bf16),
            pltpu.VMEM((4, share, wide), bf16),
            pltpu.VMEM((4, 2, share, half), bf16),
            pltpu.VMEM((4, 2, share, wide - half), bf16),
            pltpu.VMEM((4, share, half), bf16),
            pltpu.VMEM((4, share, wide - half), bf16),
            pltpu.VMEM((4, share, wide), bf16),
            dma,
            dma,
            dma((6,)),
            dma((8,)),
            dma((4,)),
            dma((4, 2)),
            dma((4, 2)),
            dma((4, 2)),
            dma((4, 5)),
            dma((4, 2, 5)),
            dma((7,)),
            dma((7,)),
            dma,
            dma,
            pltpu.SemaphoreType.REGULAR,
            dma((4, 4)),
            dma((4, 4)),
            dma((4, 2)),
            dma((4, 2)),
            dma((4,)),
            dma((4,)),
        ],
        compiler_params=pltpu.CompilerParams(
            collective_id=0, has_side_effects=True, vmem_limit_bytes=62 << 20
        ),
    )(rows, *grads, kept, router, expert_in, expert_out)


def finish_kernel(
    parts_ref,
    x_ref,
    scale_ref,
    gain_ref,
    d_hidden_ref,
    qkv_ref,
    out_ref,
    layer_ref,
    small_ref,
    rows_out,
    layer_out,
    qkv_out,
    out_out,
    small_out,
    own_rows,
    right_in,
    left_in,
    sums,
    from_c,
    from_x,
    from_y,
    from_z,
    mine,
    sibs,
    from_x1,
    from_y1,
    from_y2,
    from_x2,
    right_send,
    right_recv,
    left_send,
    left_recv,
    send_z,
    recv_z,
    small_send,
    small_recv,
    load_sem,
    sib_send,
    sib_recv,
    one_send,
    one_recv,
    two_send,
    two_recv,
):
    w, c, z = (lax.axis_index(a) for a in EVERYONE)
    wx, wy, wd = neighbours(w)
    dev_x, dev_y, dev_c = ((wx, c, z), (wy, c, z), (w, 1 - c, z))
    sides = ((w, c, z + 1), (w, c, z - 1))
    order = share_order(z)
    bf16, f32 = (jnp.bfloat16, jnp.float32)
    half = x_ref.shape[1] // 2
    lo, hi = (slice(0, half), slice(half, 2 * half))
    heads = out_ref.shape[3]
    both = ((qkv_ref, pl.ds(0, 3 * heads)), (out_ref, pl.ds(3 * heads, heads)))

    def loads():
        return [
            pltpu.make_async_copy(ref.at[:, c], mine.at[:, :, cols], load_sem.at[i])
            for i, (ref, cols) in enumerate(both)
        ]

    for load in loads():
        load.start()
    barrier = pltpu.get_barrier_semaphore()
    around = [(w, c, (z + k) % 4) for k in range(1, 4)]
    for device in [dev_x, dev_y, dev_c] + around:
        pl.semaphore_signal(barrier, inc=1, device_id=device, device_id_type=MESH)
    pl.semaphore_wait(barrier, 6)

    def remote(src, dst, send, got, device):
        return pltpu.make_async_remote_copy(
            src_ref=src,
            dst_ref=dst,
            send_sem=send,
            recv_sem=got,
            device_id=device,
            device_id_type=MESH,
        )


    def to_right(s):
        return remote(
            parts_ref.at[s], right_in.at[s], right_send.at[s], right_recv.at[s], sides[0]
        )

    def to_left(s):
        return remote(parts_ref.at[s], left_in.at[s], left_send.at[s], left_recv.at[s], sides[1])

    def pass_right(s):
        @pl.when(z < s)
        def _():
            @pl.when(z > 0)
            def _():
                to_right(s).wait_recv()
                parts_ref[s] = (parts_ref[s].astype(f32) + right_in[s].astype(f32)).astype(bf16)

            to_right(s).start()

    def pass_left(s):
        @pl.when(z > s)
        def _():
            @pl.when(z < 3)
            def _():
                to_left(s).wait_recv()
                parts_ref[s] = (parts_ref[s].astype(f32) + left_in[s].astype(f32)).astype(bf16)

            to_left(s).start()


    def to_sibling():
        return [
            remote(
                ref.at[:, 1 - c], sibs.at[:, :, cols], sib_send.at[i], sib_recv.at[i], dev_c
            )
            for i, (ref, cols) in enumerate(both)
        ]

    def first_hops():
        moves = (
            (wx, lo, from_x1.at[0], dev_x),
            (wd, lo, from_x1.at[1], dev_x),
            (wy, hi, from_y1.at[0], dev_y),
            (wd, hi, from_y1.at[1], dev_y),
        )
        return [
            remote(mine.at[ww, :, cols], dst, one_send.at[i], one_recv.at[i], device)
            for i, (ww, cols, dst, device) in enumerate(moves)
        ]

    def second_hops():
        moves = ((wy, lo, from_y2, dev_y), (wx, hi, from_x2, dev_x))
        return [
            remote(mine.at[ww, :, cols], dst, two_send.at[i], two_recv.at[i], device)
            for i, (ww, cols, dst, device) in enumerate(moves)
        ]

    def add(*terms):
        added = terms[0].astype(f32)
        for term in terms[1:]:
            added = added + term.astype(f32)
        return added

    def weights_first():
        for load in loads():
            load.wait()
        for part in to_sibling():
            part.wait_recv()
        for k in range(4):
            mine[k] = add(mine[k], sibs[k]).astype(bf16)
        for hop in first_hops():
            hop.start()

    def weights_second():
        for hop in first_hops():
            hop.wait_recv()
        mine[wy, :, lo] = add(mine[wy, :, lo], from_x1[1]).astype(bf16)
        mine[wx, :, hi] = add(mine[wx, :, hi], from_y1[1]).astype(bf16)
        for hop in second_hops():
            hop.start()

    def weights_last():
        for hop in second_hops():
            hop.wait_recv()
        low = add(mine[w, :, lo], from_x1[0], from_y2[...])
        high = add(mine[w, :, hi], from_y1[0], from_x2[...])
        for k in range(4):
            part = (low if (k + 1) * heads <= half else high)[
                :, k * heads % half : k * heads % half + heads
            ]
            if k < 3:
                qkv_out[k] = part
            else:
                out_out[...] = part


    spread = ((own_rows, rows_out), (layer_ref, layer_out))

    def moved(i, j, side):
        own, whole = spread[i]
        return remote(
            own if j == 0 else whole.at[order[j]],
            whole.at[order[j]],
            send_z.at[i, j, side],
            recv_z.at[i, order[j]],
            sides[side],
        )

    def onward(j):
        return (((order[j] <= z) & (z < 3), 0), ((order[j] >= z) & (z > 0), 1))

    def along(i, j):
        for there, side in onward(j):
            pl.when(there)(lambda: moved(i, j, side).start())

    def passed_on(i, j):
        moved(i, j, 0).wait_recv()
        along(i, j)


    def small(i, src, dst, device):
        return remote(src, dst, small_send.at[i], small_recv.at[i], device)

    def small_sibling(k):
        return small(k, small_ref.at[k, 1 - c], from_c.at[k], dev_c)

    def small_x(k):
        return small(4 + k, sums.at[(wx, wd)[k]], from_x.at[k], dev_x)

    def small_y():
        return small(6, sums.at[wy], from_y, dev_y)

    def small_z(target, source):
        return remote(
            sums.at[w],
            from_z.at[source],
            small_send.at[7 + target],
            small_recv.at[7 + source],
            (w, c, target),
        )

    for part in to_sibling():
        part.start()
    inner = (z > 0) & (z < 3)
    pl.when(inner)(lambda: along(1, 0))
    for s in range(3):
        pass_right(3 - s)
        pass_left(s)
        if s == 0:
            passed_on(1, 1)
    pl.when((z == 0) | (z == 3))(lambda: along(1, 0))
    weights_first()
    d_normed = parts_ref[z].astype(f32)
    right_in[0] = jnp.zeros(right_in.shape[1:], bf16)
    left_in[3] = jnp.zeros(left_in.shape[1:], bf16)

    @pl.when(z > 0)
    def _():
        to_right(z).wait_recv()

    @pl.when(z < 3)
    def _():
        to_left(z).wait_recv()

    d_normed = d_normed + right_in[z].astype(f32) + left_in[z].astype(f32)
    scale = scale_ref[...]
    unit = x_ref[...].astype(f32) * scale
    scaled = gain_ref[...] * d_normed
    shift = jnp.mean(scaled * unit, axis=1, keepdims=True)
    own_rows[...] = (d_hidden_ref[...] + scale * (scaled - unit * shift)).astype(bf16)
    along(0, 0)
    rows_out[z] = own_rows[...]
    layer_out[z] = layer_ref[...]
    d_gain = jnp.sum(d_normed * unit, axis=0, keepdims=True)
    for k in range(8):
        for i in range(2):
            at = (2 * k + i) * 128
            small_ref[k // 2, k % 2, i : i + 1, :] = d_gain[:, at : at + 128]
    for k in range(4):
        small_sibling(k).start()
    for k in range(4):
        small_sibling(k).wait_recv()
        sums[k] = small_ref[k, c] + from_c[k]
    for k in range(2):
        small_x(k).start()
    weights_second()
    for k in range(2):
        small_x(k).wait_recv()
    sums[w] = sums[w] + from_x[0]
    sums[wy] = sums[wy] + from_x[1]
    small_y().start()
    passed_on(1, 2)
    passed_on(0, 1)
    small_y().wait_recv()
    sums[w] = sums[w] + from_y[...]
    for k in range(1, 4):
        small_z((z + k) % 4, z).start()
    passed_on(1, 3)
    passed_on(0, 2)
    weights_last()
    for k in range(1, 4):
        small_z(z, (z + k) % 4).wait_recv()
    from_z[z] = sums[w]
    small_out[...] = add(*(from_z[k] for k in range(4)))
    passed_on(0, 3)
    for s in range(3):

        @pl.when(z < 3 - s)
        def _():
            to_right(3 - s).wait_send()

        @pl.when(z > s)
        def _():
            to_left(s).wait_send()

    for hop in to_sibling() + first_hops() + second_hops():
        hop.wait_send()
    for k in range(4):
        small_sibling(k).wait_send()
    for k in range(2):
        small_x(k).wait_send()
    small_y().wait_send()
    for k in range(1, 4):
        small_z((z + k) % 4, z).wait_send()
    for i in range(2):
        for j in range(4):
            for there, side in onward(j):
                pl.when(there)(lambda: moved(i, j, side).wait_send())


def finish_call(parts, rows, scale, gain, d_hidden, d_qkv, d_out, layer, small):
    dma = pltpu.SemaphoreType.DMA
    anywhere, vmem = (pl.BlockSpec(memory_space=pl.ANY), pl.BlockSpec(memory_space=pltpu.VMEM))
    share, width = rows.shape
    count, heads = d_out.shape[2:]
    half = width // 2
    block = small.shape[2:]
    bf16, f32 = (jnp.bfloat16, jnp.float32)

    def body(*refs):
        ins, outs, rest = (refs[:9], refs[9:14], refs[14:])
        parts_in, small_in = (ins[0], ins[8])
        parts_own, small_own = rest[:2]
        parts_own[...] = parts_in[...]
        small_own[...] = small_in[...]
        finish_kernel(parts_own, *ins[1:8], small_own, *outs, *rest[2:])

    return pl.pallas_call(
        body,
        out_shape=(
            jax.ShapeDtypeStruct((4, share, width), bf16),
            jax.ShapeDtypeStruct((4, share, width), bf16),
            jax.ShapeDtypeStruct((3, count, heads), f32),
            jax.ShapeDtypeStruct((count, heads), f32),
            jax.ShapeDtypeStruct(block, f32),
        ),
        in_specs=[vmem] * 5 + [anywhere, anywhere, vmem, vmem],
        out_specs=(vmem,) * 5,
        scratch_shapes=[
            pltpu.VMEM((4, share, width), bf16),
            pltpu.VMEM((4, 2) + block, f32),
            pltpu.VMEM((share, width), bf16),
            pltpu.VMEM((4, share, width), bf16),
            pltpu.VMEM((4, share, width), bf16),
            pltpu.VMEM((4,) + block, f32),
            pltpu.VMEM((4,) + block, f32),
            pltpu.VMEM((2,) + block, f32),
            pltpu.VMEM(block, f32),
            pltpu.VMEM((4,) + block, f32),
            pltpu.VMEM((4, count, width), bf16),
            pltpu.VMEM((4, count, width), bf16),
            pltpu.VMEM((2, count, half), bf16),
            pltpu.VMEM((2, count, half), bf16),
            pltpu.VMEM((count, half), bf16),
            pltpu.VMEM((count, half), bf16),
            dma((4,)),
            dma((4,)),
            dma((4,)),
            dma((4,)),
            dma((2, 4, 2)),
            dma((2, 4)),
            dma((11,)),
            dma((11,)),
            dma((2,)),
            dma((2,)),
            dma((2,)),
            dma((4,)),
            dma((4,)),
            dma((2,)),
            dma((2,)),
        ],
        compiler_params=pltpu.CompilerParams(
            collective_id=1, has_side_effects=True, vmem_limit_bytes=48 << 20
        ),
    )(parts, rows, scale, gain, d_hidden, d_qkv, d_out, layer, small)


def swapped(rows, flip):
    return lax.ppermute(rows, WEIGHTS, [(k, k ^ flip) for k in range(4)])


def grads_around(rows, x_low, y_high, share):
    half = rows.shape[1] // 2
    parts = (
        rows,
        x_low,
        swapped(rows[:, half:], 1),
        swapped(rows[:, :half], 2),
        y_high,
        swapped(x_low, 2),
        swapped(y_high, 1),
    )
    return [part.reshape(-1, share, part.shape[1]) for part in parts]


def shares_around(rows):
    z = lax.axis_index(TENSOR)
    parts = [rows] + [
        lax.ppermute(rows, TENSOR, [(k, (k + step) % 4) for k in range(4)]) for step in (1, 3, 2)
    ]
    whole = jnp.zeros((4,) + rows.shape, rows.dtype)
    for part, step in zip(parts, (0, 1, 3, 2)):
        whole = lax.dynamic_update_index_in_dim(whole, part, (z + 4 - step) % 4, 0)
    return whole.reshape((-1,) + rows.shape[1:])


def gathered(rows, axes):
    return lax.all_gather(rows, axes, axis=0, tiled=True)


def scattered(rows, axes):
    return lax.psum_scatter(rows, axes, scatter_dimension=0, tiled=True)


def fit_rows(values, rows):
    flat = values.reshape(-1)
    columns = -(-flat.shape[0] // rows)
    return jnp.pad(flat, (0, rows * columns - flat.shape[0])).reshape(rows, columns)


def per_device_dense(
    layer_in,
    norm_gains,
    qkv_weight,
    qk_gains,
    out_weight,
    router,
    expert_in,
    expert_out,
    grad_out,
    segments,
    routes,
    route_order,
):
    group = GROUP
    everyone = EVERYONE
    group_count = lax.axis_size(group)
    tensor_count = lax.axis_size(TENSOR)
    context_rank = lax.axis_index(CONTEXT)
    tensor_rank = lax.axis_index(TENSOR)
    seq_count, half_len, model_width = layer_in.shape
    token_count = seq_count * half_len
    top_count = routes.shape[2]
    weight_rows, _, head_width = qkv_weight.shape
    expert_total = router.shape[1]
    local_experts = expert_in.shape[0]
    hidden_width = expert_in.shape[3]
    head_rows, _, local_heads = qk_gains.shape
    head_size = head_rows * group_count
    share = token_count // tensor_count
    bf16, f32 = jnp.bfloat16, jnp.float32

    capacity = token_count * top_count * 9 // (8 * expert_total)
    routed, slot_of = pair_slots(
        routes.reshape(token_count, top_count),
        route_order.reshape(token_count, top_count),
        expert_total,
    )
    kept = routed & (slot_of < capacity)

    front_small = jnp.concatenate(
        [norm_gains, fit_rows(qk_gains, weight_rows)], axis=1
    )
    front = gathered(
        jnp.concatenate([qkv_weight.reshape(weight_rows, -1), front_small], axis=1), group
    )
    own_grads = grad_out.reshape(token_count, model_width)
    front, own_grads = lax.optimization_barrier((front, own_grads))
    half = model_width // 2
    x_low, y_high = (swapped(own_grads[:, :half], 1), swapped(own_grads[:, half:], 2))
    back_small = jnp.concatenate(
        [router, fit_rows(kept.astype(bf16), weight_rows)], axis=1
    )
    back = gathered(jnp.concatenate([out_weight, back_small], axis=1), group)
    qkv_full = front[:, : 3 * head_width]
    gain_full = front[:, 3 * head_width : 3 * head_width + 2].astype(f32)
    gain_attn, gain_ffn = (gain_full[:, 0], gain_full[:, 1])
    qk_gain_full = (
        front[:, 3 * head_width + 2 :]
        .reshape(group_count, -1)[:, : head_rows * 2 * local_heads]
        .reshape(head_size, 2, local_heads)
        .astype(f32)
    )
    query_gain = qk_gain_full[:, 0, :].T.reshape(-1)
    key_gain = qk_gain_full[:, 1, :].T.reshape(-1)
    out_full = back[:, :head_width]
    router_full = back[:, head_width : head_width + expert_total]
    kept_all = (
        back[:, head_width + expert_total :]
        .reshape(group_count, -1)[:, : expert_total * token_count]
        .reshape(group_count, expert_total, token_count)
    )
    inv_root = 1.0 / math.sqrt(head_size)
    residual = layer_in.reshape(token_count, model_width).astype(f32)
    scale_one = lax.rsqrt(jnp.mean(residual * residual, axis=1, keepdims=True) + epsilon)
    normed_one = (residual * scale_one * gain_attn).astype(bf16)
    projected = jnp.dot(normed_one, qkv_full, preferred_element_type=f32)
    query_raw = projected[:, :head_width]
    key_raw = projected[:, head_width : 2 * head_width]
    value_raw = projected[:, 2 * head_width :]
    square_sums = row_sums(
        jnp.stack(
            [jnp.sum(query_raw * query_raw, axis=1), jnp.sum(key_raw * key_raw, axis=1)], axis=1
        )
    )
    query_scale = lax.rsqrt(square_sums[:, 0:1] / model_width + epsilon)
    key_scale = lax.rsqrt(square_sums[:, 1:2] / model_width + epsilon)
    heads_shape = (seq_count, half_len, local_heads, head_size)
    query_hat = (query_raw * query_scale * query_gain).reshape(heads_shape)
    key_hat = (key_raw * key_scale * key_gain).reshape(heads_shape)
    query_pos = context_rank * half_len + jnp.arange(half_len, dtype=jnp.int32)
    cosine_table, sine_table = rotary_tables(query_pos, head_size)
    cosine_table = cosine_table[None, :, None, :]
    sine_table = sine_table[None, :, None, :]
    query_rot = (query_hat * cosine_table + rotate_half(query_hat) * sine_table).astype(bf16)
    key_rot = (key_hat * cosine_table + rotate_half(key_hat) * sine_table).astype(bf16)
    value_low = value_raw.astype(bf16).reshape(heads_shape)
    key_prev, value_prev = passed_along((key_rot, value_low), CONTEXT, 1)
    all_keys = jnp.concatenate([key_prev, key_rot], axis=1)
    all_values = jnp.concatenate([value_prev, value_low], axis=1)
    key_pos = jnp.concatenate([query_pos - half_len, query_pos])
    seg_query = lax.dynamic_slice_in_dim(segments, context_rank * half_len, half_len, 1)
    seg_prev = lax.dynamic_slice_in_dim(
        segments, jnp.maximum(context_rank - 1, 0) * half_len, half_len, 1
    )
    seg_keys = jnp.concatenate([seg_prev, seg_query], axis=1)
    causal = (key_pos[None, :] >= 0) & (key_pos[None, :] <= query_pos[:, None])
    allowed = causal[None] & (seg_query[:, :, None] == seg_keys[:, None, :])

    def score_block(queries, key_rows):
        raw_scores = (
            jnp.einsum(BY_SCORE, queries, key_rows, preferred_element_type=f32) * inv_root
        )
        return jnp.where(allowed[:, None], raw_scores, -1e30)

    scores = score_block(query_rot, all_keys)
    row_max = jnp.max(scores, axis=-1, keepdims=True)
    exponent = jnp.exp(scores - row_max)
    row_total = jnp.sum(exponent, axis=-1, keepdims=True)
    log_total = row_max + jnp.log(row_total)
    attn_probs = (exponent / row_total).astype(bf16)
    attended = jnp.einsum(BY_QUERY, attn_probs, all_values, preferred_element_type=f32)
    attended_low = attended.reshape(token_count, -1).astype(bf16)
    x_low, y_high, attended_low = lax.optimization_barrier((x_low, y_high, attended_low))
    around = grads_around(own_grads, x_low, y_high, share)
    attn_partial = jnp.einsum("tf,df->td", attended_low, out_full, preferred_element_type=f32)

    own_rows = lambda rows: lax.dynamic_slice_in_dim(rows, tensor_rank * share, share, 0)
    residual_own = own_rows(residual)
    hidden = residual_own + scattered(attn_partial.astype(bf16), TENSOR).astype(f32)
    scale_two = lax.rsqrt(jnp.mean(hidden * hidden, axis=1, keepdims=True) + epsilon)
    unit_two = hidden * scale_two
    normed_two = (unit_two * gain_ffn).astype(bf16)
    upstream = own_rows(grad_out.reshape(token_count, model_width)).astype(f32)

    pad_experts = lambda rows: jnp.pad(rows, ((0, 0), (0, 128 - expert_total)))
    kept_rows = kept_all.transpose(0, 2, 1).reshape(-1, expert_total)
    normed_all, grads_all, gated, d_both, moe_all, d_sums = experts_call(
        normed_two,
        around,
        pad_experts(kept_rows).reshape(4, 2, 4, share, 128),
        pad_experts(router_full),
        expert_in,
        expert_out,
        expert_total,
    )
    normed_all, grads_all, gated, d_both, moe_all = (
        rows.reshape(group_count * token_count, -1)
        for rows in (normed_all, grads_all, gated, d_both, moe_all)
    )
    moe_plane = scattered(moe_all, group)
    kept_own = own_rows(kept.T).astype(f32)
    probs_own = jax.nn.softmax(
        jnp.dot(normed_two, router_full, preferred_element_type=f32), axis=1
    )
    d_probs = d_sums[:, model_width : model_width + expert_total] * kept_own
    d_logits = (
        probs_own * (d_probs - jnp.sum(probs_own * d_probs, axis=1, keepdims=True))
    ).astype(bf16)
    d_normed_two = d_sums[:, :model_width] + jnp.dot(
        d_logits, router_full.T, preferred_element_type=f32
    )
    d_router = jnp.dot(normed_two.T, d_logits, preferred_element_type=f32)
    d_gain_ffn = jnp.sum(d_normed_two * unit_two, axis=0)
    scaled_ffn = gain_ffn * d_normed_two
    d_hidden = upstream + scale_two * (
        scaled_ffn - unit_two * jnp.mean(scaled_ffn * unit_two, axis=1, keepdims=True)
    )
    d_hidden_own, normed_all, grads_all, gated, d_both = lax.optimization_barrier(
        (d_hidden.astype(bf16), normed_all, grads_all, gated, d_both)
    )
    d_hidden_low = shares_around(d_hidden_own)
    grad_expert_in = (
        jnp.dot(normed_all.T, d_both, preferred_element_type=f32)
        .reshape(model_width, local_experts, 2, hidden_width)
        .transpose(1, 2, 0, 3)
    )
    grad_expert_out = jnp.dot(gated.T, grads_all, preferred_element_type=f32).reshape(
        expert_out.shape
    )
    d_hidden_low, grad_expert_in, grad_expert_out = lax.optimization_barrier(
        (d_hidden_low, grad_expert_in, grad_expert_out)
    )

    d_attended = (
        jnp.dot(d_hidden_low, out_full, preferred_element_type=f32)
        .astype(bf16)
        .reshape(heads_shape)
    )
    d_out_weight = jnp.einsum("td,tf->df", d_hidden_low, attended_low, preferred_element_type=f32)
    probs_again = jnp.exp(score_block(query_rot, all_keys) - log_total)
    probs_again_low = probs_again.astype(bf16)
    d_probs_att = jnp.einsum(
        BY_SCORE, d_attended, all_values, preferred_element_type=f32
    )
    d_values_all = jnp.einsum(
        BY_KEY, probs_again_low, d_attended, preferred_element_type=f32
    )
    row_dot = jnp.sum(probs_again * d_probs_att, axis=-1, keepdims=True)
    d_scores = (probs_again * (d_probs_att - row_dot)).astype(bf16)
    d_query_rot = (
        jnp.einsum(BY_QUERY, d_scores, all_keys, preferred_element_type=f32) * inv_root
    )
    d_keys_all = (
        jnp.einsum(BY_KEY, d_scores, query_rot, preferred_element_type=f32) * inv_root
    )
    back_key, back_value = (
        passed_along(d_keys_all[:, :half_len].astype(bf16), CONTEXT, -1).astype(f32),
        passed_along(d_values_all[:, :half_len].astype(bf16), CONTEXT, -1).astype(f32),
    )
    d_key_rot = d_keys_all[:, half_len:] + back_key
    d_value = (d_values_all[:, half_len:] + back_value).reshape(token_count, -1)
    d_query_hat = (d_query_rot * cosine_table + rotate_back(d_query_rot * sine_table)).reshape(
        token_count, -1
    )
    d_key_hat = (d_key_rot * cosine_table + rotate_back(d_key_rot * sine_table)).reshape(
        token_count, -1
    )
    centre_own = (
        jnp.stack(
            [
                jnp.sum(query_gain * d_query_hat * query_raw, axis=1),
                jnp.sum(key_gain * d_key_hat * key_raw, axis=1),
            ],
            axis=1,
        )
    )
    centre, moe_plane = lax.optimization_barrier((row_sums(centre_own), moe_plane))
    moe_own = scattered(moe_plane, TENSOR).astype(f32)
    d_query_raw = (
        query_scale * query_gain * d_query_hat
        - query_raw * (query_scale**3 / model_width) * centre[:, 0:1]
    )
    d_key_raw = (
        key_scale * key_gain * d_key_hat - key_raw * (key_scale**3 / model_width) * centre[:, 1:2]
    )
    d_query_gain = (
        jnp.sum(d_query_hat * query_raw * query_scale, axis=0).reshape(local_heads, head_size).T
    )
    d_key_gain = jnp.sum(d_key_hat * key_raw * key_scale, axis=0).reshape(local_heads, head_size).T
    d_qk_gains = jnp.stack([d_query_gain, d_key_gain], axis=1)
    d_projected = jnp.concatenate([d_query_raw, d_key_raw, d_value], axis=1).astype(bf16)
    d_normed_parts = jnp.einsum(
        "tf,df->td", d_projected, qkv_full, preferred_element_type=f32
    ).astype(bf16)
    d_qkv = jnp.einsum("td,tf->df", normed_one, d_projected, preferred_element_type=f32)

    own_slot = (jnp.arange(tensor_count) == tensor_rank).astype(f32)[None, :, None]
    lines = lambda values: values.reshape(group_count, -1, 128)
    small = jnp.concatenate(
        [
            jnp.zeros((group_count, weight_rows // 128, 128), f32),
            lines(d_gain_ffn),
            lines(d_router),
            lines(d_qk_gains) * own_slot,
        ],
        axis=1,
    )
    d_normed_parts, d_qkv, d_out_weight, moe_own = lax.optimization_barrier(
        (d_normed_parts, d_qkv.astype(bf16), d_out_weight.astype(bf16), moe_own)
    )
    grad_in, layer_out, grad_qkv, grad_out_weight, small = finish_call(
        d_normed_parts.reshape(tensor_count, share, model_width),
        own_rows(layer_in.reshape(token_count, model_width)),
        own_rows(scale_one),
        gain_attn[None],
        d_hidden,
        d_qkv.reshape(4, 2, weight_rows, -1),
        d_out_weight.reshape(4, 2, weight_rows, -1),
        (hidden + moe_own).astype(bf16),
        small.reshape((4, 2) + small.shape[1:]),
    )
    grad_in = grad_in.astype(f32).reshape(layer_in.shape)
    layer_out = layer_out.reshape(layer_in.shape)
    grad_qkv = grad_qkv.transpose(1, 0, 2)
    lines_of = weight_rows // 128
    gain_share = weight_rows // tensor_count
    router_share = expert_total // tensor_count
    router_lines = weight_rows * expert_total // 128
    part_of = lambda rows, count, axis: lax.dynamic_slice_in_dim(
        rows, tensor_rank * count, count, axis
    )
    gains = small[: 2 * lines_of].reshape(2, weight_rows)
    routers = small[2 * lines_of : 2 * lines_of + router_lines].reshape(weight_rows, expert_total)
    qk_lines = small[2 * lines_of + router_lines :]
    return (
        layer_out,
        grad_in,
        part_of(gains, gain_share, 1).T,
        grad_qkv,
        part_of(qk_lines, 1, 0).reshape(head_rows, 2, local_heads),
        grad_out_weight,
        part_of(routers, router_share, 1),
        grad_expert_in,
        grad_expert_out,
    )


def solution(mesh):
    placed = (
        P(WEIGHTS, CONTEXT, None),
        P(GROUP, None),
        P(GROUP, None, TENSOR),
        P(GROUP, None, TENSOR),
        P(GROUP, TENSOR),
        P(GROUP, None),
        P(GROUP, None, None, TENSOR),
        P(GROUP, TENSOR, None),
        P(WEIGHTS, CONTEXT, None),
        P(WEIGHTS, None),
        P(WEIGHTS, CONTEXT, None),
        P(WEIGHTS, CONTEXT, None),
    )
    axes = tuple(mesh.shape[axis] for axis in EVERYONE)

    def per_device(*blocks):
        dense = axes == (4, 2, 4) and blocks[5].shape[1] <= 2 * blocks[10].shape[2]
        return (per_device_dense if dense else per_device_slots)(*blocks)

    return jax.shard_map(
        per_device,
        mesh=mesh,
        in_specs=placed,
        out_specs=(
            P(WEIGHTS, CONTEXT, None),
            P(WEIGHTS, CONTEXT, None),
            P(EVERYONE, None),
            P(GROUP, None, TENSOR),
            P(GROUP, None, TENSOR),
            P(GROUP, TENSOR),
            P(GROUP, TENSOR),
            P(GROUP, None, None, TENSOR),
            P(GROUP, TENSOR, None),
        ),
        check_vma=False,
    )
```
